32 devices in a mesh: groups: 2 (over y), seq: 4 (over z), chan: 4 (over x, core).
Axes of the slice: x: 2, y: 2, z: 4, core: 2. Of those that a mesh axis runs over, the one named last changes fastest.
Arguments:
- tokens: int32 [6144], P(('groups', 'seq')), parts along dimension 0, may hold values from 0 to 3
- cotangent: bfloat16 [6144, 768], P(('groups', 'seq'), 'chan'), parts along dimension 0, may hold values from -6 to 6
- embed: bfloat16 [4, 768], P(None, 'chan'), may hold values from -6 to 6
- taps: bfloat16 [2, 5, 768], P(None, None, 'chan'), may hold values from -2.5 to 2.5
- mix: bfloat16 [2, 768, 768], P(None, None, 'chan'), may hold values from -0.21875 to 0.21875
- dilations: int32 [2], replicated, may hold values from 1 to 8, as said below
Outputs:
- output: bfloat16 [6144, 768], P(('groups', 'seq'), 'chan'), parts along dimension 0
- grad_mix: float32 [4, 768, 768], P('groups', None, 'chan'), parts along dimension 0
- grad_taps: float32 [4, 5, 768], P('groups', None, 'chan'), parts along dimension 0
- grad_embed: float32 [8, 768], P('groups', 'chan'), parts along dimension 0
The draws below stay inside these ranges and needn't reach their ends.
There are 2 independent parts, one for each index of `groups`. The reference program is written for one: setup_inputs(seed, part) draws one part's arguments, and reference() takes and returns one part's arrays. A program takes and returns all parts, laid end to end along the dimension named above; an argument that names none is the same for every part. Nothing has to cross between parts.
Inputs may be any that keep to these rules, and one draw needn't show every extreme that they name: `dilations`: each block's dilation lies in 1 to 8, and at least one block has exactly 8.
All inputs are finite; a program needn't handle non-finite values.
Results may differ from the reference program's by a relative error of at most 0.025.
Values may be sent and summed in bfloat16 or wider, within the bound.
No kernel may reach another device: no remote copies, remote signals or barrier semaphores. Data moves between devices by JAX's collectives and lax.ppermute only.
A program may use at most 64 MiB of HBM per device.

```python
import math
import jax
import jax.numpy as jnp
from jax import lax

C = 768
TAPS = 5
BASES = 4
BLOCKS = 2
DMAX = 8
LENGTH = 3072
N_CHAN = 4


def draw_dilations(key, part):
    first_key, second_key = jax.random.split(key)
    rates_drawn = jax.random.randint(first_key, (BLOCKS,), 1, DMAX + 1)
    chosen = jax.random.randint(second_key, (), 0, BLOCKS)
    return jnp.where(jnp.arange(BLOCKS) == chosen, DMAX, rates_drawn).astype(jnp.int32)


def plant(drawn, own_key, least, largest):
    shape = drawn.shape
    place = [jax.random.randint(jax.random.fold_in(own_key, axis), (), 0, shape[axis]) for axis in range(len(shape))]
    drawn = drawn.at[tuple(place)].set(least)
    longest = shape.index(max(shape))
    place[longest] = (place[longest] + 1) % shape[longest]
    return drawn.at[tuple(place)].set(largest)


def level_of(rng, dims, pieces, low, top_value):
    loudness = 1.0
    for position, parts in pieces:
        draws = jax.random.uniform(jax.random.fold_in(jax.random.fold_in(rng, 6), position), (parts,), jnp.float32, low / len(pieces), top_value / len(pieces))
        loudness = loudness * jnp.repeat(jnp.exp(draws), dims[position] // parts).reshape((-1,) + (1,) * (len(dims) - 1 - position))
    return loudness


def centred(key, extent, width, most, cuts=(), kind=jnp.bfloat16):
    values = width * jax.random.normal(key, extent, jnp.float32)
    if cuts:
        values = values * level_of(key, extent, cuts, -0.22, 0.18)
    return jnp.clip(values, -most, most).astype(kind)


def setup_inputs(seed: int = 0, part: int = 0) -> dict:
    arg_keys = jax.random.split(jax.random.key(seed), 7)
    part_splits = jax.random.split(jax.random.fold_in(arg_keys[6], part), 7)
    tokens = plant(jax.random.randint(part_splits[0], (LENGTH,), 0, 4), jax.random.fold_in(part_splits[0], 1), 0, 3).astype(jnp.int32)
    cotangent = centred(part_splits[1], (LENGTH, C), 1.0, 6.0, ((0, 4), (1, 4)))
    embed = centred(arg_keys[2], (BASES, C), 1.0, 6.0, ((1, 4),))
    taps = centred(arg_keys[3], (BLOCKS, TAPS, C), TAPS ** -0.5, 2.5, ((2, 4),))
    mix = centred(arg_keys[4], (BLOCKS, C, C), C ** -0.5, 0.21875, ((2, 4),))
    dilations = draw_dilations(jax.random.fold_in(arg_keys[6], 71), part)
    return dict(tokens=tokens, cotangent=cotangent, embed=embed, taps=taps, mix=mix, dilations=dilations)


gelu_scale = math.sqrt(2.0 / math.pi)
cubic_term = 0.044715

def gelu_value(inputs):
    inner = gelu_scale * (inputs + cubic_term * inputs * inputs * inputs)
    return 0.5 * inputs * (1.0 + jnp.tanh(inner))

def gelu_slope(inputs):
    tangent = jnp.tanh(gelu_scale * (inputs + cubic_term * inputs * inputs * inputs))
    return 0.5 * (1.0 + tangent) + 0.5 * inputs * (1.0 - tangent * tangent) * gelu_scale * (1.0 + 3.0 * cubic_term * inputs * inputs)

def taps_apply(padded, taps_block, dilation, rows_out, orient):
    reach = TAPS // 2 * DMAX
    result = jnp.zeros((rows_out, padded.shape[1]), jnp.float32)
    for offset in range(TAPS):
        first = (reach + orient * (offset - TAPS // 2) * dilation).astype(jnp.int32)
        window = lax.dynamic_slice_in_dim(padded, first, rows_out, 0).astype(jnp.float32)
        result = result + taps_block[offset].astype(jnp.float32)[None, :] * window
    return result

def reference(tokens, cotangent, embed, taps, mix, dilations):
    reach = TAPS // 2 * DMAX
    length = tokens.shape[0]
    channels = embed.shape[1]
    block_cols = channels // N_CHAN
    current = jnp.zeros((length, channels), jnp.float32)
    for letter in range(BASES):
        current = current + jnp.where(tokens[:, None] == letter, embed[letter].astype(jnp.float32)[None, :], 0.0)
    current = current.astype(jnp.bfloat16)
    saved = []
    for layer_index in range(BLOCKS):
        dilation = dilations[layer_index]
        padded = jnp.pad(current, ((reach, reach), (0, 0)))
        conv_out = taps_apply(padded, taps[layer_index], dilation, length, 1).astype(jnp.bfloat16)
        mixed = (conv_out.astype(jnp.float32) + conv_out[::-1, ::-1].astype(jnp.float32)).astype(jnp.bfloat16)
        preact = jnp.dot(mixed, mix[layer_index], preferred_element_type=jnp.float32)
        saved.append((padded, mixed, preact, dilation))
        current = (current.astype(jnp.float32) + gelu_value(preact)).astype(jnp.bfloat16)
    output = current
    upstream = cotangent.astype(jnp.float32) * (1.0 / math.sqrt(length))
    mix_grads = []
    taps_grads = []
    for layer_index in reversed(range(BLOCKS)):
        padded, mixed, preact, dilation = saved[layer_index]
        slope_in = (upstream * gelu_slope(preact)).astype(jnp.bfloat16)
        mix_grads.insert(0, jnp.dot(mixed.T, slope_in, preferred_element_type=jnp.float32))
        summed = jnp.zeros((length, channels), jnp.float32)
        for shard_index in range(N_CHAN):
            lower = shard_index * block_cols
            product = jnp.dot(slope_in[:, lower:lower + block_cols], mix[layer_index][:, lower:lower + block_cols].T, preferred_element_type=jnp.float32)
            summed = summed + lax.optimization_barrier(product.astype(jnp.bfloat16)).astype(jnp.float32)
        mix_back = lax.optimization_barrier(summed.astype(jnp.bfloat16)).astype(jnp.float32)
        folded = mix_back + mix_back[::-1, ::-1]
        rows_taps = []
        for offset in range(TAPS):
            first = (reach + (offset - TAPS // 2) * dilation).astype(jnp.int32)
            window = lax.dynamic_slice_in_dim(padded, first, length, 0).astype(jnp.float32)
            rows_taps.append(lax.optimization_barrier(jnp.sum(folded * window, axis=0)))
        taps_grads.insert(0, jnp.stack(rows_taps))
        grad_padded = jnp.pad(folded, ((reach, reach), (0, 0)))
        upstream = upstream + taps_apply(grad_padded, taps[layer_index], dilation, length, -1)
    masks = (jnp.arange(BASES, dtype=jnp.int32)[:, None] == tokens[None, :]).astype(jnp.float32)
    grad_embed = jnp.dot(masks, upstream, precision=lax.Precision.HIGHEST)
    return (output, jnp.stack(mix_grads), jnp.stack(taps_grads), grad_embed)
```

```python
import functools
import math

import jax
import jax.numpy as jnp
from jax import lax
from jax.experimental import pallas as pl
from jax.experimental.pallas import tpu as pltpu
from jax.sharding import PartitionSpec as P

TAPS = 5
BASES = 4
BLOCKS = 2
DMAX = 8
HALF = TAPS // 2
REACH = HALF * DMAX
LANE = 128
JB = 32
GELU_SCALE = math.sqrt(2.0 / math.pi)
CUBIC = 0.044715
BF = jnp.bfloat16
F32 = jnp.float32
ROW_EMBED, ROW_TAPS0, ROW_TAPS1, TABLE = 0, BASES, BASES + TAPS, 16
ROW_GT0, ROW_GT1, ROW_GE, SUMS = 2 * JB, 2 * JB + 8, 2 * JB + 16, 2 * JB + 24


def dot(a, b, **kw):
    return jnp.dot(a, b, preferred_element_type=F32, **kw)


def dot_t(a, b):
    return lax.dot_general(a, b, (((1,), (1,)), ((), ())), preferred_element_type=F32)


def t_dot(a, b):
    return lax.dot_general(a, b, (((0,), (0,)), ((), ())), preferred_element_type=F32)


def iotas(shape):
    return lax.broadcasted_iota(jnp.int32, shape, 0), lax.broadcasted_iota(jnp.int32, shape, 1)


def as_bf(mask):
    return mask.astype(F32).astype(BF)


def reversal(size):
    row, col = iotas((size, size))
    return as_bf(row + col == size - 1)


def split_bf(x):
    high = x.astype(BF)
    return high, (x - high.astype(F32)).astype(BF)


def flip_exact(x, rev):
    high, rest = split_bf(x)
    mid, low = split_bf(rest.astype(F32))
    rest2 = (x - high.astype(F32) - mid.astype(F32)).astype(BF)
    del rest, low
    return dot(high, rev) + dot(mid, rev) + dot(rest2, rev)


def gelu_parts(v):
    square = v * v
    tangent = jnp.tanh(v * (GELU_SCALE + (GELU_SCALE * CUBIC) * square))
    half = 0.5 + 0.5 * tangent
    value = v * half
    slope = half + (v * (1.0 - tangent * tangent)) * (
        0.5 * GELU_SCALE + (1.5 * GELU_SCALE * CUBIC) * square
    )
    return value, slope


def select_rows(kind, rows):
    row, col = iotas((rows, TABLE))
    local = row % JB
    used = local < TAPS * BASES
    tap, letter = local // BASES, local % BASES
    want = {"tap0": ROW_TAPS0 + tap, "tap1": ROW_TAPS1 + tap, "letter": ROW_EMBED + letter}[kind]
    return as_bf(used & (col == want))


def one_hot_t(tokens):
    n = tokens.shape[1]
    row = lax.broadcasted_iota(jnp.int32, (2 * JB, n), 0)
    local = row % JB
    group = jnp.where(local < TAPS * BASES, local // BASES + TAPS * (row // JB), -1)
    seen = jnp.zeros((2 * JB, n), jnp.int32)
    for g in range(2 * TAPS):
        seen = jnp.where(group == g, jnp.broadcast_to(tokens[g : g + 1, :], (2 * JB, n)), seen)
    return (seen == local % BASES + 1).astype(F32)


def pair_table(pks, rev_w):
    sel_t, sel_e = select_rows("tap0", JB), select_rows("letter", JB)
    tables = [pk[0:TABLE, :] for pk in pks]
    plain = [dot(sel_t, t) * dot(sel_e, t) for t in tables]
    n = len(pks)
    out = []
    for k in range(n):
        high, low = split_bf(plain[k])
        fhigh, flow = split_bf(plain[n - 1 - k])
        out.append((high, dot(fhigh, rev_w).astype(BF), low, dot(flow, rev_w).astype(BF)))
    return out


def forward_kernel(
    n_chan, rows, width, scale,
    scal, tok, *refs,
):
    pks = refs[:n_chan]
    mix_ref, cot_ref = refs[n_chan : n_chan + 2]
    x2_ref, gm_ref, s_ref, x1_ref, gp_ref = refs[n_chan + 2 : n_chan + 7]
    w_ref, e_ref, wt_ref, et_ref, a_ref, m_ref, mixl_ref = refs[n_chan + 7 :]
    tiles = n_chan * width // LANE
    ext = rows + 2 * REACH
    me, dil = scal[0], scal[2]
    rev, rev_w = reversal(LANE), reversal(width)

    hot = one_hot_t(tok[...])
    a_ref[...] = jnp.concatenate([hot, hot], axis=0).T.astype(BF)

    stacks = [jnp.concatenate(p, axis=0) for p in pair_table(pks, rev_w)]
    starts = [pl.multiple_of(lax.bitwise_xor(me, k) * width, width) for k in range(n_chan)]
    for k in range(n_chan):
        total = jnp.zeros((4 * JB, width), F32)
        for kk in range(n_chan):
            total = total + dot(stacks[kk], pks[k][pl.ds(TABLE + starts[kk], width), :])
        high, low = split_bf(total[: 2 * JB] + total[2 * JB :])
        w_ref[:, k * width : (k + 1) * width] = jnp.concatenate([high, low], axis=0)
        e_ref[:, k * width : (k + 1) * width] = pks[k][0:TABLE, :]
        mixl_ref[k * width : (k + 1) * width, :] = mix_ref[pl.ds(starts[k], width), :]

    for t in range(tiles):
        src = slice((tiles - 1 - t) * LANE, (tiles - t) * LANE)
        dst = slice(t * LANE, (t + 1) * LANE)
        flipped = dot(w_ref[:, src], rev).astype(BF)
        wt_ref[:, dst] = jnp.concatenate(
            [flipped[JB : 2 * JB], flipped[:JB], flipped[3 * JB :], flipped[2 * JB : 3 * JB]], axis=0
        )
        et_ref[:, dst] = dot(e_ref[:, src], rev).astype(BF)

    row, col = iotas((4 * JB, TABLE))
    centre = HALF * BASES
    pick_f = as_bf((row - centre == col) & (col < BASES))
    pick_r = as_bf((row - centre - JB == col) & (col < BASES))
    chunk = ext // 5
    for t in range(tiles):
        dst = slice(t * LANE, (t + 1) * LANE)
        for strand, (wr, er, pick) in enumerate(((w_ref, e_ref, pick_f), (wt_ref, et_ref, pick_r))):
            rhs = jnp.concatenate([wr[:, dst], dot(pick, er[:, dst]).astype(BF)], axis=1)

            @pl.loop(0, 5)
            def _(i, t=t, strand=strand, rhs=rhs):
                where = pl.ds(pl.multiple_of(i * chunk, 16), chunk)
                both = dot(a_ref[where, :], rhs)
                value, slope = gelu_parts(both[:, :LANE])
                x1 = (both[:, LANE:] + value).astype(BF).astype(F32)
                x1_ref[strand, t, where, :] = x1
                gp_ref[strand, t, where, :] = slope.astype(BF)

    mchunk = rows // 6
    for t in range(tiles):
        dst = slice(t * LANE, (t + 1) * LANE)
        taps_f = e_ref[:, dst].astype(F32)
        taps_r = et_ref[:, dst].astype(F32)

        @pl.loop(0, 6)
        def _(i, t=t, dst=dst, taps_f=taps_f, taps_r=taps_r):
            first = i * mchunk
            u = jnp.zeros((mchunk, LANE), F32)
            v = jnp.zeros((mchunk, LANE), F32)
            for j in range(TAPS):
                shift = (j - HALF) * dil
                u += taps_f[ROW_TAPS1 + j : ROW_TAPS1 + j + 1, :] * x1_ref[0, t, pl.ds(first + REACH + shift, mchunk), :]
                v += taps_r[ROW_TAPS1 + j : ROW_TAPS1 + j + 1, :] * x1_ref[1, t, pl.ds(first + REACH - shift, mchunk), :]
            total = u.astype(BF).astype(F32) + v.astype(BF).astype(F32)
            m_ref[pl.ds(pl.multiple_of(first, 16), mchunk), dst] = total.astype(BF)

    @pl.loop(0, 6)
    def _(i):
        where = pl.ds(pl.multiple_of(i * mchunk, 16), mchunk)
        value, slope = gelu_parts(dot(m_ref[where, :], mixl_ref[...]))
        inner = pl.ds(pl.multiple_of(REACH + i * mchunk, 16), mchunk)
        n_own = pl.cdiv(width, LANE)
        own = jnp.concatenate([x1_ref[0, t, inner, :] for t in range(n_own)], axis=1)[:, :width]
        x2_ref[where, :] = (own + value).astype(BF)
        s_ref[where, :] = ((cot_ref[where, :].astype(F32) * scale) * slope).astype(BF)

    for k in range(n_chan):
        part = t_dot(m_ref[:, k * width : (k + 1) * width], s_ref[...])
        gm_ref[pl.ds(starts[k], width), :] = part.astype(BF)


def backward_kernel(
    n_chan, rows, width, scale,
    scal, tok, tok1, *refs,
):
    pks = refs[:n_chan]
    mix_ref, cot_ref, s_ref, x1_ref, gp_ref = refs[n_chan : n_chan + 5]
    out_ref = refs[n_chan + 5]
    p_ref, g2_ref, s0_ref, e_ref, et_ref, mixl_ref, dw_ref, gt_ref, g1_ref, pb_ref = refs[n_chan + 6 :]
    chans = n_chan * width
    tiles = chans // LANE
    ext = rows + 2 * REACH
    padded = tok.shape[1]
    me, dil = scal[0], scal[2]
    rev, rev_w = reversal(LANE), reversal(width)
    starts = [pl.multiple_of(lax.bitwise_xor(me, k) * width, width) for k in range(n_chan)]
    for k in range(n_chan):
        e_ref[:, k * width : (k + 1) * width] = pks[k][0:TABLE, :]
        mixl_ref[k * width : (k + 1) * width, :] = mix_ref[pl.ds(starts[k], width), :]
    for t in range(tiles):
        src = slice((tiles - 1 - t) * LANE, (tiles - t) * LANE)
        et_ref[:, t * LANE : (t + 1) * LANE] = dot(e_ref[:, src], rev).astype(BF)

    edge = 2 * REACH
    n_own = pl.cdiv(width, LANE)
    g2 = cot_ref[...].astype(F32) * scale
    g2_ref[:, :REACH, :] = jnp.zeros((n_own, REACH, LANE), F32)
    g2_ref[:, rows + REACH :, :] = jnp.zeros((n_own, REACH, LANE), F32)
    g2 = jnp.concatenate([g2, jnp.zeros((rows, n_own * LANE - width), F32)], axis=1)
    for t in range(n_own):
        g2_ref[t, REACH : rows + REACH, :] = g2[:, t * LANE : (t + 1) * LANE]
    s0_ref[:, ext:, :] = jnp.zeros((2, padded - ext, chans), BF)
    for t in range(tiles):
        p_ref[t, :edge, :] = jnp.zeros((edge, LANE), F32)
        p_ref[t, rows + edge :, :] = jnp.zeros((edge, LANE), F32)
        part = dot_t(s_ref[...], mixl_ref[t * LANE : (t + 1) * LANE, :])
        p_ref[t, edge : rows + edge, :] = part
        pb_ref[:, t * LANE : (t + 1) * LANE] = part.astype(BF)

    mchunk, chunk = rows // 6, ext // 5
    for t in range(tiles):
        dst = slice(t * LANE, (t + 1) * LANE)
        taps_f = e_ref[:, dst].astype(F32)
        taps_r = et_ref[:, dst].astype(F32)

        @pl.loop(0, 5)
        def _(i, t=t, dst=dst, taps_f=taps_f, taps_r=taps_r):
            first = i * chunk
            where = pl.ds(pl.multiple_of(first, 16), chunk)
            f = jnp.zeros((chunk, LANE), F32)
            r = jnp.zeros((chunk, LANE), F32)
            for j in range(TAPS):
                shift = (j - HALF) * dil
                tap_f = taps_f[ROW_TAPS1 + j : ROW_TAPS1 + j + 1, :]
                tap_r = taps_r[ROW_TAPS1 + j : ROW_TAPS1 + j + 1, :]
                f += tap_f * p_ref[t, pl.ds(first + REACH - shift, chunk), :]
                r += tap_r * p_ref[t, pl.ds(first + REACH + shift, chunk), :]
            if t < n_own:
                f += g2_ref[t, where, :]
            s0_ref[0, where, dst] = (f * gp_ref[0, t, where, :].astype(F32)).astype(BF)
            s0_ref[1, where, dst] = (r * gp_ref[1, t, where, :].astype(F32)).astype(BF)

        def taps_step(i, carry, t=t):
            first = i * mchunk
            here = p_ref[t, pl.ds(pl.multiple_of(edge + first, 16), mchunk), :]
            out = []
            for strand in range(2):
                for j in range(TAPS):
                    shift = (j - HALF) * dil * (1 - 2 * strand)
                    prod = here * x1_ref[strand, t, pl.ds(first + REACH + shift, mchunk), :]
                    out.append(carry[strand * TAPS + j] + prod.reshape(mchunk // 8, 8, LANE).sum(0))
            return tuple(out)

        sums = lax.fori_loop(0, 6, taps_step, tuple(jnp.zeros((8, LANE), F32) for _ in range(2 * TAPS)))
        for strand in range(2):
            rows_t = [jnp.sum(sums[strand * TAPS + j], axis=0, keepdims=True) for j in range(TAPS)]
            gt_ref[strand, :, dst] = jnp.concatenate(rows_t + [jnp.zeros((8 - TAPS, LANE), F32)], axis=0)

    hot = one_hot_t(tok[...]).astype(BF)
    hot1 = one_hot_t(tok1[...]).astype(BF)
    dw_ref[...] = dot(hot, s0_ref[0])
    other = dot(hot, s0_ref[1])
    by_tap = dot(hot1, pb_ref[...])
    own_letters = dot(hot1[: 16, :], cot_ref[...]) * scale
    srow, scol = iotas((8, JB))
    sum_letter = as_bf((scol % BASES == srow) & (scol < TAPS * BASES))
    sum_tap = as_bf((scol // BASES == srow) & (scol < TAPS * BASES))

    def sums_of(sel, x):
        high, rest = split_bf(x)
        return dot(sel, high) + dot(sel, rest)

    sel1 = select_rows("tap1", JB)
    g1_other = []
    for t in range(tiles):
        dst = slice(t * LANE, (t + 1) * LANE)
        g1_ref[:, dst] = sums_of(sum_letter, by_tap[:JB, dst] * dot(sel1, e_ref[:, dst]))
        g1_other.append(sums_of(sum_letter, by_tap[JB:, dst] * dot(sel1, et_ref[:, dst])))
    for t in range(tiles):
        dst = slice(t * LANE, (t + 1) * LANE)
        src = slice((tiles - 1 - t) * LANE, (tiles - t) * LANE)
        flipped = flip_exact(other[:, src], rev)
        dw_ref[:, dst] += jnp.concatenate([flipped[JB:], flipped[:JB]], axis=0)
        g1_ref[:, dst] += flip_exact(g1_other[tiles - 1 - t], rev)
        gt_ref[0, :, dst] += flip_exact(gt_ref[1, :, src], rev)

    sel_t, sel_e = select_rows("tap0", JB), select_rows("letter", JB)
    grads = []
    for kk in range(n_chan):
        total = jnp.zeros((2 * JB, width), F32)
        for k in range(n_chan):
            part = dw_ref[:, k * width : (k + 1) * width].astype(BF)
            total = total + dot_t(part, pks[k][pl.ds(TABLE + starts[kk], width), :])
        grads.append(total)
    for kk in range(n_chan):
        both = grads[kk][:JB] + flip_exact(grads[n_chan - 1 - kk][JB:], rev_w)
        table = pks[kk][0:TABLE, :]
        lanes = slice(kk * width, (kk + 1) * width)
        out_ref[kk, : 2 * JB, :] = dw_ref[:, lanes]
        out_ref[kk, ROW_GT0 : ROW_GT0 + 8, :] = sums_of(sum_tap, both * dot(sel_e, table))
        out_ref[kk, ROW_GT1 : ROW_GT1 + 8, :] = gt_ref[0, :, lanes]
        letters = sums_of(sum_letter, both * dot(sel_t, table)) + g1_ref[:, lanes]
        if kk == 0:
            zeros = jnp.zeros((BASES, width), F32)
            own = own_letters[HALF * BASES : (HALF + 1) * BASES, :]
            letters = letters + jnp.concatenate([own, zeros], axis=0)
        out_ref[kk, ROW_GE : ROW_GE + 8, :] = letters


def finish_kernel(n_chan, width, scal, *refs):
    pks = refs[:n_chan]
    sa_ref, sb_ref, ga_ref, gb_ref = refs[n_chan : n_chan + 4]
    gm_ref, gt_ref, ge_ref = refs[n_chan + 4 :]
    me = scal[0]
    rev_w = reversal(width)
    sums = sa_ref[...] + sb_ref[...]
    dw = sums[: 2 * JB].astype(BF)
    for k, (high, fhigh, _, _) in enumerate(pair_table(pks, rev_w)):
        start = pl.multiple_of(lax.bitwise_xor(me, k) * width, width)
        gm_ref[0, pl.ds(start, width), :] = t_dot(jnp.concatenate([high, fhigh], axis=0), dw)
    gm_ref[1] = ga_ref[...].astype(F32) + gb_ref[...].astype(F32)
    gt_ref[0] = sums[ROW_GT0 : ROW_GT0 + TAPS]
    gt_ref[1] = sums[ROW_GT1 : ROW_GT1 + TAPS]
    ge_ref[...] = sums[ROW_GE : ROW_GE + BASES]


def call(kernel, n_in, out_shape, scratch, limit):
    vmem = pl.BlockSpec(memory_space=pltpu.VMEM)
    return pl.pallas_call(
        kernel,
        out_shape=out_shape,
        in_specs=[pl.BlockSpec(memory_space=pltpu.SMEM)] + [vmem] * n_in,
        out_specs=[vmem] * len(out_shape),
        scratch_shapes=scratch,
        compiler_params=pltpu.CompilerParams(vmem_limit_bytes=limit),
    )


def flip_bits(x, axis, mask):
    return lax.ppermute(x, axis, [(i, i ^ mask) for i in range(lax.axis_size(axis))])


def body(tokens, cotangent, embed, taps, mix, dilations):
    rows, width = cotangent.shape
    n_seq, n_chan = lax.axis_size("seq"), lax.axis_size("chan")
    chans = n_chan * width
    tiles = chans // LANE
    ext = rows + 2 * REACH
    padded = pl.cdiv(ext, LANE) * LANE
    edge = 2 * REACH
    scale = 1.0 / math.sqrt(rows * n_seq)
    scal = jnp.concatenate([lax.axis_index("chan").astype(jnp.int32)[None], dilations])

    pk = jnp.concatenate(
        [embed, taps[0], taps[1], jnp.zeros((TABLE - BASES - 2 * TAPS, width), BF), mix[0]], axis=0
    )
    pks = [pk]
    bits = n_chan.bit_length() - 1
    for bit in reversed(range(bits)):
        moved = [flip_bits(p, "chan", 1 << bit) for p in pks]
        pks = [q for pair in zip(pks, moved) for q in pair]

    shifted = tokens + 1
    before = lax.ppermute(shifted[rows - edge :], "seq", [(i, i + 1) for i in range(n_seq - 1)])
    after = lax.ppermute(shifted[:edge], "seq", [(i + 1, i) for i in range(n_seq - 1)])
    wide = jnp.concatenate([before, shifted, after])
    other = lax.ppermute(wide, "seq", [(i, n_seq - 1 - i) for i in range(n_seq)])[::-1]

    def windows(dilation, margin, count, total):
        out = []
        for strand, source in ((1, wide), (-1, other)):
            for j in range(TAPS):
                first = margin + strand * (j - HALF) * dilation
                out.append(lax.dynamic_slice_in_dim(source, first, count, 0))
        table = jnp.stack(out)
        table = jnp.where(table[HALF : HALF + 1] == 0, 0, table)
        return jnp.pad(table, ((0, 0), (0, total - count)))

    tok0 = windows(dilations[0], REACH, ext, padded)
    tok1 = windows(dilations[1], edge, rows, rows)

    shape = jax.ShapeDtypeStruct
    x2, gm1, s1, x1, gp = call(
        functools.partial(forward_kernel, n_chan, rows, width, scale),
        1 + n_chan + 2,
        [
            shape((rows, width), BF),
            shape((chans, width), BF),
            shape((rows, width), BF),
            shape((2, tiles, ext, LANE), F32),
            shape((2, tiles, ext, LANE), BF),
        ],
        [
            pltpu.VMEM((4 * JB, chans), BF),
            pltpu.VMEM((TABLE, chans), BF),
            pltpu.VMEM((4 * JB, chans), BF),
            pltpu.VMEM((TABLE, chans), BF),
            pltpu.VMEM((padded, 4 * JB), BF),
            pltpu.VMEM((rows, chans), BF),
            pltpu.VMEM((chans, width), BF),
        ],
        32 << 20,
    )(scal, tok0, *pks, mix[1], cotangent)

    (sums,) = call(
        functools.partial(backward_kernel, n_chan, rows, width, scale),
        2 + n_chan + 5,
        [shape((n_chan, SUMS, width), F32)],
        [
            pltpu.VMEM((tiles, rows + 2 * edge, LANE), F32),
            pltpu.VMEM((pl.cdiv(width, LANE), ext, LANE), F32),
            pltpu.VMEM((2, padded, chans), BF),
            pltpu.VMEM((TABLE, chans), BF),
            pltpu.VMEM((TABLE, chans), BF),
            pltpu.VMEM((chans, width), BF),
            pltpu.VMEM((2 * JB, chans), F32),
            pltpu.VMEM((2, 8, chans), F32),
            pltpu.VMEM((8, chans), F32),
            pltpu.VMEM((rows, chans), BF),
        ],
        40 << 20,
    )(scal, tok0, tok1, *pks, mix[1], cotangent, s1, x1, gp)

    g_mine = gm1
    seq_bits = n_seq.bit_length() - 1
    for bit in range(seq_bits):
        g_other = flip_bits(g_mine, "seq", 1 << bit)
        if bit < seq_bits - 1:
            g_mine = lax.optimization_barrier(
                (g_mine.astype(F32) + g_other.astype(F32)).astype(BF)
            )
    pieces = [sums[0]] + [flip_bits(sums[k], "chan", k) for k in range(1, n_chan)]
    s_mine = functools.reduce(jnp.add, pieces)
    for bit in range(seq_bits):
        s_other = flip_bits(s_mine, "seq", 1 << bit)
        if bit < seq_bits - 1:
            s_mine = s_mine + s_other

    grad_mix, grad_taps, grad_embed = call(
        functools.partial(finish_kernel, n_chan, width),
        n_chan + 4,
        [
            shape((BLOCKS, chans, width), F32),
            shape((BLOCKS, TAPS, width), F32),
            shape((BASES, width), F32),
        ],
        [],
        32 << 20,
    )(scal, *[p[:TABLE] for p in pks], s_mine, s_other, g_mine, g_other)
    return x2, grad_mix, grad_taps, grad_embed


def solution(mesh):
    in_specs = (
        P(("groups", "seq")),
        P(("groups", "seq"), "chan"),
        P(None, "chan"),
        P(None, None, "chan"),
        P(None, None, "chan"),
        P(),
    )
    out_specs = (
        P(("groups", "seq"), "chan"),
        P("groups", None, "chan"),
        P("groups", None, "chan"),
        P("groups", "chan"),
    )
    return jax.shard_map(body, mesh=mesh, in_specs=in_specs, out_specs=out_specs, check_vma=False)
```

```python
import functools
import math

import jax
import jax.numpy as jnp
from jax import lax
from jax.experimental import pallas as pl
from jax.experimental.pallas import tpu as pltpu
from jax.sharding import PartitionSpec as P

TAPS = 5
BASES = 4
BLOCKS = 2
DMAX = 8
HALF = TAPS // 2
REACH = HALF * DMAX
LANE = 128
JB = 32
GELU_SCALE = math.sqrt(2.0 / math.pi)
CUBIC = 0.044715
BF = jnp.bfloat16
F32 = jnp.float32
ROW_EMBED, ROW_TAPS0, ROW_TAPS1, TABLE = 0, BASES, BASES + TAPS, 16
ROW_GT0, ROW_GT1, ROW_GE, SUMS = 2 * JB, 2 * JB + 8, 2 * JB + 16, 2 * JB + 24


def dot(a, b, **kw):
    return jnp.dot(a, b, preferred_element_type=F32, **kw)


def dot_t(a, b):
    return lax.dot_general(a, b, (((1,), (1,)), ((), ())), preferred_element_type=F32)


def t_dot(a, b):
    return lax.dot_general(a, b, (((0,), (0,)), ((), ())), preferred_element_type=F32)


def iotas(shape):
    return lax.broadcasted_iota(jnp.int32, shape, 0), lax.broadcasted_iota(jnp.int32, shape, 1)


def as_bf(mask):
    return mask.astype(F32).astype(BF)


def reversal(size):
    row, col = iotas((size, size))
    return as_bf(row + col == size - 1)


def split_bf(x):
    high = x.astype(BF)
    return high, (x - high.astype(F32)).astype(BF)


def flip_exact(x, rev):
    high, rest = split_bf(x)
    mid, low = split_bf(x - high.astype(F32))
    del rest
    return dot(high, rev) + dot(mid, rev) + dot(low, rev)


def xor_blocks(blocks, me):
    for bit in range(len(blocks).bit_length() - 1):
        swap = lax.bitwise_and(lax.shift_right_logical(me, bit), 1) == 1
        blocks = [jnp.where(swap, blocks[k ^ (1 << bit)], blocks[k]) for k in range(len(blocks))]
    return blocks


def gelu_parts(v):
    square = v * v
    tangent = jnp.tanh(v * (GELU_SCALE + (GELU_SCALE * CUBIC) * square))
    half = 0.5 + 0.5 * tangent
    value = v * half
    slope = half + (v * (1.0 - tangent * tangent)) * (
        0.5 * GELU_SCALE + (1.5 * GELU_SCALE * CUBIC) * square
    )
    return value, slope


def select_rows(kind, rows):
    row, col = iotas((rows, TABLE))
    local = row % JB
    used = local < TAPS * BASES
    tap, letter = local // BASES, local % BASES
    want = {"tap0": ROW_TAPS0 + tap, "tap1": ROW_TAPS1 + tap, "letter": ROW_EMBED + letter}[kind]
    return as_bf(used & (col == want))


def one_hot_t(tokens):
    n = tokens[0].shape[1]
    inside = tokens[HALF] != 0
    row = lax.broadcasted_iota(jnp.int32, (2 * JB, n), 0)
    local = row % JB
    group = jnp.where(local < TAPS * BASES, local // BASES + TAPS * (row // JB), -1)
    seen = jnp.zeros((2 * JB, n), jnp.int32)
    for g, line in enumerate(tokens):
        line = jnp.where(inside, line, 0)
        seen = jnp.where(group == g, jnp.broadcast_to(line, (2 * JB, n)), seen)
    return (seen == local % BASES + 1).astype(F32)


def pair_table(tables, rev_w):
    sel_t, sel_e = select_rows("tap0", JB), select_rows("letter", JB)
    plain = [dot(sel_t, t) * dot(sel_e, t) for t in tables]
    n = len(tables)
    out = []
    for k in range(n):
        high, low = split_bf(plain[k])
        fhigh, flow = split_bf(plain[n - 1 - k])
        out.append((high, dot(fhigh, rev_w).astype(BF), low, dot(flow, rev_w).astype(BF)))
    return out


def pack_kernel(width, mix_ref, embed_ref, taps_ref, out_ref, sem):
    copy = pltpu.make_async_copy(mix_ref.at[0], out_ref.at[pl.ds(0, width)], sem)
    copy.start()
    taps = taps_ref[...].astype(F32)
    lines = [embed_ref[...].astype(F32)]
    lines += [taps[j, block : block + 1, :] for block in range(BLOCKS) for j in range(TAPS)]
    lines.append(jnp.zeros((TABLE - BASES - 2 * TAPS, width), F32))
    table = jnp.concatenate(lines, axis=0).astype(BF)
    out_ref[width:, :] = jnp.zeros((TABLE, out_ref.shape[1]), BF)
    out_ref[width:, :width] = table
    copy.wait()


def prep_kernel(n_chan, n_seq, rows, width, scal, tok_ref, mix_ref, a_ref, hot_ref, hot1_ref, mixl_ref):
    me, place = scal[0], scal[1]
    blocks = [mix_ref[0, :, k * width : (k + 1) * width] for k in range(n_chan)]
    for k, block in enumerate(xor_blocks(blocks, me)):
        mixl_ref[:, k * width : (k + 1) * width] = block

    def line(block):
        inside = jnp.logical_and(block >= 0, block < n_seq)
        safe = jnp.clip(block, 0, n_seq - 1)
        letters = tok_ref[pl.ds(lax.bitwise_xor(safe, place), 1), :] + 1
        return jnp.where(inside, letters, 0)

    def around(block):
        lines = [line(block - 1)[:, rows - LANE :], line(block), line(block + 1)[:, :LANE]]
        return jnp.concatenate(lines, axis=1)

    total = rows + 2 * LANE
    this = jnp.broadcast_to(around(place), (8, total))
    mirror = jnp.broadcast_to(around(n_seq - 1 - place), (8, total)).astype(F32).astype(BF)
    rev, n_tiles = reversal(LANE), total // LANE
    other = jnp.concatenate(
        [dot(mirror[:, t * LANE : (t + 1) * LANE], rev) for t in reversed(range(n_tiles))], axis=1
    ).astype(jnp.int32)

    def windows(dilation, margin, count):
        out = []
        for strand, source in ((1, this), (-1, other)):
            for j in range(TAPS):
                first = LANE - margin + strand * (j - HALF) * dilation
                out.append(pltpu.roll(source, total - first, 1)[:1, :count])
        return out

    hot = one_hot_t(windows(scal[2], REACH, a_ref.shape[0]))
    a_ref[...] = jnp.concatenate([hot, hot], axis=0).T.astype(BF)
    hot_ref[...] = hot.astype(BF)
    hot1_ref[...] = one_hot_t(windows(scal[3], 0, rows)).astype(BF)


def forward_kernel(n_chan, rows, width, scale, scal, *refs):
    pks = refs[:n_chan]
    a_ref, mixl_ref, cot_ref = refs[n_chan : n_chan + 3]
    x2_ref, gm_ref, s_ref, x1_ref, gp_ref, st_ref = refs[n_chan + 3 : n_chan + 9]
    w_ref, e_ref, wt_ref, et_ref, m_ref = refs[n_chan + 9 :]
    tiles = n_chan * width // LANE
    ext = rows + 2 * REACH
    me, dil = scal[0], scal[3]
    rev, rev_w = reversal(LANE), reversal(width)

    tables = [pk[width:, :width] for pk in pks]
    stacks = [jnp.concatenate(p, axis=0) for p in pair_table(tables, rev_w)]
    for k, stack in enumerate(xor_blocks(stacks, me)):
        st_ref[:, k * width : (k + 1) * width] = stack
    for k in range(n_chan):
        total = dot_t(st_ref[...], pks[k][:width, :])
        high, low = split_bf(total[: 2 * JB] + total[2 * JB :])
        w_ref[:, k * width : (k + 1) * width] = jnp.concatenate([high, low], axis=0)
        e_ref[:, k * width : (k + 1) * width] = tables[k]

    for t in range(tiles):
        src = slice((tiles - 1 - t) * LANE, (tiles - t) * LANE)
        dst = slice(t * LANE, (t + 1) * LANE)
        flipped = dot(w_ref[:, src], rev).astype(BF)
        wt_ref[:, dst] = jnp.concatenate(
            [flipped[JB : 2 * JB], flipped[:JB], flipped[3 * JB :], flipped[2 * JB : 3 * JB]], axis=0
        )
        et_ref[:, dst] = dot(e_ref[:, src], rev).astype(BF)

    row, col = iotas((4 * JB, TABLE))
    centre = HALF * BASES
    pick_f = as_bf((row - centre == col) & (col < BASES))
    pick_r = as_bf((row - centre - JB == col) & (col < BASES))
    chunk = ext // 5
    for t in range(tiles):
        dst = slice(t * LANE, (t + 1) * LANE)
        for strand, (wr, er, pick) in enumerate(((w_ref, e_ref, pick_f), (wt_ref, et_ref, pick_r))):
            rhs = jnp.concatenate([wr[:, dst], dot(pick, er[:, dst]).astype(BF)], axis=1)

            for i in range(5):
                where = pl.ds(i * chunk, chunk)
                both = dot(a_ref[where, :], rhs)
                value, slope = gelu_parts(both[:, :LANE])
                x1 = (both[:, LANE:] + value).astype(BF).astype(F32)
                x1_ref[strand, t, where, :] = x1
                gp_ref[strand, t, where, :] = slope.astype(BF)

    mchunk = rows // 6
    for t in range(tiles):
        dst = slice(t * LANE, (t + 1) * LANE)
        taps_f = e_ref[:, dst].astype(F32)
        taps_r = et_ref[:, dst].astype(F32)

        for i in range(6):
            first = i * mchunk
            u = jnp.zeros((mchunk, LANE), F32)
            v = jnp.zeros((mchunk, LANE), F32)
            for j in range(TAPS):
                shift = (j - HALF) * dil
                u += taps_f[ROW_TAPS1 + j : ROW_TAPS1 + j + 1, :] * x1_ref[0, t, pl.ds(first + REACH + shift, mchunk), :]
                v += taps_r[ROW_TAPS1 + j : ROW_TAPS1 + j + 1, :] * x1_ref[1, t, pl.ds(first + REACH - shift, mchunk), :]
            total = u.astype(BF).astype(F32) + v.astype(BF).astype(F32)
            m_ref[first : first + mchunk, dst] = total.astype(BF)

    half = rows // 2
    for i in range(2):
        where = pl.ds(i * half, half)
        value, slope = gelu_parts(dot_t(m_ref[where, :], mixl_ref[...]))
        inner = pl.ds(REACH + i * half, half)
        n_own = pl.cdiv(width, LANE)
        own = jnp.concatenate([x1_ref[0, t, inner, :] for t in range(n_own)], axis=1)[:, :width]
        x2_ref[where, :] = (own + value).astype(BF)
        s_ref[where, :] = ((cot_ref[where, :].astype(F32) * scale) * slope).astype(BF)

    gm_ref[...] = t_dot(s_ref[...], m_ref[...]).astype(BF)


def backward_kernel(n_chan, rows, width, scale, scal, *refs):
    pks = refs[:n_chan]
    hot_ref, hot1_ref, mixl_ref, cot_ref, s_ref, x1_ref, gp_ref = refs[n_chan : n_chan + 7]
    out_ref = refs[n_chan + 7]
    p_ref, g2_ref, s0_ref, e_ref, et_ref, dw_ref, gt_ref, g1_ref, pb_ref, st_ref = refs[n_chan + 8 :]
    chans = n_chan * width
    tiles = chans // LANE
    ext = rows + 2 * REACH
    padded = hot_ref.shape[1]
    me, dil = scal[0], scal[3]
    rev, rev_w = reversal(LANE), reversal(width)
    tables = [pk[width:, :width] for pk in pks]
    for k in range(n_chan):
        e_ref[:, k * width : (k + 1) * width] = tables[k]
    for t in range(tiles):
        src = slice((tiles - 1 - t) * LANE, (tiles - t) * LANE)
        et_ref[:, t * LANE : (t + 1) * LANE] = dot(e_ref[:, src], rev).astype(BF)

    edge = 2 * REACH
    n_own = pl.cdiv(width, LANE)
    g2 = cot_ref[...].astype(F32) * scale
    g2_ref[:, :REACH, :] = jnp.zeros((n_own, REACH, LANE), F32)
    g2_ref[:, rows + REACH :, :] = jnp.zeros((n_own, REACH, LANE), F32)
    g2 = jnp.concatenate([g2, jnp.zeros((rows, n_own * LANE - width), F32)], axis=1)
    for t in range(n_own):
        g2_ref[t, REACH : rows + REACH, :] = g2[:, t * LANE : (t + 1) * LANE]
    s0_ref[:, ext:, :] = jnp.zeros((2, padded - ext, chans), BF)
    for t in range(tiles):
        p_ref[t, :edge, :] = jnp.zeros((edge, LANE), F32)
        p_ref[t, rows + edge :, :] = jnp.zeros((edge, LANE), F32)
        part = dot(s_ref[...], mixl_ref[:, t * LANE : (t + 1) * LANE])
        p_ref[t, edge : rows + edge, :] = part
        pb_ref[:, t * LANE : (t + 1) * LANE] = part.astype(BF)

    mchunk, chunk = rows // 6, ext // 5
    for t in range(tiles):
        dst = slice(t * LANE, (t + 1) * LANE)
        taps_f = e_ref[:, dst].astype(F32)
        taps_r = et_ref[:, dst].astype(F32)

        for i in range(5):
            first = i * chunk
            where = pl.ds(first, chunk)
            f = jnp.zeros((chunk, LANE), F32)
            r = jnp.zeros((chunk, LANE), F32)
            for j in range(TAPS):
                shift = (j - HALF) * dil
                tap_f = taps_f[ROW_TAPS1 + j : ROW_TAPS1 + j + 1, :]
                tap_r = taps_r[ROW_TAPS1 + j : ROW_TAPS1 + j + 1, :]
                f += tap_f * p_ref[t, pl.ds(first + REACH - shift, chunk), :]
                r += tap_r * p_ref[t, pl.ds(first + REACH + shift, chunk), :]
            if t < n_own:
                f += g2_ref[t, where, :]
            s0_ref[0, where, dst] = (f * gp_ref[0, t, where, :].astype(F32)).astype(BF)
            s0_ref[1, where, dst] = (r * gp_ref[1, t, where, :].astype(F32)).astype(BF)

        def taps_step(i, carry, t=t):
            first = i * mchunk
            here = p_ref[t, pl.ds(edge + first, mchunk), :]
            out = []
            for strand in range(2):
                for j in range(TAPS):
                    shift = (j - HALF) * dil * (1 - 2 * strand)
                    prod = here * x1_ref[strand, t, pl.ds(first + REACH + shift, mchunk), :]
                    out.append(carry[strand * TAPS + j] + prod.reshape(mchunk // 8, 8, LANE).sum(0))
            return tuple(out)

        sums = tuple(jnp.zeros((8, LANE), F32) for _ in range(2 * TAPS))
        for i in range(6):
            sums = taps_step(i, sums)
        for strand in range(2):
            rows_t = [jnp.sum(sums[strand * TAPS + j], axis=0, keepdims=True) for j in range(TAPS)]
            gt_ref[strand, :, dst] = jnp.concatenate(rows_t + [jnp.zeros((8 - TAPS, LANE), F32)], axis=0)

    hot, hot1 = hot_ref[...], hot1_ref[...]
    dw_ref[...] = dot(hot, s0_ref[0])
    other = dot(hot, s0_ref[1])
    by_tap = dot(hot1, pb_ref[...])
    own_letters = dot(hot1[: 16, :], cot_ref[...]) * scale
    srow, scol = iotas((8, JB))
    sum_letter = as_bf((scol % BASES == srow) & (scol < TAPS * BASES))
    sum_tap = as_bf((scol // BASES == srow) & (scol < TAPS * BASES))

    def sums_of(sel, x):
        high, rest = split_bf(x)
        return dot(sel, high) + dot(sel, rest)

    sel1 = select_rows("tap1", JB)
    g1_other = []
    for t in range(tiles):
        dst = slice(t * LANE, (t + 1) * LANE)
        g1_ref[:, dst] = sums_of(sum_letter, by_tap[:JB, dst] * dot(sel1, e_ref[:, dst]))
        g1_other.append(sums_of(sum_letter, by_tap[JB:, dst] * dot(sel1, et_ref[:, dst])))
    for t in range(tiles):
        dst = slice(t * LANE, (t + 1) * LANE)
        src = slice((tiles - 1 - t) * LANE, (tiles - t) * LANE)
        flipped = flip_exact(other[:, src], rev)
        dw_ref[:, dst] += jnp.concatenate([flipped[JB:], flipped[:JB]], axis=0)
        g1_ref[:, dst] += flip_exact(g1_other[tiles - 1 - t], rev)
        gt_ref[0, :, dst] += flip_exact(gt_ref[1, :, src], rev)

    sel_t, sel_e = select_rows("tap0", JB), select_rows("letter", JB)
    total = jnp.zeros((2 * JB, chans), F32)
    for k in range(n_chan):
        part = dw_ref[:, k * width : (k + 1) * width].astype(BF)
        total = total + dot(part, pks[k][:width, :])
    st_ref[...] = total
    grads = xor_blocks([st_ref[:, k * width : (k + 1) * width] for k in range(n_chan)], me)
    for kk in range(n_chan):
        both = grads[kk][:JB] + flip_exact(grads[n_chan - 1 - kk][JB:], rev_w)
        table = tables[kk]
        lanes = slice(kk * width, (kk + 1) * width)
        out_ref[kk, : 2 * JB, :] = dw_ref[:, lanes]
        out_ref[kk, ROW_GT0 : ROW_GT0 + 8, :] = sums_of(sum_tap, both * dot(sel_e, table))
        out_ref[kk, ROW_GT1 : ROW_GT1 + 8, :] = gt_ref[0, :, lanes]
        letters = sums_of(sum_letter, both * dot(sel_t, table)) + g1_ref[:, lanes]
        if kk == 0:
            zeros = jnp.zeros((BASES, width), F32)
            own = own_letters[HALF * BASES : (HALF + 1) * BASES, :]
            letters = letters + jnp.concatenate([own, zeros], axis=0)
        out_ref[kk, ROW_GE : ROW_GE + 8, :] = letters


def mix1_kernel(n_chan, width, scal, a_ref, b_ref, out_ref, held, sem):
    def block(k):
        lanes = slice(k * width, (k + 1) * width)
        return a_ref[:, lanes].astype(F32) + b_ref[:, lanes].astype(F32)

    for k, part in enumerate(xor_blocks([block(k) for k in range(n_chan)], scal[0])):
        held[:, k * width : (k + 1) * width] = part
    copy = pltpu.make_async_copy(held, out_ref.at[1], sem)
    copy.start()
    copy.wait()


def finish_kernel(n_chan, width, scal, st_ref, sa_ref, sb_ref, _, gm_ref, gt_ref, ge_ref, held, sem):
    sums = sa_ref[...] + sb_ref[...]
    dw = sums[: 2 * JB].astype(BF)
    held[...] = t_dot(dw, st_ref[: 2 * JB, :])
    copy = pltpu.make_async_copy(held, gm_ref.at[0], sem)
    copy.start()
    for j in range(TAPS):
        gt_ref[j, 0:1, :] = sums[ROW_GT0 + j : ROW_GT0 + j + 1]
        gt_ref[j, 1:2, :] = sums[ROW_GT1 + j : ROW_GT1 + j + 1]
    ge_ref[...] = sums[ROW_GE : ROW_GE + BASES]
    copy.wait()


VMEM = pl.BlockSpec(memory_space=pltpu.VMEM)
SMEM = pl.BlockSpec(memory_space=pltpu.SMEM)
HBM = pl.BlockSpec(memory_space=pltpu.HBM)


def call(kernel, in_specs, out_shape, out_specs, scratch, limit, cost, aliases=None):
    flops, moved = cost
    return pl.pallas_call(
        kernel,
        out_shape=out_shape,
        in_specs=in_specs,
        out_specs=out_specs,
        scratch_shapes=scratch,
        input_output_aliases=aliases or {},
        compiler_params=pltpu.CompilerParams(vmem_limit_bytes=limit << 20),
        cost_estimate=pl.CostEstimate(flops=flops, bytes_accessed=moved, transcendentals=0),
    )


def flip_bits(x, axis, mask):
    return lax.ppermute(x, axis, [(i, i ^ mask) for i in range(lax.axis_size(axis))])


def body(tokens, cotangent, embed, taps, mix, dilations):
    rows, width = cotangent.shape
    n_seq, n_chan = lax.axis_size("seq"), lax.axis_size("chan")
    chans = n_chan * width
    tiles = chans // LANE
    ext = rows + 2 * REACH
    padded = pl.cdiv(ext, LANE) * LANE
    edge = 2 * REACH
    own_tiles = pl.cdiv(width, LANE)
    scale = 1.0 / math.sqrt(rows * n_seq)
    shape = jax.ShapeDtypeStruct
    place = jnp.stack([lax.axis_index("chan"), lax.axis_index("seq")]).astype(jnp.int32)
    scal = jnp.concatenate([place, dilations])
    mix_t = jnp.swapaxes(mix, 1, 2)

    (pk,) = call(
        functools.partial(pack_kernel, width),
        [HBM, VMEM, VMEM],
        [shape((width + TABLE, chans), BF)],
        [VMEM],
        [pltpu.SemaphoreType.DMA],
        8,
        (0, width * chans * 4),
    )(mix_t, embed, jnp.swapaxes(taps, 0, 1))
    pks = [pk]
    for bit in reversed(range(n_chan.bit_length() - 1)):
        moved = [flip_bits(p, "chan", 1 << bit) for p in pks]
        pks = [q for pair in zip(pks, moved) for q in pair]

    letters = tokens.reshape(1, rows)
    seq_bits = n_seq.bit_length() - 1
    for bit in range(seq_bits):
        letters = jnp.concatenate([letters, flip_bits(letters, "seq", 1 << bit)], axis=0)

    hot_t, hot, hot1, mixl = call(
        functools.partial(prep_kernel, n_chan, n_seq, rows, width),
        [SMEM, VMEM, VMEM],
        [
            shape((padded, 4 * JB), BF),
            shape((2 * JB, padded), BF),
            shape((2 * JB, rows), BF),
            shape((width, chans), BF),
        ],
        [VMEM] * 4,
        [],
        16,
        (1 << 20, 1 << 20),
    )(scal, letters, mix_t[1:])

    x2, gm1, s1, x1, gp, stack = call(
        functools.partial(forward_kernel, n_chan, rows, width, scale),
        [SMEM] + [VMEM] * (n_chan + 3),
        [
            shape((rows, width), BF),
            shape((width, chans), BF),
            shape((rows, width), BF),
            shape((2, tiles, ext, LANE), F32),
            shape((2, tiles, ext, LANE), BF),
            shape((4 * JB, chans), BF),
        ],
        [VMEM] * 6,
        [
            pltpu.VMEM((4 * JB, chans), BF),
            pltpu.VMEM((TABLE, chans), BF),
            pltpu.VMEM((4 * JB, chans), BF),
            pltpu.VMEM((TABLE, chans), BF),
            pltpu.VMEM((rows, chans), BF),
        ],
        32,
        (3 << 30, 8 << 20),
    )(scal, *pks, hot_t, mixl, cotangent)

    (sums,) = call(
        functools.partial(backward_kernel, n_chan, rows, width, scale),
        [SMEM] + [VMEM] * (n_chan + 7),
        [shape((n_chan, SUMS, width), F32)],
        [VMEM],
        [
            pltpu.VMEM((tiles, rows + 2 * edge, LANE), F32),
            pltpu.VMEM((own_tiles, ext, LANE), F32),
            pltpu.VMEM((2, padded, chans), BF),
            pltpu.VMEM((TABLE, chans), BF),
            pltpu.VMEM((TABLE, chans), BF),
            pltpu.VMEM((2 * JB, chans), F32),
            pltpu.VMEM((2, 8, chans), F32),
            pltpu.VMEM((8, chans), F32),
            pltpu.VMEM((rows, chans), BF),
            pltpu.VMEM((2 * JB, chans), F32),
        ],
        40,
        (3 << 30, 8 << 20),
    )(scal, *pks, hot, hot1, mixl, cotangent, s1, x1, gp)

    g_mine = gm1
    for bit in range(seq_bits):
        g_other = flip_bits(g_mine, "seq", 1 << bit)
        if bit < seq_bits - 1:
            g_mine = lax.optimization_barrier(
                (g_mine.astype(F32) + g_other.astype(F32)).astype(BF)
            )
    pieces = [sums[0]] + [flip_bits(sums[k], "chan", k) for k in range(1, n_chan)]
    s_mine = functools.reduce(jnp.add, pieces)
    for bit in range(seq_bits):
        s_other = flip_bits(s_mine, "seq", 1 << bit)
        if bit < seq_bits - 1:
            s_mine = s_mine + s_other

    big = pltpu.VMEM((width, chans), F32)
    (grad_mix,) = call(
        functools.partial(mix1_kernel, n_chan, width),
        [SMEM, VMEM, VMEM],
        [shape((BLOCKS, width, chans), F32)],
        [HBM],
        [big, pltpu.SemaphoreType.DMA],
        16,
        (1 << 20, 1 << 21),
    )(scal, g_mine, g_other)
    grad_mix, grad_taps, grad_embed = call(
        functools.partial(finish_kernel, n_chan, width),
        [SMEM, VMEM, VMEM, VMEM, HBM],
        [
            shape((BLOCKS, width, chans), F32),
            shape((TAPS, BLOCKS, width), F32),
            shape((BASES, width), F32),
        ],
        [HBM, VMEM, VMEM],
        [big, pltpu.SemaphoreType.DMA],
        16,
        (1 << 24, 1 << 21),
        {4: 0},
    )(scal, stack, s_mine, s_other, grad_mix)
    return x2, jnp.swapaxes(grad_mix, 1, 2), jnp.swapaxes(grad_taps, 0, 1), grad_embed


def solution(mesh):
    in_specs = (
        P(("groups", "seq")),
        P(("groups", "seq"), "chan"),
        P(None, "chan"),
        P(None, None, "chan"),
        P(None, None, "chan"),
        P(),
    )
    out_specs = (
        P(("groups", "seq"), "chan"),
        P("groups", None, "chan"),
        P("groups", None, "chan"),
        P("groups", "chan"),
    )
    return jax.shard_map(body, mesh=mesh, in_specs=in_specs, out_specs=out_specs, check_vma=False)
```

```python
import functools
import math

import jax
import jax.numpy as jnp
from jax import lax
from jax.experimental import pallas as pl
from jax.experimental.pallas import tpu as pltpu
from jax.sharding import PartitionSpec as P

TAPS = 5
BASES = 4
BLOCKS = 2
DMAX = 8
HALF = TAPS // 2
REACH = HALF * DMAX
LANE = 128
JB = 32
GELU_SCALE = math.sqrt(2.0 / math.pi)
CUBIC = 0.044715
BF = jnp.bfloat16
F32 = jnp.float32
ROW_EMBED, ROW_TAPS0, ROW_TAPS1, TABLE = 0, BASES, BASES + TAPS, 16
ROW_GE, ROW_R, ROW_GT0, ROW_GT1, SUMS = 20, 24, 48, 56, 64


def dot(a, b, **kw):
    return jnp.dot(a, b, preferred_element_type=F32, **kw)


def dot_t(a, b):
    return lax.dot_general(a, b, (((1,), (1,)), ((), ())), preferred_element_type=F32)


def t_dot(a, b):
    return lax.dot_general(a, b, (((0,), (0,)), ((), ())), preferred_element_type=F32)


def iotas(shape):
    return lax.broadcasted_iota(jnp.int32, shape, 0), lax.broadcasted_iota(jnp.int32, shape, 1)


def as_bf(mask):
    return mask.astype(F32).astype(BF)


def reversal(size):
    row, col = iotas((size, size))
    return as_bf(row + col == size - 1)


def split_bf(x):
    high = x.astype(BF)
    return high, (x - high.astype(F32)).astype(BF)


def flip_exact(x, rev):
    high, rest = split_bf(x)
    mid, low = split_bf(x - high.astype(F32))
    del rest
    return dot(high, rev) + dot(mid, rev) + dot(low, rev)


def xor_blocks(blocks, me):
    for bit in range(len(blocks).bit_length() - 1):
        swap = lax.bitwise_and(lax.shift_right_logical(me, bit), 1) == 1
        blocks = [jnp.where(swap, blocks[k ^ (1 << bit)], blocks[k]) for k in range(len(blocks))]
    return blocks


def gelu_parts(v):
    square = v * v
    tangent = jnp.tanh(v * (GELU_SCALE + (GELU_SCALE * CUBIC) * square))
    half = 0.5 + 0.5 * tangent
    value = v * half
    slope = half + (v * (1.0 - tangent * tangent)) * (
        0.5 * GELU_SCALE + (1.5 * GELU_SCALE * CUBIC) * square
    )
    return value, slope


def select_rows(kind, rows):
    row, col = iotas((rows, TABLE))
    local = row % JB
    used = local < TAPS * BASES
    tap, letter = local // BASES, local % BASES
    want = {"tap0": ROW_TAPS0 + tap, "tap1": ROW_TAPS1 + tap, "letter": ROW_EMBED + letter}[kind]
    return as_bf(used & (col == want))


def one_hot_t(tokens):
    n = tokens[0].shape[1]
    inside = tokens[HALF] != 0
    row = lax.broadcasted_iota(jnp.int32, (2 * JB, n), 0)
    local = row % JB
    group = jnp.where(local < TAPS * BASES, local // BASES + TAPS * (row // JB), -1)
    seen = jnp.zeros((2 * JB, n), jnp.int32)
    for g, line in enumerate(tokens):
        line = jnp.where(inside, line, 0)
        seen = jnp.where(group == g, jnp.broadcast_to(line, (2 * JB, n)), seen)
    return (seen == local % BASES + 1).astype(F32)


def pair_table(tables, rev_w):
    sel_t, sel_e = select_rows("tap0", JB), select_rows("letter", JB)
    plain = [dot(sel_t, t) * dot(sel_e, t) for t in tables]
    n = len(tables)
    out = []
    for k in range(n):
        high, low = split_bf(plain[k])
        fhigh, flow = split_bf(plain[n - 1 - k])
        out.append((high, dot(fhigh, rev_w).astype(BF), low, dot(flow, rev_w).astype(BF)))
    return out


def pack_kernel(width, mix_ref, embed_ref, taps_ref, out_ref, e_ref, t_ref, sems):
    big = pltpu.make_async_copy(mix_ref.at[0], out_ref.at[pl.ds(0, width)], sems.at[0])
    small = [
        pltpu.make_async_copy(embed_ref, e_ref, sems.at[1]),
        pltpu.make_async_copy(taps_ref, t_ref, sems.at[2]),
    ]
    for copy in small + [big]:
        copy.start()
    out_ref[width:, :] = jnp.zeros((TABLE, out_ref.shape[1]), BF)
    for copy in small:
        copy.wait()
    taps = t_ref[...].astype(F32)
    lines = [e_ref[...].astype(F32)]
    lines += [taps[j, block : block + 1, :] for block in range(BLOCKS) for j in range(TAPS)]
    lines.append(jnp.zeros((TABLE - BASES - 2 * TAPS, width), F32))
    out_ref[width:, :width] = jnp.concatenate(lines, axis=0).astype(BF)
    big.wait()


def local_kernel(n_chan, width, scal, mix_ref, cot_ref, mixl_ref, cotl_ref, m_ref, c_ref, sems):
    first = pltpu.make_async_copy(mix_ref.at[1], m_ref, sems.at[0])
    second = pltpu.make_async_copy(cot_ref, c_ref, sems.at[1])
    first.start()
    second.start()
    first.wait()
    blocks = [m_ref[:, k * width : (k + 1) * width] for k in range(n_chan)]
    for k, block in enumerate(xor_blocks(blocks, scal[0])):
        mixl_ref[:, k * width : (k + 1) * width] = block
    second.wait()
    cotl_ref[...] = c_ref[...].astype(F32).T.astype(BF)


def prep_kernel(n_seq, rows, scal, tok_ref, a_ref, hot_ref, hot1_ref):
    place = scal[1]

    def line(block):
        inside = jnp.logical_and(block >= 0, block < n_seq)
        safe = jnp.clip(block, 0, n_seq - 1)
        letters = tok_ref[pl.ds(lax.bitwise_xor(safe, place), 1), :] + 1
        return jnp.where(inside, letters, 0)

    def around(block):
        lines = [line(block - 1)[:, rows - LANE :], line(block), line(block + 1)[:, :LANE]]
        return jnp.concatenate(lines, axis=1)

    total = rows + 2 * LANE
    this = jnp.broadcast_to(around(place), (8, total))
    mirror = jnp.broadcast_to(around(n_seq - 1 - place), (8, total)).astype(F32).astype(BF)
    rev, n_tiles = reversal(LANE), total // LANE
    other = jnp.concatenate(
        [dot(mirror[:, t * LANE : (t + 1) * LANE], rev) for t in reversed(range(n_tiles))], axis=1
    ).astype(jnp.int32)

    def windows(dilation, margin, count):
        out = []
        for strand, source in ((1, this), (-1, other)):
            for j in range(TAPS):
                first = LANE - margin + strand * (j - HALF) * dilation
                out.append(pltpu.roll(source, total - first, 1)[:1, :count])
        return out

    hot = one_hot_t(windows(scal[2], REACH, a_ref.shape[0]))
    a_ref[...] = jnp.concatenate([hot, hot], axis=0).T.astype(BF)
    hot_ref[...] = hot.astype(BF)
    hot1_ref[...] = one_hot_t(windows(scal[3], 0, rows)).astype(BF)


def forward_kernel(n_chan, rows, width, scale, scal, *refs):
    pks = refs[:n_chan]
    a_ref, mixl_ref, cot_ref = refs[n_chan : n_chan + 3]
    x2_ref, gm_ref, s_ref, x1_ref, gp_ref, st_ref = refs[n_chan + 3 : n_chan + 9]
    w_ref, e_ref, wt_ref, et_ref, m_ref = refs[n_chan + 9 :]
    tiles = n_chan * width // LANE
    ext = rows + 2 * REACH
    me, dil = scal[0], scal[3]
    rev, rev_w = reversal(LANE), reversal(width)

    tables = [pk[width:, :width] for pk in pks]
    stacks = [jnp.concatenate(p, axis=0) for p in pair_table(tables, rev_w)]
    for k, stack in enumerate(xor_blocks(stacks, me)):
        st_ref[:, k * width : (k + 1) * width] = stack
    for k in range(n_chan):
        total = dot_t(st_ref[...], pks[k][:width, :])
        high, low = split_bf(total[: 2 * JB] + total[2 * JB :])
        w_ref[:, k * width : (k + 1) * width] = jnp.concatenate([high, low], axis=0)
        e_ref[:, k * width : (k + 1) * width] = tables[k]

    for t in range(tiles):
        src = slice((tiles - 1 - t) * LANE, (tiles - t) * LANE)
        dst = slice(t * LANE, (t + 1) * LANE)
        flipped = dot(w_ref[:, src], rev).astype(BF)
        wt_ref[:, dst] = jnp.concatenate(
            [flipped[JB : 2 * JB], flipped[:JB], flipped[3 * JB :], flipped[2 * JB : 3 * JB]], axis=0
        )
        et_ref[:, dst] = dot(e_ref[:, src], rev).astype(BF)

    row, col = iotas((4 * JB, TABLE))
    centre = HALF * BASES
    pick_f = as_bf((row - centre == col) & (col < BASES))
    pick_r = as_bf((row - centre - JB == col) & (col < BASES))
    chunk = ext // 5
    for t in range(tiles):
        dst = slice(t * LANE, (t + 1) * LANE)
        for strand, (wr, er, pick) in enumerate(((w_ref, e_ref, pick_f), (wt_ref, et_ref, pick_r))):
            rhs = jnp.concatenate([wr[:, dst], dot(pick, er[:, dst]).astype(BF)], axis=1)

            for i in range(5):
                where = pl.ds(i * chunk, chunk)
                both = dot(a_ref[where, :], rhs)
                value, slope = gelu_parts(both[:, :LANE])
                x1 = (both[:, LANE:] + value).astype(BF).astype(F32)
                x1_ref[strand, t, where, :] = x1
                gp_ref[strand, t, where, :] = slope.astype(BF)

    mchunk = rows // 6
    for t in range(tiles):
        dst = slice(t * LANE, (t + 1) * LANE)
        taps_f = e_ref[:, dst].astype(F32)
        taps_r = et_ref[:, dst].astype(F32)

        for i in range(6):
            first = i * mchunk
            u = jnp.zeros((mchunk, LANE), F32)
            v = jnp.zeros((mchunk, LANE), F32)
            for j in range(TAPS):
                shift = (j - HALF) * dil
                u += taps_f[ROW_TAPS1 + j : ROW_TAPS1 + j + 1, :] * x1_ref[0, t, pl.ds(first + REACH + shift, mchunk), :]
                v += taps_r[ROW_TAPS1 + j : ROW_TAPS1 + j + 1, :] * x1_ref[1, t, pl.ds(first + REACH - shift, mchunk), :]
            total = u.astype(BF).astype(F32) + v.astype(BF).astype(F32)
            m_ref[first : first + mchunk, dst] = total.astype(BF)

    half = rows // 2
    for i in range(2):
        where = pl.ds(i * half, half)
        value, slope = gelu_parts(dot_t(m_ref[where, :], mixl_ref[...]))
        inner = pl.ds(REACH + i * half, half)
        n_own = pl.cdiv(width, LANE)
        own = jnp.concatenate([x1_ref[0, t, inner, :] for t in range(n_own)], axis=1)[:, :width]
        x2_ref[where, :] = (own + value).astype(BF)
        s_ref[where, :] = ((cot_ref[where, :].astype(F32) * scale) * slope).astype(BF)

    gm_ref[...] = t_dot(s_ref[...], m_ref[...]).astype(BF)


def backward_kernel(n_chan, rows, width, scale, scal, *refs):
    pks = refs[:n_chan]
    hot_ref, hot1_ref, mixl_ref, cot_ref, s_ref, x1_ref, gp_ref = refs[n_chan : n_chan + 7]
    keep_ref, send_ref = refs[n_chan + 7 : n_chan + 9]
    p_ref, g2_ref, s0_ref, e_ref, et_ref, dw_ref, gt_ref, g1_ref, pb_ref, st_ref = refs[n_chan + 9 :]
    chans = n_chan * width
    tiles = chans // LANE
    ext = rows + 2 * REACH
    padded = hot_ref.shape[1]
    me, dil = scal[0], scal[3]
    rev, rev_w = reversal(LANE), reversal(width)
    tables = [pk[width:, :width] for pk in pks]
    for k in range(n_chan):
        e_ref[:, k * width : (k + 1) * width] = tables[k]
    for t in range(tiles):
        src = slice((tiles - 1 - t) * LANE, (tiles - t) * LANE)
        et_ref[:, t * LANE : (t + 1) * LANE] = dot(e_ref[:, src], rev).astype(BF)

    edge = 2 * REACH
    n_own = pl.cdiv(width, LANE)
    g2 = cot_ref[...].astype(F32) * scale
    g2_ref[:, :REACH, :] = jnp.zeros((n_own, REACH, LANE), F32)
    g2_ref[:, rows + REACH :, :] = jnp.zeros((n_own, REACH, LANE), F32)
    g2 = jnp.concatenate([g2, jnp.zeros((rows, n_own * LANE - width), F32)], axis=1)
    for t in range(n_own):
        g2_ref[t, REACH : rows + REACH, :] = g2[:, t * LANE : (t + 1) * LANE]
    s0_ref[:, ext:, :] = jnp.zeros((2, padded - ext, chans), BF)
    for t in range(tiles):
        p_ref[t, :edge, :] = jnp.zeros((edge, LANE), F32)
        p_ref[t, rows + edge :, :] = jnp.zeros((edge, LANE), F32)
        part = dot(s_ref[...], mixl_ref[:, t * LANE : (t + 1) * LANE])
        p_ref[t, edge : rows + edge, :] = part
        pb_ref[:, t * LANE : (t + 1) * LANE] = part.astype(BF)

    mchunk, chunk = rows // 6, ext // 5
    for t in range(tiles):
        dst = slice(t * LANE, (t + 1) * LANE)
        taps_f = e_ref[:, dst].astype(F32)
        taps_r = et_ref[:, dst].astype(F32)

        for i in range(5):
            first = i * chunk
            where = pl.ds(first, chunk)
            f = jnp.zeros((chunk, LANE), F32)
            r = jnp.zeros((chunk, LANE), F32)
            for j in range(TAPS):
                shift = (j - HALF) * dil
                tap_f = taps_f[ROW_TAPS1 + j : ROW_TAPS1 + j + 1, :]
                tap_r = taps_r[ROW_TAPS1 + j : ROW_TAPS1 + j + 1, :]
                f += tap_f * p_ref[t, pl.ds(first + REACH - shift, chunk), :]
                r += tap_r * p_ref[t, pl.ds(first + REACH + shift, chunk), :]
            if t < n_own:
                f += g2_ref[t, where, :]
            s0_ref[0, where, dst] = (f * gp_ref[0, t, where, :].astype(F32)).astype(BF)
            s0_ref[1, where, dst] = (r * gp_ref[1, t, where, :].astype(F32)).astype(BF)

        def taps_step(i, carry, t=t):
            first = i * mchunk
            here = p_ref[t, pl.ds(edge + first, mchunk), :]
            out = []
            for strand in range(2):
                for j in range(TAPS):
                    shift = (j - HALF) * dil * (1 - 2 * strand)
                    prod = here * x1_ref[strand, t, pl.ds(first + REACH + shift, mchunk), :]
                    out.append(carry[strand * TAPS + j] + prod.reshape(mchunk // 8, 8, LANE).sum(0))
            return tuple(out)

        sums = tuple(jnp.zeros((8, LANE), F32) for _ in range(2 * TAPS))
        for i in range(6):
            sums = taps_step(i, sums)
        for strand in range(2):
            rows_t = [jnp.sum(sums[strand * TAPS + j], axis=0, keepdims=True) for j in range(TAPS)]
            gt_ref[strand, :, dst] = jnp.concatenate(rows_t + [jnp.zeros((8 - TAPS, LANE), F32)], axis=0)

    hot, hot1 = hot_ref[...], hot1_ref[...]
    dw_ref[...] = dot(hot, s0_ref[0])
    other = dot(hot, s0_ref[1])
    by_tap = dot(hot1, pb_ref[...])
    own_letters = dot(hot1[: 16, :], cot_ref[...]) * scale
    srow, scol = iotas((8, JB))
    sum_letter = as_bf((scol % BASES == srow) & (scol < TAPS * BASES))
    sum_tap = as_bf((scol // BASES == srow) & (scol < TAPS * BASES))

    def sums_of(sel, x):
        high, rest = split_bf(x)
        return dot(sel, high) + dot(sel, rest)

    sel1 = select_rows("tap1", JB)
    g1_other = []
    for t in range(tiles):
        dst = slice(t * LANE, (t + 1) * LANE)
        g1_ref[:, dst] = sums_of(sum_letter, by_tap[:JB, dst] * dot(sel1, e_ref[:, dst]))
        g1_other.append(sums_of(sum_letter, by_tap[JB:, dst] * dot(sel1, et_ref[:, dst])))
    for t in range(tiles):
        dst = slice(t * LANE, (t + 1) * LANE)
        src = slice((tiles - 1 - t) * LANE, (tiles - t) * LANE)
        flipped = flip_exact(other[:, src], rev)
        dw_ref[:, dst] += jnp.concatenate([flipped[JB:], flipped[:JB]], axis=0)
        g1_ref[:, dst] += flip_exact(g1_other[tiles - 1 - t], rev)
        gt_ref[0, :, dst] += flip_exact(gt_ref[1, :, src], rev)

    sel_t, sel_e = select_rows("tap0", JB), select_rows("letter", JB)
    total = jnp.zeros((2 * JB, chans), F32)
    for k in range(n_chan):
        part = dw_ref[:, k * width : (k + 1) * width].astype(BF)
        total = total + dot(part, pks[k][:width, :])
    st_ref[...] = total
    grads = xor_blocks([st_ref[:, k * width : (k + 1) * width] for k in range(n_chan)], me)
    for kk in range(n_chan):
        both = grads[kk][:JB] + flip_exact(grads[n_chan - 1 - kk][JB:], rev_w)
        table = tables[kk]
        lanes = slice(kk * width, (kk + 1) * width)
        letters = sums_of(sum_letter, both * dot(sel_t, table)) + g1_ref[:, lanes]
        if kk == 0:
            zeros = jnp.zeros((BASES, width), F32)
            own = own_letters[HALF * BASES : (HALF + 1) * BASES, :]
            letters = letters + jnp.concatenate([own, zeros], axis=0)
        place = (keep_ref, send_ref)[kk % 2]
        place[kk // 2, :ROW_R, :] = jnp.concatenate([dw_ref[:ROW_GE, lanes], letters[:BASES]], axis=0)
        place[kk // 2, ROW_R : 2 * ROW_R, :] = dw_ref[JB : JB + ROW_R, lanes]
        place[kk // 2, ROW_GT0 : ROW_GT0 + 8, :] = sums_of(sum_tap, both * dot(sel_e, table))
        place[kk // 2, ROW_GT1 : ROW_GT1 + 8, :] = gt_ref[0, :, lanes]


def mix1_kernel(n_chan, width, scal, a_ref, b_ref, out_ref, held, sem):
    def block(k):
        lanes = slice(k * width, (k + 1) * width)
        return a_ref[:, lanes].astype(F32) + b_ref[:, lanes].astype(F32)

    for k, part in enumerate(xor_blocks([block(k) for k in range(n_chan)], scal[0])):
        held[:, k * width : (k + 1) * width] = part
    copy = pltpu.make_async_copy(held, out_ref.at[1], sem)
    copy.start()
    copy.wait()


def finish_kernel(n_chan, width, scal, st_ref, sa_ref, sb_ref, _, gm_ref, gt_ref, ge_ref, held, sems):
    sums = sa_ref[...] + sb_ref[...]
    fill = jnp.zeros((JB - ROW_GE, width), F32)
    dw = jnp.concatenate([sums[:ROW_GE], fill, sums[ROW_R : ROW_R + ROW_GE], fill], axis=0).astype(BF)
    copies = []
    step = 2 * LANE
    for i in range(n_chan * width // step):
        lanes = pl.ds(i * step, step)
        held[:, lanes] = t_dot(dw, st_ref[: 2 * JB, lanes])
        copies.append(pltpu.make_async_copy(held.at[:, lanes], gm_ref.at[0, :, lanes], sems.at[i]))
        copies[-1].start()
    for j in range(TAPS):
        gt_ref[j, 0:1, :] = sums[ROW_GT0 + j : ROW_GT0 + j + 1]
        gt_ref[j, 1:2, :] = sums[ROW_GT1 + j : ROW_GT1 + j + 1]
    ge_ref[...] = sums[ROW_GE : ROW_GE + BASES]
    for copy in copies:
        copy.wait()


VMEM = pl.BlockSpec(memory_space=pltpu.VMEM)
SMEM = pl.BlockSpec(memory_space=pltpu.SMEM)
HBM = pl.BlockSpec(memory_space=pltpu.HBM)


def in_hbm(x):
    return pltpu.with_memory_space_constraint(x, pltpu.HBM)


def call(kernel, in_specs, out_shape, out_specs, scratch, limit, cost, aliases=None):
    flops, moved = cost
    return pl.pallas_call(
        kernel,
        out_shape=out_shape,
        in_specs=in_specs,
        out_specs=out_specs,
        scratch_shapes=scratch,
        input_output_aliases=aliases or {},
        compiler_params=pltpu.CompilerParams(vmem_limit_bytes=limit << 20),
        cost_estimate=pl.CostEstimate(flops=flops, bytes_accessed=moved, transcendentals=0),
    )


def flip_bits(x, axis, mask):
    return lax.ppermute(x, axis, [(i, i ^ mask) for i in range(lax.axis_size(axis))])


def body(tokens, cotangent, embed, taps, mix, dilations):
    rows, width = cotangent.shape
    n_seq, n_chan = lax.axis_size("seq"), lax.axis_size("chan")
    chans = n_chan * width
    tiles = chans // LANE
    ext = rows + 2 * REACH
    padded = pl.cdiv(ext, LANE) * LANE
    edge = 2 * REACH
    own_tiles = pl.cdiv(width, LANE)
    scale = 1.0 / math.sqrt(rows * n_seq)
    shape = jax.ShapeDtypeStruct
    place = jnp.stack([lax.axis_index("chan"), lax.axis_index("seq")]).astype(jnp.int32)
    scal = jnp.concatenate([place, dilations])
    mix_t = jnp.swapaxes(mix, 1, 2)

    (pk,) = call(
        functools.partial(pack_kernel, width),
        [HBM, HBM, HBM],
        [shape((width + TABLE, chans), BF)],
        [VMEM],
        [
            pltpu.VMEM((BASES, width), BF),
            pltpu.VMEM((TAPS, BLOCKS, width), BF),
            pltpu.SemaphoreType.DMA((3,)),
        ],
        8,
        (0, width * chans * 4),
    )(in_hbm(mix_t), in_hbm(embed), in_hbm(jnp.swapaxes(taps, 0, 1)))

    letters = tokens.reshape(1, rows)
    seq_bits = n_seq.bit_length() - 1
    for bit in range(seq_bits):
        letters = jnp.concatenate([letters, flip_bits(letters, "seq", 1 << bit)], axis=0)

    mixl, cot = call(
        functools.partial(local_kernel, n_chan, width),
        [SMEM, HBM, HBM],
        [shape((width, chans), BF), shape((rows, width), BF)],
        [VMEM] * 2,
        [
            pltpu.VMEM((width, chans), BF),
            pltpu.VMEM((width, rows), BF),
            pltpu.SemaphoreType.DMA((2,)),
        ],
        16,
        (1 << 20, 1 << 20),
    )(scal, in_hbm(mix_t), in_hbm(cotangent.T))

    pks = [pk]
    for bit in reversed(range(n_chan.bit_length() - 1)):
        ready = [pks[0]] + [lax.optimization_barrier((p, letters, mixl, cot))[0] for p in pks[1:]]
        moved = [flip_bits(p, "chan", 1 << bit) for p in ready]
        pks = [q for pair in zip(pks, moved) for q in pair]

    hot_t, hot, hot1 = call(
        functools.partial(prep_kernel, n_seq, rows),
        [SMEM, VMEM],
        [shape((padded, 4 * JB), BF), shape((2 * JB, padded), BF), shape((2 * JB, rows), BF)],
        [VMEM] * 3,
        [],
        16,
        (1 << 20, 1 << 20),
    )(scal, letters)

    x2, gm1, s1, x1, gp, stack = call(
        functools.partial(forward_kernel, n_chan, rows, width, scale),
        [SMEM] + [VMEM] * (n_chan + 3),
        [
            shape((rows, width), BF),
            shape((width, chans), BF),
            shape((rows, width), BF),
            shape((2, tiles, ext, LANE), F32),
            shape((2, tiles, ext, LANE), BF),
            shape((4 * JB, chans), BF),
        ],
        [VMEM] * 6,
        [
            pltpu.VMEM((4 * JB, chans), BF),
            pltpu.VMEM((TABLE, chans), BF),
            pltpu.VMEM((4 * JB, chans), BF),
            pltpu.VMEM((TABLE, chans), BF),
            pltpu.VMEM((rows, chans), BF),
        ],
        32,
        (3 << 30, 8 << 20),
    )(scal, *pks, hot_t, mixl, cot)

    keep, send = call(
        functools.partial(backward_kernel, n_chan, rows, width, scale),
        [SMEM] + [VMEM] * (n_chan + 7),
        [shape((n_chan // 2, SUMS, width), F32)] * 2,
        [VMEM] * 2,
        [
            pltpu.VMEM((tiles, rows + 2 * edge, LANE), F32),
            pltpu.VMEM((own_tiles, ext, LANE), F32),
            pltpu.VMEM((2, padded, chans), BF),
            pltpu.VMEM((TABLE, chans), BF),
            pltpu.VMEM((TABLE, chans), BF),
            pltpu.VMEM((2 * JB, chans), F32),
            pltpu.VMEM((2, 8, chans), F32),
            pltpu.VMEM((8, chans), F32),
            pltpu.VMEM((rows, chans), BF),
            pltpu.VMEM((2 * JB, chans), F32),
        ],
        40,
        (3 << 30, 8 << 20),
    )(scal, *pks, hot, hot1, mixl, cot, s1, x1, gp)

    g_mine = gm1
    for bit in reversed(range(seq_bits)):
        g_other = flip_bits(g_mine, "seq", 1 << bit)
        if bit:
            g_mine = lax.optimization_barrier(
                (g_mine.astype(F32) + g_other.astype(F32)).astype(BF)
            )
    s_mine = keep + flip_bits(send, "chan", 1)
    for bit in range(1, n_chan.bit_length() - 1):
        s_mine = s_mine[0::2] + flip_bits(s_mine[1::2], "chan", 1 << bit)
    s_mine = s_mine[0]
    for bit in reversed(range(seq_bits)):
        s_other = flip_bits(s_mine, "seq", 1 << bit)
        if bit:
            s_mine = s_mine + s_other

    big = pltpu.VMEM((width, chans), F32)
    (grad_mix,) = call(
        functools.partial(mix1_kernel, n_chan, width),
        [SMEM, VMEM, VMEM],
        [shape((BLOCKS, width, chans), F32)],
        [HBM],
        [big, pltpu.SemaphoreType.DMA],
        16,
        (1 << 20, 1 << 21),
    )(scal, g_mine, g_other)
    grad_mix, grad_taps, grad_embed = call(
        functools.partial(finish_kernel, n_chan, width),
        [SMEM, VMEM, VMEM, VMEM, HBM],
        [
            shape((BLOCKS, width, chans), F32),
            shape((TAPS, BLOCKS, width), F32),
            shape((BASES, width), F32),
        ],
        [HBM, VMEM, VMEM],
        [big, pltpu.SemaphoreType.DMA((chans // (2 * LANE),))],
        16,
        (1 << 24, 1 << 21),
        {4: 0},
    )(scal, stack, s_mine, s_other, grad_mix)
    return x2, jnp.swapaxes(grad_mix, 1, 2), jnp.swapaxes(grad_taps, 0, 1), grad_embed


def solution(mesh):
    in_specs = (
        P(("groups", "seq")),
        P(("groups", "seq"), "chan"),
        P(None, "chan"),
        P(None, None, "chan"),
        P(None, None, "chan"),
        P(),
    )
    out_specs = (
        P(("groups", "seq"), "chan"),
        P("groups", None, "chan"),
        P("groups", None, "chan"),
        P("groups", "chan"),
    )
    return jax.shard_map(body, mesh=mesh, in_specs=in_specs, out_specs=out_specs, check_vma=False)
```

```python
import functools
import math

import jax
import jax.numpy as jnp
from jax import lax
from jax.experimental import pallas as pl
from jax.experimental.pallas import tpu as pltpu
from jax.sharding import PartitionSpec as P

TAPS = 5
BASES = 4
BLOCKS = 2
DMAX = 8
HALF = TAPS // 2
REACH = HALF * DMAX
LANE = 128
JB = 32
GELU_SCALE = math.sqrt(2.0 / math.pi)
CUBIC = 0.044715
BF = jnp.bfloat16
F32 = jnp.float32
ROW_EMBED, ROW_TAPS0, ROW_TAPS1, TABLE = 0, BASES, BASES + TAPS, 16
ROW_GE, ROW_R, ROW_GT0, ROW_GT1, SUMS = 20, 24, 48, 56, 64


def dot(a, b, **kw):
    return jnp.dot(a, b, preferred_element_type=F32, **kw)


def dot_t(a, b):
    return lax.dot_general(a, b, (((1,), (1,)), ((), ())), preferred_element_type=F32)


def t_dot(a, b):
    return lax.dot_general(a, b, (((0,), (0,)), ((), ())), preferred_element_type=F32)


def iotas(shape):
    return lax.broadcasted_iota(jnp.int32, shape, 0), lax.broadcasted_iota(jnp.int32, shape, 1)


def as_bf(mask):
    return mask.astype(F32).astype(BF)


def reversal(size):
    row, col = iotas((size, size))
    return as_bf(row + col == size - 1)


def split_bf(x):
    high = x.astype(BF)
    return high, (x - high.astype(F32)).astype(BF)


def flip_exact(x, rev):
    high, rest = split_bf(x)
    mid, low = split_bf(x - high.astype(F32))
    del rest
    return dot(high, rev) + dot(mid, rev) + dot(low, rev)


def xor_blocks(blocks, me):
    for bit in range(len(blocks).bit_length() - 1):
        swap = lax.bitwise_and(lax.shift_right_logical(me, bit), 1) == 1
        blocks = [jnp.where(swap, blocks[k ^ (1 << bit)], blocks[k]) for k in range(len(blocks))]
    return blocks


def gelu_parts(v):
    square = v * v
    tangent = jnp.tanh(v * (GELU_SCALE + (GELU_SCALE * CUBIC) * square))
    half = 0.5 + 0.5 * tangent
    value = v * half
    slope = half + (v * (1.0 - tangent * tangent)) * (
        0.5 * GELU_SCALE + (1.5 * GELU_SCALE * CUBIC) * square
    )
    return value, slope


def select_rows(kind, rows):
    row, col = iotas((rows, TABLE))
    local = row % JB
    used = local < TAPS * BASES
    tap, letter = local // BASES, local % BASES
    want = {"tap0": ROW_TAPS0 + tap, "tap1": ROW_TAPS1 + tap, "letter": ROW_EMBED + letter}[kind]
    return as_bf(used & (col == want))


def one_hot_t(tokens):
    n = tokens[0].shape[1]
    inside = tokens[HALF] != 0
    row = lax.broadcasted_iota(jnp.int32, (2 * JB, n), 0)
    local = row % JB
    group = jnp.where(local < TAPS * BASES, local // BASES + TAPS * (row // JB), -1)
    seen = jnp.zeros((2 * JB, n), jnp.int32)
    for g, line in enumerate(tokens):
        line = jnp.where(inside, line, 0)
        seen = jnp.where(group == g, jnp.broadcast_to(line, (2 * JB, n)), seen)
    return (seen == local % BASES + 1).astype(F32)


def pair_table(tables, rev_w):
    sel_t, sel_e = select_rows("tap0", JB), select_rows("letter", JB)
    plain = [dot(sel_t, t) * dot(sel_e, t) for t in tables]
    n = len(tables)
    out = []
    for k in range(n):
        high, low = split_bf(plain[k])
        fhigh, flow = split_bf(plain[n - 1 - k])
        out.append((high, dot(fhigh, rev_w).astype(BF), low, dot(flow, rev_w).astype(BF)))
    return out


def pack_kernel(width, mix_ref, embed_ref, taps_ref, out_ref, e_ref, t_ref, sems):
    big = pltpu.make_async_copy(mix_ref.at[0], out_ref.at[pl.ds(0, width)], sems.at[0])
    small = [
        pltpu.make_async_copy(embed_ref, e_ref, sems.at[1]),
        pltpu.make_async_copy(taps_ref, t_ref, sems.at[2]),
    ]
    for copy in small + [big]:
        copy.start()
    out_ref[width:, :] = jnp.zeros((TABLE, out_ref.shape[1]), BF)
    for copy in small:
        copy.wait()
    taps = t_ref[...].astype(F32)
    lines = [e_ref[...].astype(F32)]
    lines += [taps[j, block : block + 1, :] for block in range(BLOCKS) for j in range(TAPS)]
    lines.append(jnp.zeros((TABLE - BASES - 2 * TAPS, width), F32))
    out_ref[width:, :width] = jnp.concatenate(lines, axis=0).astype(BF)
    big.wait()


def local_kernel(n_chan, width, mix_ref, cot_ref, mixl_ref, cotl_ref, m_ref, c_ref, sems):
    first = pltpu.make_async_copy(mix_ref.at[1], m_ref, sems.at[0])
    second = pltpu.make_async_copy(cot_ref, c_ref, sems.at[1])
    first.start()
    second.start()
    first.wait()
    blocks = [m_ref[:, k * width : (k + 1) * width] for k in range(n_chan)]
    for k, block in enumerate(xor_blocks(blocks, lax.axis_index("chan"))):
        mixl_ref[:, k * width : (k + 1) * width] = block
    second.wait()
    cotl_ref[...] = c_ref[...].astype(F32).T.astype(BF)


def prep_kernel(n_seq, rows, dils, tok_ref, a_ref, hot_ref, hot1_ref):
    place = lax.axis_index("seq")

    def line(block):
        inside = jnp.logical_and(block >= 0, block < n_seq)
        safe = jnp.clip(block, 0, n_seq - 1)
        letters = tok_ref[pl.ds(lax.bitwise_xor(safe, place), 1), :] + 1
        return jnp.where(inside, letters, 0)

    def around(block):
        lines = [line(block - 1)[:, rows - LANE :], line(block), line(block + 1)[:, :LANE]]
        return jnp.concatenate(lines, axis=1)

    total = rows + 2 * LANE
    this = jnp.broadcast_to(around(place), (8, total))
    mirror = jnp.broadcast_to(around(n_seq - 1 - place), (8, total)).astype(F32).astype(BF)
    rev, n_tiles = reversal(LANE), total // LANE
    other = jnp.concatenate(
        [dot(mirror[:, t * LANE : (t + 1) * LANE], rev) for t in reversed(range(n_tiles))], axis=1
    ).astype(jnp.int32)

    def windows(dilation, margin, count):
        out = []
        for strand, source in ((1, this), (-1, other)):
            for j in range(TAPS):
                first = LANE - margin + strand * (j - HALF) * dilation
                out.append(pltpu.roll(source, total - first, 1)[:1, :count])
        return out

    hot = one_hot_t(windows(dils[0], REACH, a_ref.shape[0]))
    a_ref[...] = jnp.concatenate([hot, hot], axis=0).T.astype(BF)
    hot_ref[...] = hot.astype(BF)
    hot1_ref[...] = one_hot_t(windows(dils[1], 0, rows)).astype(BF)


def forward_kernel(n_chan, rows, width, scale, dils, *refs):
    tiles = n_chan * width // LANE
    pks, refs = refs[:n_chan], refs[n_chan:]
    (a_ref, mixl_ref, cot_ref), refs = refs[:3], refs[3:]
    (x2_ref, gm_ref, s_ref, st_ref, e_ref, et_ref), refs = refs[:6], refs[6:]
    x1_refs, refs = (refs[:tiles], refs[tiles : 2 * tiles]), refs[2 * tiles :]
    gp_refs, refs = (refs[:tiles], refs[tiles : 2 * tiles]), refs[2 * tiles :]
    w_ref, wt_ref, m_ref, held, sem = refs
    ext = rows + 2 * REACH
    me, dil = lax.axis_index("chan"), dils[1]
    rev, rev_w = reversal(LANE), reversal(width)

    tables = [pk[width:, :width] for pk in pks]
    stacks = [jnp.concatenate(p, axis=0) for p in pair_table(tables, rev_w)]
    for k, stack in enumerate(xor_blocks(stacks, me)):
        st_ref[:, k * width : (k + 1) * width] = stack
    for k in range(n_chan):
        total = dot_t(st_ref[...], pks[k][:width, :])
        high, low = split_bf(total[: 2 * JB] + total[2 * JB :])
        w_ref[:, k * width : (k + 1) * width] = jnp.concatenate([high, low], axis=0)
        e_ref[:, k * width : (k + 1) * width] = tables[k]

    for t in range(tiles):
        src = slice((tiles - 1 - t) * LANE, (tiles - t) * LANE)
        dst = slice(t * LANE, (t + 1) * LANE)
        flipped = dot(w_ref[:, src], rev).astype(BF)
        wt_ref[:, dst] = jnp.concatenate(
            [flipped[JB : 2 * JB], flipped[:JB], flipped[3 * JB :], flipped[2 * JB : 3 * JB]], axis=0
        )
        et_ref[:, dst] = dot(e_ref[:, src], rev).astype(BF)

    row, col = iotas((4 * JB, TABLE))
    centre = HALF * BASES
    pick_f = as_bf((row - centre == col) & (col < BASES))
    pick_r = as_bf((row - centre - JB == col) & (col < BASES))
    chunk, mchunk = ext // 5, rows // 6
    for t in range(tiles):
        dst = slice(t * LANE, (t + 1) * LANE)
        for strand, (wr, er, pick) in enumerate(((w_ref, e_ref, pick_f), (wt_ref, et_ref, pick_r))):
            rhs = jnp.concatenate([wr[:, dst], dot(pick, er[:, dst]).astype(BF)], axis=1)
            for i in range(5):
                where = pl.ds(i * chunk, chunk)
                both = dot(a_ref[where, :], rhs)
                value, slope = gelu_parts(both[:, :LANE])
                x1_refs[strand][t][where, :] = both[:, LANE:] + value
                gp_refs[strand][t][where, :] = slope.astype(BF)

        taps_f = e_ref[:, dst].astype(F32)
        taps_r = et_ref[:, dst].astype(F32)
        for i in range(6):
            first = i * mchunk
            total = jnp.zeros((mchunk, LANE), F32)
            for j in range(TAPS):
                shift = (j - HALF) * dil
                line = slice(ROW_TAPS1 + j, ROW_TAPS1 + j + 1)
                total += taps_f[line, :] * x1_refs[0][t][pl.ds(first + REACH + shift, mchunk), :]
                total += taps_r[line, :] * x1_refs[1][t][pl.ds(first + REACH - shift, mchunk), :]
            m_ref[first : first + mchunk, dst] = total.astype(BF)

    half = rows // 2
    n_own = pl.cdiv(width, LANE)
    for i in range(2):
        where = pl.ds(i * half, half)
        value, slope = gelu_parts(dot_t(m_ref[where, :], mixl_ref[...]))
        inner = pl.ds(REACH + i * half, half)
        own = jnp.concatenate([x1_refs[0][t][inner, :] for t in range(n_own)], axis=1)[:, :width]
        held[:, where] = (own + value).T.astype(BF)
        s_ref[where, :] = ((cot_ref[where, :].astype(F32) * scale) * slope).astype(BF)
    copy = pltpu.make_async_copy(held, x2_ref, sem)
    copy.start()

    gm_ref[...] = t_dot(s_ref[...], m_ref[...]).astype(BF)
    copy.wait()


def backward_kernel(n_chan, rows, width, scale, dils, *refs):
    chans = n_chan * width
    tiles = chans // LANE
    pks, refs = refs[:n_chan], refs[n_chan:]
    (hot_ref, hot1_ref, mixl_ref, cot_ref, s_ref, e_ref, et_ref), refs = refs[:7], refs[7:]
    x1_refs, refs = (refs[:tiles], refs[tiles : 2 * tiles]), refs[2 * tiles :]
    gp_refs, refs = (refs[:tiles], refs[tiles : 2 * tiles]), refs[2 * tiles :]
    (keep_ref, send_ref), refs = refs[:2], refs[2:]
    p_refs, s0_refs, refs = refs[:tiles], refs[tiles : 2 * tiles], refs[2 * tiles :]
    g2_ref, dw_ref, gt_ref, g1_ref, pb_ref, st_ref = refs
    ext = rows + 2 * REACH
    padded = hot_ref.shape[1]
    me, dil = lax.axis_index("chan"), dils[1]
    rev, rev_w = reversal(LANE), reversal(width)
    tables = [pk[width:, :width] for pk in pks]

    edge = 2 * REACH
    n_own = pl.cdiv(width, LANE)
    g2 = cot_ref[...].astype(F32) * scale
    g2_ref[:, :REACH, :] = jnp.zeros((n_own, REACH, LANE), F32)
    g2_ref[:, rows + REACH :, :] = jnp.zeros((n_own, REACH, LANE), F32)
    g2 = jnp.concatenate([g2, jnp.zeros((rows, n_own * LANE - width), F32)], axis=1)
    for t in range(n_own):
        g2_ref[t, REACH : rows + REACH, :] = g2[:, t * LANE : (t + 1) * LANE]

    mchunk, chunk = rows // 6, ext // 5
    others = [None] * tiles
    for t in range(tiles):
        dst = slice(t * LANE, (t + 1) * LANE)
        p_ref, s0_ref = p_refs[t], s0_refs[t]
        if t % 2 == 0:
            pair = dot(s_ref[...], mixl_ref[:, t * LANE : (t + 2) * LANE])
            pb_ref[:, t * LANE : (t + 2) * LANE] = pair.astype(BF)
        p_ref[:edge, :] = jnp.zeros((edge, LANE), F32)
        p_ref[rows + edge :, :] = jnp.zeros((edge, LANE), F32)
        p_ref[edge : rows + edge, :] = pair[:, (t % 2) * LANE : (t % 2 + 1) * LANE]
        s0_ref[ext:, :] = jnp.zeros((padded - ext, 2 * LANE), BF)
        taps_f = e_ref[:, dst].astype(F32)
        taps_r = et_ref[:, dst].astype(F32)
        for i in range(5):
            first = i * chunk
            where = pl.ds(first, chunk)
            f = jnp.zeros((chunk, LANE), F32)
            r = jnp.zeros((chunk, LANE), F32)
            for j in range(TAPS):
                shift = (j - HALF) * dil
                line = slice(ROW_TAPS1 + j, ROW_TAPS1 + j + 1)
                f += taps_f[line, :] * p_ref[pl.ds(first + REACH - shift, chunk), :]
                r += taps_r[line, :] * p_ref[pl.ds(first + REACH + shift, chunk), :]
            if t < n_own:
                f += g2_ref[t, where, :]
            s0_ref[where, :LANE] = (f * gp_refs[0][t][where, :].astype(F32)).astype(BF)
            s0_ref[where, LANE:] = (r * gp_refs[1][t][where, :].astype(F32)).astype(BF)
        both = dot(hot_ref[...], s0_ref[...])
        dw_ref[:, dst] = both[:, :LANE]
        others[t] = both[:, LANE:]

        sums = [jnp.zeros((8, LANE), F32) for _ in range(2 * TAPS)]
        for i in range(6):
            first = i * mchunk
            here = p_ref[pl.ds(edge + first, mchunk), :]
            for strand in range(2):
                for j in range(TAPS):
                    shift = (j - HALF) * dil * (1 - 2 * strand)
                    prod = here * x1_refs[strand][t][pl.ds(first + REACH + shift, mchunk), :]
                    sums[strand * TAPS + j] += prod.reshape(mchunk // 8, 8, LANE).sum(0)
        for strand in range(2):
            lines = [jnp.sum(sums[strand * TAPS + j], axis=0, keepdims=True) for j in range(TAPS)]
            gt_ref[strand, :, dst] = jnp.concatenate(lines + [jnp.zeros((8 - TAPS, LANE), F32)], axis=0)

    hot1 = hot1_ref[...]
    by_tap = dot(hot1, pb_ref[...])
    own_letters = dot(hot1[: 16, :], cot_ref[...]) * scale
    srow, scol = iotas((8, JB))
    sum_letter = as_bf((scol % BASES == srow) & (scol < TAPS * BASES))
    sum_tap = as_bf((scol // BASES == srow) & (scol < TAPS * BASES))

    def sums_of(sel, x):
        high, rest = split_bf(x)
        return dot(sel, high) + dot(sel, rest)

    sel1 = select_rows("tap1", JB)
    g1_other = []
    for t in range(tiles):
        dst = slice(t * LANE, (t + 1) * LANE)
        g1_ref[:, dst] = sums_of(sum_letter, by_tap[:JB, dst] * dot(sel1, e_ref[:, dst]))
        g1_other.append(sums_of(sum_letter, by_tap[JB:, dst] * dot(sel1, et_ref[:, dst])))
    for t in range(tiles):
        dst = slice(t * LANE, (t + 1) * LANE)
        src = slice((tiles - 1 - t) * LANE, (tiles - t) * LANE)
        flipped = flip_exact(others[tiles - 1 - t], rev)
        dw_ref[:, dst] += jnp.concatenate([flipped[JB:], flipped[:JB]], axis=0)
        g1_ref[:, dst] += flip_exact(g1_other[tiles - 1 - t], rev)
        gt_ref[0, :, dst] += flip_exact(gt_ref[1, :, src], rev)

    sel_t, sel_e = select_rows("tap0", JB), select_rows("letter", JB)
    total = jnp.zeros((2 * JB, chans), F32)
    for k in range(n_chan):
        part = dw_ref[:, k * width : (k + 1) * width].astype(BF)
        total = total + dot(part, pks[k][:width, :])
    st_ref[...] = total
    grads = xor_blocks([st_ref[:, k * width : (k + 1) * width] for k in range(n_chan)], me)
    for kk in range(n_chan):
        both = grads[kk][:JB] + flip_exact(grads[n_chan - 1 - kk][JB:], rev_w)
        table = tables[kk]
        lanes = slice(kk * width, (kk + 1) * width)
        letters = sums_of(sum_letter, both * dot(sel_t, table)) + g1_ref[:, lanes]
        if kk == 0:
            zeros = jnp.zeros((BASES, width), F32)
            own = own_letters[HALF * BASES : (HALF + 1) * BASES, :]
            letters = letters + jnp.concatenate([own, zeros], axis=0)
        place = (keep_ref, send_ref)[kk % 2]
        place[kk // 2, :ROW_R, :] = jnp.concatenate([dw_ref[:ROW_GE, lanes], letters[:BASES]], axis=0)
        place[kk // 2, ROW_R : 2 * ROW_R, :] = dw_ref[JB : JB + ROW_R, lanes]
        place[kk // 2, ROW_GT0 : ROW_GT0 + 8, :] = sums_of(sum_tap, both * dot(sel_e, table))
        place[kk // 2, ROW_GT1 : ROW_GT1 + 8, :] = gt_ref[0, :, lanes]


def mix1_kernel(n_chan, width, a_ref, b_ref, out_ref, held, sem):
    def block(k):
        lanes = slice(k * width, (k + 1) * width)
        return a_ref[:, lanes].astype(F32) + b_ref[:, lanes].astype(F32)

    for k, part in enumerate(xor_blocks([block(k) for k in range(n_chan)], lax.axis_index("chan"))):
        held[:, k * width : (k + 1) * width] = part
    copy = pltpu.make_async_copy(held, out_ref.at[1], sem)
    copy.start()
    copy.wait()


def finish_kernel(n_chan, width, st_ref, sa_ref, sb_ref, _, gm_ref, gt_ref, ge_ref, held, sems):
    sums = sa_ref[...] + sb_ref[...]
    fill = jnp.zeros((JB - ROW_GE, width), F32)
    dw = jnp.concatenate([sums[:ROW_GE], fill, sums[ROW_R : ROW_R + ROW_GE], fill], axis=0).astype(BF)
    copies = []
    step = 2 * LANE
    for i in range(n_chan * width // step):
        lanes = pl.ds(i * step, step)
        held[:, lanes] = t_dot(dw, st_ref[: 2 * JB, lanes])
        copies.append(pltpu.make_async_copy(held.at[:, lanes], gm_ref.at[0, :, lanes], sems.at[i]))
        copies[-1].start()
    for j in range(TAPS):
        gt_ref[j, 0:1, :] = sums[ROW_GT0 + j : ROW_GT0 + j + 1]
        gt_ref[j, 1:2, :] = sums[ROW_GT1 + j : ROW_GT1 + j + 1]
    ge_ref[...] = sums[ROW_GE : ROW_GE + BASES]
    for copy in copies:
        copy.wait()


VMEM = pl.BlockSpec(memory_space=pltpu.VMEM)
SMEM = pl.BlockSpec(memory_space=pltpu.SMEM)
HBM = pl.BlockSpec(memory_space=pltpu.HBM)


def in_hbm(x):
    return pltpu.with_memory_space_constraint(x, pltpu.HBM)


def call(kernel, in_specs, out_shape, out_specs, scratch, limit, cost, aliases=None):
    flops, moved = cost
    return pl.pallas_call(
        kernel,
        out_shape=out_shape,
        in_specs=in_specs,
        out_specs=out_specs,
        scratch_shapes=scratch,
        input_output_aliases=aliases or {},
        compiler_params=pltpu.CompilerParams(vmem_limit_bytes=limit << 20),
        cost_estimate=pl.CostEstimate(flops=flops, bytes_accessed=moved, transcendentals=0),
    )


def flip_bits(x, axis, mask):
    return lax.ppermute(x, axis, [(i, i ^ mask) for i in range(lax.axis_size(axis))])


def body(tokens, cotangent, embed, taps, mix, dilations):
    rows, width = cotangent.shape
    n_seq, n_chan = lax.axis_size("seq"), lax.axis_size("chan")
    chans = n_chan * width
    tiles = chans // LANE
    ext = rows + 2 * REACH
    padded = pl.cdiv(ext, LANE) * LANE
    edge = 2 * REACH
    own_tiles = pl.cdiv(width, LANE)
    scale = 1.0 / math.sqrt(rows * n_seq)
    shape = jax.ShapeDtypeStruct
    mix_t = jnp.swapaxes(mix, 1, 2)

    (pk,) = call(
        functools.partial(pack_kernel, width),
        [HBM, HBM, HBM],
        [shape((width + TABLE, chans), BF)],
        [VMEM],
        [
            pltpu.VMEM((BASES, width), BF),
            pltpu.VMEM((TAPS, BLOCKS, width), BF),
            pltpu.SemaphoreType.DMA((3,)),
        ],
        8,
        (0, width * chans * 4),
    )(in_hbm(mix_t), in_hbm(embed), in_hbm(jnp.swapaxes(taps, 0, 1)))

    letters = lax.optimization_barrier((tokens.reshape(1, rows), pk))[0]
    seq_bits = n_seq.bit_length() - 1
    for bit in range(seq_bits):
        letters = jnp.concatenate([letters, flip_bits(letters, "seq", 1 << bit)], axis=0)

    mixl, cot = call(
        functools.partial(local_kernel, n_chan, width),
        [HBM, HBM],
        [shape((width, chans), BF), shape((rows, width), BF)],
        [VMEM] * 2,
        [
            pltpu.VMEM((width, chans), BF),
            pltpu.VMEM((width, rows), BF),
            pltpu.SemaphoreType.DMA((2,)),
        ],
        16,
        (1 << 20, 1 << 20),
    )(in_hbm(mix_t), in_hbm(cotangent.T))

    pks = [pk]
    for bit in reversed(range(n_chan.bit_length() - 1)):
        ready = [pks[0]] + [lax.optimization_barrier((p, letters, mixl, cot))[0] for p in pks[1:]]
        moved = [flip_bits(p, "chan", 1 << bit) for p in ready]
        pks = [q for pair in zip(pks, moved) for q in pair]

    hot_t, hot, hot1 = call(
        functools.partial(prep_kernel, n_seq, rows),
        [SMEM, VMEM],
        [shape((padded, 4 * JB), BF), shape((2 * JB, padded), BF), shape((2 * JB, rows), BF)],
        [VMEM] * 3,
        [],
        16,
        (1 << 20, 1 << 20),
    )(dilations, letters)

    rows_ext, slopes = shape((ext, LANE), F32), shape((ext, LANE), BF)
    x2, gm1, s1, stack, table, table_r, *strands = call(
        functools.partial(forward_kernel, n_chan, rows, width, scale),
        [SMEM] + [VMEM] * (n_chan + 3),
        [
            shape((width, rows), BF),
            shape((width, chans), BF),
            shape((rows, width), BF),
            shape((4 * JB, chans), BF),
            shape((TABLE, chans), BF),
            shape((TABLE, chans), BF),
        ]
        + [rows_ext] * (2 * tiles)
        + [slopes] * (2 * tiles),
        [HBM] + [VMEM] * (5 + 4 * tiles),
        [
            pltpu.VMEM((4 * JB, chans), BF),
            pltpu.VMEM((4 * JB, chans), BF),
            pltpu.VMEM((rows, chans), BF),
            pltpu.VMEM((width, rows), BF),
            pltpu.SemaphoreType.DMA,
        ],
        32,
        (3 << 30, 8 << 20),
    )(dilations, *pks, hot_t, mixl, cot)

    keep, send = call(
        functools.partial(backward_kernel, n_chan, rows, width, scale),
        [SMEM] + [VMEM] * (n_chan + 7 + 4 * tiles),
        [shape((n_chan // 2, SUMS, width), F32)] * 2,
        [VMEM] * 2,
        [pltpu.VMEM((rows + 2 * edge, LANE), F32)] * tiles
        + [pltpu.VMEM((padded, 2 * LANE), BF)] * tiles
        + [
            pltpu.VMEM((own_tiles, ext, LANE), F32),
            pltpu.VMEM((2 * JB, chans), F32),
            pltpu.VMEM((2, 8, chans), F32),
            pltpu.VMEM((8, chans), F32),
            pltpu.VMEM((rows, chans), BF),
            pltpu.VMEM((2 * JB, chans), F32),
        ],
        40,
        (3 << 30, 8 << 20),
    )(dilations, *pks, hot, hot1, mixl, cot, s1, table, table_r, *strands)

    g_mine = gm1
    for bit in reversed(range(seq_bits)):
        g_other = flip_bits(g_mine, "seq", 1 << bit)
        if bit:
            g_mine = lax.optimization_barrier(
                (g_mine.astype(F32) + g_other.astype(F32)).astype(BF)
            )
    s_mine = keep + flip_bits(send, "chan", 1)
    for bit in range(1, n_chan.bit_length() - 1):
        s_mine = s_mine[0::2] + flip_bits(s_mine[1::2], "chan", 1 << bit)
    s_mine = s_mine[0]
    for bit in reversed(range(seq_bits)):
        s_other = flip_bits(s_mine, "seq", 1 << bit)
        if bit:
            s_mine = s_mine + s_other

    big = pltpu.VMEM((width, chans), F32)
    (grad_mix,) = call(
        functools.partial(mix1_kernel, n_chan, width),
        [VMEM, VMEM],
        [shape((BLOCKS, width, chans), F32)],
        [HBM],
        [big, pltpu.SemaphoreType.DMA],
        16,
        (1 << 20, 1 << 21),
    )(g_mine, g_other)
    grad_mix, grad_taps, grad_embed = call(
        functools.partial(finish_kernel, n_chan, width),
        [VMEM, VMEM, VMEM, HBM],
        [
            shape((BLOCKS, width, chans), F32),
            shape((TAPS, BLOCKS, width), F32),
            shape((BASES, width), F32),
        ],
        [HBM, VMEM, VMEM],
        [big, pltpu.SemaphoreType.DMA((chans // (2 * LANE),))],
        16,
        (1 << 24, 1 << 21),
        {3: 0},
    )(stack, s_mine, s_other, grad_mix)
    return x2.T, jnp.swapaxes(grad_mix, 1, 2), jnp.swapaxes(grad_taps, 0, 1), grad_embed


def solution(mesh):
    in_specs = (
        P(("groups", "seq")),
        P(("groups", "seq"), "chan"),
        P(None, "chan"),
        P(None, None, "chan"),
        P(None, None, "chan"),
        P(),
    )
    out_specs = (
        P(("groups", "seq"), "chan"),
        P("groups", None, "chan"),
        P("groups", None, "chan"),
        P("groups", "chan"),
    )
    return jax.shard_map(body, mesh=mesh, in_specs=in_specs, out_specs=out_specs, check_vma=False)
```

```python
import functools
import math

import jax
import jax.numpy as jnp
from jax import lax
from jax.experimental import pallas as pl
from jax.experimental.pallas import tpu as pltpu
from jax.sharding import PartitionSpec as P

TAPS = 5
BASES = 4
BLOCKS = 2
DMAX = 8
HALF = TAPS // 2
REACH = HALF * DMAX
LANE = 128
JB = 32
GELU_SCALE = math.sqrt(2.0 / math.pi)
CUBIC = 0.044715
BF = jnp.bfloat16
F32 = jnp.float32
ROW_EMBED, ROW_TAPS0, ROW_TAPS1, TABLE = 0, BASES, BASES + TAPS, 16
ROW_GE, ROW_R, ROW_GT0, ROW_GT1, SUMS = 20, 24, 48, 56, 64


def dot(a, b, **kw):
    return jnp.dot(a, b, preferred_element_type=F32, **kw)


def dot_t(a, b):
    return lax.dot_general(a, b, (((1,), (1,)), ((), ())), preferred_element_type=F32)


def t_dot(a, b):
    return lax.dot_general(a, b, (((0,), (0,)), ((), ())), preferred_element_type=F32)


def iotas(shape):
    return lax.broadcasted_iota(jnp.int32, shape, 0), lax.broadcasted_iota(jnp.int32, shape, 1)


def as_bf(mask):
    return mask.astype(F32).astype(BF)


def reversal(size):
    row, col = iotas((size, size))
    return as_bf(row + col == size - 1)


def split_bf(x):
    high = x.astype(BF)
    return high, (x - high.astype(F32)).astype(BF)


def reverse_lanes(parts, rev):
    n = parts[0].shape[1] // LANE
    rows = [p.shape[0] for p in parts]
    pile = [p[:, t * LANE : (t + 1) * LANE] for p in parts for t in range(n)]
    turned = dot(jnp.concatenate(pile, axis=0), rev)
    out, first = [], 0
    for count in rows:
        tiles = [turned[first + t * count : first + (t + 1) * count] for t in range(n)]
        out.append(jnp.concatenate(tiles[::-1], axis=1))
        first += n * count
    return out


def reverse_wide(parts, rev):
    split = [split_bf(p) for p in parts]
    turned = reverse_lanes([q for pair in split for q in pair], rev)
    return [turned[2 * i] + turned[2 * i + 1] for i in range(len(parts))]


def xor_blocks(blocks, me):
    for bit in range(len(blocks).bit_length() - 1):
        swap = lax.bitwise_and(lax.shift_right_logical(me, bit), 1) == 1
        blocks = [jnp.where(swap, blocks[k ^ (1 << bit)], blocks[k]) for k in range(len(blocks))]
    return blocks


def gelu_parts(v):
    square = v * v
    tangent = jnp.tanh(v * (GELU_SCALE + (GELU_SCALE * CUBIC) * square))
    half = 0.5 + 0.5 * tangent
    value = v * half
    slope = half + (v * (1.0 - tangent * tangent)) * (
        0.5 * GELU_SCALE + (1.5 * GELU_SCALE * CUBIC) * square
    )
    return value, slope


def gelu_doubled(half):
    square = half * half
    cubic = (8.0 * GELU_SCALE * CUBIC) * square
    above = 1.0 + jnp.tanh(half * (2.0 * GELU_SCALE + cubic))
    value = half * above
    slope = above + value * ((2.0 - above) * (2.0 * GELU_SCALE + 3.0 * cubic))
    return value, slope


def select_rows(kind, rows):
    row, col = iotas((rows, TABLE))
    local = row % JB
    used = local < TAPS * BASES
    tap, letter = local // BASES, local % BASES
    want = {"tap0": ROW_TAPS0 + tap, "tap1": ROW_TAPS1 + tap, "letter": ROW_EMBED + letter}[kind]
    return as_bf(used & (col == want))


def one_hot_t(tokens):
    n = tokens[0].shape[1]
    inside = tokens[HALF] != 0
    row = lax.broadcasted_iota(jnp.int32, (2 * JB, n), 0)
    local = row % JB
    group = jnp.where(local < TAPS * BASES, local // BASES + TAPS * (row // JB), -1)
    seen = jnp.zeros((2 * JB, n), jnp.int32)
    for g, line in enumerate(tokens):
        line = jnp.where(inside, line, 0)
        seen = jnp.where(group == g, jnp.broadcast_to(line, (2 * JB, n)), seen)
    return (seen == local % BASES + 1).astype(F32)


def pack_kernel(width, mix_ref, embed_ref, taps_ref, tok_ref, out_ref, letters_ref, e_ref, t_ref, sems):
    big = pltpu.make_async_copy(mix_ref.at[0], out_ref.at[pl.ds(0, width)], sems.at[0])
    small = [
        pltpu.make_async_copy(embed_ref, e_ref, sems.at[1]),
        pltpu.make_async_copy(taps_ref, t_ref, sems.at[2]),
        pltpu.make_async_copy(tok_ref, letters_ref.at[0], sems.at[3]),
    ]
    for copy in small + [big]:
        copy.start()
    out_ref[width:, :] = jnp.zeros((TABLE, out_ref.shape[1]), BF)
    for copy in small:
        copy.wait()
    taps = t_ref[...].astype(F32)
    lines = [e_ref[...].astype(F32)]
    lines += [taps[j, block : block + 1, :] for block in range(BLOCKS) for j in range(TAPS)]
    lines.append(jnp.zeros((TABLE - BASES - 2 * TAPS, width), F32))
    out_ref[width:, :width] = jnp.concatenate(lines, axis=0).astype(BF)
    big.wait()


def local_kernel(n_chan, width, mix_ref, cot_ref, mixl_ref, cotl_ref, m_ref, c_ref, sems):
    first = pltpu.make_async_copy(mix_ref.at[1], m_ref, sems.at[0])
    second = pltpu.make_async_copy(cot_ref, c_ref, sems.at[1])
    first.start()
    second.start()
    first.wait()
    blocks = [m_ref[:, k * width : (k + 1) * width] for k in range(n_chan)]
    for k, block in enumerate(xor_blocks(blocks, lax.axis_index("chan"))):
        mixl_ref[:, k * width : (k + 1) * width] = block
    second.wait()
    cotl_ref[...] = c_ref[...].astype(F32).T.astype(BF)


def prep_kernel(n_seq, rows, dils, tok_ref, a_ref, hot_ref, hot1_ref):
    place = lax.axis_index("seq")

    def line(block):
        inside = jnp.logical_and(block >= 0, block < n_seq)
        safe = jnp.clip(block, 0, n_seq - 1)
        letters = tok_ref[pl.ds(lax.bitwise_xor(safe, place), 1), :] + 1
        return jnp.where(inside, letters, 0)

    def around(block):
        lines = [line(block - 1)[:, rows - LANE :], line(block), line(block + 1)[:, :LANE]]
        return jnp.concatenate(lines, axis=1)

    total = rows + 2 * LANE
    this = jnp.broadcast_to(around(place), (8, total))
    mirror = jnp.broadcast_to(around(n_seq - 1 - place), (8, total)).astype(F32).astype(BF)
    rev, n_tiles = reversal(LANE), total // LANE
    other = jnp.concatenate(
        [dot(mirror[:, t * LANE : (t + 1) * LANE], rev) for t in reversed(range(n_tiles))], axis=1
    ).astype(jnp.int32)

    def windows(dilation, margin, count):
        out = []
        for strand, source in ((1, this), (-1, other)):
            for j in range(TAPS):
                first = LANE - margin + strand * (j - HALF) * dilation
                out.append(pltpu.roll(source, total - first, 1)[:1, :count])
        return out

    hot = one_hot_t(windows(dils[0], REACH, a_ref.shape[0]))
    a_ref[...] = jnp.concatenate([hot, hot], axis=0).T.astype(BF)
    hot_ref[...] = hot.astype(BF)
    hot1_ref[...] = one_hot_t(windows(dils[1], 0, rows)).astype(BF)


def forward_kernel(n_chan, rows, width, scale, dils, *refs):
    tiles = n_chan * width // LANE
    pks, refs = refs[:n_chan], refs[n_chan:]
    (a_ref, mixl_ref, cot_ref), refs = refs[:3], refs[3:]
    (x2_ref, gm_ref, s_ref, st_ref, e_ref, et_ref), refs = refs[:6], refs[6:]
    x1_refs, refs = (refs[:tiles], refs[tiles : 2 * tiles]), refs[2 * tiles :]
    gp_refs, refs = (refs[:tiles], refs[tiles : 2 * tiles]), refs[2 * tiles :]
    w_ref, b_ref, m_ref, held, sem = refs
    chans = n_chan * width
    ext = rows + 2 * REACH
    me, dil = lax.axis_index("chan"), dils[1]
    rev = reversal(LANE)
    blocks = [slice(k * width, (k + 1) * width) for k in range(n_chan)]

    for k in range(n_chan):
        e_ref[:, blocks[k]] = pks[k][width:, :width]
    table = e_ref[...]
    plain = dot(select_rows("tap0", JB), table) * dot(select_rows("letter", JB), table)
    high, low = split_bf(plain)
    turned, turned_low, table_r = reverse_lanes([high, low, table], rev)
    et_ref[...] = table_r.astype(BF)
    b_ref[...] = jnp.concatenate([high, turned.astype(BF), low, turned_low.astype(BF)], axis=0)
    for k, block in enumerate(xor_blocks([b_ref[:, lanes] for lanes in blocks], me)):
        st_ref[:, blocks[k]] = block
    for k in range(n_chan):
        total = 0.5 * dot_t(st_ref[...], pks[k][:width, :])
        high, low = split_bf(total[: 2 * JB] + total[2 * JB :])
        w_ref[:, blocks[k]] = jnp.concatenate([high, low], axis=0)
    weights = w_ref[...]
    (swapped,) = reverse_lanes([weights], rev)
    order = [swapped[JB : 2 * JB], swapped[:JB], swapped[3 * JB :], swapped[2 * JB : 3 * JB]]
    weights_r = jnp.concatenate(order, axis=0).astype(BF)

    table, table_r = table.astype(F32), et_ref[...].astype(F32)
    centre = HALF * BASES
    keep = lax.broadcasted_iota(jnp.int32, (8, chans), 0) < BASES

    def lookup(source, first):
        lines = jnp.where(keep, source[:8], 0.0)
        above, below = jnp.zeros((first, chans), F32), jnp.zeros((4 * JB - first - 8, chans), F32)
        return jnp.concatenate([above, lines, below], axis=0).astype(BF)

    look, look_r = lookup(table, centre), lookup(table_r, JB + centre)
    chunk, mchunk = ext // 5, rows // 6
    for t in range(tiles):
        dst = slice(t * LANE, (t + 1) * LANE)
        for strand, (wr, er) in enumerate(((weights, look), (weights_r, look_r))):
            rhs = jnp.concatenate([wr[:, dst], er[:, dst]], axis=1)
            for i in range(5):
                where = pl.ds(i * chunk, chunk)
                both = dot(a_ref[where, :], rhs)
                value, slope = gelu_doubled(both[:, :LANE])
                x1_refs[strand][t][where, :] = both[:, LANE:] + value
                gp_refs[strand][t][where, :] = slope

        for i in range(6):
            first = i * mchunk
            terms = []
            for j in range(TAPS):
                shift = (j - HALF) * dil
                line = slice(ROW_TAPS1 + j, ROW_TAPS1 + j + 1)
                terms.append(table[line, dst] * x1_refs[0][t][pl.ds(first + REACH + shift, mchunk), :])
                terms.append(table_r[line, dst] * x1_refs[1][t][pl.ds(first + REACH - shift, mchunk), :])
            m_ref[first : first + mchunk, dst] = functools.reduce(jnp.add, terms).astype(BF)

    half = rows // 2
    n_own = pl.cdiv(width, LANE)
    for i in range(2):
        where = pl.ds(i * half, half)
        value, slope = gelu_parts(dot_t(m_ref[where, :], mixl_ref[...]))
        inner = pl.ds(REACH + i * half, half)
        own = jnp.concatenate([x1_refs[0][t][inner, :] for t in range(n_own)], axis=1)[:, :width]
        held[:, where] = (own + value).T.astype(BF)
        s_ref[where, :] = ((cot_ref[where, :].astype(F32) * scale) * slope).astype(BF)
    copy = pltpu.make_async_copy(held, x2_ref, sem)
    copy.start()

    gm_ref[...] = t_dot(s_ref[...], m_ref[...]).astype(BF)
    copy.wait()


def backward_kernel(n_chan, rows, width, scale, dils, *refs):
    chans = n_chan * width
    tiles = chans // LANE
    pks, refs = refs[:n_chan], refs[n_chan:]
    (hot_ref, hot1_ref, mixl_ref, cot_ref, s_ref, e_ref, et_ref), refs = refs[:7], refs[7:]
    x1_refs, refs = (refs[:tiles], refs[tiles : 2 * tiles]), refs[2 * tiles :]
    gp_refs, refs = (refs[:tiles], refs[tiles : 2 * tiles]), refs[2 * tiles :]
    (keep_ref, send_ref), refs = refs[:2], refs[2:]
    p_refs, s0_refs, refs = refs[:tiles], refs[tiles : 2 * tiles], refs[2 * tiles :]
    g2_ref, gt_ref, pb_ref, dw_ref, st_ref, back_ref, tail_ref = refs
    ext = rows + 2 * REACH
    padded = hot_ref.shape[1]
    me, dil = lax.axis_index("chan"), dils[1]
    rev = reversal(LANE)
    blocks = [slice(k * width, (k + 1) * width) for k in range(n_chan)]
    table, table_r = e_ref[...], et_ref[...]
    taps_f, taps_r = 0.5 * table.astype(F32), 0.5 * table_r.astype(F32)

    edge = 2 * REACH
    n_own = pl.cdiv(width, LANE)
    g2 = cot_ref[...].astype(F32) * scale
    g2_ref[:, :REACH, :] = jnp.zeros((n_own, REACH, LANE), F32)
    g2_ref[:, rows + REACH :, :] = jnp.zeros((n_own, REACH, LANE), F32)
    g2 = jnp.concatenate([g2, jnp.zeros((rows, n_own * LANE - width), F32)], axis=1)
    for t in range(n_own):
        g2_ref[t, REACH : rows + REACH, :] = 0.5 * g2[:, t * LANE : (t + 1) * LANE]

    mchunk, chunk = rows // 6, ext // 5
    plains, others = [None] * tiles, [None] * tiles
    for t in range(tiles):
        dst = slice(t * LANE, (t + 1) * LANE)
        p_ref, s0_ref = p_refs[t], s0_refs[t]
        if t % 2 == 0:
            pair = dot(s_ref[...], mixl_ref[:, t * LANE : (t + 2) * LANE])
            pb_ref[:, t * LANE : (t + 2) * LANE] = pair.astype(BF)
        p_ref[:edge, :] = jnp.zeros((edge, LANE), F32)
        p_ref[rows + edge :, :] = jnp.zeros((edge, LANE), F32)
        p_ref[edge : rows + edge, :] = pair[:, (t % 2) * LANE : (t % 2 + 1) * LANE]
        s0_ref[ext:, :] = jnp.zeros((padded - ext, 2 * LANE), BF)
        for i in range(5):
            first = i * chunk
            where = pl.ds(first, chunk)
            fs, rs = [], []
            for j in range(TAPS):
                window = p_ref[pl.ds(first + REACH + (j - HALF) * dil, chunk), :]
                ahead, back = ROW_TAPS1 + j, ROW_TAPS1 + TAPS - 1 - j
                fs.append(taps_f[back : back + 1, dst] * window)
                rs.append(taps_r[ahead : ahead + 1, dst] * window)
            if t < n_own:
                fs.append(g2_ref[t, where, :])
            f, r = functools.reduce(jnp.add, fs), functools.reduce(jnp.add, rs)
            s0_ref[where, :LANE] = (f * gp_refs[0][t][where, :]).astype(BF)
            s0_ref[where, LANE:] = (r * gp_refs[1][t][where, :]).astype(BF)
        both = dot(hot_ref[...], s0_ref[...])
        plains[t], others[t] = both[:, :LANE], both[:, LANE:]

        sums = [None] * (2 * TAPS)
        for i in range(6):
            first = i * mchunk
            here = p_ref[pl.ds(edge + first, mchunk), :]
            for strand in range(2):
                for j in range(TAPS):
                    shift = (j - HALF) * dil * (1 - 2 * strand)
                    prod = here * x1_refs[strand][t][pl.ds(first + REACH + shift, mchunk), :]
                    part = prod.reshape(mchunk // 8, 8, LANE).sum(0)
                    slot = strand * TAPS + j
                    sums[slot] = part if i == 0 else sums[slot] + part
        for strand in range(2):
            lines = [jnp.sum(sums[strand * TAPS + j], axis=0, keepdims=True) for j in range(TAPS)]
            gt_ref[strand, :, dst] = jnp.concatenate(lines + [jnp.zeros((8 - TAPS, LANE), F32)], axis=0)

    by_tap = dot(hot1_ref[...], pb_ref[...])
    own_letters = dot(hot1_ref[:16, :], cot_ref[...]) * scale
    srow, scol = iotas((8, JB))
    sum_letter = as_bf((scol % BASES == srow) & (scol < TAPS * BASES))
    sum_tap = as_bf((scol // BASES == srow) & (scol < TAPS * BASES))

    def sums_of(sel, x):
        high, rest = split_bf(x)
        return dot(sel, high) + dot(sel, rest)

    sel1 = select_rows("tap1", JB)
    ahead = by_tap[:JB] * dot(sel1, table)
    other = by_tap[JB:] * dot(sel1, table_r)
    turned, other, taps_turned = reverse_wide(
        [jnp.concatenate(others, axis=1), other, gt_ref[1]], rev
    )
    sums = jnp.concatenate(plains, axis=1) + jnp.concatenate([turned[JB:], turned[:JB]], axis=0)
    dw_ref[...] = sums
    letters = sums_of(sum_letter, ahead + other)
    tail_ref[8:16, :] = gt_ref[0] + taps_turned

    total = jnp.zeros((2 * JB, chans), F32)
    for k in range(n_chan):
        total = total + dot(dw_ref[:, blocks[k]].astype(BF), pks[k][:width, :])
    st_ref[...] = total
    for k, block in enumerate(xor_blocks([st_ref[:, lanes] for lanes in blocks], me)):
        back_ref[:, blocks[k]] = block
    (turned,) = reverse_wide([back_ref[JB:, :]], rev)
    both = back_ref[:JB, :] + turned
    tail_ref[0:8, :] = sums_of(sum_tap, both * dot(select_rows("letter", JB), table))
    letters = letters + sums_of(sum_letter, both * dot(select_rows("tap0", JB), table))
    tail_ref[16:24, :] = letters
    zeros = jnp.zeros((BASES, width), F32)
    own = jnp.concatenate([own_letters[HALF * BASES : (HALF + 1) * BASES, :], zeros], axis=0)
    for kk, lanes in enumerate(blocks):
        place, at = (keep_ref, send_ref)[kk % 2], kk // 2
        letters = tail_ref[16:24, lanes]
        if kk == 0:
            letters = letters + own
        place[at, :ROW_R, :] = jnp.concatenate([dw_ref[:ROW_GE, lanes], letters[:BASES]], axis=0)
        place[at, ROW_R : 2 * ROW_R, :] = dw_ref[JB : JB + ROW_R, lanes]
        place[at, ROW_GT0:, :] = tail_ref[0:16, lanes]


def mix1_kernel(n_chan, width, a_ref, b_ref, out_ref, held, sem):
    def block(k):
        lanes = slice(k * width, (k + 1) * width)
        return a_ref[:, lanes].astype(F32) + b_ref[:, lanes].astype(F32)

    for k, part in enumerate(xor_blocks([block(k) for k in range(n_chan)], lax.axis_index("chan"))):
        held[:, k * width : (k + 1) * width] = part
    copy = pltpu.make_async_copy(held, out_ref.at[1], sem)
    copy.start()
    copy.wait()


def finish_kernel(n_chan, width, st_ref, sa_ref, sb_ref, _, gm_ref, gt_ref, ge_ref, held, sems):
    sums = sa_ref[...] + sb_ref[...]
    fill = jnp.zeros((JB - ROW_GE, width), F32)
    dw = jnp.concatenate([sums[:ROW_GE], fill, sums[ROW_R : ROW_R + ROW_GE], fill], axis=0).astype(BF)
    copies = []
    step = 2 * LANE
    for i in range(n_chan * width // step):
        lanes = pl.ds(i * step, step)
        held[:, lanes] = t_dot(dw, st_ref[: 2 * JB, lanes])
        copies.append(pltpu.make_async_copy(held.at[:, lanes], gm_ref.at[0, :, lanes], sems.at[i]))
        copies[-1].start()
    for j in range(TAPS):
        gt_ref[j, 0:1, :] = sums[ROW_GT0 + j : ROW_GT0 + j + 1]
        gt_ref[j, 1:2, :] = sums[ROW_GT1 + j : ROW_GT1 + j + 1]
    ge_ref[...] = sums[ROW_GE : ROW_GE + BASES]
    for copy in copies:
        copy.wait()


VMEM = pl.BlockSpec(memory_space=pltpu.VMEM)
SMEM = pl.BlockSpec(memory_space=pltpu.SMEM)
HBM = pl.BlockSpec(memory_space=pltpu.HBM)


def in_hbm(x):
    return pltpu.with_memory_space_constraint(x, pltpu.HBM)


def call(kernel, in_specs, out_shape, out_specs, scratch, limit, cost, aliases=None):
    flops, moved = cost
    return pl.pallas_call(
        kernel,
        out_shape=out_shape,
        in_specs=in_specs,
        out_specs=out_specs,
        scratch_shapes=scratch,
        input_output_aliases=aliases or {},
        compiler_params=pltpu.CompilerParams(vmem_limit_bytes=limit << 20),
        cost_estimate=pl.CostEstimate(flops=flops, bytes_accessed=moved, transcendentals=0),
    )


def flip_bits(x, axis, mask):
    return lax.ppermute(x, axis, [(i, i ^ mask) for i in range(lax.axis_size(axis))])


def body(tokens, cotangent, embed, taps, mix, dilations):
    rows, width = cotangent.shape
    n_seq, n_chan = lax.axis_size("seq"), lax.axis_size("chan")
    chans = n_chan * width
    tiles = chans // LANE
    ext = rows + 2 * REACH
    padded = pl.cdiv(ext, LANE) * LANE
    edge = 2 * REACH
    own_tiles = pl.cdiv(width, LANE)
    scale = 1.0 / math.sqrt(rows * n_seq)
    shape = jax.ShapeDtypeStruct
    mix_t = jnp.swapaxes(mix, 1, 2)

    pk, letters = call(
        functools.partial(pack_kernel, width),
        [HBM] * 4,
        [shape((width + TABLE, chans), BF), shape((1, rows), jnp.int32)],
        [VMEM] * 2,
        [
            pltpu.VMEM((BASES, width), BF),
            pltpu.VMEM((TAPS, BLOCKS, width), BF),
            pltpu.SemaphoreType.DMA((4,)),
        ],
        8,
        (0, width * chans * 4),
    )(in_hbm(mix_t), in_hbm(embed), in_hbm(jnp.swapaxes(taps, 0, 1)), in_hbm(tokens))

    seq_bits = n_seq.bit_length() - 1
    for bit in range(seq_bits):
        letters = jnp.concatenate([letters, flip_bits(letters, "seq", 1 << bit)], axis=0)

    mixl, cot = call(
        functools.partial(local_kernel, n_chan, width),
        [HBM, HBM],
        [shape((width, chans), BF), shape((rows, width), BF)],
        [VMEM] * 2,
        [
            pltpu.VMEM((width, chans), BF),
            pltpu.VMEM((width, rows), BF),
            pltpu.SemaphoreType.DMA((2,)),
        ],
        16,
        (1 << 20, 1 << 20),
    )(in_hbm(mix_t), in_hbm(cotangent.T))

    pks = [pk]
    for bit in reversed(range(n_chan.bit_length() - 1)):
        ready = [pks[0]] + [lax.optimization_barrier((p, letters, mixl, cot))[0] for p in pks[1:]]
        moved = [flip_bits(p, "chan", 1 << bit) for p in ready]
        pks = [q for pair in zip(pks, moved) for q in pair]

    hot_t, hot, hot1 = call(
        functools.partial(prep_kernel, n_seq, rows),
        [SMEM, VMEM],
        [shape((padded, 4 * JB), BF), shape((2 * JB, padded), BF), shape((2 * JB, rows), BF)],
        [VMEM] * 3,
        [],
        16,
        (1 << 20, 1 << 20),
    )(dilations, letters)

    rows_ext = shape((ext, LANE), F32)
    x2, gm1, s1, stack, table, table_r, *strands = call(
        functools.partial(forward_kernel, n_chan, rows, width, scale),
        [SMEM] + [VMEM] * (n_chan + 3),
        [
            shape((width, rows), BF),
            shape((width, chans), BF),
            shape((rows, width), BF),
            shape((4 * JB, chans), BF),
            shape((TABLE, chans), BF),
            shape((TABLE, chans), BF),
        ]
        + [rows_ext] * (4 * tiles),
        [HBM] + [VMEM] * (5 + 4 * tiles),
        [
            pltpu.VMEM((4 * JB, chans), BF),
            pltpu.VMEM((4 * JB, chans), BF),
            pltpu.VMEM((rows, chans), BF),
            pltpu.VMEM((width, rows), BF),
            pltpu.SemaphoreType.DMA,
        ],
        32,
        (3 << 30, 8 << 20),
    )(dilations, *pks, hot_t, mixl, cot)

    keep, send = call(
        functools.partial(backward_kernel, n_chan, rows, width, scale),
        [SMEM] + [VMEM] * (n_chan + 7 + 4 * tiles),
        [shape((n_chan // 2, SUMS, width), F32)] * 2,
        [VMEM] * 2,
        [pltpu.VMEM((rows + 2 * edge, LANE), F32)] * tiles
        + [pltpu.VMEM((padded, 2 * LANE), BF)] * tiles
        + [
            pltpu.VMEM((own_tiles, ext, LANE), F32),
            pltpu.VMEM((2, 8, chans), F32),
            pltpu.VMEM((rows, chans), BF),
            pltpu.VMEM((2 * JB, chans), F32),
            pltpu.VMEM((2 * JB, chans), F32),
            pltpu.VMEM((2 * JB, chans), F32),
            pltpu.VMEM((24, chans), F32),
        ],
        40,
        (3 << 30, 8 << 20),
    )(dilations, *pks, hot, hot1, mixl, cot, s1, table, table_r, *strands)

    g_mine = gm1
    for bit in reversed(range(seq_bits)):
        g_other = flip_bits(g_mine, "seq", 1 << bit)
        if bit:
            g_mine = lax.optimization_barrier(
                (g_mine.astype(F32) + g_other.astype(F32)).astype(BF)
            )
    s_mine = keep + flip_bits(send, "chan", 1)
    for bit in range(1, n_chan.bit_length() - 1):
        s_mine = s_mine[0::2] + flip_bits(s_mine[1::2], "chan", 1 << bit)
    s_mine = s_mine[0]
    for bit in reversed(range(seq_bits)):
        s_other = flip_bits(s_mine, "seq", 1 << bit)
        if bit:
            s_mine = s_mine + s_other

    big = pltpu.VMEM((width, chans), F32)
    (grad_mix,) = call(
        functools.partial(mix1_kernel, n_chan, width),
        [VMEM, VMEM],
        [shape((BLOCKS, width, chans), F32)],
        [HBM],
        [big, pltpu.SemaphoreType.DMA],
        16,
        (1 << 20, 1 << 21),
    )(g_mine, g_other)
    grad_mix, grad_taps, grad_embed = call(
        functools.partial(finish_kernel, n_chan, width),
        [VMEM, VMEM, VMEM, HBM],
        [
            shape((BLOCKS, width, chans), F32),
            shape((TAPS, BLOCKS, width), F32),
            shape((BASES, width), F32),
        ],
        [HBM, VMEM, VMEM],
        [big, pltpu.SemaphoreType.DMA((chans // (2 * LANE),))],
        16,
        (1 << 24, 1 << 21),
        {3: 0},
    )(stack, s_mine, s_other, grad_mix)
    return x2.T, jnp.swapaxes(grad_mix, 1, 2), jnp.swapaxes(grad_taps, 0, 1), grad_embed


def solution(mesh):
    in_specs = (
        P(("groups", "seq")),
        P(("groups", "seq"), "chan"),
        P(None, "chan"),
        P(None, None, "chan"),
        P(None, None, "chan"),
        P(),
    )
    out_specs = (
        P(("groups", "seq"), "chan"),
        P("groups", None, "chan"),
        P("groups", None, "chan"),
        P("groups", "chan"),
    )
    return jax.shard_map(body, mesh=mesh, in_specs=in_specs, out_specs=out_specs, check_vma=False)
```

```python
import functools
import math

import jax
import jax.numpy as jnp
from jax import lax
from jax.experimental import pallas as pl
from jax.experimental.pallas import tpu as pltpu
from jax.sharding import PartitionSpec as P

TAPS = 5
BASES = 4
BLOCKS = 2
DMAX = 8
HALF = TAPS // 2
REACH = HALF * DMAX
LANE = 128
JB = 32
GELU_SCALE = math.sqrt(2.0 / math.pi)
CUBIC = 0.044715
BF = jnp.bfloat16
F32 = jnp.float32
ROW_EMBED, ROW_TAPS0, ROW_TAPS1, TABLE = 0, BASES, BASES + TAPS, 16
ROW_GE, ROW_R, ROW_GT0, ROW_GT1, SUMS = 20, 24, 48, 56, 64


def dot(a, b, **kw):
    return jnp.dot(a, b, preferred_element_type=F32, **kw)


def dot_t(a, b):
    return lax.dot_general(a, b, (((1,), (1,)), ((), ())), preferred_element_type=F32)


def t_dot(a, b):
    return lax.dot_general(a, b, (((0,), (0,)), ((), ())), preferred_element_type=F32)


def iotas(shape):
    return lax.broadcasted_iota(jnp.int32, shape, 0), lax.broadcasted_iota(jnp.int32, shape, 1)


def as_bf(mask):
    return mask.astype(F32).astype(BF)


def reversal(size):
    row, col = iotas((size, size))
    return as_bf(row + col == size - 1)


def split_bf(x):
    high = x.astype(BF)
    return high, (x - high.astype(F32)).astype(BF)


def reverse_lanes(parts, rev):
    n = parts[0].shape[1] // LANE
    rows = [p.shape[0] for p in parts]
    pile = [p[:, t * LANE : (t + 1) * LANE] for p in parts for t in range(n)]
    turned = dot(jnp.concatenate(pile, axis=0), rev)
    out, first = [], 0
    for count in rows:
        tiles = [turned[first + t * count : first + (t + 1) * count] for t in range(n)]
        out.append(jnp.concatenate(tiles[::-1], axis=1))
        first += n * count
    return out


def reverse_wide(parts, rev):
    split = [split_bf(p) for p in parts]
    turned = reverse_lanes([q for pair in split for q in pair], rev)
    return [turned[2 * i] + turned[2 * i + 1] for i in range(len(parts))]


def xor_blocks(blocks, me):
    for bit in range(len(blocks).bit_length() - 1):
        swap = lax.bitwise_and(lax.shift_right_logical(me, bit), 1) == 1
        blocks = [jnp.where(swap, blocks[k ^ (1 << bit)], blocks[k]) for k in range(len(blocks))]
    return blocks


def gelu_parts(v):
    square = v * v
    tangent = jnp.tanh(v * (GELU_SCALE + (GELU_SCALE * CUBIC) * square))
    half = 0.5 + 0.5 * tangent
    value = v * half
    slope = half + (v * (1.0 - tangent * tangent)) * (
        0.5 * GELU_SCALE + (1.5 * GELU_SCALE * CUBIC) * square
    )
    return value, slope


def gelu_doubled(half):
    square = half * half
    cubic = (8.0 * GELU_SCALE * CUBIC) * square
    above = 1.0 + jnp.tanh(half * (2.0 * GELU_SCALE + cubic))
    value = half * above
    slope = above + value * ((2.0 - above) * (2.0 * GELU_SCALE + 3.0 * cubic))
    return value, slope


def select_rows(kind, rows):
    row, col = iotas((rows, TABLE))
    local = row % JB
    used = local < TAPS * BASES
    tap, letter = local // BASES, local % BASES
    want = {"tap0": ROW_TAPS0 + tap, "tap1": ROW_TAPS1 + tap, "letter": ROW_EMBED + letter}[kind]
    return as_bf(used & (col == want))


def one_hot_t(tokens):
    n = tokens[0].shape[1]
    inside = tokens[HALF] != 0
    row = lax.broadcasted_iota(jnp.int32, (2 * JB, n), 0)
    local = row % JB
    group = jnp.where(local < TAPS * BASES, local // BASES + TAPS * (row // JB), -1)
    seen = jnp.zeros((2 * JB, n), jnp.int32)
    for g, line in enumerate(tokens):
        line = jnp.where(inside, line, 0)
        seen = jnp.where(group == g, jnp.broadcast_to(line, (2 * JB, n)), seen)
    return (seen == local % BASES + 1).astype(F32)


def pack_kernel(width, mix_ref, embed_ref, taps_ref, tok_ref, out_ref, letters_ref, e_ref, t_ref, sems):
    big = pltpu.make_async_copy(mix_ref.at[0], out_ref.at[pl.ds(0, width)], sems.at[0])
    small = [
        pltpu.make_async_copy(embed_ref, e_ref, sems.at[1]),
        pltpu.make_async_copy(taps_ref, t_ref, sems.at[2]),
        pltpu.make_async_copy(tok_ref, letters_ref.at[0], sems.at[3]),
    ]
    for copy in small + [big]:
        copy.start()
    out_ref[width:, :] = jnp.zeros((TABLE, out_ref.shape[1]), BF)
    for copy in small:
        copy.wait()
    taps = t_ref[...].astype(F32)
    lines = [e_ref[...].astype(F32)]
    lines += [taps[j, block : block + 1, :] for block in range(BLOCKS) for j in range(TAPS)]
    lines.append(jnp.zeros((TABLE - BASES - 2 * TAPS, width), F32))
    out_ref[width:, :width] = jnp.concatenate(lines, axis=0).astype(BF)
    big.wait()


def local_kernel(n_chan, width, mix_ref, cot_ref, mixl_ref, cotl_ref, m_ref, c_ref, sems):
    first = pltpu.make_async_copy(mix_ref.at[1], m_ref, sems.at[0])
    second = pltpu.make_async_copy(cot_ref, c_ref, sems.at[1])
    first.start()
    second.start()
    first.wait()
    blocks = [m_ref[:, k * width : (k + 1) * width] for k in range(n_chan)]
    for k, block in enumerate(xor_blocks(blocks, lax.axis_index("chan"))):
        mixl_ref[:, k * width : (k + 1) * width] = block
    second.wait()
    cotl_ref[...] = c_ref[...].astype(F32).T.astype(BF)


def prep_kernel(n_seq, rows, dils, tok_ref, a_ref, hot_ref, hot1_ref):
    place = lax.axis_index("seq")

    def line(block):
        inside = jnp.logical_and(block >= 0, block < n_seq)
        safe = jnp.clip(block, 0, n_seq - 1)
        letters = tok_ref[pl.ds(lax.bitwise_xor(safe, place), 1), :] + 1
        return jnp.where(inside, letters, 0)

    def around(block):
        lines = [line(block - 1)[:, rows - LANE :], line(block), line(block + 1)[:, :LANE]]
        return jnp.concatenate(lines, axis=1)

    total = rows + 2 * LANE
    this = jnp.broadcast_to(around(place), (8, total))
    mirror = jnp.broadcast_to(around(n_seq - 1 - place), (8, total)).astype(F32).astype(BF)
    rev, n_tiles = reversal(LANE), total // LANE
    other = jnp.concatenate(
        [dot(mirror[:, t * LANE : (t + 1) * LANE], rev) for t in reversed(range(n_tiles))], axis=1
    ).astype(jnp.int32)

    def windows(dilation, margin, count):
        out = []
        for strand, source in ((1, this), (-1, other)):
            for j in range(TAPS):
                first = LANE - margin + strand * (j - HALF) * dilation
                out.append(pltpu.roll(source, total - first, 1)[:1, :count])
        return out

    hot = one_hot_t(windows(dils[0], REACH, a_ref.shape[0]))
    a_ref[...] = jnp.concatenate([hot, hot], axis=0).T.astype(BF)
    hot_ref[...] = hot.astype(BF)
    hot1_ref[...] = one_hot_t(windows(dils[1], 0, rows)).astype(BF)


def forward_kernel(n_chan, rows, width, scale, dils, *refs):
    tiles = n_chan * width // LANE
    pks, refs = refs[:n_chan], refs[n_chan:]
    (a_ref, mixl_ref, cot_ref), refs = refs[:3], refs[3:]
    (x2_ref, near_ref, far_ref, s_ref, st_ref, e_ref, et_ref), refs = refs[:7], refs[7:]
    x1_refs, refs = (refs[:tiles], refs[tiles : 2 * tiles]), refs[2 * tiles :]
    gp_refs, refs = (refs[:tiles], refs[tiles : 2 * tiles]), refs[2 * tiles :]
    w_ref, b_ref, m_ref, held, sem = refs
    chans = n_chan * width
    ext = rows + 2 * REACH
    me, dil = lax.axis_index("chan"), dils[1]
    rev = reversal(LANE)
    blocks = [slice(k * width, (k + 1) * width) for k in range(n_chan)]

    for k in range(n_chan):
        e_ref[:, blocks[k]] = pks[k][width:, :width]
    table = e_ref[...]
    plain = dot(select_rows("tap0", JB), table) * dot(select_rows("letter", JB), table)
    high, low = split_bf(plain)
    turned, turned_low, table_r = reverse_lanes([high, low, table], rev)
    et_ref[...] = table_r.astype(BF)
    b_ref[...] = jnp.concatenate([high, turned.astype(BF), low, turned_low.astype(BF)], axis=0)
    for k, block in enumerate(xor_blocks([b_ref[:, lanes] for lanes in blocks], me)):
        st_ref[:, blocks[k]] = block
    for k in range(n_chan):
        total = 0.5 * dot_t(st_ref[...], pks[k][:width, :])
        high, low = split_bf(total[: 2 * JB] + total[2 * JB :])
        w_ref[:, blocks[k]] = jnp.concatenate([high, low], axis=0)
    weights = w_ref[...]
    (swapped,) = reverse_lanes([weights], rev)
    order = [swapped[JB : 2 * JB], swapped[:JB], swapped[3 * JB :], swapped[2 * JB : 3 * JB]]
    weights_r = jnp.concatenate(order, axis=0).astype(BF)

    table, table_r = table.astype(F32), et_ref[...].astype(F32)
    centre = HALF * BASES
    keep = lax.broadcasted_iota(jnp.int32, (8, chans), 0) < BASES

    def lookup(source, first):
        lines = jnp.where(keep, source[:8], 0.0)
        above, below = jnp.zeros((first, chans), F32), jnp.zeros((4 * JB - first - 8, chans), F32)
        return jnp.concatenate([above, lines, below], axis=0).astype(BF)

    look, look_r = lookup(table, centre), lookup(table_r, JB + centre)
    chunk, mchunk = ext // 5, rows // 6
    for t in range(tiles):
        dst = slice(t * LANE, (t + 1) * LANE)
        for strand, (wr, er) in enumerate(((weights, look), (weights_r, look_r))):
            rhs = jnp.concatenate([wr[:, dst], er[:, dst]], axis=1)
            for i in range(5):
                where = pl.ds(i * chunk, chunk)
                both = dot(a_ref[where, :], rhs)
                value, slope = gelu_doubled(both[:, :LANE])
                x1_refs[strand][t][where, :] = both[:, LANE:] + value
                gp_refs[strand][t][where, :] = slope

        for i in range(6):
            first = i * mchunk
            terms = []
            for j in range(TAPS):
                shift = (j - HALF) * dil
                line = slice(ROW_TAPS1 + j, ROW_TAPS1 + j + 1)
                terms.append(table[line, dst] * x1_refs[0][t][pl.ds(first + REACH + shift, mchunk), :])
                terms.append(table_r[line, dst] * x1_refs[1][t][pl.ds(first + REACH - shift, mchunk), :])
            m_ref[first : first + mchunk, dst] = functools.reduce(jnp.add, terms).astype(BF)

    half = rows // 2
    n_own = pl.cdiv(width, LANE)
    for i in range(2):
        where = pl.ds(i * half, half)
        value, slope = gelu_parts(dot_t(m_ref[where, :], mixl_ref[...]))
        inner = pl.ds(REACH + i * half, half)
        own = jnp.concatenate([x1_refs[0][t][inner, :] for t in range(n_own)], axis=1)[:, :width]
        held[:, where] = (own + value).T.astype(BF)
        s_ref[where, :] = ((cot_ref[where, :].astype(F32) * scale) * slope).astype(BF)
    copy = pltpu.make_async_copy(held, x2_ref, sem)
    copy.start()

    part = t_dot(s_ref[...], m_ref[...]).astype(BF)
    odd = lax.axis_index("seq") % 2 == 1
    near_ref[...] = jnp.where(odd, part[width // 2 :], part[: width // 2])
    far_ref[...] = jnp.where(odd, part[: width // 2], part[width // 2 :])
    copy.wait()


def backward_kernel(n_chan, rows, width, scale, dils, *refs):
    chans = n_chan * width
    tiles = chans // LANE
    pks, refs = refs[:n_chan], refs[n_chan:]
    (hot_ref, hot1_ref, mixl_ref, cot_ref, s_ref, e_ref, et_ref), refs = refs[:7], refs[7:]
    x1_refs, refs = (refs[:tiles], refs[tiles : 2 * tiles]), refs[2 * tiles :]
    gp_refs, refs = (refs[:tiles], refs[tiles : 2 * tiles]), refs[2 * tiles :]
    (keep_ref, send_ref), refs = refs[:2], refs[2:]
    p_refs, s0_refs, refs = refs[:tiles], refs[tiles : 2 * tiles], refs[2 * tiles :]
    g2_ref, gt_ref, pb_ref, dw_ref, st_ref, back_ref, tail_ref = refs
    ext = rows + 2 * REACH
    padded = hot_ref.shape[1]
    me, dil = lax.axis_index("chan"), dils[1]
    rev = reversal(LANE)
    blocks = [slice(k * width, (k + 1) * width) for k in range(n_chan)]
    table, table_r = e_ref[...], et_ref[...]
    taps_f, taps_r = 0.5 * table.astype(F32), 0.5 * table_r.astype(F32)

    edge = 2 * REACH
    n_own = pl.cdiv(width, LANE)
    g2 = cot_ref[...].astype(F32) * scale
    g2_ref[:, :REACH, :] = jnp.zeros((n_own, REACH, LANE), F32)
    g2_ref[:, rows + REACH :, :] = jnp.zeros((n_own, REACH, LANE), F32)
    g2 = jnp.concatenate([g2, jnp.zeros((rows, n_own * LANE - width), F32)], axis=1)
    for t in range(n_own):
        g2_ref[t, REACH : rows + REACH, :] = 0.5 * g2[:, t * LANE : (t + 1) * LANE]

    mchunk, chunk = rows // 6, ext // 5
    plains, others = [None] * tiles, [None] * tiles
    for t in range(tiles):
        dst = slice(t * LANE, (t + 1) * LANE)
        p_ref, s0_ref = p_refs[t], s0_refs[t]
        if t % 2 == 0:
            pair = dot(s_ref[...], mixl_ref[:, t * LANE : (t + 2) * LANE])
            pb_ref[:, t * LANE : (t + 2) * LANE] = pair.astype(BF)
        p_ref[:edge, :] = jnp.zeros((edge, LANE), F32)
        p_ref[rows + edge :, :] = jnp.zeros((edge, LANE), F32)
        p_ref[edge : rows + edge, :] = pair[:, (t % 2) * LANE : (t % 2 + 1) * LANE]
        s0_ref[ext:, :] = jnp.zeros((padded - ext, 2 * LANE), BF)
        for i in range(5):
            first = i * chunk
            where = pl.ds(first, chunk)
            fs, rs = [], []
            for j in range(TAPS):
                window = p_ref[pl.ds(first + REACH + (j - HALF) * dil, chunk), :]
                ahead, back = ROW_TAPS1 + j, ROW_TAPS1 + TAPS - 1 - j
                fs.append(taps_f[back : back + 1, dst] * window)
                rs.append(taps_r[ahead : ahead + 1, dst] * window)
            if t < n_own:
                fs.append(g2_ref[t, where, :])
            f, r = functools.reduce(jnp.add, fs), functools.reduce(jnp.add, rs)
            s0_ref[where, :LANE] = (f * gp_refs[0][t][where, :]).astype(BF)
            s0_ref[where, LANE:] = (r * gp_refs[1][t][where, :]).astype(BF)
        both = dot(hot_ref[...], s0_ref[...])
        plains[t], others[t] = both[:, :LANE], both[:, LANE:]

        sums = [None] * (2 * TAPS)
        for i in range(6):
            first = i * mchunk
            here = p_ref[pl.ds(edge + first, mchunk), :]
            for strand in range(2):
                for j in range(TAPS):
                    shift = (j - HALF) * dil * (1 - 2 * strand)
                    prod = here * x1_refs[strand][t][pl.ds(first + REACH + shift, mchunk), :]
                    part = prod.reshape(mchunk // 8, 8, LANE).sum(0)
                    slot = strand * TAPS + j
                    sums[slot] = part if i == 0 else sums[slot] + part
        for strand in range(2):
            lines = [jnp.sum(sums[strand * TAPS + j], axis=0, keepdims=True) for j in range(TAPS)]
            gt_ref[strand, :, dst] = jnp.concatenate(lines + [jnp.zeros((8 - TAPS, LANE), F32)], axis=0)

    by_tap = dot(hot1_ref[...], pb_ref[...])
    own_letters = dot(hot1_ref[:16, :], cot_ref[...]) * scale
    srow, scol = iotas((8, JB))
    sum_letter = as_bf((scol % BASES == srow) & (scol < TAPS * BASES))
    sum_tap = as_bf((scol // BASES == srow) & (scol < TAPS * BASES))

    def sums_of(sel, x):
        high, rest = split_bf(x)
        return dot(sel, high) + dot(sel, rest)

    sel1 = select_rows("tap1", JB)
    ahead = by_tap[:JB] * dot(sel1, table)
    other = by_tap[JB:] * dot(sel1, table_r)
    turned, other, taps_turned = reverse_wide(
        [jnp.concatenate(others, axis=1), other, gt_ref[1]], rev
    )
    sums = jnp.concatenate(plains, axis=1) + jnp.concatenate([turned[JB:], turned[:JB]], axis=0)
    dw_ref[...] = sums
    letters = sums_of(sum_letter, ahead + other)
    tail_ref[8:16, :] = gt_ref[0] + taps_turned

    total = jnp.zeros((2 * JB, chans), F32)
    for k in range(n_chan):
        total = total + dot(dw_ref[:, blocks[k]].astype(BF), pks[k][:width, :])
    st_ref[...] = total
    for k, block in enumerate(xor_blocks([st_ref[:, lanes] for lanes in blocks], me)):
        back_ref[:, blocks[k]] = block
    (turned,) = reverse_wide([back_ref[JB:, :]], rev)
    both = back_ref[:JB, :] + turned
    tail_ref[0:8, :] = sums_of(sum_tap, both * dot(select_rows("letter", JB), table))
    letters = letters + sums_of(sum_letter, both * dot(select_rows("tap0", JB), table))
    tail_ref[16:24, :] = letters
    zeros = jnp.zeros((BASES, width), F32)
    own = jnp.concatenate([own_letters[HALF * BASES : (HALF + 1) * BASES, :], zeros], axis=0)
    for kk, lanes in enumerate(blocks):
        place, at = (keep_ref, send_ref)[kk % 2], kk // 2
        letters = tail_ref[16:24, lanes]
        if kk == 0:
            letters = letters + own
        place[at, :ROW_R, :] = jnp.concatenate([dw_ref[:ROW_GE, lanes], letters[:BASES]], axis=0)
        place[at, ROW_R : 2 * ROW_R, :] = dw_ref[JB : JB + ROW_R, lanes]
        place[at, ROW_GT0:, :] = tail_ref[0:16, lanes]


def mix1_kernel(n_chan, width, near_ref, far_ref, out_ref, held, sem):
    me, odd = lax.axis_index("chan"), lax.axis_index("seq") % 2
    half = width // 2
    for source, first in ((near_ref, odd * half), (far_ref, (1 - odd) * half)):
        blocks = [source[:, k * width : (k + 1) * width].astype(F32) for k in range(n_chan)]
        for k, part in enumerate(xor_blocks(blocks, me)):
            held[pl.ds(pl.multiple_of(first, half), half), k * width : (k + 1) * width] = part
    copy = pltpu.make_async_copy(held, out_ref.at[1], sem)
    copy.start()
    copy.wait()


def finish_kernel(n_chan, width, st_ref, sa_ref, sb_ref, _, gm_ref, gt_ref, ge_ref, held, sems):
    sums = sa_ref[...] + sb_ref[...]
    fill = jnp.zeros((JB - ROW_GE, width), F32)
    dw = jnp.concatenate([sums[:ROW_GE], fill, sums[ROW_R : ROW_R + ROW_GE], fill], axis=0).astype(BF)
    copies = []
    step = 2 * LANE
    for i in range(n_chan * width // step):
        lanes = pl.ds(i * step, step)
        held[:, lanes] = t_dot(dw, st_ref[: 2 * JB, lanes])
        copies.append(pltpu.make_async_copy(held.at[:, lanes], gm_ref.at[0, :, lanes], sems.at[i]))
        copies[-1].start()
    for j in range(TAPS):
        gt_ref[j, 0:1, :] = sums[ROW_GT0 + j : ROW_GT0 + j + 1]
        gt_ref[j, 1:2, :] = sums[ROW_GT1 + j : ROW_GT1 + j + 1]
    ge_ref[...] = sums[ROW_GE : ROW_GE + BASES]
    for copy in copies:
        copy.wait()


VMEM = pl.BlockSpec(memory_space=pltpu.VMEM)
SMEM = pl.BlockSpec(memory_space=pltpu.SMEM)
HBM = pl.BlockSpec(memory_space=pltpu.HBM)


def in_hbm(x):
    return pltpu.with_memory_space_constraint(x, pltpu.HBM)


def call(kernel, in_specs, out_shape, out_specs, scratch, limit, cost, aliases=None):
    flops, moved = cost
    return pl.pallas_call(
        kernel,
        out_shape=out_shape,
        in_specs=in_specs,
        out_specs=out_specs,
        scratch_shapes=scratch,
        input_output_aliases=aliases or {},
        compiler_params=pltpu.CompilerParams(vmem_limit_bytes=limit << 20),
        cost_estimate=pl.CostEstimate(flops=flops, bytes_accessed=moved, transcendentals=0),
    )


def flip_bits(x, axis, mask):
    return lax.ppermute(x, axis, [(i, i ^ mask) for i in range(lax.axis_size(axis))])


def body(tokens, cotangent, embed, taps, mix, dilations):
    rows, width = cotangent.shape
    n_seq, n_chan = lax.axis_size("seq"), lax.axis_size("chan")
    chans = n_chan * width
    tiles = chans // LANE
    ext = rows + 2 * REACH
    padded = pl.cdiv(ext, LANE) * LANE
    edge = 2 * REACH
    own_tiles = pl.cdiv(width, LANE)
    scale = 1.0 / math.sqrt(rows * n_seq)
    shape = jax.ShapeDtypeStruct
    mix_t = jnp.swapaxes(mix, 1, 2)

    pk, letters = call(
        functools.partial(pack_kernel, width),
        [HBM] * 4,
        [shape((width + TABLE, chans), BF), shape((1, rows), jnp.int32)],
        [VMEM] * 2,
        [
            pltpu.VMEM((BASES, width), BF),
            pltpu.VMEM((TAPS, BLOCKS, width), BF),
            pltpu.SemaphoreType.DMA((4,)),
        ],
        8,
        (0, width * chans * 4),
    )(in_hbm(mix_t), in_hbm(embed), in_hbm(jnp.swapaxes(taps, 0, 1)), in_hbm(tokens))

    seq_bits = n_seq.bit_length() - 1
    for bit in range(seq_bits):
        letters = jnp.concatenate([letters, flip_bits(letters, "seq", 1 << bit)], axis=0)

    mixl, cot = call(
        functools.partial(local_kernel, n_chan, width),
        [HBM, HBM],
        [shape((width, chans), BF), shape((rows, width), BF)],
        [VMEM] * 2,
        [
            pltpu.VMEM((width, chans), BF),
            pltpu.VMEM((width, rows), BF),
            pltpu.SemaphoreType.DMA((2,)),
        ],
        16,
        (1 << 20, 1 << 20),
    )(in_hbm(mix_t), in_hbm(cotangent.T))

    pks = [pk]
    for bit in reversed(range(n_chan.bit_length() - 1)):
        ready = [pks[0]] + [lax.optimization_barrier((p, letters, mixl, cot))[0] for p in pks[1:]]
        moved = [flip_bits(p, "chan", 1 << bit) for p in ready]
        pks = [q for pair in zip(pks, moved) for q in pair]

    hot_t, hot, hot1 = call(
        functools.partial(prep_kernel, n_seq, rows),
        [SMEM, VMEM],
        [shape((padded, 4 * JB), BF), shape((2 * JB, padded), BF), shape((2 * JB, rows), BF)],
        [VMEM] * 3,
        [],
        16,
        (1 << 20, 1 << 20),
    )(dilations, letters)

    rows_ext = shape((ext, LANE), F32)
    x2, near, far, s1, stack, table, table_r, *strands = call(
        functools.partial(forward_kernel, n_chan, rows, width, scale),
        [SMEM] + [VMEM] * (n_chan + 3),
        [
            shape((width, rows), BF),
            shape((width // 2, chans), BF),
            shape((width // 2, chans), BF),
            shape((rows, width), BF),
            shape((4 * JB, chans), BF),
            shape((TABLE, chans), BF),
            shape((TABLE, chans), BF),
        ]
        + [rows_ext] * (4 * tiles),
        [HBM] + [VMEM] * (6 + 4 * tiles),
        [
            pltpu.VMEM((4 * JB, chans), BF),
            pltpu.VMEM((4 * JB, chans), BF),
            pltpu.VMEM((rows, chans), BF),
            pltpu.VMEM((width, rows), BF),
            pltpu.SemaphoreType.DMA,
        ],
        32,
        (3 << 30, 8 << 20),
    )(dilations, *pks, hot_t, mixl, cot)

    keep, send = call(
        functools.partial(backward_kernel, n_chan, rows, width, scale),
        [SMEM] + [VMEM] * (n_chan + 7 + 4 * tiles),
        [shape((n_chan // 2, SUMS, width), F32)] * 2,
        [VMEM] * 2,
        [pltpu.VMEM((rows + 2 * edge, LANE), F32)] * tiles
        + [pltpu.VMEM((padded, 2 * LANE), BF)] * tiles
        + [
            pltpu.VMEM((own_tiles, ext, LANE), F32),
            pltpu.VMEM((2, 8, chans), F32),
            pltpu.VMEM((rows, chans), BF),
            pltpu.VMEM((2 * JB, chans), F32),
            pltpu.VMEM((2 * JB, chans), F32),
            pltpu.VMEM((2 * JB, chans), F32),
            pltpu.VMEM((24, chans), F32),
        ],
        40,
        (3 << 30, 8 << 20),
    )(dilations, *pks, hot, hot1, mixl, cot, s1, table, table_r, *strands)

    def rounded_sum(a, b):
        return lax.optimization_barrier((a.astype(F32) + b.astype(F32)).astype(BF))

    arrived = lax.optimization_barrier((flip_bits(far, "seq", 1), keep))[0]
    g_mine = rounded_sum(near, arrived)
    for bit in range(1, seq_bits):
        g_mine = rounded_sum(g_mine, flip_bits(g_mine, "seq", 1 << bit))
    g_other = flip_bits(g_mine, "seq", 1)
    s_mine = keep + flip_bits(send, "chan", 1)
    for bit in range(1, n_chan.bit_length() - 1):
        s_mine = s_mine[0::2] + flip_bits(s_mine[1::2], "chan", 1 << bit)
    s_mine = s_mine[0]
    for bit in reversed(range(seq_bits)):
        s_other = flip_bits(s_mine, "seq", 1 << bit)
        if bit:
            s_mine = s_mine + s_other

    big = pltpu.VMEM((width, chans), F32)
    (grad_mix,) = call(
        functools.partial(mix1_kernel, n_chan, width),
        [VMEM, VMEM],
        [shape((BLOCKS, width, chans), F32)],
        [HBM],
        [big, pltpu.SemaphoreType.DMA],
        16,
        (1 << 20, 1 << 21),
    )(g_mine, g_other)
    grad_mix, grad_taps, grad_embed = call(
        functools.partial(finish_kernel, n_chan, width),
        [VMEM, VMEM, VMEM, HBM],
        [
            shape((BLOCKS, width, chans), F32),
            shape((TAPS, BLOCKS, width), F32),
            shape((BASES, width), F32),
        ],
        [HBM, VMEM, VMEM],
        [big, pltpu.SemaphoreType.DMA((chans // (2 * LANE),))],
        16,
        (1 << 24, 1 << 21),
        {3: 0},
    )(stack, s_mine, s_other, grad_mix)
    return x2.T, jnp.swapaxes(grad_mix, 1, 2), jnp.swapaxes(grad_taps, 0, 1), grad_embed


def solution(mesh):
    in_specs = (
        P(("groups", "seq")),
        P(("groups", "seq"), "chan"),
        P(None, "chan"),
        P(None, None, "chan"),
        P(None, None, "chan"),
        P(),
    )
    out_specs = (
        P(("groups", "seq"), "chan"),
        P("groups", None, "chan"),
        P("groups", None, "chan"),
        P("groups", "chan"),
    )
    return jax.shard_map(body, mesh=mesh, in_specs=in_specs, out_specs=out_specs, check_vma=False)
```

```python
import functools
import math

import jax
import jax.numpy as jnp
from jax import lax
from jax.experimental import pallas as pl
from jax.experimental.pallas import tpu as pltpu
from jax.sharding import PartitionSpec as P

TAPS = 5
BASES = 4
BLOCKS = 2
DMAX = 8
HALF = TAPS // 2
REACH = HALF * DMAX
LANE = 128
JB = 32
GELU_SCALE = math.sqrt(2.0 / math.pi)
CUBIC = 0.044715
BF = jnp.bfloat16
F32 = jnp.float32
ROW_EMBED, ROW_TAPS0, ROW_TAPS1, TABLE = 0, BASES, BASES + TAPS, 16
ROW_GE, ROW_R, ROW_GT0, ROW_GT1, SUMS = 20, 24, 48, 56, 64


def dot(a, b, **kw):
    return jnp.dot(a, b, preferred_element_type=F32, **kw)


def dot_t(a, b):
    return lax.dot_general(a, b, (((1,), (1,)), ((), ())), preferred_element_type=F32)


def t_dot(a, b):
    return lax.dot_general(a, b, (((0,), (0,)), ((), ())), preferred_element_type=F32)


def iotas(shape):
    return lax.broadcasted_iota(jnp.int32, shape, 0), lax.broadcasted_iota(jnp.int32, shape, 1)


def as_bf(mask):
    return mask.astype(F32).astype(BF)


def reversal(size):
    row, col = iotas((size, size))
    return as_bf(row + col == size - 1)


def split_bf(x):
    high = x.astype(BF)
    return high, (x - high.astype(F32)).astype(BF)


def reverse_lanes(parts, rev):
    n = parts[0].shape[1] // LANE
    rows = [p.shape[0] for p in parts]
    pile = [p[:, t * LANE : (t + 1) * LANE] for p in parts for t in range(n)]
    turned = dot(jnp.concatenate(pile, axis=0), rev)
    out, first = [], 0
    for count in rows:
        tiles = [turned[first + t * count : first + (t + 1) * count] for t in range(n)]
        out.append(jnp.concatenate(tiles[::-1], axis=1))
        first += n * count
    return out


def reverse_wide(parts, rev):
    split = [split_bf(p) for p in parts]
    turned = reverse_lanes([q for pair in split for q in pair], rev)
    return [turned[2 * i] + turned[2 * i + 1] for i in range(len(parts))]


def xor_blocks(blocks, me):
    for bit in range(len(blocks).bit_length() - 1):
        swap = lax.bitwise_and(lax.shift_right_logical(me, bit), 1) == 1
        blocks = [jnp.where(swap, blocks[k ^ (1 << bit)], blocks[k]) for k in range(len(blocks))]
    return blocks


def gelu_parts(v):
    square = v * v
    tangent = jnp.tanh(v * (GELU_SCALE + (GELU_SCALE * CUBIC) * square))
    half = 0.5 + 0.5 * tangent
    value = v * half
    slope = half + (v * (1.0 - tangent * tangent)) * (
        0.5 * GELU_SCALE + (1.5 * GELU_SCALE * CUBIC) * square
    )
    return value, slope


def gelu_doubled(half):
    square = half * half
    cubic = (8.0 * GELU_SCALE * CUBIC) * square
    above = 1.0 + jnp.tanh(half * (2.0 * GELU_SCALE + cubic))
    value = half * above
    slope = above + value * ((2.0 - above) * (2.0 * GELU_SCALE + 3.0 * cubic))
    return value, slope


def select_rows(kind, rows):
    row, col = iotas((rows, TABLE))
    local = row % JB
    used = local < TAPS * BASES
    tap, letter = local // BASES, local % BASES
    want = {"tap0": ROW_TAPS0 + tap, "tap1": ROW_TAPS1 + tap, "letter": ROW_EMBED + letter}[kind]
    return as_bf(used & (col == want))


def one_hot_t(tokens):
    n = tokens[0].shape[1]
    inside = tokens[HALF] != 0
    row = lax.broadcasted_iota(jnp.int32, (2 * JB, n), 0)
    local = row % JB
    group = jnp.where(local < TAPS * BASES, local // BASES + TAPS * (row // JB), -1)
    seen = jnp.zeros((2 * JB, n), jnp.int32)
    for g, line in enumerate(tokens):
        line = jnp.where(inside, line, 0)
        seen = jnp.where(group == g, jnp.broadcast_to(line, (2 * JB, n)), seen)
    return (seen == local % BASES + 1).astype(F32)


def pack_kernel(width, mix_ref, embed_ref, taps_ref, tok_ref, out_ref, letters_ref, e_ref, t_ref, sems):
    big = pltpu.make_async_copy(mix_ref.at[0], out_ref.at[pl.ds(0, width)], sems.at[0])
    small = [
        pltpu.make_async_copy(embed_ref, e_ref, sems.at[1]),
        pltpu.make_async_copy(taps_ref, t_ref, sems.at[2]),
        pltpu.make_async_copy(tok_ref, letters_ref.at[0], sems.at[3]),
    ]
    for copy in small + [big]:
        copy.start()
    out_ref[width:, :] = jnp.zeros((TABLE, out_ref.shape[1]), BF)
    for copy in small:
        copy.wait()
    taps = t_ref[...].astype(F32)
    lines = [e_ref[...].astype(F32)]
    lines += [taps[j, block : block + 1, :] for block in range(BLOCKS) for j in range(TAPS)]
    lines.append(jnp.zeros((TABLE - BASES - 2 * TAPS, width), F32))
    out_ref[width:, :width] = jnp.concatenate(lines, axis=0).astype(BF)
    big.wait()


def local_kernel(n_chan, width, mix_ref, cot_ref, mixl_ref, cotl_ref, m_ref, c_ref, sems):
    first = pltpu.make_async_copy(mix_ref.at[1], m_ref, sems.at[0])
    second = pltpu.make_async_copy(cot_ref, c_ref, sems.at[1])
    first.start()
    second.start()
    first.wait()
    blocks = [m_ref[:, k * width : (k + 1) * width] for k in range(n_chan)]
    for k, block in enumerate(xor_blocks(blocks, lax.axis_index("chan"))):
        mixl_ref[:, k * width : (k + 1) * width] = block
    second.wait()
    cotl_ref[...] = c_ref[...].astype(F32).T.astype(BF)


def prep_kernel(n_seq, rows, dils, tok_ref, a_ref, hot_ref, hot1_ref):
    place = lax.axis_index("seq")

    def line(block):
        inside = jnp.logical_and(block >= 0, block < n_seq)
        safe = jnp.clip(block, 0, n_seq - 1)
        letters = tok_ref[pl.ds(lax.bitwise_xor(safe, place), 1), :] + 1
        return jnp.where(inside, letters, 0)

    def around(block):
        lines = [line(block - 1)[:, rows - LANE :], line(block), line(block + 1)[:, :LANE]]
        return jnp.concatenate(lines, axis=1)

    total = rows + 2 * LANE
    this = jnp.broadcast_to(around(place), (8, total))
    mirror = jnp.broadcast_to(around(n_seq - 1 - place), (8, total)).astype(F32).astype(BF)
    rev, n_tiles = reversal(LANE), total // LANE
    other = jnp.concatenate(
        [dot(mirror[:, t * LANE : (t + 1) * LANE], rev) for t in reversed(range(n_tiles))], axis=1
    ).astype(jnp.int32)

    def windows(dilation, margin, count):
        out = []
        for strand, source in ((1, this), (-1, other)):
            for j in range(TAPS):
                first = LANE - margin + strand * (j - HALF) * dilation
                out.append(pltpu.roll(source, total - first, 1)[:1, :count])
        return out

    hot = one_hot_t(windows(dils[0], REACH, a_ref.shape[0]))
    a_ref[...] = jnp.concatenate([hot, hot], axis=0).T.astype(BF)
    hot_ref[...] = hot.astype(BF)
    hot1_ref[...] = one_hot_t(windows(dils[1], 0, rows)).astype(BF)


def forward_kernel(n_chan, rows, width, scale, dils, *refs):
    tiles = n_chan * width // LANE
    pks, refs = refs[:n_chan], refs[n_chan:]
    (a_ref, mixl_ref, cot_ref), refs = refs[:3], refs[3:]
    (x2_ref, near_ref, far_ref, s_ref, st_ref, e_ref, et_ref), refs = refs[:7], refs[7:]
    x1_refs, refs = (refs[:tiles], refs[tiles : 2 * tiles]), refs[2 * tiles :]
    gp_refs, refs = (refs[:tiles], refs[tiles : 2 * tiles]), refs[2 * tiles :]
    w_ref, b_ref, m_ref, held, sem = refs
    chans = n_chan * width
    ext = rows + 2 * REACH
    me, dil = lax.axis_index("chan"), dils[1]
    rev = reversal(LANE)
    blocks = [slice(k * width, (k + 1) * width) for k in range(n_chan)]

    for k in range(n_chan):
        e_ref[:, blocks[k]] = pks[k][width:, :width]
    table = e_ref[...]
    plain = dot(select_rows("tap0", JB), table) * dot(select_rows("letter", JB), table)
    high, low = split_bf(plain)
    turned, turned_low, table_r = reverse_lanes([high, low, table], rev)
    et_ref[...] = table_r.astype(BF)
    b_ref[...] = jnp.concatenate([high, turned.astype(BF), low, turned_low.astype(BF)], axis=0)
    for k, block in enumerate(xor_blocks([b_ref[:, lanes] for lanes in blocks], me)):
        st_ref[:, blocks[k]] = block
    for k in range(n_chan):
        total = 0.5 * dot_t(st_ref[...], pks[k][:width, :])
        high, low = split_bf(total[: 2 * JB] + total[2 * JB :])
        w_ref[:, blocks[k]] = jnp.concatenate([high, low], axis=0)
    weights = w_ref[...]
    (swapped,) = reverse_lanes([weights], rev)
    order = [swapped[JB : 2 * JB], swapped[:JB], swapped[3 * JB :], swapped[2 * JB : 3 * JB]]
    weights_r = jnp.concatenate(order, axis=0).astype(BF)

    table, table_r = table.astype(F32), et_ref[...].astype(F32)
    centre = HALF * BASES
    keep = lax.broadcasted_iota(jnp.int32, (8, chans), 0) < BASES

    def lookup(source, first):
        lines = jnp.where(keep, source[:8], 0.0)
        above, below = jnp.zeros((first, chans), F32), jnp.zeros((4 * JB - first - 8, chans), F32)
        return jnp.concatenate([above, lines, below], axis=0).astype(BF)

    look, look_r = lookup(table, centre), lookup(table_r, JB + centre)
    chunk, mchunk = ext // 5, rows // 6
    for t in range(tiles):
        dst = slice(t * LANE, (t + 1) * LANE)
        for strand, (wr, er) in enumerate(((weights, look), (weights_r, look_r))):
            rhs = jnp.concatenate([wr[:, dst], er[:, dst]], axis=1)
            for i in range(5):
                where = pl.ds(i * chunk, chunk)
                both = dot(a_ref[where, :], rhs)
                value, slope = gelu_doubled(both[:, :LANE])
                x1_refs[strand][t][where, :] = both[:, LANE:] + value
                gp_refs[strand][t][where, :] = slope

        for i in range(6):
            first = i * mchunk
            terms = []
            for j in range(TAPS):
                shift = (j - HALF) * dil
                line = slice(ROW_TAPS1 + j, ROW_TAPS1 + j + 1)
                terms.append(table[line, dst] * x1_refs[0][t][pl.ds(first + REACH + shift, mchunk), :])
                terms.append(table_r[line, dst] * x1_refs[1][t][pl.ds(first + REACH - shift, mchunk), :])
            m_ref[first : first + mchunk, dst] = functools.reduce(jnp.add, terms).astype(BF)

    half = rows // 2
    n_own = pl.cdiv(width, LANE)
    for i in range(2):
        where = pl.ds(i * half, half)
        value, slope = gelu_parts(dot_t(m_ref[where, :], mixl_ref[...]))
        inner = pl.ds(REACH + i * half, half)
        own = jnp.concatenate([x1_refs[0][t][inner, :] for t in range(n_own)], axis=1)[:, :width]
        held[:, where] = (own + value).T.astype(BF)
        s_ref[where, :] = ((cot_ref[where, :].astype(F32) * scale) * slope).astype(BF)
    copy = pltpu.make_async_copy(held, x2_ref, sem)
    copy.start()

    part = t_dot(s_ref[...], m_ref[...]).astype(BF)
    odd = lax.axis_index("seq") % 2 == 1
    near_ref[...] = jnp.where(odd, part[width // 2 :], part[: width // 2])
    far_ref[...] = jnp.where(odd, part[: width // 2], part[width // 2 :])
    copy.wait()


def backward_kernel(n_chan, rows, width, scale, dils, *refs):
    chans = n_chan * width
    tiles = chans // LANE
    pks, refs = refs[:n_chan], refs[n_chan:]
    (hot_ref, hot1_ref, mixl_ref, cot_ref, s_ref, e_ref, et_ref), refs = refs[:7], refs[7:]
    x1_refs, refs = (refs[:tiles], refs[tiles : 2 * tiles]), refs[2 * tiles :]
    gp_refs, refs = (refs[:tiles], refs[tiles : 2 * tiles]), refs[2 * tiles :]
    (keep_ref, send_ref), refs = refs[:2], refs[2:]
    p_refs, s0_refs, refs = refs[:tiles], refs[tiles : 2 * tiles], refs[2 * tiles :]
    g2_ref, gt_ref, pb_ref, dw_ref, st_ref, back_ref, tail_ref = refs
    ext = rows + 2 * REACH
    padded = hot_ref.shape[1]
    me, dil = lax.axis_index("chan"), dils[1]
    rev = reversal(LANE)
    blocks = [slice(k * width, (k + 1) * width) for k in range(n_chan)]
    table, table_r = e_ref[...], et_ref[...]
    taps_f, taps_r = 0.5 * table.astype(F32), 0.5 * table_r.astype(F32)

    edge = 2 * REACH
    n_own = pl.cdiv(width, LANE)
    g2 = cot_ref[...].astype(F32) * scale
    g2_ref[:, :REACH, :] = jnp.zeros((n_own, REACH, LANE), F32)
    g2_ref[:, rows + REACH :, :] = jnp.zeros((n_own, REACH, LANE), F32)
    g2 = jnp.concatenate([g2, jnp.zeros((rows, n_own * LANE - width), F32)], axis=1)
    for t in range(n_own):
        g2_ref[t, REACH : rows + REACH, :] = 0.5 * g2[:, t * LANE : (t + 1) * LANE]

    mchunk, chunk = rows // 6, ext // 5
    plains, others = [None] * tiles, [None] * tiles
    for t in range(tiles):
        dst = slice(t * LANE, (t + 1) * LANE)
        p_ref, s0_ref = p_refs[t], s0_refs[t]
        if t % 2 == 0:
            pair = dot(s_ref[...], mixl_ref[:, t * LANE : (t + 2) * LANE])
            pb_ref[:, t * LANE : (t + 2) * LANE] = pair.astype(BF)
        p_ref[:edge, :] = jnp.zeros((edge, LANE), F32)
        p_ref[rows + edge :, :] = jnp.zeros((edge, LANE), F32)
        p_ref[edge : rows + edge, :] = pair[:, (t % 2) * LANE : (t % 2 + 1) * LANE]
        s0_ref[ext:, :] = jnp.zeros((padded - ext, 2 * LANE), BF)
        for i in range(5):
            first = i * chunk
            where = pl.ds(first, chunk)
            fs, rs = [], []
            for j in range(TAPS):
                window = p_ref[pl.ds(first + REACH + (j - HALF) * dil, chunk), :]
                ahead, back = ROW_TAPS1 + j, ROW_TAPS1 + TAPS - 1 - j
                fs.append(taps_f[back : back + 1, dst] * window)
                rs.append(taps_r[ahead : ahead + 1, dst] * window)
            if t < n_own:
                fs.append(g2_ref[t, where, :])
            f, r = functools.reduce(jnp.add, fs), functools.reduce(jnp.add, rs)
            s0_ref[where, :LANE] = (f * gp_refs[0][t][where, :]).astype(BF)
            s0_ref[where, LANE:] = (r * gp_refs[1][t][where, :]).astype(BF)
        both = dot(hot_ref[...], s0_ref[...])
        plains[t], others[t] = both[:, :LANE], both[:, LANE:]

        sums = [None] * (2 * TAPS)
        for i in range(6):
            first = i * mchunk
            here = p_ref[pl.ds(edge + first, mchunk), :]
            for strand in range(2):
                for j in range(TAPS):
                    shift = (j - HALF) * dil * (1 - 2 * strand)
                    prod = here * x1_refs[strand][t][pl.ds(first + REACH + shift, mchunk), :]
                    part = prod.reshape(mchunk // 8, 8, LANE).sum(0)
                    slot = strand * TAPS + j
                    sums[slot] = part if i == 0 else sums[slot] + part
        for strand in range(2):
            lines = [jnp.sum(sums[strand * TAPS + j], axis=0, keepdims=True) for j in range(TAPS)]
            gt_ref[strand, :, dst] = jnp.concatenate(lines + [jnp.zeros((8 - TAPS, LANE), F32)], axis=0)

    by_tap = dot(hot1_ref[...], pb_ref[...])
    own_letters = dot(hot1_ref[:16, :], cot_ref[...]) * scale
    srow, scol = iotas((8, JB))
    sum_letter = as_bf((scol % BASES == srow) & (scol < TAPS * BASES))
    sum_tap = as_bf((scol // BASES == srow) & (scol < TAPS * BASES))

    def sums_of(sel, x):
        high, rest = split_bf(x)
        return dot(sel, high) + dot(sel, rest)

    sel1 = select_rows("tap1", JB)
    ahead = by_tap[:JB] * dot(sel1, table)
    other = by_tap[JB:] * dot(sel1, table_r)
    turned, other, taps_turned = reverse_wide(
        [jnp.concatenate(others, axis=1), other, gt_ref[1]], rev
    )
    sums = jnp.concatenate(plains, axis=1) + jnp.concatenate([turned[JB:], turned[:JB]], axis=0)
    dw_ref[...] = sums
    letters = sums_of(sum_letter, ahead + other)
    tail_ref[8:16, :] = gt_ref[0] + taps_turned

    total = jnp.zeros((2 * JB, chans), F32)
    for k in range(n_chan):
        total = total + dot(dw_ref[:, blocks[k]].astype(BF), pks[k][:width, :])
    st_ref[...] = total
    for k, block in enumerate(xor_blocks([st_ref[:, lanes] for lanes in blocks], me)):
        back_ref[:, blocks[k]] = block
    (turned,) = reverse_wide([back_ref[JB:, :]], rev)
    both = back_ref[:JB, :] + turned
    tail_ref[0:8, :] = sums_of(sum_tap, both * dot(select_rows("letter", JB), table))
    letters = letters + sums_of(sum_letter, both * dot(select_rows("tap0", JB), table))
    tail_ref[16:24, :] = letters
    zeros = jnp.zeros((BASES, width), F32)
    own = jnp.concatenate([own_letters[HALF * BASES : (HALF + 1) * BASES, :], zeros], axis=0)
    for kk, lanes in enumerate(blocks):
        place, at = (keep_ref, send_ref)[kk % 2], kk // 2
        letters = tail_ref[16:24, lanes]
        if kk == 0:
            letters = letters + own
        place[at, :ROW_R, :] = jnp.concatenate([dw_ref[:ROW_GE, lanes], letters[:BASES]], axis=0)
        place[at, ROW_R : 2 * ROW_R, :] = dw_ref[JB : JB + ROW_R, lanes]
        place[at, ROW_GT0:, :] = tail_ref[0:16, lanes]


def mix1_kernel(n_chan, width, near_ref, far_ref, out_ref, held, sem):
    me, odd = lax.axis_index("chan"), lax.axis_index("seq") % 2
    half = width // 2
    for source, first in ((near_ref, odd * half), (far_ref, (1 - odd) * half)):
        blocks = [source[:, k * width : (k + 1) * width].astype(F32) for k in range(n_chan)]
        for k, part in enumerate(xor_blocks(blocks, me)):
            held[pl.ds(pl.multiple_of(first, half), half), k * width : (k + 1) * width] = part
    copy = pltpu.make_async_copy(held, out_ref.at[1], sem)
    copy.start()
    copy.wait()


def finish_kernel(n_chan, width, st_ref, sa_ref, sb_ref, _, gm_ref, gt_ref, ge_ref, held, sems):
    sums = sa_ref[...] + sb_ref[...]
    fill = jnp.zeros((JB - ROW_GE, width), F32)
    dw = jnp.concatenate([sums[:ROW_GE], fill, sums[ROW_R : ROW_R + ROW_GE], fill], axis=0).astype(BF)
    copies = []
    step = 2 * LANE
    for i in range(n_chan * width // step):
        lanes = pl.ds(i * step, step)
        held[:, lanes] = t_dot(dw, st_ref[: 2 * JB, lanes])
        copies.append(pltpu.make_async_copy(held.at[:, lanes], gm_ref.at[0, :, lanes], sems.at[i]))
        copies[-1].start()
    for j in range(TAPS):
        gt_ref[j, 0:1, :] = sums[ROW_GT0 + j : ROW_GT0 + j + 1]
        gt_ref[j, 1:2, :] = sums[ROW_GT1 + j : ROW_GT1 + j + 1]
    ge_ref[...] = sums[ROW_GE : ROW_GE + BASES]
    for copy in copies:
        copy.wait()


VMEM = pl.BlockSpec(memory_space=pltpu.VMEM)
SMEM = pl.BlockSpec(memory_space=pltpu.SMEM)
HBM = pl.BlockSpec(memory_space=pltpu.HBM)


def in_hbm(x):
    return pltpu.with_memory_space_constraint(x, pltpu.HBM)


def call(kernel, in_specs, out_shape, out_specs, scratch, limit, cost, aliases=None):
    flops, moved = cost
    return pl.pallas_call(
        kernel,
        out_shape=out_shape,
        in_specs=in_specs,
        out_specs=out_specs,
        scratch_shapes=scratch,
        input_output_aliases=aliases or {},
        compiler_params=pltpu.CompilerParams(vmem_limit_bytes=limit << 20),
        cost_estimate=pl.CostEstimate(flops=flops, bytes_accessed=moved, transcendentals=0),
    )


def flip_bits(x, axis, mask):
    return lax.ppermute(x, axis, [(i, i ^ mask) for i in range(lax.axis_size(axis))])


def body(tokens, cotangent, embed, taps, mix, dilations):
    rows, width = cotangent.shape
    n_seq, n_chan = lax.axis_size("seq"), lax.axis_size("chan")
    chans = n_chan * width
    tiles = chans // LANE
    ext = rows + 2 * REACH
    padded = pl.cdiv(ext, LANE) * LANE
    edge = 2 * REACH
    own_tiles = pl.cdiv(width, LANE)
    scale = 1.0 / math.sqrt(rows * n_seq)
    shape = jax.ShapeDtypeStruct
    mix_t = jnp.swapaxes(mix, 1, 2)

    pk, letters = call(
        functools.partial(pack_kernel, width),
        [HBM] * 4,
        [shape((width + TABLE, chans), BF), shape((1, rows), jnp.int32)],
        [VMEM] * 2,
        [
            pltpu.VMEM((BASES, width), BF),
            pltpu.VMEM((TAPS, BLOCKS, width), BF),
            pltpu.SemaphoreType.DMA((4,)),
        ],
        8,
        (0, width * chans * 4),
    )(in_hbm(mix_t), in_hbm(embed), in_hbm(jnp.swapaxes(taps, 0, 1)), in_hbm(tokens))

    seq_bits = n_seq.bit_length() - 1
    for bit in range(seq_bits):
        letters = jnp.concatenate([letters, flip_bits(letters, "seq", 1 << bit)], axis=0)

    mixl, cot = call(
        functools.partial(local_kernel, n_chan, width),
        [HBM, HBM],
        [shape((width, chans), BF), shape((rows, width), BF)],
        [VMEM] * 2,
        [
            pltpu.VMEM((width, chans), BF),
            pltpu.VMEM((width, rows), BF),
            pltpu.SemaphoreType.DMA((2,)),
        ],
        16,
        (1 << 20, 1 << 20),
    )(in_hbm(mix_t), in_hbm(cotangent.T))

    pks = [pk]
    for bit in reversed(range(n_chan.bit_length() - 1)):
        ready = [pks[0]] + [lax.optimization_barrier((p, letters, mixl, cot))[0] for p in pks[1:]]
        moved = [flip_bits(p, "chan", 1 << bit) for p in ready]
        pks = [q for pair in zip(pks, moved) for q in pair]

    hot_t, hot, hot1 = call(
        functools.partial(prep_kernel, n_seq, rows),
        [SMEM, VMEM],
        [shape((padded, 4 * JB), BF), shape((2 * JB, padded), BF), shape((2 * JB, rows), BF)],
        [VMEM] * 3,
        [],
        16,
        (1 << 20, 1 << 20),
    )(dilations, letters)

    rows_ext = shape((ext, LANE), F32)
    x2, near, far, s1, stack, table, table_r, *strands = call(
        functools.partial(forward_kernel, n_chan, rows, width, scale),
        [SMEM] + [VMEM] * (n_chan + 3),
        [
            shape((width, rows), BF),
            shape((width // 2, chans), BF),
            shape((width // 2, chans), BF),
            shape((rows, width), BF),
            shape((4 * JB, chans), BF),
            shape((TABLE, chans), BF),
            shape((TABLE, chans), BF),
        ]
        + [rows_ext] * (4 * tiles),
        [HBM] + [VMEM] * (6 + 4 * tiles),
        [
            pltpu.VMEM((4 * JB, chans), BF),
            pltpu.VMEM((4 * JB, chans), BF),
            pltpu.VMEM((rows, chans), BF),
            pltpu.VMEM((width, rows), BF),
            pltpu.SemaphoreType.DMA,
        ],
        32,
        (3 << 30, 8 << 20),
    )(dilations, *pks, hot_t, mixl, cot)

    keep, send = call(
        functools.partial(backward_kernel, n_chan, rows, width, scale),
        [SMEM] + [VMEM] * (n_chan + 7 + 4 * tiles),
        [shape((n_chan // 2, SUMS, width), F32)] * 2,
        [VMEM] * 2,
        [pltpu.VMEM((rows + 2 * edge, LANE), F32)] * tiles
        + [pltpu.VMEM((padded, 2 * LANE), BF)] * tiles
        + [
            pltpu.VMEM((own_tiles, ext, LANE), F32),
            pltpu.VMEM((2, 8, chans), F32),
            pltpu.VMEM((rows, chans), BF),
            pltpu.VMEM((2 * JB, chans), F32),
            pltpu.VMEM((2 * JB, chans), F32),
            pltpu.VMEM((2 * JB, chans), F32),
            pltpu.VMEM((24, chans), F32),
        ],
        40,
        (3 << 30, 8 << 20),
    )(dilations, *pks, hot, hot1, mixl, cot, s1, table, table_r, *strands)

    def rounded_sum(a, b):
        return lax.optimization_barrier((a.astype(F32) + b.astype(F32)).astype(BF))

    def after(value, *others):
        return lax.optimization_barrier((value, *others))[0]

    arrived = flip_bits(far, "seq", 1)
    s_mine = keep + flip_bits(send, "chan", 1)
    arrived = after(arrived, s_mine)
    g_mine = rounded_sum(near, arrived)
    for bit in range(1, n_chan.bit_length() - 1):
        s_mine = s_mine[0::2] + flip_bits(s_mine[1::2], "chan", 1 << bit)
    s_mine = s_mine[0]
    far_sums = [s_mine]
    for bit in reversed(range(seq_bits)):
        s_other = flip_bits(s_mine, "seq", 1 << bit)
        if bit:
            s_mine = s_mine + s_other
            far_sums.append(s_mine)
    for bit in range(1, seq_bits):
        g_mine = rounded_sum(g_mine, after(flip_bits(g_mine, "seq", 1 << bit), far_sums[bit]))
    g_other = flip_bits(g_mine, "seq", 1)

    big = pltpu.VMEM((width, chans), F32)
    (grad_mix,) = call(
        functools.partial(mix1_kernel, n_chan, width),
        [VMEM, VMEM],
        [shape((BLOCKS, width, chans), F32)],
        [HBM],
        [big, pltpu.SemaphoreType.DMA],
        16,
        (1 << 20, 1 << 21),
    )(g_mine, g_other)
    grad_mix, grad_taps, grad_embed = call(
        functools.partial(finish_kernel, n_chan, width),
        [VMEM, VMEM, VMEM, HBM],
        [
            shape((BLOCKS, width, chans), F32),
            shape((TAPS, BLOCKS, width), F32),
            shape((BASES, width), F32),
        ],
        [HBM, VMEM, VMEM],
        [big, pltpu.SemaphoreType.DMA((chans // (2 * LANE),))],
        16,
        (1 << 24, 1 << 21),
        {3: 0},
    )(stack, s_mine, s_other, grad_mix)
    return x2.T, jnp.swapaxes(grad_mix, 1, 2), jnp.swapaxes(grad_taps, 0, 1), grad_embed


def solution(mesh):
    in_specs = (
        P(("groups", "seq")),
        P(("groups", "seq"), "chan"),
        P(None, "chan"),
        P(None, None, "chan"),
        P(None, None, "chan"),
        P(),
    )
    out_specs = (
        P(("groups", "seq"), "chan"),
        P("groups", None, "chan"),
        P("groups", None, "chan"),
        P("groups", "chan"),
    )
    return jax.shard_map(body, mesh=mesh, in_specs=in_specs, out_specs=out_specs, check_vma=False)
```

```python
import functools
import math

import jax
import jax.numpy as jnp
from jax import lax
from jax.experimental import pallas as pl
from jax.experimental.pallas import tpu as pltpu
from jax.sharding import PartitionSpec as P

TAPS = 5
BASES = 4
BLOCKS = 2
DMAX = 8
HALF = TAPS // 2
REACH = HALF * DMAX
LANE = 128
JB = 32
GELU_SCALE = math.sqrt(2.0 / math.pi)
CUBIC = 0.044715
BF = jnp.bfloat16
F32 = jnp.float32
ROW_EMBED, ROW_TAPS0, ROW_TAPS1, TABLE = 0, BASES, BASES + TAPS, 16
ROW_GE, ROW_R, ROW_GT0, ROW_GT1, SUMS = 20, 24, 48, 56, 64


def dot(a, b, **kw):
    return jnp.dot(a, b, preferred_element_type=F32, **kw)


def dot_t(a, b):
    return lax.dot_general(a, b, (((1,), (1,)), ((), ())), preferred_element_type=F32)


def t_dot(a, b):
    return lax.dot_general(a, b, (((0,), (0,)), ((), ())), preferred_element_type=F32)


def iotas(shape):
    return lax.broadcasted_iota(jnp.int32, shape, 0), lax.broadcasted_iota(jnp.int32, shape, 1)


def as_bf(mask):
    return mask.astype(F32).astype(BF)


def reversal(size):
    row, col = iotas((size, size))
    return as_bf(row + col == size - 1)


def split_bf(x):
    high = x.astype(BF)
    return high, (x - high.astype(F32)).astype(BF)


def reverse_lanes(parts, rev):
    n = parts[0].shape[1] // LANE
    rows = [p.shape[0] for p in parts]
    pile = [p[:, t * LANE : (t + 1) * LANE] for p in parts for t in range(n)]
    turned = dot(jnp.concatenate(pile, axis=0), rev)
    out, first = [], 0
    for count in rows:
        tiles = [turned[first + t * count : first + (t + 1) * count] for t in range(n)]
        out.append(jnp.concatenate(tiles[::-1], axis=1))
        first += n * count
    return out


def reverse_wide(parts, rev):
    split = [split_bf(p) for p in parts]
    turned = reverse_lanes([q for pair in split for q in pair], rev)
    return [turned[2 * i] + turned[2 * i + 1] for i in range(len(parts))]


def xor_blocks(blocks, me):
    for bit in range(len(blocks).bit_length() - 1):
        swap = lax.bitwise_and(lax.shift_right_logical(me, bit), 1) == 1
        blocks = [jnp.where(swap, blocks[k ^ (1 << bit)], blocks[k]) for k in range(len(blocks))]
    return blocks


def gelu_parts(v):
    square = v * v
    tangent = jnp.tanh(v * (GELU_SCALE + (GELU_SCALE * CUBIC) * square))
    half = 0.5 + 0.5 * tangent
    value = v * half
    slope = half + (v * (1.0 - tangent * tangent)) * (
        0.5 * GELU_SCALE + (1.5 * GELU_SCALE * CUBIC) * square
    )
    return value, slope


def gelu_doubled(half):
    square = half * half
    cubic = (8.0 * GELU_SCALE * CUBIC) * square
    above = 1.0 + jnp.tanh(half * (2.0 * GELU_SCALE + cubic))
    value = half * above
    slope = above + value * ((2.0 - above) * (2.0 * GELU_SCALE + 3.0 * cubic))
    return value, slope


def select_rows(kind, rows):
    row, col = iotas((rows, TABLE))
    local = row % JB
    used = local < TAPS * BASES
    tap, letter = local // BASES, local % BASES
    want = {"tap0": ROW_TAPS0 + tap, "tap1": ROW_TAPS1 + tap, "letter": ROW_EMBED + letter}[kind]
    return as_bf(used & (col == want))


def one_hot_t(tokens):
    n = tokens[0].shape[1]
    inside = tokens[HALF] != 0
    row = lax.broadcasted_iota(jnp.int32, (2 * JB, n), 0)
    local = row % JB
    group = jnp.where(local < TAPS * BASES, local // BASES + TAPS * (row // JB), -1)
    seen = jnp.zeros((2 * JB, n), jnp.int32)
    for g, line in enumerate(tokens):
        line = jnp.where(inside, line, 0)
        seen = jnp.where(group == g, jnp.broadcast_to(line, (2 * JB, n)), seen)
    return (seen == local % BASES + 1).astype(F32)


def pack_kernel(width, mix_ref, embed_ref, taps_ref, tok_ref, out_ref, letters_ref, e_ref, t_ref, sems):
    big = pltpu.make_async_copy(mix_ref.at[0], out_ref.at[pl.ds(0, width)], sems.at[0])
    small = [
        pltpu.make_async_copy(embed_ref, e_ref, sems.at[1]),
        pltpu.make_async_copy(taps_ref, t_ref, sems.at[2]),
        pltpu.make_async_copy(tok_ref, letters_ref.at[0], sems.at[3]),
    ]
    for copy in small + [big]:
        copy.start()
    out_ref[width:, :] = jnp.zeros((TABLE, out_ref.shape[1]), BF)
    for copy in small:
        copy.wait()
    taps = t_ref[...].astype(F32)
    lines = [e_ref[...].astype(F32)]
    lines += [taps[j, block : block + 1, :] for block in range(BLOCKS) for j in range(TAPS)]
    lines.append(jnp.zeros((TABLE - BASES - 2 * TAPS, width), F32))
    out_ref[width:, :width] = jnp.concatenate(lines, axis=0).astype(BF)
    big.wait()


def local_kernel(n_chan, width, mix_ref, cot_ref, mixl_ref, cotl_ref, m_ref, c_ref, sems):
    first = pltpu.make_async_copy(mix_ref.at[1], m_ref, sems.at[0])
    second = pltpu.make_async_copy(cot_ref, c_ref, sems.at[1])
    first.start()
    second.start()
    first.wait()
    blocks = [m_ref[:, k * width : (k + 1) * width] for k in range(n_chan)]
    for k, block in enumerate(xor_blocks(blocks, lax.axis_index("chan"))):
        mixl_ref[:, k * width : (k + 1) * width] = block
    second.wait()
    cotl_ref[...] = c_ref[...].astype(F32).T.astype(BF)


def prep_kernel(n_seq, rows, dils, tok_ref, a_ref, hot_ref, hot1_ref):
    place = lax.axis_index("seq")

    def line(block):
        inside = jnp.logical_and(block >= 0, block < n_seq)
        safe = jnp.clip(block, 0, n_seq - 1)
        letters = tok_ref[pl.ds(lax.bitwise_xor(safe, place), 1), :] + 1
        return jnp.where(inside, letters, 0)

    def around(block):
        lines = [line(block - 1)[:, rows - LANE :], line(block), line(block + 1)[:, :LANE]]
        return jnp.concatenate(lines, axis=1)

    total = rows + 2 * LANE
    this = jnp.broadcast_to(around(place), (8, total))
    mirror = jnp.broadcast_to(around(n_seq - 1 - place), (8, total)).astype(F32).astype(BF)
    rev, n_tiles = reversal(LANE), total // LANE
    other = jnp.concatenate(
        [dot(mirror[:, t * LANE : (t + 1) * LANE], rev) for t in reversed(range(n_tiles))], axis=1
    ).astype(jnp.int32)

    def windows(dilation, margin, count):
        out = []
        for strand, source in ((1, this), (-1, other)):
            for j in range(TAPS):
                first = LANE - margin + strand * (j - HALF) * dilation
                out.append(pltpu.roll(source, total - first, 1)[:1, :count])
        return out

    hot = one_hot_t(windows(dils[0], REACH, a_ref.shape[0]))
    a_ref[...] = jnp.concatenate([hot, hot], axis=0).T.astype(BF)
    hot_ref[...] = hot.astype(BF)
    hot1_ref[...] = one_hot_t(windows(dils[1], 0, rows)).astype(BF)


def forward_kernel(n_chan, rows, width, scale, dils, *refs):
    tiles = n_chan * width // LANE
    pks, refs = refs[:n_chan], refs[n_chan:]
    (a_ref, mixl_ref, cot_ref), refs = refs[:3], refs[3:]
    (x2_ref, near_ref, far_ref, s_ref, st_ref, e_ref, et_ref), refs = refs[:7], refs[7:]
    x1_refs, refs = (refs[:tiles], refs[tiles : 2 * tiles]), refs[2 * tiles :]
    gp_refs, refs = (refs[:tiles], refs[tiles : 2 * tiles]), refs[2 * tiles :]
    w_ref, b_ref, m_ref, held, sem = refs
    chans = n_chan * width
    ext = rows + 2 * REACH
    me, dil = lax.axis_index("chan"), dils[1]
    rev = reversal(LANE)
    blocks = [slice(k * width, (k + 1) * width) for k in range(n_chan)]

    for k in range(n_chan):
        e_ref[:, blocks[k]] = pks[k][width:, :width]
    table = e_ref[...]
    plain = dot(select_rows("tap0", JB), table) * dot(select_rows("letter", JB), table)
    high, low = split_bf(plain)
    turned, turned_low, table_r = reverse_lanes([high, low, table], rev)
    et_ref[...] = table_r.astype(BF)
    b_ref[...] = jnp.concatenate([high, turned.astype(BF), low, turned_low.astype(BF)], axis=0)
    for k, block in enumerate(xor_blocks([b_ref[:, lanes] for lanes in blocks], me)):
        st_ref[:, blocks[k]] = block
    for k in range(n_chan):
        total = 0.5 * dot_t(st_ref[...], pks[k][:width, :])
        high, low = split_bf(total[: 2 * JB] + total[2 * JB :])
        w_ref[:, blocks[k]] = jnp.concatenate([high, low], axis=0)
    weights = w_ref[...]
    (swapped,) = reverse_lanes([weights], rev)
    order = [swapped[JB : 2 * JB], swapped[:JB], swapped[3 * JB :], swapped[2 * JB : 3 * JB]]
    weights_r = jnp.concatenate(order, axis=0).astype(BF)

    table, table_r = table.astype(F32), et_ref[...].astype(F32)
    centre = HALF * BASES
    keep = lax.broadcasted_iota(jnp.int32, (8, chans), 0) < BASES

    def lookup(source, first):
        lines = jnp.where(keep, source[:8], 0.0)
        above, below = jnp.zeros((first, chans), F32), jnp.zeros((4 * JB - first - 8, chans), F32)
        return jnp.concatenate([above, lines, below], axis=0).astype(BF)

    look, look_r = lookup(table, centre), lookup(table_r, JB + centre)
    chunk, mchunk = ext // 5, rows // 6
    for t in range(tiles):
        dst = slice(t * LANE, (t + 1) * LANE)
        for strand, (wr, er) in enumerate(((weights, look), (weights_r, look_r))):
            rhs = jnp.concatenate([wr[:, dst], er[:, dst]], axis=1)
            for i in range(5):
                where = pl.ds(i * chunk, chunk)
                both = dot(a_ref[where, :], rhs)
                value, slope = gelu_doubled(both[:, :LANE])
                x1_refs[strand][t][where, :] = both[:, LANE:] + value
                gp_refs[strand][t][where, :] = slope

        for i in range(6):
            first = i * mchunk
            terms = []
            for j in range(TAPS):
                shift = (j - HALF) * dil
                line = slice(ROW_TAPS1 + j, ROW_TAPS1 + j + 1)
                terms.append(table[line, dst] * x1_refs[0][t][pl.ds(first + REACH + shift, mchunk), :])
                terms.append(table_r[line, dst] * x1_refs[1][t][pl.ds(first + REACH - shift, mchunk), :])
            m_ref[first : first + mchunk, dst] = functools.reduce(jnp.add, terms).astype(BF)

    half = rows // 2
    n_own = pl.cdiv(width, LANE)
    for i in range(2):
        where = pl.ds(i * half, half)
        value, slope = gelu_parts(dot_t(m_ref[where, :], mixl_ref[...]))
        inner = pl.ds(REACH + i * half, half)
        own = jnp.concatenate([x1_refs[0][t][inner, :] for t in range(n_own)], axis=1)[:, :width]
        held[:, where] = (own + value).T.astype(BF)
        s_ref[where, :] = ((cot_ref[where, :].astype(F32) * scale) * slope).astype(BF)
    copy = pltpu.make_async_copy(held, x2_ref, sem)
    copy.start()

    part = t_dot(s_ref[...], m_ref[...]).astype(BF)
    odd = lax.axis_index("seq") % 2 == 1
    near_ref[...] = jnp.where(odd, part[width // 2 :], part[: width // 2])
    far_ref[...] = jnp.where(odd, part[: width // 2], part[width // 2 :])
    copy.wait()


def backward_kernel(n_chan, rows, width, scale, dils, *refs):
    tiles = n_chan * width // LANE
    (hot_ref, mixl_ref, cot_ref, s_ref, e_ref, et_ref), refs = refs[:6], refs[6:]
    x1_refs, refs = (refs[:tiles], refs[tiles : 2 * tiles]), refs[2 * tiles :]
    gp_refs, refs = (refs[:tiles], refs[tiles : 2 * tiles]), refs[2 * tiles :]
    (pb_ref, gt_ref, plain_ref, other_ref), refs = refs[:4], refs[4:]
    p_refs, s0_refs, (g2_ref,) = refs[:tiles], refs[tiles : 2 * tiles], refs[2 * tiles :]
    ext = rows + 2 * REACH
    padded = hot_ref.shape[1]
    dil = dils[1]
    taps_f, taps_r = 0.5 * e_ref[...].astype(F32), 0.5 * et_ref[...].astype(F32)

    edge = 2 * REACH
    n_own = pl.cdiv(width, LANE)
    g2 = cot_ref[...].astype(F32) * scale
    g2_ref[:, :REACH, :] = jnp.zeros((n_own, REACH, LANE), F32)
    g2_ref[:, rows + REACH :, :] = jnp.zeros((n_own, REACH, LANE), F32)
    g2 = jnp.concatenate([g2, jnp.zeros((rows, n_own * LANE - width), F32)], axis=1)
    for t in range(n_own):
        g2_ref[t, REACH : rows + REACH, :] = 0.5 * g2[:, t * LANE : (t + 1) * LANE]

    mchunk, chunk = rows // 6, ext // 5
    for t in range(tiles):
        dst = slice(t * LANE, (t + 1) * LANE)
        p_ref, s0_ref = p_refs[t], s0_refs[t]
        if t % 2 == 0:
            pair = dot(s_ref[...], mixl_ref[:, t * LANE : (t + 2) * LANE])
            pb_ref[:, t * LANE : (t + 2) * LANE] = pair.astype(BF)
        p_ref[:edge, :] = jnp.zeros((edge, LANE), F32)
        p_ref[rows + edge :, :] = jnp.zeros((edge, LANE), F32)
        p_ref[edge : rows + edge, :] = pair[:, (t % 2) * LANE : (t % 2 + 1) * LANE]
        s0_ref[ext:, :] = jnp.zeros((padded - ext, 2 * LANE), BF)
        for i in range(5):
            first = i * chunk
            where = pl.ds(first, chunk)
            fs, rs = [], []
            for j in range(TAPS):
                window = p_ref[pl.ds(first + REACH + (j - HALF) * dil, chunk), :]
                ahead, back = ROW_TAPS1 + j, ROW_TAPS1 + TAPS - 1 - j
                fs.append(taps_f[back : back + 1, dst] * window)
                rs.append(taps_r[ahead : ahead + 1, dst] * window)
            if t < n_own:
                fs.append(g2_ref[t, where, :])
            f, r = functools.reduce(jnp.add, fs), functools.reduce(jnp.add, rs)
            s0_ref[where, :LANE] = (f * gp_refs[0][t][where, :]).astype(BF)
            s0_ref[where, LANE:] = (r * gp_refs[1][t][where, :]).astype(BF)
        both = dot(hot_ref[...], s0_ref[...])
        plain_ref[:, dst], other_ref[:, dst] = both[:, :LANE], both[:, LANE:]

        sums = [None] * (2 * TAPS)
        for i in range(6):
            first = i * mchunk
            here = p_ref[pl.ds(edge + first, mchunk), :]
            for strand in range(2):
                for j in range(TAPS):
                    shift = (j - HALF) * dil * (1 - 2 * strand)
                    prod = here * x1_refs[strand][t][pl.ds(first + REACH + shift, mchunk), :]
                    part = prod.reshape(mchunk // 8, 8, LANE).sum(0)
                    slot = strand * TAPS + j
                    sums[slot] = part if i == 0 else sums[slot] + part
        for strand in range(2):
            lines = [jnp.sum(sums[strand * TAPS + j], axis=0, keepdims=True) for j in range(TAPS)]
            gt_ref[strand, :, dst] = jnp.concatenate(lines + [jnp.zeros((8 - TAPS, LANE), F32)], axis=0)


def collect_kernel(n_chan, width, scale, *refs):
    pks, refs = refs[:n_chan], refs[n_chan:]
    hot1_ref, cot_ref, e_ref, et_ref, pb_ref, gt_ref, plain_ref, other_ref = refs[:8]
    keep_ref, send_ref, dw_ref, st_ref, back_ref, tail_ref = refs[8:]
    chans = n_chan * width
    me, rev = lax.axis_index("chan"), reversal(LANE)
    blocks = [slice(k * width, (k + 1) * width) for k in range(n_chan)]
    table, table_r = e_ref[...], et_ref[...]

    by_tap = dot(hot1_ref[...], pb_ref[...])
    own_letters = dot(hot1_ref[:16, :], cot_ref[...]) * scale
    srow, scol = iotas((8, JB))
    sum_letter = as_bf((scol % BASES == srow) & (scol < TAPS * BASES))
    sum_tap = as_bf((scol // BASES == srow) & (scol < TAPS * BASES))

    def sums_of(sel, x):
        high, rest = split_bf(x)
        return dot(sel, high) + dot(sel, rest)

    sel1 = select_rows("tap1", JB)
    ahead = by_tap[:JB] * dot(sel1, table)
    other = by_tap[JB:] * dot(sel1, table_r)
    turned, other, taps_turned = reverse_wide([other_ref[...], other, gt_ref[1]], rev)
    sums = plain_ref[...] + jnp.concatenate([turned[JB:], turned[:JB]], axis=0)
    dw_ref[...] = sums
    letters = sums_of(sum_letter, ahead + other)
    tail_ref[8:16, :] = gt_ref[0] + taps_turned

    total = jnp.zeros((2 * JB, chans), F32)
    for k in range(n_chan):
        total = total + dot(dw_ref[:, blocks[k]].astype(BF), pks[k][:width, :])
    st_ref[...] = total
    for k, block in enumerate(xor_blocks([st_ref[:, lanes] for lanes in blocks], me)):
        back_ref[:, blocks[k]] = block
    (turned,) = reverse_wide([back_ref[JB:, :]], rev)
    both = back_ref[:JB, :] + turned
    tail_ref[0:8, :] = sums_of(sum_tap, both * dot(select_rows("letter", JB), table))
    letters = letters + sums_of(sum_letter, both * dot(select_rows("tap0", JB), table))
    tail_ref[16:24, :] = letters
    zeros = jnp.zeros((BASES, width), F32)
    own = jnp.concatenate([own_letters[HALF * BASES : (HALF + 1) * BASES, :], zeros], axis=0)
    for kk, lanes in enumerate(blocks):
        place, at = (keep_ref, send_ref)[kk % 2], kk // 2
        letters = tail_ref[16:24, lanes]
        if kk == 0:
            letters = letters + own
        place[at, :ROW_R, :] = jnp.concatenate([dw_ref[:ROW_GE, lanes], letters[:BASES]], axis=0)
        place[at, ROW_R : 2 * ROW_R, :] = dw_ref[JB : JB + ROW_R, lanes]
        place[at, ROW_GT0:, :] = tail_ref[0:16, lanes]


def mix1_kernel(n_chan, width, near_ref, far_ref, out_ref, held, sem):
    me, odd = lax.axis_index("chan"), lax.axis_index("seq") % 2
    half = width // 2
    for source, first in ((near_ref, odd * half), (far_ref, (1 - odd) * half)):
        blocks = [source[:, k * width : (k + 1) * width].astype(F32) for k in range(n_chan)]
        for k, part in enumerate(xor_blocks(blocks, me)):
            held[pl.ds(pl.multiple_of(first, half), half), k * width : (k + 1) * width] = part
    copy = pltpu.make_async_copy(held, out_ref.at[1], sem)
    copy.start()
    copy.wait()


def finish_kernel(n_chan, width, st_ref, sa_ref, sb_ref, _, gm_ref, gt_ref, ge_ref, held, sems):
    sums = sa_ref[...] + sb_ref[...]
    fill = jnp.zeros((JB - ROW_GE, width), F32)
    dw = jnp.concatenate([sums[:ROW_GE], fill, sums[ROW_R : ROW_R + ROW_GE], fill], axis=0).astype(BF)
    copies = []
    step = 2 * LANE
    for i in range(n_chan * width // step):
        lanes = pl.ds(i * step, step)
        held[:, lanes] = t_dot(dw, st_ref[: 2 * JB, lanes])
        copies.append(pltpu.make_async_copy(held.at[:, lanes], gm_ref.at[0, :, lanes], sems.at[i]))
        copies[-1].start()
    for j in range(TAPS):
        gt_ref[j, 0:1, :] = sums[ROW_GT0 + j : ROW_GT0 + j + 1]
        gt_ref[j, 1:2, :] = sums[ROW_GT1 + j : ROW_GT1 + j + 1]
    ge_ref[...] = sums[ROW_GE : ROW_GE + BASES]
    for copy in copies:
        copy.wait()


VMEM = pl.BlockSpec(memory_space=pltpu.VMEM)
SMEM = pl.BlockSpec(memory_space=pltpu.SMEM)
HBM = pl.BlockSpec(memory_space=pltpu.HBM)


def in_hbm(x):
    return pltpu.with_memory_space_constraint(x, pltpu.HBM)


def call(kernel, in_specs, out_shape, out_specs, scratch, limit, cost, aliases=None):
    flops, moved = cost
    return pl.pallas_call(
        kernel,
        out_shape=out_shape,
        in_specs=in_specs,
        out_specs=out_specs,
        scratch_shapes=scratch,
        input_output_aliases=aliases or {},
        compiler_params=pltpu.CompilerParams(vmem_limit_bytes=limit << 20),
        cost_estimate=pl.CostEstimate(flops=flops, bytes_accessed=moved, transcendentals=0),
    )


def flip_bits(x, axis, mask):
    return lax.ppermute(x, axis, [(i, i ^ mask) for i in range(lax.axis_size(axis))])


def body(tokens, cotangent, embed, taps, mix, dilations):
    rows, width = cotangent.shape
    n_seq, n_chan = lax.axis_size("seq"), lax.axis_size("chan")
    chans = n_chan * width
    tiles = chans // LANE
    ext = rows + 2 * REACH
    padded = pl.cdiv(ext, LANE) * LANE
    edge = 2 * REACH
    own_tiles = pl.cdiv(width, LANE)
    scale = 1.0 / math.sqrt(rows * n_seq)
    shape = jax.ShapeDtypeStruct
    mix_t = jnp.swapaxes(mix, 1, 2)

    pk, letters = call(
        functools.partial(pack_kernel, width),
        [HBM] * 4,
        [shape((width + TABLE, chans), BF), shape((1, rows), jnp.int32)],
        [VMEM] * 2,
        [
            pltpu.VMEM((BASES, width), BF),
            pltpu.VMEM((TAPS, BLOCKS, width), BF),
            pltpu.SemaphoreType.DMA((4,)),
        ],
        8,
        (0, width * chans * 4),
    )(in_hbm(mix_t), in_hbm(embed), in_hbm(jnp.swapaxes(taps, 0, 1)), in_hbm(tokens))

    seq_bits = n_seq.bit_length() - 1
    for bit in range(seq_bits):
        letters = jnp.concatenate([letters, flip_bits(letters, "seq", 1 << bit)], axis=0)

    mixl, cot = call(
        functools.partial(local_kernel, n_chan, width),
        [HBM, HBM],
        [shape((width, chans), BF), shape((rows, width), BF)],
        [VMEM] * 2,
        [
            pltpu.VMEM((width, chans), BF),
            pltpu.VMEM((width, rows), BF),
            pltpu.SemaphoreType.DMA((2,)),
        ],
        16,
        (1 << 20, 1 << 20),
    )(in_hbm(mix_t), in_hbm(cotangent.T))

    pks = [pk]
    for bit in reversed(range(n_chan.bit_length() - 1)):
        ready = [pks[0]] + [lax.optimization_barrier((p, letters, mixl, cot))[0] for p in pks[1:]]
        moved = [flip_bits(p, "chan", 1 << bit) for p in ready]
        pks = [q for pair in zip(pks, moved) for q in pair]

    hot_t, hot, hot1 = call(
        functools.partial(prep_kernel, n_seq, rows),
        [SMEM, VMEM],
        [shape((padded, 4 * JB), BF), shape((2 * JB, padded), BF), shape((2 * JB, rows), BF)],
        [VMEM] * 3,
        [],
        16,
        (1 << 20, 1 << 20),
    )(dilations, letters)

    rows_ext = shape((ext, LANE), F32)
    x2, near, far, s1, stack, table, table_r, *strands = call(
        functools.partial(forward_kernel, n_chan, rows, width, scale),
        [SMEM] + [VMEM] * (n_chan + 3),
        [
            shape((width, rows), BF),
            shape((width // 2, chans), BF),
            shape((width // 2, chans), BF),
            shape((rows, width), BF),
            shape((4 * JB, chans), BF),
            shape((TABLE, chans), BF),
            shape((TABLE, chans), BF),
        ]
        + [rows_ext] * (4 * tiles),
        [HBM] + [VMEM] * (6 + 4 * tiles),
        [
            pltpu.VMEM((4 * JB, chans), BF),
            pltpu.VMEM((4 * JB, chans), BF),
            pltpu.VMEM((rows, chans), BF),
            pltpu.VMEM((width, rows), BF),
            pltpu.SemaphoreType.DMA,
        ],
        32,
        (3 << 30, 8 << 20),
    )(dilations, *pks, hot_t, mixl, cot)

    arrived = flip_bits(far, "seq", 1)
    pb, gt, plain, other = call(
        functools.partial(backward_kernel, n_chan, rows, width, scale),
        [SMEM] + [VMEM] * (6 + 4 * tiles),
        [
            shape((rows, chans), BF),
            shape((2, 8, chans), F32),
            shape((2 * JB, chans), F32),
            shape((2 * JB, chans), F32),
        ],
        [VMEM] * 4,
        [pltpu.VMEM((rows + 2 * edge, LANE), F32)] * tiles
        + [pltpu.VMEM((padded, 2 * LANE), BF)] * tiles
        + [pltpu.VMEM((own_tiles, ext, LANE), F32)],
        40,
        (3 << 30, 8 << 20),
    )(dilations, hot, mixl, cot, s1, table, table_r, *strands)

    def rounded_sum(a, b):
        return lax.optimization_barrier((a.astype(F32) + b.astype(F32)).astype(BF))

    g_mine = rounded_sum(near, lax.optimization_barrier((arrived, plain))[0])
    gt = lax.optimization_barrier((gt, g_mine))[0]
    keep, send = call(
        functools.partial(collect_kernel, n_chan, width, scale),
        [VMEM] * (n_chan + 8),
        [shape((n_chan // 2, SUMS, width), F32)] * 2,
        [VMEM] * 2,
        [
            pltpu.VMEM((2 * JB, chans), F32),
            pltpu.VMEM((2 * JB, chans), F32),
            pltpu.VMEM((2 * JB, chans), F32),
            pltpu.VMEM((24, chans), F32),
        ],
        24,
        (1 << 30, 8 << 20),
    )(*pks, hot1, cot, table, table_r, pb, gt, plain, other)

    for bit in range(1, seq_bits):
        g_mine = rounded_sum(g_mine, flip_bits(g_mine, "seq", 1 << bit))
    g_other = flip_bits(g_mine, "seq", 1)
    s_mine = keep + flip_bits(send, "chan", 1)
    for bit in range(1, n_chan.bit_length() - 1):
        s_mine = s_mine[0::2] + flip_bits(s_mine[1::2], "chan", 1 << bit)
    s_mine = s_mine[0]
    for bit in reversed(range(seq_bits)):
        s_other = flip_bits(s_mine, "seq", 1 << bit)
        if bit:
            s_mine = s_mine + s_other

    big = pltpu.VMEM((width, chans), F32)
    (grad_mix,) = call(
        functools.partial(mix1_kernel, n_chan, width),
        [VMEM, VMEM],
        [shape((BLOCKS, width, chans), F32)],
        [HBM],
        [big, pltpu.SemaphoreType.DMA],
        16,
        (1 << 20, 1 << 21),
    )(g_mine, g_other)
    grad_mix, grad_taps, grad_embed = call(
        functools.partial(finish_kernel, n_chan, width),
        [VMEM, VMEM, VMEM, HBM],
        [
            shape((BLOCKS, width, chans), F32),
            shape((TAPS, BLOCKS, width), F32),
            shape((BASES, width), F32),
        ],
        [HBM, VMEM, VMEM],
        [big, pltpu.SemaphoreType.DMA((chans // (2 * LANE),))],
        16,
        (1 << 24, 1 << 21),
        {3: 0},
    )(stack, s_mine, s_other, grad_mix)
    return x2.T, jnp.swapaxes(grad_mix, 1, 2), jnp.swapaxes(grad_taps, 0, 1), grad_embed


def solution(mesh):
    in_specs = (
        P(("groups", "seq")),
        P(("groups", "seq"), "chan"),
        P(None, "chan"),
        P(None, None, "chan"),
        P(None, None, "chan"),
        P(),
    )
    out_specs = (
        P(("groups", "seq"), "chan"),
        P("groups", None, "chan"),
        P("groups", None, "chan"),
        P("groups", "chan"),
    )
    return jax.shard_map(body, mesh=mesh, in_specs=in_specs, out_specs=out_specs, check_vma=False)
```

```python
import functools
import math

import jax
import jax.numpy as jnp
from jax import lax
from jax.experimental import pallas as pl
from jax.experimental.pallas import tpu as pltpu
from jax.sharding import PartitionSpec as P

TAPS = 5
BASES = 4
BLOCKS = 2
DMAX = 8
HALF = TAPS // 2
REACH = HALF * DMAX
LANE = 128
JB = 32
GELU_SCALE = math.sqrt(2.0 / math.pi)
CUBIC = 0.044715
BF = jnp.bfloat16
F32 = jnp.float32
ROW_EMBED, ROW_TAPS0, ROW_TAPS1, TABLE = 0, BASES, BASES + TAPS, 16
ROW_GE, ROW_R, ROW_GT0, ROW_GT1, SUMS = 20, 24, 48, 56, 64


def dot(a, b, **kw):
    return jnp.dot(a, b, preferred_element_type=F32, **kw)


def dot_t(a, b):
    return lax.dot_general(a, b, (((1,), (1,)), ((), ())), preferred_element_type=F32)


def t_dot(a, b):
    return lax.dot_general(a, b, (((0,), (0,)), ((), ())), preferred_element_type=F32)


def iotas(shape):
    return lax.broadcasted_iota(jnp.int32, shape, 0), lax.broadcasted_iota(jnp.int32, shape, 1)


def as_bf(mask):
    return mask.astype(F32).astype(BF)


def reversal(size):
    row, col = iotas((size, size))
    return as_bf(row + col == size - 1)


def split_bf(x):
    high = x.astype(BF)
    return high, (x - high.astype(F32)).astype(BF)


def reverse_lanes(parts, rev):
    n = parts[0].shape[1] // LANE
    rows = [p.shape[0] for p in parts]
    pile = [p[:, t * LANE : (t + 1) * LANE] for p in parts for t in range(n)]
    turned = dot(jnp.concatenate(pile, axis=0), rev)
    out, first = [], 0
    for count in rows:
        tiles = [turned[first + t * count : first + (t + 1) * count] for t in range(n)]
        out.append(jnp.concatenate(tiles[::-1], axis=1))
        first += n * count
    return out


def reverse_wide(parts, rev):
    split = [split_bf(p) for p in parts]
    turned = reverse_lanes([q for pair in split for q in pair], rev)
    return [turned[2 * i] + turned[2 * i + 1] for i in range(len(parts))]


def xor_blocks(blocks, me):
    for bit in range(len(blocks).bit_length() - 1):
        swap = lax.bitwise_and(lax.shift_right_logical(me, bit), 1) == 1
        blocks = [jnp.where(swap, blocks[k ^ (1 << bit)], blocks[k]) for k in range(len(blocks))]
    return blocks


def gelu_parts(v):
    square = v * v
    tangent = jnp.tanh(v * (GELU_SCALE + (GELU_SCALE * CUBIC) * square))
    half = 0.5 + 0.5 * tangent
    value = v * half
    slope = half + (v * (1.0 - tangent * tangent)) * (
        0.5 * GELU_SCALE + (1.5 * GELU_SCALE * CUBIC) * square
    )
    return value, slope


def gelu_doubled(half):
    square = half * half
    cubic = (8.0 * GELU_SCALE * CUBIC) * square
    above = 1.0 + jnp.tanh(half * (2.0 * GELU_SCALE + cubic))
    value = half * above
    slope = above + value * ((2.0 - above) * (2.0 * GELU_SCALE + 3.0 * cubic))
    return value, slope


def select_rows(kind, rows):
    row, col = iotas((rows, TABLE))
    local = row % JB
    used = local < TAPS * BASES
    tap, letter = local // BASES, local % BASES
    want = {"tap0": ROW_TAPS0 + tap, "tap1": ROW_TAPS1 + tap, "letter": ROW_EMBED + letter}[kind]
    return as_bf(used & (col == want))


def one_hot_t(tokens):
    n = tokens[0].shape[1]
    inside = tokens[HALF] != 0
    row = lax.broadcasted_iota(jnp.int32, (2 * JB, n), 0)
    local = row % JB
    group = jnp.where(local < TAPS * BASES, local // BASES + TAPS * (row // JB), -1)
    seen = jnp.zeros((2 * JB, n), jnp.int32)
    for g, line in enumerate(tokens):
        line = jnp.where(inside, line, 0)
        seen = jnp.where(group == g, jnp.broadcast_to(line, (2 * JB, n)), seen)
    return (seen == local % BASES + 1).astype(F32)


def pack_kernel(width, mix_ref, embed_ref, taps_ref, tok_ref, out_ref, letters_ref, e_ref, t_ref, sems):
    big = pltpu.make_async_copy(mix_ref.at[0], out_ref.at[pl.ds(0, width)], sems.at[0])
    small = [
        pltpu.make_async_copy(embed_ref, e_ref, sems.at[1]),
        pltpu.make_async_copy(taps_ref, t_ref, sems.at[2]),
        pltpu.make_async_copy(tok_ref, letters_ref.at[0], sems.at[3]),
    ]
    for copy in small + [big]:
        copy.start()
    out_ref[width:, :] = jnp.zeros((TABLE, out_ref.shape[1]), BF)
    for copy in small:
        copy.wait()
    taps = t_ref[...].astype(F32)
    lines = [e_ref[...].astype(F32)]
    lines += [taps[j, block : block + 1, :] for block in range(BLOCKS) for j in range(TAPS)]
    lines.append(jnp.zeros((TABLE - BASES - 2 * TAPS, width), F32))
    out_ref[width:, :width] = jnp.concatenate(lines, axis=0).astype(BF)
    big.wait()


def local_kernel(n_chan, width, mix_ref, cot_ref, mixl_ref, cotl_ref, m_ref, c_ref, sems):
    first = pltpu.make_async_copy(mix_ref.at[1], m_ref, sems.at[0])
    second = pltpu.make_async_copy(cot_ref, c_ref, sems.at[1])
    first.start()
    second.start()
    first.wait()
    blocks = [m_ref[:, k * width : (k + 1) * width] for k in range(n_chan)]
    for k, block in enumerate(xor_blocks(blocks, lax.axis_index("chan"))):
        mixl_ref[:, k * width : (k + 1) * width] = block
    second.wait()
    cotl_ref[...] = c_ref[...].astype(F32).T.astype(BF)


def prep_kernel(n_seq, rows, dils, tok_ref, a_ref, hot_ref, hot1_ref):
    place = lax.axis_index("seq")

    def line(block):
        inside = jnp.logical_and(block >= 0, block < n_seq)
        safe = jnp.clip(block, 0, n_seq - 1)
        letters = tok_ref[pl.ds(lax.bitwise_xor(safe, place), 1), :] + 1
        return jnp.where(inside, letters, 0)

    def around(block):
        lines = [line(block - 1)[:, rows - LANE :], line(block), line(block + 1)[:, :LANE]]
        return jnp.concatenate(lines, axis=1)

    total = rows + 2 * LANE
    this = jnp.broadcast_to(around(place), (8, total))
    mirror = jnp.broadcast_to(around(n_seq - 1 - place), (8, total)).astype(F32).astype(BF)
    rev, n_tiles = reversal(LANE), total // LANE
    other = jnp.concatenate(
        [dot(mirror[:, t * LANE : (t + 1) * LANE], rev) for t in reversed(range(n_tiles))], axis=1
    ).astype(jnp.int32)

    def windows(dilation, margin, count):
        out = []
        for strand, source in ((1, this), (-1, other)):
            for j in range(TAPS):
                first = LANE - margin + strand * (j - HALF) * dilation
                out.append(pltpu.roll(source, total - first, 1)[:1, :count])
        return out

    hot = one_hot_t(windows(dils[0], REACH, a_ref.shape[0]))
    a_ref[...] = jnp.concatenate([hot, hot], axis=0).T.astype(BF)
    hot_ref[...] = hot.astype(BF)
    hot1_ref[...] = one_hot_t(windows(dils[1], 0, rows)).astype(BF)


def forward_kernel(n_chan, rows, width, scale, dils, *refs):
    tiles = n_chan * width // LANE
    pks, refs = refs[:n_chan], refs[n_chan:]
    (a_ref, mixl_ref, cot_ref), refs = refs[:3], refs[3:]
    (x2_ref, near_ref, far_ref, s_ref, st_ref, e_ref, et_ref), refs = refs[:7], refs[7:]
    x1_refs, refs = (refs[:tiles], refs[tiles : 2 * tiles]), refs[2 * tiles :]
    gp_refs, refs = (refs[:tiles], refs[tiles : 2 * tiles]), refs[2 * tiles :]
    w_ref, b_ref, m_ref, held, sem = refs
    chans = n_chan * width
    ext = rows + 2 * REACH
    me, dil = lax.axis_index("chan"), dils[1]
    rev = reversal(LANE)
    blocks = [slice(k * width, (k + 1) * width) for k in range(n_chan)]

    for k in range(n_chan):
        e_ref[:, blocks[k]] = pks[k][width:, :width]
    table = e_ref[...]
    plain = dot(select_rows("tap0", JB), table) * dot(select_rows("letter", JB), table)
    high, low = split_bf(plain)
    turned, turned_low, table_r = reverse_lanes([high, low, table], rev)
    et_ref[...] = table_r.astype(BF)
    b_ref[...] = jnp.concatenate([high, turned.astype(BF), low, turned_low.astype(BF)], axis=0)
    for k, block in enumerate(xor_blocks([b_ref[:, lanes] for lanes in blocks], me)):
        st_ref[:, blocks[k]] = block
    for k in range(n_chan):
        total = 0.5 * dot_t(st_ref[...], pks[k][:width, :])
        high, low = split_bf(total[: 2 * JB] + total[2 * JB :])
        w_ref[:, blocks[k]] = jnp.concatenate([high, low], axis=0)
    weights = w_ref[...]
    (swapped,) = reverse_lanes([weights], rev)
    order = [swapped[JB : 2 * JB], swapped[:JB], swapped[3 * JB :], swapped[2 * JB : 3 * JB]]
    weights_r = jnp.concatenate(order, axis=0).astype(BF)

    table, table_r = table.astype(F32), et_ref[...].astype(F32)
    centre = HALF * BASES
    keep = lax.broadcasted_iota(jnp.int32, (8, chans), 0) < BASES

    def lookup(source, first):
        lines = jnp.where(keep, source[:8], 0.0)
        above, below = jnp.zeros((first, chans), F32), jnp.zeros((4 * JB - first - 8, chans), F32)
        return jnp.concatenate([above, lines, below], axis=0).astype(BF)

    look, look_r = lookup(table, centre), lookup(table_r, JB + centre)
    chunk, mchunk = ext // 5, rows // 6
    for t in range(tiles):
        dst = slice(t * LANE, (t + 1) * LANE)
        for strand, (wr, er) in enumerate(((weights, look), (weights_r, look_r))):
            rhs = jnp.concatenate([wr[:, dst], er[:, dst]], axis=1)
            for i in range(5):
                where = pl.ds(i * chunk, chunk)
                both = dot(a_ref[where, :], rhs)
                value, slope = gelu_doubled(both[:, :LANE])
                x1_refs[strand][t][where, :] = both[:, LANE:] + value
                gp_refs[strand][t][where, :] = slope

        for i in range(6):
            first = i * mchunk
            terms = []
            for j in range(TAPS):
                shift = (j - HALF) * dil
                line = slice(ROW_TAPS1 + j, ROW_TAPS1 + j + 1)
                terms.append(table[line, dst] * x1_refs[0][t][pl.ds(first + REACH + shift, mchunk), :])
                terms.append(table_r[line, dst] * x1_refs[1][t][pl.ds(first + REACH - shift, mchunk), :])
            m_ref[first : first + mchunk, dst] = functools.reduce(jnp.add, terms).astype(BF)

    half = rows // 2
    n_own = pl.cdiv(width, LANE)
    for i in range(2):
        where = pl.ds(i * half, half)
        value, slope = gelu_parts(dot_t(m_ref[where, :], mixl_ref[...]))
        inner = pl.ds(REACH + i * half, half)
        own = jnp.concatenate([x1_refs[0][t][inner, :] for t in range(n_own)], axis=1)[:, :width]
        held[:, where] = (own + value).T.astype(BF)
        s_ref[where, :] = ((cot_ref[where, :].astype(F32) * scale) * slope).astype(BF)
    copy = pltpu.make_async_copy(held, x2_ref, sem)
    copy.start()

    part = t_dot(s_ref[...], m_ref[...]).astype(BF)
    odd = lax.axis_index("seq") % 2 == 1
    near_ref[...] = jnp.where(odd, part[width // 2 :], part[: width // 2])
    far_ref[...] = jnp.where(odd, part[: width // 2], part[width // 2 :])
    copy.wait()


def backward_kernel(n_chan, rows, width, scale, dils, *refs):
    tiles = n_chan * width // LANE
    (hot_ref, mixl_ref, cot_ref, s_ref, e_ref, et_ref), refs = refs[:6], refs[6:]
    x1_refs, refs = (refs[:tiles], refs[tiles : 2 * tiles]), refs[2 * tiles :]
    gp_refs, refs = (refs[:tiles], refs[tiles : 2 * tiles]), refs[2 * tiles :]
    (pb_ref, gt_ref, plain_ref, other_ref), refs = refs[:4], refs[4:]
    p_refs, s0_refs, (g2_ref,) = refs[:tiles], refs[tiles : 2 * tiles], refs[2 * tiles :]
    ext = rows + 2 * REACH
    padded = hot_ref.shape[1]
    dil = dils[1]
    taps_f, taps_r = 0.5 * e_ref[...].astype(F32), 0.5 * et_ref[...].astype(F32)

    edge = 2 * REACH
    n_own = pl.cdiv(width, LANE)
    g2 = cot_ref[...].astype(F32) * scale
    g2_ref[:, :REACH, :] = jnp.zeros((n_own, REACH, LANE), F32)
    g2_ref[:, rows + REACH :, :] = jnp.zeros((n_own, REACH, LANE), F32)
    g2 = jnp.concatenate([g2, jnp.zeros((rows, n_own * LANE - width), F32)], axis=1)
    for t in range(n_own):
        g2_ref[t, REACH : rows + REACH, :] = 0.5 * g2[:, t * LANE : (t + 1) * LANE]

    mchunk, chunk = rows // 6, ext // 5
    for t in range(tiles):
        dst = slice(t * LANE, (t + 1) * LANE)
        p_ref, s0_ref = p_refs[t], s0_refs[t]
        if t % 2 == 0:
            pair = dot(s_ref[...], mixl_ref[:, t * LANE : (t + 2) * LANE])
            pb_ref[:, t * LANE : (t + 2) * LANE] = pair.astype(BF)
        p_ref[:edge, :] = jnp.zeros((edge, LANE), F32)
        p_ref[rows + edge :, :] = jnp.zeros((edge, LANE), F32)
        p_ref[edge : rows + edge, :] = pair[:, (t % 2) * LANE : (t % 2 + 1) * LANE]
        s0_ref[ext:, :] = jnp.zeros((padded - ext, 2 * LANE), BF)
        for i in range(5):
            first = i * chunk
            where = pl.ds(first, chunk)
            fs, rs = [], []
            for j in range(TAPS):
                window = p_ref[pl.ds(first + REACH + (j - HALF) * dil, chunk), :]
                ahead, back = ROW_TAPS1 + j, ROW_TAPS1 + TAPS - 1 - j
                fs.append(taps_f[back : back + 1, dst] * window)
                rs.append(taps_r[ahead : ahead + 1, dst] * window)
            if t < n_own:
                fs.append(g2_ref[t, where, :])
            f, r = functools.reduce(jnp.add, fs), functools.reduce(jnp.add, rs)
            s0_ref[where, :LANE] = (f * gp_refs[0][t][where, :]).astype(BF)
            s0_ref[where, LANE:] = (r * gp_refs[1][t][where, :]).astype(BF)
        both = dot(hot_ref[...], s0_ref[...])
        plain_ref[:, dst], other_ref[:, dst] = both[:, :LANE], both[:, LANE:]

        sums = [None] * (2 * TAPS)
        for i in range(6):
            first = i * mchunk
            here = p_ref[pl.ds(edge + first, mchunk), :]
            for strand in range(2):
                for j in range(TAPS):
                    shift = (j - HALF) * dil * (1 - 2 * strand)
                    prod = here * x1_refs[strand][t][pl.ds(first + REACH + shift, mchunk), :]
                    part = prod.reshape(mchunk // 8, 8, LANE).sum(0)
                    slot = strand * TAPS + j
                    sums[slot] = part if i == 0 else sums[slot] + part
        for strand in range(2):
            lines = [jnp.sum(sums[strand * TAPS + j], axis=0, keepdims=True) for j in range(TAPS)]
            gt_ref[strand, :, dst] = jnp.concatenate(lines + [jnp.zeros((8 - TAPS, LANE), F32)], axis=0)


def collect_kernel(n_chan, width, scale, *refs):
    pks, refs = refs[:n_chan], refs[n_chan:]
    hot1_ref, cot_ref, e_ref, et_ref, pb_ref, gt_ref, plain_ref, other_ref = refs[:8]
    keep_ref, send_ref, dw_ref, st_ref, back_ref, tail_ref = refs[8:]
    chans = n_chan * width
    me, rev = lax.axis_index("chan"), reversal(LANE)
    blocks = [slice(k * width, (k + 1) * width) for k in range(n_chan)]
    table, table_r = e_ref[...], et_ref[...]

    by_tap = dot(hot1_ref[...], pb_ref[...])
    own_letters = dot(hot1_ref[:16, :], cot_ref[...]) * scale
    srow, scol = iotas((8, JB))
    sum_letter = as_bf((scol % BASES == srow) & (scol < TAPS * BASES))
    sum_tap = as_bf((scol // BASES == srow) & (scol < TAPS * BASES))

    def sums_of(sel, x):
        high, rest = split_bf(x)
        return dot(sel, high) + dot(sel, rest)

    sel1 = select_rows("tap1", JB)
    ahead = by_tap[:JB] * dot(sel1, table)
    other = by_tap[JB:] * dot(sel1, table_r)
    turned, other, taps_turned = reverse_wide([other_ref[...], other, gt_ref[1]], rev)
    sums = plain_ref[...] + jnp.concatenate([turned[JB:], turned[:JB]], axis=0)
    dw_ref[...] = sums
    letters = sums_of(sum_letter, ahead + other)
    tail_ref[8:16, :] = gt_ref[0] + taps_turned

    total = jnp.zeros((2 * JB, chans), F32)
    for k in range(n_chan):
        total = total + dot(dw_ref[:, blocks[k]].astype(BF), pks[k][:width, :])
    st_ref[...] = total
    for k, block in enumerate(xor_blocks([st_ref[:, lanes] for lanes in blocks], me)):
        back_ref[:, blocks[k]] = block
    (turned,) = reverse_wide([back_ref[JB:, :]], rev)
    both = back_ref[:JB, :] + turned
    tail_ref[0:8, :] = sums_of(sum_tap, both * dot(select_rows("letter", JB), table))
    letters = letters + sums_of(sum_letter, both * dot(select_rows("tap0", JB), table))
    tail_ref[16:24, :] = letters
    zeros = jnp.zeros((BASES, width), F32)
    own = jnp.concatenate([own_letters[HALF * BASES : (HALF + 1) * BASES, :], zeros], axis=0)
    for kk, lanes in enumerate(blocks):
        place, at = (keep_ref, send_ref)[kk % 2], kk // 2
        letters = tail_ref[16:24, lanes]
        if kk == 0:
            letters = letters + own
        place[at, :ROW_R, :] = jnp.concatenate([dw_ref[:ROW_GE, lanes], letters[:BASES]], axis=0)
        place[at, ROW_R : 2 * ROW_R, :] = dw_ref[JB : JB + ROW_R, lanes]
        place[at, ROW_GT0:, :] = tail_ref[0:16, lanes]


def add_kernel(a_ref, b_ref, first_ref, second_ref):
    first_ref[...] = a_ref[0] + b_ref[0]
    second_ref[...] = a_ref[1] + b_ref[1]


def mix1_kernel(n_chan, width, near_ref, far_ref, out_ref, held, sem):
    me, odd = lax.axis_index("chan"), lax.axis_index("seq") % 2
    half = width // 2
    for source, first in ((near_ref, odd * half), (far_ref, (1 - odd) * half)):
        blocks = [source[:, k * width : (k + 1) * width].astype(F32) for k in range(n_chan)]
        for k, part in enumerate(xor_blocks(blocks, me)):
            held[pl.ds(pl.multiple_of(first, half), half), k * width : (k + 1) * width] = part
    copy = pltpu.make_async_copy(held, out_ref.at[1], sem)
    copy.start()
    copy.wait()


def finish_kernel(n_chan, width, st_ref, sa_ref, sb_ref, _, gm_ref, gt_ref, ge_ref, held, sems):
    sums = sa_ref[...] + sb_ref[...]
    fill = jnp.zeros((JB - ROW_GE, width), F32)
    dw = jnp.concatenate([sums[:ROW_GE], fill, sums[ROW_R : ROW_R + ROW_GE], fill], axis=0).astype(BF)
    copies = []
    step = 2 * LANE
    for i in range(n_chan * width // step):
        lanes = pl.ds(i * step, step)
        held[:, lanes] = t_dot(dw, st_ref[: 2 * JB, lanes])
        copies.append(pltpu.make_async_copy(held.at[:, lanes], gm_ref.at[0, :, lanes], sems.at[i]))
        copies[-1].start()
    for j in range(TAPS):
        gt_ref[j, 0:1, :] = sums[ROW_GT0 + j : ROW_GT0 + j + 1]
        gt_ref[j, 1:2, :] = sums[ROW_GT1 + j : ROW_GT1 + j + 1]
    ge_ref[...] = sums[ROW_GE : ROW_GE + BASES]
    for copy in copies:
        copy.wait()


VMEM = pl.BlockSpec(memory_space=pltpu.VMEM)
SMEM = pl.BlockSpec(memory_space=pltpu.SMEM)
HBM = pl.BlockSpec(memory_space=pltpu.HBM)


def in_hbm(x):
    return pltpu.with_memory_space_constraint(x, pltpu.HBM)


def call(kernel, in_specs, out_shape, out_specs, scratch, limit, cost, aliases=None):
    flops, moved = cost
    return pl.pallas_call(
        kernel,
        out_shape=out_shape,
        in_specs=in_specs,
        out_specs=out_specs,
        scratch_shapes=scratch,
        input_output_aliases=aliases or {},
        compiler_params=pltpu.CompilerParams(vmem_limit_bytes=limit << 20),
        cost_estimate=pl.CostEstimate(flops=flops, bytes_accessed=moved, transcendentals=0),
    )


def flip_bits(x, axis, mask):
    return lax.ppermute(x, axis, [(i, i ^ mask) for i in range(lax.axis_size(axis))])


def body(tokens, cotangent, embed, taps, mix, dilations):
    rows, width = cotangent.shape
    n_seq, n_chan = lax.axis_size("seq"), lax.axis_size("chan")
    chans = n_chan * width
    tiles = chans // LANE
    ext = rows + 2 * REACH
    padded = pl.cdiv(ext, LANE) * LANE
    edge = 2 * REACH
    own_tiles = pl.cdiv(width, LANE)
    scale = 1.0 / math.sqrt(rows * n_seq)
    shape = jax.ShapeDtypeStruct
    mix_t = jnp.swapaxes(mix, 1, 2)

    pk, letters = call(
        functools.partial(pack_kernel, width),
        [HBM] * 4,
        [shape((width + TABLE, chans), BF), shape((1, rows), jnp.int32)],
        [VMEM] * 2,
        [
            pltpu.VMEM((BASES, width), BF),
            pltpu.VMEM((TAPS, BLOCKS, width), BF),
            pltpu.SemaphoreType.DMA((4,)),
        ],
        8,
        (0, width * chans * 4),
    )(in_hbm(mix_t), in_hbm(embed), in_hbm(jnp.swapaxes(taps, 0, 1)), in_hbm(tokens))

    seq_bits = n_seq.bit_length() - 1
    for bit in range(seq_bits):
        letters = jnp.concatenate([letters, flip_bits(letters, "seq", 1 << bit)], axis=0)

    mixl, cot = call(
        functools.partial(local_kernel, n_chan, width),
        [HBM, HBM],
        [shape((width, chans), BF), shape((rows, width), BF)],
        [VMEM] * 2,
        [
            pltpu.VMEM((width, chans), BF),
            pltpu.VMEM((width, rows), BF),
            pltpu.SemaphoreType.DMA((2,)),
        ],
        16,
        (1 << 20, 1 << 20),
    )(in_hbm(mix_t), in_hbm(cotangent.T))

    pks = [pk]
    for bit in reversed(range(n_chan.bit_length() - 1)):
        ready = [pks[0]] + [lax.optimization_barrier((p, letters, mixl, cot))[0] for p in pks[1:]]
        moved = [flip_bits(p, "chan", 1 << bit) for p in ready]
        pks = [q for pair in zip(pks, moved) for q in pair]

    hot_t, hot, hot1 = call(
        functools.partial(prep_kernel, n_seq, rows),
        [SMEM, VMEM],
        [shape((padded, 4 * JB), BF), shape((2 * JB, padded), BF), shape((2 * JB, rows), BF)],
        [VMEM] * 3,
        [],
        16,
        (1 << 20, 1 << 20),
    )(dilations, letters)

    rows_ext = shape((ext, LANE), F32)
    x2, near, far, s1, stack, table, table_r, *strands = call(
        functools.partial(forward_kernel, n_chan, rows, width, scale),
        [SMEM] + [VMEM] * (n_chan + 3),
        [
            shape((width, rows), BF),
            shape((width // 2, chans), BF),
            shape((width // 2, chans), BF),
            shape((rows, width), BF),
            shape((4 * JB, chans), BF),
            shape((TABLE, chans), BF),
            shape((TABLE, chans), BF),
        ]
        + [rows_ext] * (4 * tiles),
        [HBM] + [VMEM] * (6 + 4 * tiles),
        [
            pltpu.VMEM((4 * JB, chans), BF),
            pltpu.VMEM((4 * JB, chans), BF),
            pltpu.VMEM((rows, chans), BF),
            pltpu.VMEM((width, rows), BF),
            pltpu.SemaphoreType.DMA,
        ],
        32,
        (3 << 30, 8 << 20),
    )(dilations, *pks, hot_t, mixl, cot)

    arrived = flip_bits(far, "seq", 1)
    pb, gt, plain, other = call(
        functools.partial(backward_kernel, n_chan, rows, width, scale),
        [SMEM] + [VMEM] * (6 + 4 * tiles),
        [
            shape((rows, chans), BF),
            shape((2, 8, chans), F32),
            shape((2 * JB, chans), F32),
            shape((2 * JB, chans), F32),
        ],
        [VMEM] * 4,
        [pltpu.VMEM((rows + 2 * edge, LANE), F32)] * tiles
        + [pltpu.VMEM((padded, 2 * LANE), BF)] * tiles
        + [pltpu.VMEM((own_tiles, ext, LANE), F32)],
        40,
        (3 << 30, 8 << 20),
    )(dilations, hot, mixl, cot, s1, table, table_r, *strands)

    def rounded_sum(a, b):
        return lax.optimization_barrier((a.astype(F32) + b.astype(F32)).astype(BF))

    g_mine = rounded_sum(near, lax.optimization_barrier((arrived, plain))[0])
    gt = lax.optimization_barrier((gt, g_mine))[0]
    keep, send = call(
        functools.partial(collect_kernel, n_chan, width, scale),
        [VMEM] * (n_chan + 8),
        [shape((n_chan // 2, SUMS, width), F32)] * 2,
        [VMEM] * 2,
        [
            pltpu.VMEM((2 * JB, chans), F32),
            pltpu.VMEM((2 * JB, chans), F32),
            pltpu.VMEM((2 * JB, chans), F32),
            pltpu.VMEM((24, chans), F32),
        ],
        24,
        (1 << 20, 1 << 16),
    )(*pks, hot1, cot, table, table_r, pb, gt, plain, other)

    for bit in range(1, seq_bits):
        g_mine = rounded_sum(g_mine, flip_bits(g_mine, "seq", 1 << bit))
    g_other = flip_bits(g_mine, "seq", 1)
    last = n_chan.bit_length() - 2
    mine, theirs = keep, flip_bits(send, "chan", 1)
    for bit in range(1, last):
        mine = mine + theirs
        mine, theirs = mine[0::2], flip_bits(mine[1::2], "chan", 1 << bit)
    s_mine = call(
        add_kernel,
        [VMEM] * 2,
        [shape((SUMS, width), F32)] * 2,
        [VMEM] * 2,
        [],
        8,
        (0, 0),
    )(mine, theirs)
    across = flip_bits(s_mine[1], "chan", 1 << last)
    along = flip_bits(s_mine[0], "seq", 1)
    places = [(i, j) for i in range(n_seq) for j in range(n_chan)]
    pairs = [(i * n_chan + j, (i ^ 1) * n_chan + (j ^ (1 << last))) for i, j in places]
    corner = lax.ppermute(s_mine[1], ("seq", "chan"), pairs)
    s_mine = (s_mine[0] + across) + (along + corner)
    for bit in range(1, seq_bits):
        s_other = flip_bits(s_mine, "seq", 1 << bit)
        if bit < seq_bits - 1:
            s_mine = s_mine + s_other

    big = pltpu.VMEM((width, chans), F32)
    (grad_mix,) = call(
        functools.partial(mix1_kernel, n_chan, width),
        [VMEM, VMEM],
        [shape((BLOCKS, width, chans), F32)],
        [HBM],
        [big, pltpu.SemaphoreType.DMA],
        16,
        (1 << 20, 1 << 21),
    )(g_mine, g_other)
    grad_mix, grad_taps, grad_embed = call(
        functools.partial(finish_kernel, n_chan, width),
        [VMEM, VMEM, VMEM, HBM],
        [
            shape((BLOCKS, width, chans), F32),
            shape((TAPS, BLOCKS, width), F32),
            shape((BASES, width), F32),
        ],
        [HBM, VMEM, VMEM],
        [big, pltpu.SemaphoreType.DMA((chans // (2 * LANE),))],
        16,
        (1 << 24, 1 << 21),
        {3: 0},
    )(stack, s_mine, s_other, grad_mix)
    return x2.T, jnp.swapaxes(grad_mix, 1, 2), jnp.swapaxes(grad_taps, 0, 1), grad_embed


def solution(mesh):
    in_specs = (
        P(("groups", "seq")),
        P(("groups", "seq"), "chan"),
        P(None, "chan"),
        P(None, None, "chan"),
        P(None, None, "chan"),
        P(),
    )
    out_specs = (
        P(("groups", "seq"), "chan"),
        P("groups", None, "chan"),
        P("groups", None, "chan"),
        P("groups", "chan"),
    )
    return jax.shard_map(body, mesh=mesh, in_specs=in_specs, out_specs=out_specs, check_vma=False)
```

```python
import functools
import math

import jax
import jax.numpy as jnp
from jax import lax
from jax.experimental import pallas as pl
from jax.experimental.pallas import tpu as pltpu
from jax.sharding import PartitionSpec as P

TAPS = 5
BASES = 4
BLOCKS = 2
DMAX = 8
HALF = TAPS // 2
REACH = HALF * DMAX
LANE = 128
JB = 32
GELU_SCALE = math.sqrt(2.0 / math.pi)
CUBIC = 0.044715
BF = jnp.bfloat16
F32 = jnp.float32
ROW_EMBED, ROW_TAPS0, ROW_TAPS1, TABLE = 0, BASES, BASES + TAPS, 16
ROW_GE, ROW_R, ROW_GT0, ROW_GT1, SUMS = 20, 24, 48, 56, 64


def dot(a, b, **kw):
    return jnp.dot(a, b, preferred_element_type=F32, **kw)


def dot_t(a, b):
    return lax.dot_general(a, b, (((1,), (1,)), ((), ())), preferred_element_type=F32)


def t_dot(a, b):
    return lax.dot_general(a, b, (((0,), (0,)), ((), ())), preferred_element_type=F32)


def iotas(shape):
    return lax.broadcasted_iota(jnp.int32, shape, 0), lax.broadcasted_iota(jnp.int32, shape, 1)


def as_bf(mask):
    return mask.astype(F32).astype(BF)


def reversal(size):
    row, col = iotas((size, size))
    return as_bf(row + col == size - 1)


def split_bf(x):
    high = x.astype(BF)
    return high, (x - high.astype(F32)).astype(BF)


def reverse_lanes(parts, rev):
    n = parts[0].shape[1] // LANE
    rows = [p.shape[0] for p in parts]
    pile = [p[:, t * LANE : (t + 1) * LANE] for p in parts for t in range(n)]
    turned = dot(jnp.concatenate(pile, axis=0), rev)
    out, first = [], 0
    for count in rows:
        tiles = [turned[first + t * count : first + (t + 1) * count] for t in range(n)]
        out.append(jnp.concatenate(tiles[::-1], axis=1))
        first += n * count
    return out


def reverse_wide(parts, rev):
    split = [split_bf(p) for p in parts]
    turned = reverse_lanes([q for pair in split for q in pair], rev)
    return [turned[2 * i] + turned[2 * i + 1] for i in range(len(parts))]


def xor_blocks(blocks, me):
    for bit in range(len(blocks).bit_length() - 1):
        swap = lax.bitwise_and(lax.shift_right_logical(me, bit), 1) == 1
        blocks = [jnp.where(swap, blocks[k ^ (1 << bit)], blocks[k]) for k in range(len(blocks))]
    return blocks


def gelu_parts(v):
    square = v * v
    tangent = jnp.tanh(v * (GELU_SCALE + (GELU_SCALE * CUBIC) * square))
    half = 0.5 + 0.5 * tangent
    value = v * half
    slope = half + (v * (1.0 - tangent * tangent)) * (
        0.5 * GELU_SCALE + (1.5 * GELU_SCALE * CUBIC) * square
    )
    return value, slope


def gelu_doubled(half):
    square = half * half
    cubic = (8.0 * GELU_SCALE * CUBIC) * square
    above = 1.0 + jnp.tanh(half * (2.0 * GELU_SCALE + cubic))
    value = half * above
    slope = above + value * ((2.0 - above) * (2.0 * GELU_SCALE + 3.0 * cubic))
    return value, slope


def select_rows(kind, rows):
    row, col = iotas((rows, TABLE))
    local = row % JB
    used = local < TAPS * BASES
    tap, letter = local // BASES, local % BASES
    want = {"tap0": ROW_TAPS0 + tap, "tap1": ROW_TAPS1 + tap, "letter": ROW_EMBED + letter}[kind]
    return as_bf(used & (col == want))


def one_hot_t(tokens):
    n = tokens[0].shape[1]
    inside = tokens[HALF] != 0
    row = lax.broadcasted_iota(jnp.int32, (2 * JB, n), 0)
    local = row % JB
    group = jnp.where(local < TAPS * BASES, local // BASES + TAPS * (row // JB), -1)
    seen = jnp.zeros((2 * JB, n), jnp.int32)
    for g, line in enumerate(tokens):
        line = jnp.where(inside, line, 0)
        seen = jnp.where(group == g, jnp.broadcast_to(line, (2 * JB, n)), seen)
    return (seen == local % BASES + 1).astype(F32)


def pack_kernel(width, mix_ref, embed_ref, taps_ref, tok_ref, out_ref, letters_ref, e_ref, t_ref, sems):
    big = pltpu.make_async_copy(mix_ref.at[0], out_ref.at[pl.ds(0, width)], sems.at[0])
    small = [
        pltpu.make_async_copy(embed_ref, e_ref, sems.at[1]),
        pltpu.make_async_copy(taps_ref, t_ref, sems.at[2]),
        pltpu.make_async_copy(tok_ref, letters_ref.at[0], sems.at[3]),
    ]
    for copy in small + [big]:
        copy.start()
    out_ref[width:, :] = jnp.zeros((TABLE, out_ref.shape[1]), BF)
    for copy in small:
        copy.wait()
    taps = t_ref[...].astype(F32)
    lines = [e_ref[...].astype(F32)]
    lines += [taps[j, block : block + 1, :] for block in range(BLOCKS) for j in range(TAPS)]
    lines.append(jnp.zeros((TABLE - BASES - 2 * TAPS, width), F32))
    out_ref[width:, :width] = jnp.concatenate(lines, axis=0).astype(BF)
    big.wait()


def local_kernel(n_chan, width, mix_ref, cot_ref, mixl_ref, cotl_ref, m_ref, c_ref, sems):
    first = pltpu.make_async_copy(mix_ref.at[1], m_ref, sems.at[0])
    second = pltpu.make_async_copy(cot_ref, c_ref, sems.at[1])
    first.start()
    second.start()
    first.wait()
    blocks = [m_ref[:, k * width : (k + 1) * width] for k in range(n_chan)]
    for k, block in enumerate(xor_blocks(blocks, lax.axis_index("chan"))):
        mixl_ref[:, k * width : (k + 1) * width] = block
    second.wait()
    cotl_ref[...] = c_ref[...].astype(F32).T.astype(BF)


def prep_kernel(n_seq, rows, dils, tok_ref, a_ref, hot_ref, hot1_ref):
    place = lax.axis_index("seq")

    def line(block):
        inside = jnp.logical_and(block >= 0, block < n_seq)
        safe = jnp.clip(block, 0, n_seq - 1)
        letters = tok_ref[pl.ds(lax.bitwise_xor(safe, place), 1), :] + 1
        return jnp.where(inside, letters, 0)

    def around(block):
        lines = [line(block - 1)[:, rows - LANE :], line(block), line(block + 1)[:, :LANE]]
        return jnp.concatenate(lines, axis=1)

    total = rows + 2 * LANE
    this = jnp.broadcast_to(around(place), (8, total))
    mirror = jnp.broadcast_to(around(n_seq - 1 - place), (8, total)).astype(F32).astype(BF)
    rev, n_tiles = reversal(LANE), total // LANE
    other = jnp.concatenate(
        [dot(mirror[:, t * LANE : (t + 1) * LANE], rev) for t in reversed(range(n_tiles))], axis=1
    ).astype(jnp.int32)

    def windows(dilation, margin, count):
        out = []
        for strand, source in ((1, this), (-1, other)):
            for j in range(TAPS):
                first = LANE - margin + strand * (j - HALF) * dilation
                out.append(pltpu.roll(source, total - first, 1)[:1, :count])
        return out

    hot = one_hot_t(windows(dils[0], REACH, a_ref.shape[0]))
    a_ref[...] = jnp.concatenate([hot, hot], axis=0).T.astype(BF)
    hot_ref[...] = hot.astype(BF)
    hot1_ref[...] = one_hot_t(windows(dils[1], 0, rows)).astype(BF)


def forward_kernel(n_chan, rows, width, scale, dils, *refs):
    tiles = n_chan * width // LANE
    pks, refs = refs[:n_chan], refs[n_chan:]
    (a_ref, mixl_ref, cot_ref), refs = refs[:3], refs[3:]
    (x2_ref, near_ref, far_ref, s_ref, st_ref, e_ref, et_ref), refs = refs[:7], refs[7:]
    x1_refs, refs = (refs[:tiles], refs[tiles : 2 * tiles]), refs[2 * tiles :]
    gp_refs, refs = (refs[:tiles], refs[tiles : 2 * tiles]), refs[2 * tiles :]
    w_ref, b_ref, m_ref, held, sem = refs
    chans = n_chan * width
    ext = rows + 2 * REACH
    me, dil = lax.axis_index("chan"), dils[1]
    rev = reversal(LANE)
    blocks = [slice(k * width, (k + 1) * width) for k in range(n_chan)]

    for k in range(n_chan):
        e_ref[:, blocks[k]] = pks[k][width:, :width]
    table = e_ref[...]
    plain = dot(select_rows("tap0", JB), table) * dot(select_rows("letter", JB), table)
    high, low = split_bf(plain)
    turned, turned_low, table_r = reverse_lanes([high, low, table], rev)
    et_ref[...] = table_r.astype(BF)
    b_ref[...] = jnp.concatenate([high, turned.astype(BF), low, turned_low.astype(BF)], axis=0)
    for k, block in enumerate(xor_blocks([b_ref[:, lanes] for lanes in blocks], me)):
        st_ref[:, blocks[k]] = block
    for k in range(n_chan):
        total = 0.5 * dot_t(st_ref[...], pks[k][:width, :])
        high, low = split_bf(total[: 2 * JB] + total[2 * JB :])
        w_ref[:, blocks[k]] = jnp.concatenate([high, low], axis=0)
    weights = w_ref[...]
    (swapped,) = reverse_lanes([weights], rev)
    order = [swapped[JB : 2 * JB], swapped[:JB], swapped[3 * JB :], swapped[2 * JB : 3 * JB]]
    weights_r = jnp.concatenate(order, axis=0).astype(BF)

    table, table_r = table.astype(F32), et_ref[...].astype(F32)
    centre = HALF * BASES
    keep = lax.broadcasted_iota(jnp.int32, (8, chans), 0) < BASES

    def lookup(source, first):
        lines = jnp.where(keep, source[:8], 0.0)
        above, below = jnp.zeros((first, chans), F32), jnp.zeros((4 * JB - first - 8, chans), F32)
        return jnp.concatenate([above, lines, below], axis=0).astype(BF)

    look, look_r = lookup(table, centre), lookup(table_r, JB + centre)
    chunk, mchunk = ext // 5, rows // 6
    for t in range(tiles):
        dst = slice(t * LANE, (t + 1) * LANE)
        for strand, (wr, er) in enumerate(((weights, look), (weights_r, look_r))):
            rhs = jnp.concatenate([wr[:, dst], er[:, dst]], axis=1)
            for i in range(5):
                where = pl.ds(i * chunk, chunk)
                both = dot(a_ref[where, :], rhs)
                value, slope = gelu_doubled(both[:, :LANE])
                x1_refs[strand][t][where, :] = both[:, LANE:] + value
                gp_refs[strand][t][where, :] = slope

        for i in range(6):
            first = i * mchunk
            terms = []
            for j in range(TAPS):
                shift = (j - HALF) * dil
                line = slice(ROW_TAPS1 + j, ROW_TAPS1 + j + 1)
                terms.append(table[line, dst] * x1_refs[0][t][pl.ds(first + REACH + shift, mchunk), :])
                terms.append(table_r[line, dst] * x1_refs[1][t][pl.ds(first + REACH - shift, mchunk), :])
            m_ref[first : first + mchunk, dst] = functools.reduce(jnp.add, terms).astype(BF)

    half = rows // 2
    n_own = pl.cdiv(width, LANE)
    for i in range(2):
        where = pl.ds(i * half, half)
        value, slope = gelu_parts(dot_t(m_ref[where, :], mixl_ref[...]))
        inner = pl.ds(REACH + i * half, half)
        own = jnp.concatenate([x1_refs[0][t][inner, :] for t in range(n_own)], axis=1)[:, :width]
        held[:, where] = (own + value).T.astype(BF)
        s_ref[where, :] = ((cot_ref[where, :].astype(F32) * scale) * slope).astype(BF)
    copy = pltpu.make_async_copy(held, x2_ref, sem)
    copy.start()

    part = t_dot(s_ref[...], m_ref[...]).astype(BF)
    odd = lax.axis_index("seq") % 2 == 1
    near_ref[...] = jnp.where(odd, part[width // 2 :], part[: width // 2])
    far_ref[...] = jnp.where(odd, part[: width // 2], part[width // 2 :])
    copy.wait()


def backward_kernel(n_chan, rows, width, scale, dils, *refs):
    tiles = n_chan * width // LANE
    (hot_ref, mixl_ref, cot_ref, s_ref, e_ref, et_ref), refs = refs[:6], refs[6:]
    x1_refs, refs = (refs[:tiles], refs[tiles : 2 * tiles]), refs[2 * tiles :]
    gp_refs, refs = (refs[:tiles], refs[tiles : 2 * tiles]), refs[2 * tiles :]
    (pb_ref, gt_ref, plain_ref, other_ref), refs = refs[:4], refs[4:]
    p_refs, s0_refs, (g2_ref,) = refs[:tiles], refs[tiles : 2 * tiles], refs[2 * tiles :]
    ext = rows + 2 * REACH
    padded = hot_ref.shape[1]
    dil = dils[1]
    taps_f, taps_r = 0.5 * e_ref[...].astype(F32), 0.5 * et_ref[...].astype(F32)

    edge = 2 * REACH
    n_own = pl.cdiv(width, LANE)
    g2 = cot_ref[...].astype(F32) * scale
    g2_ref[:, :REACH, :] = jnp.zeros((n_own, REACH, LANE), F32)
    g2_ref[:, rows + REACH :, :] = jnp.zeros((n_own, REACH, LANE), F32)
    g2 = jnp.concatenate([g2, jnp.zeros((rows, n_own * LANE - width), F32)], axis=1)
    for t in range(n_own):
        g2_ref[t, REACH : rows + REACH, :] = 0.5 * g2[:, t * LANE : (t + 1) * LANE]

    mchunk, chunk = rows // 6, ext // 5
    for t in range(tiles):
        dst = slice(t * LANE, (t + 1) * LANE)
        p_ref, s0_ref = p_refs[t], s0_refs[t]
        if t % 2 == 0:
            pair = dot(s_ref[...], mixl_ref[:, t * LANE : (t + 2) * LANE])
            pb_ref[:, t * LANE : (t + 2) * LANE] = pair.astype(BF)
        p_ref[:edge, :] = jnp.zeros((edge, LANE), F32)
        p_ref[rows + edge :, :] = jnp.zeros((edge, LANE), F32)
        p_ref[edge : rows + edge, :] = pair[:, (t % 2) * LANE : (t % 2 + 1) * LANE]
        s0_ref[ext:, :] = jnp.zeros((padded - ext, 2 * LANE), BF)
        for i in range(5):
            first = i * chunk
            where = pl.ds(first, chunk)
            fs, rs = [], []
            for j in range(TAPS):
                window = p_ref[pl.ds(first + REACH + (j - HALF) * dil, chunk), :]
                ahead, back = ROW_TAPS1 + j, ROW_TAPS1 + TAPS - 1 - j
                fs.append(taps_f[back : back + 1, dst] * window)
                rs.append(taps_r[ahead : ahead + 1, dst] * window)
            if t < n_own:
                fs.append(g2_ref[t, where, :])
            f, r = functools.reduce(jnp.add, fs), functools.reduce(jnp.add, rs)
            s0_ref[where, :LANE] = (f * gp_refs[0][t][where, :]).astype(BF)
            s0_ref[where, LANE:] = (r * gp_refs[1][t][where, :]).astype(BF)
        both = dot(hot_ref[...], s0_ref[...])
        plain_ref[:, dst], other_ref[:, dst] = both[:, :LANE], both[:, LANE:]

        sums = [None] * (2 * TAPS)
        for i in range(6):
            first = i * mchunk
            here = p_ref[pl.ds(edge + first, mchunk), :]
            for strand in range(2):
                for j in range(TAPS):
                    shift = (j - HALF) * dil * (1 - 2 * strand)
                    prod = here * x1_refs[strand][t][pl.ds(first + REACH + shift, mchunk), :]
                    part = prod.reshape(mchunk // 8, 8, LANE).sum(0)
                    slot = strand * TAPS + j
                    sums[slot] = part if i == 0 else sums[slot] + part
        for strand in range(2):
            lines = [jnp.sum(sums[strand * TAPS + j], axis=0, keepdims=True) for j in range(TAPS)]
            gt_ref[strand, :, dst] = jnp.concatenate(lines + [jnp.zeros((8 - TAPS, LANE), F32)], axis=0)


def collect_kernel(n_chan, width, scale, *refs):
    pks, refs = refs[:n_chan], refs[n_chan:]
    hot1_ref, cot_ref, e_ref, et_ref, pb_ref, gt_ref, plain_ref, other_ref = refs[:8]
    keep_ref, send_ref, dw_ref, st_ref, back_ref, tail_ref = refs[8:]
    chans = n_chan * width
    me, rev = lax.axis_index("chan"), reversal(LANE)
    blocks = [slice(k * width, (k + 1) * width) for k in range(n_chan)]
    table, table_r = e_ref[...], et_ref[...]

    by_tap = dot(hot1_ref[...], pb_ref[...])
    own_letters = dot(hot1_ref[:16, :], cot_ref[...]) * scale
    srow, scol = iotas((8, JB))
    sum_letter = as_bf((scol % BASES == srow) & (scol < TAPS * BASES))
    sum_tap = as_bf((scol // BASES == srow) & (scol < TAPS * BASES))

    def sums_of(sel, x):
        high, rest = split_bf(x)
        return dot(sel, high) + dot(sel, rest)

    sel1 = select_rows("tap1", JB)
    ahead = by_tap[:JB] * dot(sel1, table)
    other = by_tap[JB:] * dot(sel1, table_r)
    turned, other, taps_turned = reverse_wide([other_ref[...], other, gt_ref[1]], rev)
    sums = plain_ref[...] + jnp.concatenate([turned[JB:], turned[:JB]], axis=0)
    dw_ref[...] = sums
    letters = sums_of(sum_letter, ahead + other)
    tail_ref[8:16, :] = gt_ref[0] + taps_turned

    total = jnp.zeros((2 * JB, chans), F32)
    for k in range(n_chan):
        total = total + dot(dw_ref[:, blocks[k]].astype(BF), pks[k][:width, :])
    st_ref[...] = total
    for k, block in enumerate(xor_blocks([st_ref[:, lanes] for lanes in blocks], me)):
        back_ref[:, blocks[k]] = block
    (turned,) = reverse_wide([back_ref[JB:, :]], rev)
    both = back_ref[:JB, :] + turned
    tail_ref[0:8, :] = sums_of(sum_tap, both * dot(select_rows("letter", JB), table))
    letters = letters + sums_of(sum_letter, both * dot(select_rows("tap0", JB), table))
    tail_ref[16:24, :] = letters
    zeros = jnp.zeros((BASES, width), F32)
    own = jnp.concatenate([own_letters[HALF * BASES : (HALF + 1) * BASES, :], zeros], axis=0)
    for kk, lanes in enumerate(blocks):
        place, at = (keep_ref, send_ref)[kk % 2], kk // 2
        letters = tail_ref[16:24, lanes]
        if kk == 0:
            letters = letters + own
        place[at, :ROW_R, :] = jnp.concatenate([dw_ref[:ROW_GE, lanes], letters[:BASES]], axis=0)
        place[at, ROW_R : 2 * ROW_R, :] = dw_ref[JB : JB + ROW_R, lanes]
        place[at, ROW_GT0:, :] = tail_ref[0:16, lanes]


def add_kernel(a_ref, b_ref, first_ref, second_ref):
    first_ref[...] = a_ref[0] + b_ref[0]
    second_ref[...] = a_ref[1] + b_ref[1]


def mix1_kernel(n_chan, width, near_ref, far_ref, out_ref, held, sem):
    me, odd = lax.axis_index("chan"), lax.axis_index("seq") % 2
    half = width // 2
    for source, first in ((near_ref, odd * half), (far_ref, (1 - odd) * half)):
        blocks = [source[:, k * width : (k + 1) * width].astype(F32) for k in range(n_chan)]
        for k, part in enumerate(xor_blocks(blocks, me)):
            held[pl.ds(pl.multiple_of(first, half), half), k * width : (k + 1) * width] = part
    copy = pltpu.make_async_copy(held, out_ref.at[1], sem)
    copy.start()
    copy.wait()


def finish_kernel(n_chan, width, st_ref, sa_ref, sb_ref, _, gm_ref, gt_ref, ge_ref, held, sems):
    sums = sa_ref[...] + sb_ref[...]
    fill = jnp.zeros((JB - ROW_GE, width), F32)
    dw = jnp.concatenate([sums[:ROW_GE], fill, sums[ROW_R : ROW_R + ROW_GE], fill], axis=0).astype(BF)
    copies = []
    step = 2 * LANE
    for i in range(n_chan * width // step):
        lanes = pl.ds(i * step, step)
        held[:, lanes] = t_dot(dw, st_ref[: 2 * JB, lanes])
        copies.append(pltpu.make_async_copy(held.at[:, lanes], gm_ref.at[0, :, lanes], sems.at[i]))
        copies[-1].start()
    for j in range(TAPS):
        gt_ref[j, 0:1, :] = sums[ROW_GT0 + j : ROW_GT0 + j + 1]
        gt_ref[j, 1:2, :] = sums[ROW_GT1 + j : ROW_GT1 + j + 1]
    ge_ref[...] = sums[ROW_GE : ROW_GE + BASES]
    for copy in copies:
        copy.wait()


VMEM = pl.BlockSpec(memory_space=pltpu.VMEM)
SMEM = pl.BlockSpec(memory_space=pltpu.SMEM)
HBM = pl.BlockSpec(memory_space=pltpu.HBM)


def in_hbm(x):
    return pltpu.with_memory_space_constraint(x, pltpu.HBM)


def call(kernel, in_specs, out_shape, out_specs, scratch, limit, cost, aliases=None):
    flops, moved = cost
    return pl.pallas_call(
        kernel,
        out_shape=out_shape,
        in_specs=in_specs,
        out_specs=out_specs,
        scratch_shapes=scratch,
        input_output_aliases=aliases or {},
        compiler_params=pltpu.CompilerParams(vmem_limit_bytes=limit << 20),
        cost_estimate=pl.CostEstimate(flops=flops, bytes_accessed=moved, transcendentals=0),
    )


def flip_bits(x, axis, mask):
    return lax.ppermute(x, axis, [(i, i ^ mask) for i in range(lax.axis_size(axis))])


def body(tokens, cotangent, embed, taps, mix, dilations):
    rows, width = cotangent.shape
    n_seq, n_chan = lax.axis_size("seq"), lax.axis_size("chan")
    chans = n_chan * width
    tiles = chans // LANE
    ext = rows + 2 * REACH
    padded = pl.cdiv(ext, LANE) * LANE
    edge = 2 * REACH
    own_tiles = pl.cdiv(width, LANE)
    scale = 1.0 / math.sqrt(rows * n_seq)
    shape = jax.ShapeDtypeStruct
    mix_t = jnp.swapaxes(mix, 1, 2)

    pk, letters = call(
        functools.partial(pack_kernel, width),
        [HBM] * 4,
        [shape((width + TABLE, chans), BF), shape((1, rows), jnp.int32)],
        [VMEM] * 2,
        [
            pltpu.VMEM((BASES, width), BF),
            pltpu.VMEM((TAPS, BLOCKS, width), BF),
            pltpu.SemaphoreType.DMA((4,)),
        ],
        8,
        (0, width * chans * 4),
    )(in_hbm(mix_t), in_hbm(embed), in_hbm(jnp.swapaxes(taps, 0, 1)), in_hbm(tokens))

    seq_bits = n_seq.bit_length() - 1
    for bit in range(0, seq_bits, 2):
        masks = [k << bit for k in range(1, 1 << min(2, seq_bits - bit))]
        letters = jnp.concatenate([letters] + [flip_bits(letters, "seq", m) for m in masks], axis=0)

    mixl, cot = call(
        functools.partial(local_kernel, n_chan, width),
        [HBM, HBM],
        [shape((width, chans), BF), shape((rows, width), BF)],
        [VMEM] * 2,
        [
            pltpu.VMEM((width, chans), BF),
            pltpu.VMEM((width, rows), BF),
            pltpu.SemaphoreType.DMA((2,)),
        ],
        16,
        (1 << 20, 1 << 20),
    )(in_hbm(mix_t), in_hbm(cotangent.T))

    pks = [pk]
    for bit in reversed(range(n_chan.bit_length() - 1)):
        ready = [pks[0]] + [lax.optimization_barrier((p, letters, mixl, cot))[0] for p in pks[1:]]
        moved = [flip_bits(p, "chan", 1 << bit) for p in ready]
        pks = [q for pair in zip(pks, moved) for q in pair]

    hot_t, hot, hot1 = call(
        functools.partial(prep_kernel, n_seq, rows),
        [SMEM, VMEM],
        [shape((padded, 4 * JB), BF), shape((2 * JB, padded), BF), shape((2 * JB, rows), BF)],
        [VMEM] * 3,
        [],
        16,
        (1 << 20, 1 << 20),
    )(dilations, letters)

    rows_ext = shape((ext, LANE), F32)
    x2, near, far, s1, stack, table, table_r, *strands = call(
        functools.partial(forward_kernel, n_chan, rows, width, scale),
        [SMEM] + [VMEM] * (n_chan + 3),
        [
            shape((width, rows), BF),
            shape((width // 2, chans), BF),
            shape((width // 2, chans), BF),
            shape((rows, width), BF),
            shape((4 * JB, chans), BF),
            shape((TABLE, chans), BF),
            shape((TABLE, chans), BF),
        ]
        + [rows_ext] * (4 * tiles),
        [HBM] + [VMEM] * (6 + 4 * tiles),
        [
            pltpu.VMEM((4 * JB, chans), BF),
            pltpu.VMEM((4 * JB, chans), BF),
            pltpu.VMEM((rows, chans), BF),
            pltpu.VMEM((width, rows), BF),
            pltpu.SemaphoreType.DMA,
        ],
        32,
        (3 << 30, 8 << 20),
    )(dilations, *pks, hot_t, mixl, cot)

    arrived = flip_bits(far, "seq", 1)
    pb, gt, plain, other = call(
        functools.partial(backward_kernel, n_chan, rows, width, scale),
        [SMEM] + [VMEM] * (6 + 4 * tiles),
        [
            shape((rows, chans), BF),
            shape((2, 8, chans), F32),
            shape((2 * JB, chans), F32),
            shape((2 * JB, chans), F32),
        ],
        [VMEM] * 4,
        [pltpu.VMEM((rows + 2 * edge, LANE), F32)] * tiles
        + [pltpu.VMEM((padded, 2 * LANE), BF)] * tiles
        + [pltpu.VMEM((own_tiles, ext, LANE), F32)],
        40,
        (3 << 30, 8 << 20),
    )(dilations, hot, mixl, cot, s1, table, table_r, *strands)

    def rounded_sum(a, b):
        return lax.optimization_barrier((a.astype(F32) + b.astype(F32)).astype(BF))

    g_mine = rounded_sum(near, lax.optimization_barrier((arrived, plain))[0])
    gt = lax.optimization_barrier((gt, g_mine))[0]
    keep, send = call(
        functools.partial(collect_kernel, n_chan, width, scale),
        [VMEM] * (n_chan + 8),
        [shape((n_chan // 2, SUMS, width), F32)] * 2,
        [VMEM] * 2,
        [
            pltpu.VMEM((2 * JB, chans), F32),
            pltpu.VMEM((2 * JB, chans), F32),
            pltpu.VMEM((2 * JB, chans), F32),
            pltpu.VMEM((24, chans), F32),
        ],
        24,
        (1 << 20, 1 << 16),
    )(*pks, hot1, cot, table, table_r, pb, gt, plain, other)

    for bit in range(1, seq_bits):
        g_mine = rounded_sum(g_mine, flip_bits(g_mine, "seq", 1 << bit))
    g_other = flip_bits(g_mine, "seq", 1)
    last = n_chan.bit_length() - 2
    mine, theirs = keep, flip_bits(send, "chan", 1)
    for bit in range(1, last):
        mine = mine + theirs
        mine, theirs = mine[0::2], flip_bits(mine[1::2], "chan", 1 << bit)
    s_mine = call(
        add_kernel,
        [VMEM] * 2,
        [shape((SUMS, width), F32)] * 2,
        [VMEM] * 2,
        [],
        8,
        (0, 0),
    )(mine, theirs)
    across = flip_bits(s_mine[1], "chan", 1 << last)
    along = flip_bits(s_mine[0], "seq", 1)
    places = [(i, j) for i in range(n_seq) for j in range(n_chan)]
    pairs = [(i * n_chan + j, (i ^ 1) * n_chan + (j ^ (1 << last))) for i, j in places]
    corner = lax.ppermute(s_mine[1], ("seq", "chan"), pairs)
    s_mine = (s_mine[0] + across) + (along + corner)
    for bit in range(1, seq_bits):
        s_other = flip_bits(s_mine, "seq", 1 << bit)
        if bit < seq_bits - 1:
            s_mine = s_mine + s_other

    big = pltpu.VMEM((width, chans), F32)
    (grad_mix,) = call(
        functools.partial(mix1_kernel, n_chan, width),
        [VMEM, VMEM],
        [shape((BLOCKS, width, chans), F32)],
        [HBM],
        [big, pltpu.SemaphoreType.DMA],
        16,
        (1 << 20, 1 << 21),
    )(g_mine, g_other)
    grad_mix, grad_taps, grad_embed = call(
        functools.partial(finish_kernel, n_chan, width),
        [VMEM, VMEM, VMEM, HBM],
        [
            shape((BLOCKS, width, chans), F32),
            shape((TAPS, BLOCKS, width), F32),
            shape((BASES, width), F32),
        ],
        [HBM, VMEM, VMEM],
        [big, pltpu.SemaphoreType.DMA((chans // (2 * LANE),))],
        16,
        (1 << 24, 1 << 21),
        {3: 0},
    )(stack, s_mine, s_other, grad_mix)
    return x2.T, jnp.swapaxes(grad_mix, 1, 2), jnp.swapaxes(grad_taps, 0, 1), grad_embed


def solution(mesh):
    in_specs = (
        P(("groups", "seq")),
        P(("groups", "seq"), "chan"),
        P(None, "chan"),
        P(None, None, "chan"),
        P(None, None, "chan"),
        P(),
    )
    out_specs = (
        P(("groups", "seq"), "chan"),
        P("groups", None, "chan"),
        P("groups", None, "chan"),
        P("groups", "chan"),
    )
    return jax.shard_map(body, mesh=mesh, in_specs=in_specs, out_specs=out_specs, check_vma=False)
```

```python
import functools
import math

import jax
import jax.numpy as jnp
from jax import lax
from jax.experimental import pallas as pl
from jax.experimental.pallas import tpu as pltpu
from jax.sharding import PartitionSpec as P

TAPS = 5
BASES = 4
BLOCKS = 2
DMAX = 8
HALF = TAPS // 2
REACH = HALF * DMAX
LANE = 128
JB = 32
GELU_SCALE = math.sqrt(2.0 / math.pi)
CUBIC = 0.044715
BF = jnp.bfloat16
F32 = jnp.float32
ROW_EMBED, ROW_TAPS0, ROW_TAPS1, TABLE = 0, BASES, BASES + TAPS, 16
ROW_GE, ROW_R, ROW_GT0, ROW_GT1, SUMS = 20, 24, 48, 56, 64


def dot(a, b, **kw):
    return jnp.dot(a, b, preferred_element_type=F32, **kw)


def dot_t(a, b):
    return lax.dot_general(a, b, (((1,), (1,)), ((), ())), preferred_element_type=F32)


def t_dot(a, b):
    return lax.dot_general(a, b, (((0,), (0,)), ((), ())), preferred_element_type=F32)


def iotas(shape):
    return lax.broadcasted_iota(jnp.int32, shape, 0), lax.broadcasted_iota(jnp.int32, shape, 1)


def as_bf(mask):
    return mask.astype(F32).astype(BF)


def reversal(size):
    row, col = iotas((size, size))
    return as_bf(row + col == size - 1)


def split_bf(x):
    high = x.astype(BF)
    return high, (x - high.astype(F32)).astype(BF)


def reverse_lanes(parts, rev):
    n = parts[0].shape[1] // LANE
    rows = [p.shape[0] for p in parts]
    pile = [p[:, t * LANE : (t + 1) * LANE] for p in parts for t in range(n)]
    turned = dot(jnp.concatenate(pile, axis=0), rev)
    out, first = [], 0
    for count in rows:
        tiles = [turned[first + t * count : first + (t + 1) * count] for t in range(n)]
        out.append(jnp.concatenate(tiles[::-1], axis=1))
        first += n * count
    return out


def reverse_wide(parts, rev):
    split = [split_bf(p) for p in parts]
    turned = reverse_lanes([q for pair in split for q in pair], rev)
    return [turned[2 * i] + turned[2 * i + 1] for i in range(len(parts))]


def xor_blocks(blocks, me):
    for bit in range(len(blocks).bit_length() - 1):
        swap = lax.bitwise_and(lax.shift_right_logical(me, bit), 1) == 1
        blocks = [jnp.where(swap, blocks[k ^ (1 << bit)], blocks[k]) for k in range(len(blocks))]
    return blocks


def gelu_parts(v):
    square = v * v
    tangent = jnp.tanh(v * (GELU_SCALE + (GELU_SCALE * CUBIC) * square))
    half = 0.5 + 0.5 * tangent
    value = v * half
    slope = half + (v * (1.0 - tangent * tangent)) * (
        0.5 * GELU_SCALE + (1.5 * GELU_SCALE * CUBIC) * square
    )
    return value, slope


def gelu_doubled(half):
    square = half * half
    cubic = (8.0 * GELU_SCALE * CUBIC) * square
    above = 1.0 + jnp.tanh(half * (2.0 * GELU_SCALE + cubic))
    value = half * above
    slope = above + value * ((2.0 - above) * (2.0 * GELU_SCALE + 3.0 * cubic))
    return value, slope


def select_rows(kind, rows):
    row, col = iotas((rows, TABLE))
    local = row % JB
    used = local < TAPS * BASES
    tap, letter = local // BASES, local % BASES
    want = {"tap0": ROW_TAPS0 + tap, "tap1": ROW_TAPS1 + tap, "letter": ROW_EMBED + letter}[kind]
    return as_bf(used & (col == want))


def one_hot_t(tokens):
    n = tokens[0].shape[1]
    inside = tokens[HALF] != 0
    row = lax.broadcasted_iota(jnp.int32, (2 * JB, n), 0)
    local = row % JB
    group = jnp.where(local < TAPS * BASES, local // BASES + TAPS * (row // JB), -1)
    seen = jnp.zeros((2 * JB, n), jnp.int32)
    for g, line in enumerate(tokens):
        line = jnp.where(inside, line, 0)
        seen = jnp.where(group == g, jnp.broadcast_to(line, (2 * JB, n)), seen)
    return (seen == local % BASES + 1).astype(F32)


def pack_kernel(width, mix_ref, embed_ref, taps_ref, tok_ref, out_ref, letters_ref, e_ref, t_ref, sems):
    big = pltpu.make_async_copy(mix_ref.at[0], out_ref.at[pl.ds(0, width)], sems.at[0])
    small = [
        pltpu.make_async_copy(embed_ref, e_ref, sems.at[1]),
        pltpu.make_async_copy(taps_ref, t_ref, sems.at[2]),
        pltpu.make_async_copy(tok_ref, letters_ref.at[0], sems.at[3]),
    ]
    for copy in small + [big]:
        copy.start()
    out_ref[width:, :] = jnp.zeros((TABLE, out_ref.shape[1]), BF)
    for copy in small:
        copy.wait()
    taps = t_ref[...].astype(F32)
    lines = [e_ref[...].astype(F32)]
    lines += [taps[j, block : block + 1, :] for block in range(BLOCKS) for j in range(TAPS)]
    lines.append(jnp.zeros((TABLE - BASES - 2 * TAPS, width), F32))
    out_ref[width:, :width] = jnp.concatenate(lines, axis=0).astype(BF)
    big.wait()


def local_kernel(n_chan, width, mix_ref, cot_ref, mixl_ref, cotl_ref, m_ref, c_ref, sems):
    first = pltpu.make_async_copy(mix_ref.at[1], m_ref, sems.at[0])
    second = pltpu.make_async_copy(cot_ref, c_ref, sems.at[1])
    first.start()
    second.start()
    first.wait()
    blocks = [m_ref[:, k * width : (k + 1) * width] for k in range(n_chan)]
    for k, block in enumerate(xor_blocks(blocks, lax.axis_index("chan"))):
        mixl_ref[:, k * width : (k + 1) * width] = block
    second.wait()
    cotl_ref[...] = c_ref[...].astype(F32).T.astype(BF)


def prep_kernel(n_seq, rows, dils, tok_ref, a_ref, hot_ref, hot1_ref):
    place = lax.axis_index("seq")

    def line(block):
        inside = jnp.logical_and(block >= 0, block < n_seq)
        safe = jnp.clip(block, 0, n_seq - 1)
        letters = tok_ref[pl.ds(lax.bitwise_xor(safe, place), 1), :] + 1
        return jnp.where(inside, letters, 0)

    def around(block):
        lines = [line(block - 1)[:, rows - LANE :], line(block), line(block + 1)[:, :LANE]]
        return jnp.concatenate(lines, axis=1)

    total = rows + 2 * LANE
    this = jnp.broadcast_to(around(place), (8, total))
    mirror = jnp.broadcast_to(around(n_seq - 1 - place), (8, total)).astype(F32).astype(BF)
    rev, n_tiles = reversal(LANE), total // LANE
    other = jnp.concatenate(
        [dot(mirror[:, t * LANE : (t + 1) * LANE], rev) for t in reversed(range(n_tiles))], axis=1
    ).astype(jnp.int32)

    def windows(dilation, margin, count):
        out = []
        for strand, source in ((1, this), (-1, other)):
            for j in range(TAPS):
                first = LANE - margin + strand * (j - HALF) * dilation
                out.append(pltpu.roll(source, total - first, 1)[:1, :count])
        return out

    hot = one_hot_t(windows(dils[0], REACH, a_ref.shape[0]))
    a_ref[...] = jnp.concatenate([hot, hot], axis=0).T.astype(BF)
    hot_ref[...] = hot.astype(BF)
    hot1_ref[...] = one_hot_t(windows(dils[1], 0, rows)).astype(BF)


def forward_kernel(n_chan, rows, width, scale, dils, *refs):
    tiles = n_chan * width // LANE
    pks, refs = refs[:n_chan], refs[n_chan:]
    (a_ref, mixl_ref, cot_ref), refs = refs[:3], refs[3:]
    (x2_ref, near_ref, far_ref, s_ref, st_ref, e_ref, et_ref), refs = refs[:7], refs[7:]
    x1_refs, refs = (refs[:tiles], refs[tiles : 2 * tiles]), refs[2 * tiles :]
    gp_refs, refs = (refs[:tiles], refs[tiles : 2 * tiles]), refs[2 * tiles :]
    w_ref, b_ref, m_ref, held, sem = refs
    chans = n_chan * width
    ext = rows + 2 * REACH
    me, dil = lax.axis_index("chan"), dils[1]
    rev = reversal(LANE)
    blocks = [slice(k * width, (k + 1) * width) for k in range(n_chan)]

    for k in range(n_chan):
        e_ref[:, blocks[k]] = pks[k][width:, :width]
    table = e_ref[...]
    plain = dot(select_rows("tap0", JB), table) * dot(select_rows("letter", JB), table)
    high, low = split_bf(plain)
    turned, turned_low, table_r = reverse_lanes([high, low, table], rev)
    et_ref[...] = table_r.astype(BF)
    b_ref[...] = jnp.concatenate([high, turned.astype(BF), low, turned_low.astype(BF)], axis=0)
    for k, block in enumerate(xor_blocks([b_ref[:, lanes] for lanes in blocks], me)):
        st_ref[:, blocks[k]] = block
    for k in range(n_chan):
        total = 0.5 * dot_t(st_ref[...], pks[k][:width, :])
        high, low = split_bf(total[: 2 * JB] + total[2 * JB :])
        w_ref[:, blocks[k]] = jnp.concatenate([high, low], axis=0)
    weights = w_ref[...]
    (swapped,) = reverse_lanes([weights], rev)
    order = [swapped[JB : 2 * JB], swapped[:JB], swapped[3 * JB :], swapped[2 * JB : 3 * JB]]
    weights_r = jnp.concatenate(order, axis=0).astype(BF)

    table, table_r = table.astype(F32), et_ref[...].astype(F32)
    centre = HALF * BASES
    keep = lax.broadcasted_iota(jnp.int32, (8, chans), 0) < BASES

    def lookup(source, first):
        lines = jnp.where(keep, source[:8], 0.0)
        above, below = jnp.zeros((first, chans), F32), jnp.zeros((4 * JB - first - 8, chans), F32)
        return jnp.concatenate([above, lines, below], axis=0).astype(BF)

    look, look_r = lookup(table, centre), lookup(table_r, JB + centre)
    chunk, mchunk = ext // 5, rows // 6
    for t in range(tiles):
        dst = slice(t * LANE, (t + 1) * LANE)
        for strand, (wr, er) in enumerate(((weights, look), (weights_r, look_r))):
            rhs = jnp.concatenate([wr[:, dst], er[:, dst]], axis=1)
            for i in range(5):
                where = pl.ds(i * chunk, chunk)
                both = dot(a_ref[where, :], rhs)
                value, slope = gelu_doubled(both[:, :LANE])
                x1_refs[strand][t][where, :] = both[:, LANE:] + value
                gp_refs[strand][t][where, :] = slope

        for i in range(6):
            first = i * mchunk
            terms = []
            for j in range(TAPS):
                shift = (j - HALF) * dil
                line = slice(ROW_TAPS1 + j, ROW_TAPS1 + j + 1)
                terms.append(table[line, dst] * x1_refs[0][t][pl.ds(first + REACH + shift, mchunk), :])
                terms.append(table_r[line, dst] * x1_refs[1][t][pl.ds(first + REACH - shift, mchunk), :])
            m_ref[first : first + mchunk, dst] = functools.reduce(jnp.add, terms).astype(BF)

    half = rows // 2
    n_own = pl.cdiv(width, LANE)
    for i in range(2):
        where = pl.ds(i * half, half)
        value, slope = gelu_parts(dot_t(m_ref[where, :], mixl_ref[...]))
        inner = pl.ds(REACH + i * half, half)
        own = jnp.concatenate([x1_refs[0][t][inner, :] for t in range(n_own)], axis=1)[:, :width]
        held[:, where] = (own + value).T.astype(BF)
        s_ref[where, :] = ((cot_ref[where, :].astype(F32) * scale) * slope).astype(BF)
    copy = pltpu.make_async_copy(held, x2_ref, sem)
    copy.start()

    part = t_dot(s_ref[...], m_ref[...]).astype(BF)
    odd = lax.axis_index("seq") % 2 == 1
    near_ref[...] = jnp.where(odd, part[width // 2 :], part[: width // 2])
    far_ref[...] = jnp.where(odd, part[: width // 2], part[width // 2 :])
    copy.wait()


def backward_kernel(n_chan, rows, width, scale, dils, *refs):
    tiles = n_chan * width // LANE
    (hot_ref, mixl_ref, cot_ref, s_ref, e_ref, et_ref), refs = refs[:6], refs[6:]
    x1_refs, refs = (refs[:tiles], refs[tiles : 2 * tiles]), refs[2 * tiles :]
    gp_refs, refs = (refs[:tiles], refs[tiles : 2 * tiles]), refs[2 * tiles :]
    (pb_ref, gt_ref, plain_ref, other_ref), refs = refs[:4], refs[4:]
    p_refs, s0_refs, (g2_ref,) = refs[:tiles], refs[tiles : 2 * tiles], refs[2 * tiles :]
    ext = rows + 2 * REACH
    padded = hot_ref.shape[1]
    dil = dils[1]
    taps_f, taps_r = 0.5 * e_ref[...].astype(F32), 0.5 * et_ref[...].astype(F32)

    edge = 2 * REACH
    n_own = pl.cdiv(width, LANE)
    g2 = cot_ref[...].astype(F32) * scale
    g2_ref[:, :REACH, :] = jnp.zeros((n_own, REACH, LANE), F32)
    g2_ref[:, rows + REACH :, :] = jnp.zeros((n_own, REACH, LANE), F32)
    g2 = jnp.concatenate([g2, jnp.zeros((rows, n_own * LANE - width), F32)], axis=1)
    for t in range(n_own):
        g2_ref[t, REACH : rows + REACH, :] = 0.5 * g2[:, t * LANE : (t + 1) * LANE]

    mchunk, chunk = rows // 6, ext // 5
    for t in range(tiles):
        dst = slice(t * LANE, (t + 1) * LANE)
        p_ref, s0_ref = p_refs[t], s0_refs[t]
        if t % 2 == 0:
            pair = dot(s_ref[...], mixl_ref[:, t * LANE : (t + 2) * LANE])
            pb_ref[:, t * LANE : (t + 2) * LANE] = pair.astype(BF)
        p_ref[:edge, :] = jnp.zeros((edge, LANE), F32)
        p_ref[rows + edge :, :] = jnp.zeros((edge, LANE), F32)
        p_ref[edge : rows + edge, :] = pair[:, (t % 2) * LANE : (t % 2 + 1) * LANE]
        s0_ref[ext:, :] = jnp.zeros((padded - ext, 2 * LANE), BF)
        for i in range(5):
            first = i * chunk
            where = pl.ds(first, chunk)
            fs, rs = [], []
            for j in range(TAPS):
                window = p_ref[pl.ds(first + REACH + (j - HALF) * dil, chunk), :]
                ahead, back = ROW_TAPS1 + j, ROW_TAPS1 + TAPS - 1 - j
                fs.append(taps_f[back : back + 1, dst] * window)
                rs.append(taps_r[ahead : ahead + 1, dst] * window)
            if t < n_own:
                fs.append(g2_ref[t, where, :])
            f, r = functools.reduce(jnp.add, fs), functools.reduce(jnp.add, rs)
            s0_ref[where, :LANE] = (f * gp_refs[0][t][where, :]).astype(BF)
            s0_ref[where, LANE:] = (r * gp_refs[1][t][where, :]).astype(BF)
        both = dot(hot_ref[...], s0_ref[...])
        plain_ref[:, dst], other_ref[:, dst] = both[:, :LANE], both[:, LANE:]

        sums = [None] * (2 * TAPS)
        for i in range(6):
            first = i * mchunk
            here = p_ref[pl.ds(edge + first, mchunk), :]
            for strand in range(2):
                for j in range(TAPS):
                    shift = (j - HALF) * dil * (1 - 2 * strand)
                    prod = here * x1_refs[strand][t][pl.ds(first + REACH + shift, mchunk), :]
                    part = prod.reshape(mchunk // 8, 8, LANE).sum(0)
                    slot = strand * TAPS + j
                    sums[slot] = part if i == 0 else sums[slot] + part
        for strand in range(2):
            lines = [jnp.sum(sums[strand * TAPS + j], axis=0, keepdims=True) for j in range(TAPS)]
            gt_ref[strand, :, dst] = jnp.concatenate(lines + [jnp.zeros((8 - TAPS, LANE), F32)], axis=0)


def collect_kernel(n_chan, width, scale, *refs):
    pks, refs = refs[:n_chan], refs[n_chan:]
    hot1_ref, cot_ref, e_ref, et_ref, pb_ref, gt_ref, plain_ref, other_ref = refs[:8]
    keep_ref, send_ref, dw_ref, st_ref, back_ref, tail_ref = refs[8:]
    chans = n_chan * width
    me, rev = lax.axis_index("chan"), reversal(LANE)
    blocks = [slice(k * width, (k + 1) * width) for k in range(n_chan)]
    table, table_r = e_ref[...], et_ref[...]

    by_tap = dot(hot1_ref[...], pb_ref[...])
    own_letters = dot(hot1_ref[:16, :], cot_ref[...]) * scale
    srow, scol = iotas((8, JB))
    sum_letter = as_bf((scol % BASES == srow) & (scol < TAPS * BASES))
    sum_tap = as_bf((scol // BASES == srow) & (scol < TAPS * BASES))

    def sums_of(sel, x):
        high, rest = split_bf(x)
        return dot(sel, high) + dot(sel, rest)

    sel1 = select_rows("tap1", JB)
    ahead = by_tap[:JB] * dot(sel1, table)
    other = by_tap[JB:] * dot(sel1, table_r)
    turned, other, taps_turned = reverse_wide([other_ref[...], other, gt_ref[1]], rev)
    sums = plain_ref[...] + jnp.concatenate([turned[JB:], turned[:JB]], axis=0)
    dw_ref[...] = sums
    letters = sums_of(sum_letter, ahead + other)
    tail_ref[8:16, :] = gt_ref[0] + taps_turned

    total = jnp.zeros((2 * JB, chans), F32)
    for k in range(n_chan):
        total = total + dot(dw_ref[:, blocks[k]].astype(BF), pks[k][:width, :])
    st_ref[...] = total
    for k, block in enumerate(xor_blocks([st_ref[:, lanes] for lanes in blocks], me)):
        back_ref[:, blocks[k]] = block
    (turned,) = reverse_wide([back_ref[JB:, :]], rev)
    both = back_ref[:JB, :] + turned
    tail_ref[0:8, :] = sums_of(sum_tap, both * dot(select_rows("letter", JB), table))
    letters = letters + sums_of(sum_letter, both * dot(select_rows("tap0", JB), table))
    tail_ref[16:24, :] = letters
    zeros = jnp.zeros((BASES, width), F32)
    own = jnp.concatenate([own_letters[HALF * BASES : (HALF + 1) * BASES, :], zeros], axis=0)
    for kk, lanes in enumerate(blocks):
        place, at = (keep_ref, send_ref)[kk % 2], kk // 2
        letters = tail_ref[16:24, lanes]
        if kk == 0:
            letters = letters + own
        place[at, :ROW_R, :] = jnp.concatenate([dw_ref[:ROW_GE, lanes], letters[:BASES]], axis=0)
        place[at, ROW_R : 2 * ROW_R, :] = dw_ref[JB : JB + ROW_R, lanes]
        place[at, ROW_GT0:, :] = tail_ref[0:16, lanes]


def add_kernel(a_ref, b_ref, first_ref, second_ref):
    first_ref[...] = (a_ref[0] + b_ref[0]).astype(BF)
    second_ref[...] = (a_ref[1] + b_ref[1]).astype(BF)


def mix1_kernel(n_chan, width, near_ref, far_ref, out_ref, held, sem):
    me, odd = lax.axis_index("chan"), lax.axis_index("seq") % 2
    half = width // 2
    for source, first in ((near_ref, odd * half), (far_ref, (1 - odd) * half)):
        blocks = [source[:, k * width : (k + 1) * width].astype(F32) for k in range(n_chan)]
        for k, part in enumerate(xor_blocks(blocks, me)):
            held[pl.ds(pl.multiple_of(first, half), half), k * width : (k + 1) * width] = part
    copy = pltpu.make_async_copy(held, out_ref.at[1], sem)
    copy.start()
    copy.wait()


def finish_kernel(n_chan, width, st_ref, sa_ref, sb_ref, _, gm_ref, gt_ref, ge_ref, held, sems):
    sums = sa_ref[...].astype(F32) + sb_ref[...].astype(F32)
    fill = jnp.zeros((JB - ROW_GE, width), F32)
    dw = jnp.concatenate([sums[:ROW_GE], fill, sums[ROW_R : ROW_R + ROW_GE], fill], axis=0).astype(BF)
    copies = []
    step = 2 * LANE
    for i in range(n_chan * width // step):
        lanes = pl.ds(i * step, step)
        held[:, lanes] = t_dot(dw, st_ref[: 2 * JB, lanes])
        copies.append(pltpu.make_async_copy(held.at[:, lanes], gm_ref.at[0, :, lanes], sems.at[i]))
        copies[-1].start()
    for j in range(TAPS):
        gt_ref[j, 0:1, :] = sums[ROW_GT0 + j : ROW_GT0 + j + 1]
        gt_ref[j, 1:2, :] = sums[ROW_GT1 + j : ROW_GT1 + j + 1]
    ge_ref[...] = sums[ROW_GE : ROW_GE + BASES]
    for copy in copies:
        copy.wait()


VMEM = pl.BlockSpec(memory_space=pltpu.VMEM)
SMEM = pl.BlockSpec(memory_space=pltpu.SMEM)
HBM = pl.BlockSpec(memory_space=pltpu.HBM)


def in_hbm(x):
    return pltpu.with_memory_space_constraint(x, pltpu.HBM)


def call(kernel, in_specs, out_shape, out_specs, scratch, limit, cost, aliases=None):
    flops, moved = cost
    return pl.pallas_call(
        kernel,
        out_shape=out_shape,
        in_specs=in_specs,
        out_specs=out_specs,
        scratch_shapes=scratch,
        input_output_aliases=aliases or {},
        compiler_params=pltpu.CompilerParams(vmem_limit_bytes=limit << 20),
        cost_estimate=pl.CostEstimate(flops=flops, bytes_accessed=moved, transcendentals=0),
    )


def flip_bits(x, axis, mask):
    return lax.ppermute(x, axis, [(i, i ^ mask) for i in range(lax.axis_size(axis))])


def body(tokens, cotangent, embed, taps, mix, dilations):
    rows, width = cotangent.shape
    n_seq, n_chan = lax.axis_size("seq"), lax.axis_size("chan")
    chans = n_chan * width
    tiles = chans // LANE
    ext = rows + 2 * REACH
    padded = pl.cdiv(ext, LANE) * LANE
    edge = 2 * REACH
    own_tiles = pl.cdiv(width, LANE)
    scale = 1.0 / math.sqrt(rows * n_seq)
    shape = jax.ShapeDtypeStruct
    mix_t = jnp.swapaxes(mix, 1, 2)

    pk, letters = call(
        functools.partial(pack_kernel, width),
        [HBM] * 4,
        [shape((width + TABLE, chans), BF), shape((1, rows), jnp.int32)],
        [VMEM] * 2,
        [
            pltpu.VMEM((BASES, width), BF),
            pltpu.VMEM((TAPS, BLOCKS, width), BF),
            pltpu.SemaphoreType.DMA((4,)),
        ],
        8,
        (0, width * chans * 4),
    )(in_hbm(mix_t), in_hbm(embed), in_hbm(jnp.swapaxes(taps, 0, 1)), in_hbm(tokens))

    seq_bits = n_seq.bit_length() - 1
    for bit in range(0, seq_bits, 2):
        masks = [k << bit for k in range(1, 1 << min(2, seq_bits - bit))]
        letters = jnp.concatenate([letters] + [flip_bits(letters, "seq", m) for m in masks], axis=0)

    mixl, cot = call(
        functools.partial(local_kernel, n_chan, width),
        [HBM, HBM],
        [shape((width, chans), BF), shape((rows, width), BF)],
        [VMEM] * 2,
        [
            pltpu.VMEM((width, chans), BF),
            pltpu.VMEM((width, rows), BF),
            pltpu.SemaphoreType.DMA((2,)),
        ],
        16,
        (1 << 20, 1 << 20),
    )(in_hbm(mix_t), in_hbm(cotangent.T))

    pks = [pk]
    for bit in reversed(range(n_chan.bit_length() - 1)):
        ready = [pks[0]] + [lax.optimization_barrier((p, letters, mixl, cot))[0] for p in pks[1:]]
        moved = [flip_bits(p, "chan", 1 << bit) for p in ready]
        pks = [q for pair in zip(pks, moved) for q in pair]

    hot_t, hot, hot1 = call(
        functools.partial(prep_kernel, n_seq, rows),
        [SMEM, VMEM],
        [shape((padded, 4 * JB), BF), shape((2 * JB, padded), BF), shape((2 * JB, rows), BF)],
        [VMEM] * 3,
        [],
        16,
        (1 << 20, 1 << 20),
    )(dilations, letters)

    rows_ext = shape((ext, LANE), F32)
    x2, near, far, s1, stack, table, table_r, *strands = call(
        functools.partial(forward_kernel, n_chan, rows, width, scale),
        [SMEM] + [VMEM] * (n_chan + 3),
        [
            shape((width, rows), BF),
            shape((width // 2, chans), BF),
            shape((width // 2, chans), BF),
            shape((rows, width), BF),
            shape((4 * JB, chans), BF),
            shape((TABLE, chans), BF),
            shape((TABLE, chans), BF),
        ]
        + [rows_ext] * (4 * tiles),
        [HBM] + [VMEM] * (6 + 4 * tiles),
        [
            pltpu.VMEM((4 * JB, chans), BF),
            pltpu.VMEM((4 * JB, chans), BF),
            pltpu.VMEM((rows, chans), BF),
            pltpu.VMEM((width, rows), BF),
            pltpu.SemaphoreType.DMA,
        ],
        32,
        (3 << 30, 8 << 20),
    )(dilations, *pks, hot_t, mixl, cot)

    arrived = flip_bits(far, "seq", 1)
    pb, gt, plain, other = call(
        functools.partial(backward_kernel, n_chan, rows, width, scale),
        [SMEM] + [VMEM] * (6 + 4 * tiles),
        [
            shape((rows, chans), BF),
            shape((2, 8, chans), F32),
            shape((2 * JB, chans), F32),
            shape((2 * JB, chans), F32),
        ],
        [VMEM] * 4,
        [pltpu.VMEM((rows + 2 * edge, LANE), F32)] * tiles
        + [pltpu.VMEM((padded, 2 * LANE), BF)] * tiles
        + [pltpu.VMEM((own_tiles, ext, LANE), F32)],
        40,
        (3 << 30, 8 << 20),
    )(dilations, hot, mixl, cot, s1, table, table_r, *strands)

    def rounded_sum(a, b):
        return lax.optimization_barrier((a.astype(F32) + b.astype(F32)).astype(BF))

    g_mine = rounded_sum(near, lax.optimization_barrier((arrived, plain))[0])
    gt = lax.optimization_barrier((gt, g_mine))[0]
    keep, send = call(
        functools.partial(collect_kernel, n_chan, width, scale),
        [VMEM] * (n_chan + 8),
        [shape((n_chan // 2, SUMS, width), F32)] * 2,
        [VMEM] * 2,
        [
            pltpu.VMEM((2 * JB, chans), F32),
            pltpu.VMEM((2 * JB, chans), F32),
            pltpu.VMEM((2 * JB, chans), F32),
            pltpu.VMEM((24, chans), F32),
        ],
        24,
        (1 << 20, 1 << 16),
    )(*pks, hot1, cot, table, table_r, pb, gt, plain, other)

    for bit in range(1, seq_bits):
        g_mine = rounded_sum(g_mine, flip_bits(g_mine, "seq", 1 << bit))
    g_other = flip_bits(g_mine, "seq", 1)
    last = n_chan.bit_length() - 2
    mine, theirs = keep, flip_bits(send, "chan", 1)
    for bit in range(1, last):
        mine = mine + theirs
        mine, theirs = mine[0::2], flip_bits(mine[1::2], "chan", 1 << bit)
    s_mine = call(
        add_kernel,
        [VMEM] * 2,
        [shape((SUMS, width), BF)] * 2,
        [VMEM] * 2,
        [],
        8,
        (0, 0),
    )(mine, theirs)
    across = flip_bits(s_mine[1], "chan", 1 << last)
    along = flip_bits(s_mine[0], "seq", 1)
    places = [(i, j) for i in range(n_seq) for j in range(n_chan)]
    pairs = [(i * n_chan + j, (i ^ 1) * n_chan + (j ^ (1 << last))) for i, j in places]
    corner = lax.ppermute(s_mine[1], ("seq", "chan"), pairs)
    here, there = (s_mine[0], across), (along, corner)
    s_mine = rounded_sum(*(a.astype(F32) + b.astype(F32) for a, b in (here, there)))
    for bit in range(1, seq_bits):
        s_other = flip_bits(s_mine, "seq", 1 << bit)
        if bit < seq_bits - 1:
            s_mine = rounded_sum(s_mine, s_other)

    big = pltpu.VMEM((width, chans), F32)
    (grad_mix,) = call(
        functools.partial(mix1_kernel, n_chan, width),
        [VMEM, VMEM],
        [shape((BLOCKS, width, chans), F32)],
        [HBM],
        [big, pltpu.SemaphoreType.DMA],
        16,
        (1 << 20, 1 << 21),
    )(g_mine, g_other)
    grad_mix, grad_taps, grad_embed = call(
        functools.partial(finish_kernel, n_chan, width),
        [VMEM, VMEM, VMEM, HBM],
        [
            shape((BLOCKS, width, chans), F32),
            shape((TAPS, BLOCKS, width), F32),
            shape((BASES, width), F32),
        ],
        [HBM, VMEM, VMEM],
        [big, pltpu.SemaphoreType.DMA((chans // (2 * LANE),))],
        16,
        (1 << 24, 1 << 21),
        {3: 0},
    )(stack, s_mine, s_other, grad_mix)
    return x2.T, jnp.swapaxes(grad_mix, 1, 2), jnp.swapaxes(grad_taps, 0, 1), grad_embed


def solution(mesh):
    in_specs = (
        P(("groups", "seq")),
        P(("groups", "seq"), "chan"),
        P(None, "chan"),
        P(None, None, "chan"),
        P(None, None, "chan"),
        P(),
    )
    out_specs = (
        P(("groups", "seq"), "chan"),
        P("groups", None, "chan"),
        P("groups", None, "chan"),
        P("groups", "chan"),
    )
    return jax.shard_map(body, mesh=mesh, in_specs=in_specs, out_specs=out_specs, check_vma=False)
```

```python
import functools
import math

import jax
import jax.numpy as jnp
from jax import lax
from jax.experimental import pallas as pl
from jax.experimental.pallas import tpu as pltpu
from jax.sharding import PartitionSpec as P

TAPS = 5
BASES = 4
BLOCKS = 2
DMAX = 8
HALF = TAPS // 2
REACH = HALF * DMAX
LANE = 128
JB = 32
GELU_SCALE = math.sqrt(2.0 / math.pi)
CUBIC = 0.044715
BF = jnp.bfloat16
F32 = jnp.float32
ROW_EMBED, ROW_TAPS0, ROW_TAPS1, TABLE = 0, BASES, BASES + TAPS, 16
ROW_GE, ROW_R, ROW_GT0, ROW_GT1, SUMS = 20, 24, 48, 56, 64


def dot(a, b, **kw):
    return jnp.dot(a, b, preferred_element_type=F32, **kw)


def dot_t(a, b):
    return lax.dot_general(a, b, (((1,), (1,)), ((), ())), preferred_element_type=F32)


def t_dot(a, b):
    return lax.dot_general(a, b, (((0,), (0,)), ((), ())), preferred_element_type=F32)


def iotas(shape):
    return lax.broadcasted_iota(jnp.int32, shape, 0), lax.broadcasted_iota(jnp.int32, shape, 1)


def as_bf(mask):
    return mask.astype(F32).astype(BF)


def reversal(size):
    row, col = iotas((size, size))
    return as_bf(row + col == size - 1)


def split_bf(x):
    high = x.astype(BF)
    return high, (x - high.astype(F32)).astype(BF)


def reverse_lanes(parts, rev):
    n = parts[0].shape[1] // LANE
    rows = [p.shape[0] for p in parts]
    pile = [p[:, t * LANE : (t + 1) * LANE] for p in parts for t in range(n)]
    turned = dot(jnp.concatenate(pile, axis=0), rev)
    out, first = [], 0
    for count in rows:
        tiles = [turned[first + t * count : first + (t + 1) * count] for t in range(n)]
        out.append(jnp.concatenate(tiles[::-1], axis=1))
        first += n * count
    return out


def reverse_wide(parts, rev):
    split = [split_bf(p) for p in parts]
    turned = reverse_lanes([q for pair in split for q in pair], rev)
    return [turned[2 * i] + turned[2 * i + 1] for i in range(len(parts))]


def xor_blocks(blocks, me):
    for bit in range(len(blocks).bit_length() - 1):
        swap = lax.bitwise_and(lax.shift_right_logical(me, bit), 1) == 1
        blocks = [jnp.where(swap, blocks[k ^ (1 << bit)], blocks[k]) for k in range(len(blocks))]
    return blocks


def gelu_parts(v):
    square = v * v
    tangent = jnp.tanh(v * (GELU_SCALE + (GELU_SCALE * CUBIC) * square))
    half = 0.5 + 0.5 * tangent
    value = v * half
    slope = half + (v * (1.0 - tangent * tangent)) * (
        0.5 * GELU_SCALE + (1.5 * GELU_SCALE * CUBIC) * square
    )
    return value, slope


def gelu_doubled(half):
    square = half * half
    cubic = (8.0 * GELU_SCALE * CUBIC) * square
    above = 1.0 + jnp.tanh(half * (2.0 * GELU_SCALE + cubic))
    value = half * above
    slope = above + value * ((2.0 - above) * (2.0 * GELU_SCALE + 3.0 * cubic))
    return value, slope


def select_rows(kind, rows):
    row, col = iotas((rows, TABLE))
    local = row % JB
    used = local < TAPS * BASES
    tap, letter = local // BASES, local % BASES
    want = {"tap0": ROW_TAPS0 + tap, "tap1": ROW_TAPS1 + tap, "letter": ROW_EMBED + letter}[kind]
    return as_bf(used & (col == want))


def one_hot_t(tokens):
    n = tokens[0].shape[1]
    inside = tokens[HALF] != 0
    row = lax.broadcasted_iota(jnp.int32, (2 * JB, n), 0)
    local = row % JB
    group = jnp.where(local < TAPS * BASES, local // BASES + TAPS * (row // JB), -1)
    seen = jnp.zeros((2 * JB, n), jnp.int32)
    for g, line in enumerate(tokens):
        line = jnp.where(inside, line, 0)
        seen = jnp.where(group == g, jnp.broadcast_to(line, (2 * JB, n)), seen)
    return (seen == local % BASES + 1).astype(F32)


def pack_kernel(width, mix_ref, embed_ref, taps_ref, tok_ref, out_ref, letters_ref, e_ref, t_ref, sems):
    big = pltpu.make_async_copy(mix_ref.at[0], out_ref.at[pl.ds(0, width)], sems.at[0])
    small = [
        pltpu.make_async_copy(embed_ref, e_ref, sems.at[1]),
        pltpu.make_async_copy(taps_ref, t_ref, sems.at[2]),
        pltpu.make_async_copy(tok_ref, letters_ref.at[0], sems.at[3]),
    ]
    for copy in small + [big]:
        copy.start()
    out_ref[width:, :] = jnp.zeros((TABLE, out_ref.shape[1]), BF)
    for copy in small:
        copy.wait()
    taps = t_ref[...].astype(F32)
    lines = [e_ref[...].astype(F32)]
    lines += [taps[j, block : block + 1, :] for block in range(BLOCKS) for j in range(TAPS)]
    lines.append(jnp.zeros((TABLE - BASES - 2 * TAPS, width), F32))
    out_ref[width:, :width] = jnp.concatenate(lines, axis=0).astype(BF)
    big.wait()


def local_kernel(n_chan, width, mix_ref, cot_ref, mixl_ref, cotl_ref, m_ref, c_ref, sems):
    first = pltpu.make_async_copy(mix_ref.at[1], m_ref, sems.at[0])
    second = pltpu.make_async_copy(cot_ref, c_ref, sems.at[1])
    first.start()
    second.start()
    first.wait()
    blocks = [m_ref[:, k * width : (k + 1) * width] for k in range(n_chan)]
    for k, block in enumerate(xor_blocks(blocks, lax.axis_index("chan"))):
        mixl_ref[:, k * width : (k + 1) * width] = block
    second.wait()
    cotl_ref[...] = c_ref[...].astype(F32).T.astype(BF)


def prep_kernel(n_seq, rows, dils, tok_ref, a_ref, hot_ref, hot1_ref):
    place = lax.axis_index("seq")

    def line(block):
        inside = jnp.logical_and(block >= 0, block < n_seq)
        safe = jnp.clip(block, 0, n_seq - 1)
        letters = tok_ref[pl.ds(lax.bitwise_xor(safe, place), 1), :] + 1
        return jnp.where(inside, letters, 0)

    def around(block):
        lines = [line(block - 1)[:, rows - LANE :], line(block), line(block + 1)[:, :LANE]]
        return jnp.concatenate(lines, axis=1)

    total = rows + 2 * LANE
    this = jnp.broadcast_to(around(place), (8, total))
    mirror = jnp.broadcast_to(around(n_seq - 1 - place), (8, total)).astype(F32).astype(BF)
    rev, n_tiles = reversal(LANE), total // LANE
    other = jnp.concatenate(
        [dot(mirror[:, t * LANE : (t + 1) * LANE], rev) for t in reversed(range(n_tiles))], axis=1
    ).astype(jnp.int32)

    def windows(dilation, margin, count):
        out = []
        for strand, source in ((1, this), (-1, other)):
            for j in range(TAPS):
                first = LANE - margin + strand * (j - HALF) * dilation
                out.append(pltpu.roll(source, total - first, 1)[:1, :count])
        return out

    hot = one_hot_t(windows(dils[0], REACH, a_ref.shape[0]))
    a_ref[...] = jnp.concatenate([hot, hot], axis=0).T.astype(BF)
    hot_ref[...] = hot.astype(BF)
    hot1_ref[...] = one_hot_t(windows(dils[1], 0, rows)).astype(BF)


def forward_kernel(n_chan, rows, width, scale, dils, *refs):
    tiles = n_chan * width // LANE
    pks, refs = refs[:n_chan], refs[n_chan:]
    (a_ref, mixl_ref, cot_ref), refs = refs[:3], refs[3:]
    (x2_ref, near_ref, far_ref, s_ref, st_ref, e_ref, et_ref), refs = refs[:7], refs[7:]
    x1_refs, refs = (refs[:tiles], refs[tiles : 2 * tiles]), refs[2 * tiles :]
    gp_refs, refs = (refs[:tiles], refs[tiles : 2 * tiles]), refs[2 * tiles :]
    w_ref, b_ref, m_ref, held, sem = refs
    chans = n_chan * width
    ext = rows + 2 * REACH
    me, dil = lax.axis_index("chan"), dils[1]
    rev = reversal(LANE)
    blocks = [slice(k * width, (k + 1) * width) for k in range(n_chan)]

    for k in range(n_chan):
        e_ref[:, blocks[k]] = pks[k][width:, :width]
    table = e_ref[...]
    plain = dot(select_rows("tap0", JB), table) * dot(select_rows("letter", JB), table)
    high, low = split_bf(plain)
    turned, turned_low, table_r = reverse_lanes([high, low, table], rev)
    et_ref[...] = table_r.astype(BF)
    b_ref[...] = jnp.concatenate([high, turned.astype(BF), low, turned_low.astype(BF)], axis=0)
    for k, block in enumerate(xor_blocks([b_ref[:, lanes] for lanes in blocks], me)):
        st_ref[:, blocks[k]] = block
    for k in range(n_chan):
        total = 0.5 * dot_t(st_ref[...], pks[k][:width, :])
        high, low = split_bf(total[: 2 * JB] + total[2 * JB :])
        w_ref[:, blocks[k]] = jnp.concatenate([high, low], axis=0)
    weights = w_ref[...]
    (swapped,) = reverse_lanes([weights], rev)
    order = [swapped[JB : 2 * JB], swapped[:JB], swapped[3 * JB :], swapped[2 * JB : 3 * JB]]
    weights_r = jnp.concatenate(order, axis=0).astype(BF)

    table, table_r = table.astype(F32), et_ref[...].astype(F32)
    centre = HALF * BASES
    keep = lax.broadcasted_iota(jnp.int32, (8, chans), 0) < BASES

    def lookup(source, first):
        lines = jnp.where(keep, source[:8], 0.0)
        above, below = jnp.zeros((first, chans), F32), jnp.zeros((4 * JB - first - 8, chans), F32)
        return jnp.concatenate([above, lines, below], axis=0).astype(BF)

    look, look_r = lookup(table, centre), lookup(table_r, JB + centre)
    chunk, mchunk = ext // 5, rows // 6
    for t in range(tiles):
        dst = slice(t * LANE, (t + 1) * LANE)
        for strand, (wr, er) in enumerate(((weights, look), (weights_r, look_r))):
            rhs = jnp.concatenate([wr[:, dst], er[:, dst]], axis=1)
            for i in range(5):
                where = pl.ds(i * chunk, chunk)
                both = dot(a_ref[where, :], rhs)
                value, slope = gelu_doubled(both[:, :LANE])
                x1_refs[strand][t][where, :] = both[:, LANE:] + value
                gp_refs[strand][t][where, :] = slope

        for i in range(6):
            first = i * mchunk
            terms = []
            for j in range(TAPS):
                shift = (j - HALF) * dil
                line = slice(ROW_TAPS1 + j, ROW_TAPS1 + j + 1)
                terms.append(table[line, dst] * x1_refs[0][t][pl.ds(first + REACH + shift, mchunk), :])
                terms.append(table_r[line, dst] * x1_refs[1][t][pl.ds(first + REACH - shift, mchunk), :])
            m_ref[first : first + mchunk, dst] = functools.reduce(jnp.add, terms).astype(BF)

    half = rows // 2
    n_own = pl.cdiv(width, LANE)
    for i in range(2):
        where = pl.ds(i * half, half)
        value, slope = gelu_parts(dot_t(m_ref[where, :], mixl_ref[...]))
        inner = pl.ds(REACH + i * half, half)
        own = jnp.concatenate([x1_refs[0][t][inner, :] for t in range(n_own)], axis=1)[:, :width]
        held[:, where] = (own + value).T.astype(BF)
        s_ref[where, :] = ((cot_ref[where, :].astype(F32) * scale) * slope).astype(BF)
    copy = pltpu.make_async_copy(held, x2_ref, sem)
    copy.start()

    part = t_dot(s_ref[...], m_ref[...]).astype(BF)
    odd = lax.axis_index("seq") % 2 == 1
    near_ref[...] = jnp.where(odd, part[width // 2 :], part[: width // 2])
    far_ref[...] = jnp.where(odd, part[: width // 2], part[width // 2 :])
    copy.wait()


def backward_kernel(n_chan, rows, width, scale, dils, *refs):
    tiles = n_chan * width // LANE
    (hot_ref, mixl_ref, cot_ref, s_ref, e_ref, et_ref), refs = refs[:6], refs[6:]
    x1_refs, refs = (refs[:tiles], refs[tiles : 2 * tiles]), refs[2 * tiles :]
    gp_refs, refs = (refs[:tiles], refs[tiles : 2 * tiles]), refs[2 * tiles :]
    (pb_ref, gt_ref, plain_ref, other_ref), refs = refs[:4], refs[4:]
    p_refs, s0_refs, (g2_ref,) = refs[:tiles], refs[tiles : 2 * tiles], refs[2 * tiles :]
    ext = rows + 2 * REACH
    padded = hot_ref.shape[1]
    dil = dils[1]
    taps_f, taps_r = 0.5 * e_ref[...].astype(F32), 0.5 * et_ref[...].astype(F32)

    edge = 2 * REACH
    n_own = pl.cdiv(width, LANE)
    g2 = cot_ref[...].astype(F32) * scale
    g2_ref[:, :REACH, :] = jnp.zeros((n_own, REACH, LANE), F32)
    g2_ref[:, rows + REACH :, :] = jnp.zeros((n_own, REACH, LANE), F32)
    g2 = jnp.concatenate([g2, jnp.zeros((rows, n_own * LANE - width), F32)], axis=1)
    for t in range(n_own):
        g2_ref[t, REACH : rows + REACH, :] = 0.5 * g2[:, t * LANE : (t + 1) * LANE]

    mchunk, chunk = rows // 6, ext // 5
    for t in range(tiles):
        dst = slice(t * LANE, (t + 1) * LANE)
        p_ref, s0_ref = p_refs[t], s0_refs[t]
        if t % 2 == 0:
            pair = dot(s_ref[...], mixl_ref[:, t * LANE : (t + 2) * LANE])
            pb_ref[:, t * LANE : (t + 2) * LANE] = pair.astype(BF)
        p_ref[:edge, :] = jnp.zeros((edge, LANE), F32)
        p_ref[rows + edge :, :] = jnp.zeros((edge, LANE), F32)
        p_ref[edge : rows + edge, :] = pair[:, (t % 2) * LANE : (t % 2 + 1) * LANE]
        s0_ref[ext:, :] = jnp.zeros((padded - ext, 2 * LANE), BF)
        for i in range(5):
            first = i * chunk
            where = pl.ds(first, chunk)
            fs, rs = [], []
            for j in range(TAPS):
                window = p_ref[pl.ds(first + REACH + (j - HALF) * dil, chunk), :]
                ahead, back = ROW_TAPS1 + j, ROW_TAPS1 + TAPS - 1 - j
                fs.append(taps_f[back : back + 1, dst] * window)
                rs.append(taps_r[ahead : ahead + 1, dst] * window)
            if t < n_own:
                fs.append(g2_ref[t, where, :])
            f, r = functools.reduce(jnp.add, fs), functools.reduce(jnp.add, rs)
            s0_ref[where, :LANE] = (f * gp_refs[0][t][where, :]).astype(BF)
            s0_ref[where, LANE:] = (r * gp_refs[1][t][where, :]).astype(BF)
        both = dot(hot_ref[...], s0_ref[...])
        plain_ref[:, dst], other_ref[:, dst] = both[:, :LANE], both[:, LANE:]

        sums = [None] * (2 * TAPS)
        for i in range(6):
            first = i * mchunk
            here = p_ref[pl.ds(edge + first, mchunk), :]
            for strand in range(2):
                for j in range(TAPS):
                    shift = (j - HALF) * dil * (1 - 2 * strand)
                    prod = here * x1_refs[strand][t][pl.ds(first + REACH + shift, mchunk), :]
                    part = prod.reshape(mchunk // 8, 8, LANE).sum(0)
                    slot = strand * TAPS + j
                    sums[slot] = part if i == 0 else sums[slot] + part
        for strand in range(2):
            lines = [jnp.sum(sums[strand * TAPS + j], axis=0, keepdims=True) for j in range(TAPS)]
            gt_ref[strand, :, dst] = jnp.concatenate(lines + [jnp.zeros((8 - TAPS, LANE), F32)], axis=0)


def collect_kernel(n_chan, width, scale, *refs):
    pks, refs = refs[:n_chan], refs[n_chan:]
    hot1_ref, cot_ref, e_ref, et_ref, pb_ref, gt_ref, plain_ref, other_ref = refs[:8]
    keep_ref, send_ref, dw_ref, st_ref, back_ref, tail_ref = refs[8:]
    chans = n_chan * width
    me, rev = lax.axis_index("chan"), reversal(LANE)
    blocks = [slice(k * width, (k + 1) * width) for k in range(n_chan)]
    table, table_r = e_ref[...], et_ref[...]

    by_tap = dot(hot1_ref[...], pb_ref[...])
    own_letters = dot(hot1_ref[:16, :], cot_ref[...]) * scale
    srow, scol = iotas((8, JB))
    sum_letter = as_bf((scol % BASES == srow) & (scol < TAPS * BASES))
    sum_tap = as_bf((scol // BASES == srow) & (scol < TAPS * BASES))

    def sums_of(sel, x):
        high, rest = split_bf(x)
        return dot(sel, high) + dot(sel, rest)

    sel1 = select_rows("tap1", JB)
    ahead = by_tap[:JB] * dot(sel1, table)
    other = by_tap[JB:] * dot(sel1, table_r)
    turned, other, taps_turned = reverse_wide([other_ref[...], other, gt_ref[1]], rev)
    sums = plain_ref[...] + jnp.concatenate([turned[JB:], turned[:JB]], axis=0)
    dw_ref[...] = sums
    letters = sums_of(sum_letter, ahead + other)
    tail_ref[8:16, :] = gt_ref[0] + taps_turned

    total = jnp.zeros((2 * JB, chans), F32)
    for k in range(n_chan):
        total = total + dot(dw_ref[:, blocks[k]].astype(BF), pks[k][:width, :])
    st_ref[...] = total
    for k, block in enumerate(xor_blocks([st_ref[:, lanes] for lanes in blocks], me)):
        back_ref[:, blocks[k]] = block
    (turned,) = reverse_wide([back_ref[JB:, :]], rev)
    both = back_ref[:JB, :] + turned
    tail_ref[0:8, :] = sums_of(sum_tap, both * dot(select_rows("letter", JB), table))
    letters = letters + sums_of(sum_letter, both * dot(select_rows("tap0", JB), table))
    tail_ref[16:24, :] = letters
    zeros = jnp.zeros((BASES, width), F32)
    own = jnp.concatenate([own_letters[HALF * BASES : (HALF + 1) * BASES, :], zeros], axis=0)
    for kk, lanes in enumerate(blocks):
        place, at = (keep_ref, send_ref)[kk % 2], kk // 2
        letters = tail_ref[16:24, lanes]
        if kk == 0:
            letters = letters + own
        place[at, :ROW_R, :] = jnp.concatenate([dw_ref[:ROW_GE, lanes], letters[:BASES]], axis=0)
        place[at, ROW_R : 2 * ROW_R, :] = dw_ref[JB : JB + ROW_R, lanes]
        place[at, ROW_GT0:, :] = tail_ref[0:16, lanes]


def add_kernel(a_ref, b_ref, first_ref, second_ref):
    first_ref[...] = (a_ref[0] + b_ref[0]).astype(BF)
    second_ref[...] = (a_ref[1] + b_ref[1]).astype(BF)


def finish_kernel(
    n_chan, width, st_ref, sa_ref, sb_ref, near_ref, far_ref, gm_ref, gt_ref, ge_ref, held, sems
):
    me, odd = lax.axis_index("chan"), lax.axis_index("seq") % 2
    half = width // 2
    copies = []

    def send(block, part):
        copies.append(pltpu.make_async_copy(held.at[block, part], gm_ref.at[block, part], sems.at[len(copies)]))
        copies[-1].start()

    for source, turn in ((near_ref, odd), (far_ref, 1 - odd)):
        lines = pl.ds(pl.multiple_of(turn * half, half), half)
        blocks = [source[:, k * width : (k + 1) * width].astype(F32) for k in range(n_chan)]
        for k, part in enumerate(xor_blocks(blocks, me)):
            held[1, lines, k * width : (k + 1) * width] = part
        send(1, lines)

    sums = sa_ref[...].astype(F32) + sb_ref[...].astype(F32)
    fill = jnp.zeros((JB - ROW_GE, width), F32)
    dw = jnp.concatenate([sums[:ROW_GE], fill, sums[ROW_R : ROW_R + ROW_GE], fill], axis=0).astype(BF)
    for i in range(2):
        lines = slice(i * half, (i + 1) * half)
        held[0, lines, :] = t_dot(dw[:, lines], st_ref[: 2 * JB, :])
        send(0, pl.ds(i * half, half))
    for j in range(TAPS):
        gt_ref[j, 0:1, :] = sums[ROW_GT0 + j : ROW_GT0 + j + 1]
        gt_ref[j, 1:2, :] = sums[ROW_GT1 + j : ROW_GT1 + j + 1]
    ge_ref[...] = sums[ROW_GE : ROW_GE + BASES]
    for copy in copies:
        copy.wait()


VMEM = pl.BlockSpec(memory_space=pltpu.VMEM)
SMEM = pl.BlockSpec(memory_space=pltpu.SMEM)
HBM = pl.BlockSpec(memory_space=pltpu.HBM)


def in_hbm(x):
    return pltpu.with_memory_space_constraint(x, pltpu.HBM)


def call(kernel, in_specs, out_shape, out_specs, scratch, limit, cost):
    flops, moved = cost
    return pl.pallas_call(
        kernel,
        out_shape=out_shape,
        in_specs=in_specs,
        out_specs=out_specs,
        scratch_shapes=scratch,
        compiler_params=pltpu.CompilerParams(vmem_limit_bytes=limit << 20),
        cost_estimate=pl.CostEstimate(flops=flops, bytes_accessed=moved, transcendentals=0),
    )


def flip_bits(x, axis, mask):
    return lax.ppermute(x, axis, [(i, i ^ mask) for i in range(lax.axis_size(axis))])


def body(tokens, cotangent, embed, taps, mix, dilations):
    rows, width = cotangent.shape
    n_seq, n_chan = lax.axis_size("seq"), lax.axis_size("chan")
    chans = n_chan * width
    tiles = chans // LANE
    ext = rows + 2 * REACH
    padded = pl.cdiv(ext, LANE) * LANE
    edge = 2 * REACH
    own_tiles = pl.cdiv(width, LANE)
    scale = 1.0 / math.sqrt(rows * n_seq)
    shape = jax.ShapeDtypeStruct
    mix_t = jnp.swapaxes(mix, 1, 2)

    pk, letters = call(
        functools.partial(pack_kernel, width),
        [HBM] * 4,
        [shape((width + TABLE, chans), BF), shape((1, rows), jnp.int32)],
        [VMEM] * 2,
        [
            pltpu.VMEM((BASES, width), BF),
            pltpu.VMEM((TAPS, BLOCKS, width), BF),
            pltpu.SemaphoreType.DMA((4,)),
        ],
        8,
        (0, width * chans * 4),
    )(in_hbm(mix_t), in_hbm(embed), in_hbm(jnp.swapaxes(taps, 0, 1)), in_hbm(tokens))

    seq_bits = n_seq.bit_length() - 1
    for bit in range(0, seq_bits, 2):
        masks = [k << bit for k in range(1, 1 << min(2, seq_bits - bit))]
        letters = jnp.concatenate([letters] + [flip_bits(letters, "seq", m) for m in masks], axis=0)

    mixl, cot = call(
        functools.partial(local_kernel, n_chan, width),
        [HBM, HBM],
        [shape((width, chans), BF), shape((rows, width), BF)],
        [VMEM] * 2,
        [
            pltpu.VMEM((width, chans), BF),
            pltpu.VMEM((width, rows), BF),
            pltpu.SemaphoreType.DMA((2,)),
        ],
        16,
        (1 << 20, 1 << 20),
    )(in_hbm(mix_t), in_hbm(cotangent.T))

    pks = [pk]
    for bit in reversed(range(n_chan.bit_length() - 1)):
        ready = [pks[0]] + [lax.optimization_barrier((p, letters, mixl, cot))[0] for p in pks[1:]]
        moved = [flip_bits(p, "chan", 1 << bit) for p in ready]
        pks = [q for pair in zip(pks, moved) for q in pair]

    hot_t, hot, hot1 = call(
        functools.partial(prep_kernel, n_seq, rows),
        [SMEM, VMEM],
        [shape((padded, 4 * JB), BF), shape((2 * JB, padded), BF), shape((2 * JB, rows), BF)],
        [VMEM] * 3,
        [],
        16,
        (1 << 20, 1 << 20),
    )(dilations, letters)

    rows_ext = shape((ext, LANE), F32)
    x2, near, far, s1, stack, table, table_r, *strands = call(
        functools.partial(forward_kernel, n_chan, rows, width, scale),
        [SMEM] + [VMEM] * (n_chan + 3),
        [
            shape((width, rows), BF),
            shape((width // 2, chans), BF),
            shape((width // 2, chans), BF),
            shape((rows, width), BF),
            shape((4 * JB, chans), BF),
            shape((TABLE, chans), BF),
            shape((TABLE, chans), BF),
        ]
        + [rows_ext] * (4 * tiles),
        [HBM] + [VMEM] * (6 + 4 * tiles),
        [
            pltpu.VMEM((4 * JB, chans), BF),
            pltpu.VMEM((4 * JB, chans), BF),
            pltpu.VMEM((rows, chans), BF),
            pltpu.VMEM((width, rows), BF),
            pltpu.SemaphoreType.DMA,
        ],
        32,
        (3 << 30, 8 << 20),
    )(dilations, *pks, hot_t, mixl, cot)

    arrived = flip_bits(far, "seq", 1)
    pb, gt, plain, other = call(
        functools.partial(backward_kernel, n_chan, rows, width, scale),
        [SMEM] + [VMEM] * (6 + 4 * tiles),
        [
            shape((rows, chans), BF),
            shape((2, 8, chans), F32),
            shape((2 * JB, chans), F32),
            shape((2 * JB, chans), F32),
        ],
        [VMEM] * 4,
        [pltpu.VMEM((rows + 2 * edge, LANE), F32)] * tiles
        + [pltpu.VMEM((padded, 2 * LANE), BF)] * tiles
        + [pltpu.VMEM((own_tiles, ext, LANE), F32)],
        40,
        (3 << 30, 8 << 20),
    )(dilations, hot, mixl, cot, s1, table, table_r, *strands)

    def rounded_sum(a, b):
        return lax.optimization_barrier((a.astype(F32) + b.astype(F32)).astype(BF))

    g_mine = rounded_sum(near, lax.optimization_barrier((arrived, plain))[0])
    gt = lax.optimization_barrier((gt, g_mine))[0]
    keep, send = call(
        functools.partial(collect_kernel, n_chan, width, scale),
        [VMEM] * (n_chan + 8),
        [shape((n_chan // 2, SUMS, width), F32)] * 2,
        [VMEM] * 2,
        [
            pltpu.VMEM((2 * JB, chans), F32),
            pltpu.VMEM((2 * JB, chans), F32),
            pltpu.VMEM((2 * JB, chans), F32),
            pltpu.VMEM((24, chans), F32),
        ],
        24,
        (1 << 20, 1 << 16),
    )(*pks, hot1, cot, table, table_r, pb, gt, plain, other)

    for bit in range(1, seq_bits):
        g_mine = rounded_sum(g_mine, flip_bits(g_mine, "seq", 1 << bit))
    g_other = flip_bits(g_mine, "seq", 1)
    last = n_chan.bit_length() - 2
    mine, theirs = keep, flip_bits(send, "chan", 1)
    for bit in range(1, last):
        mine = mine + theirs
        mine, theirs = mine[0::2], flip_bits(mine[1::2], "chan", 1 << bit)
    s_mine = call(
        add_kernel,
        [VMEM] * 2,
        [shape((SUMS, width), BF)] * 2,
        [VMEM] * 2,
        [],
        8,
        (0, 0),
    )(mine, theirs)
    across = flip_bits(s_mine[1], "chan", 1 << last)
    along = flip_bits(s_mine[0], "seq", 1)
    places = [(i, j) for i in range(n_seq) for j in range(n_chan)]
    pairs = [(i * n_chan + j, (i ^ 1) * n_chan + (j ^ (1 << last))) for i, j in places]
    corner = lax.ppermute(s_mine[1], ("seq", "chan"), pairs)
    here, there = (s_mine[0], across), (along, corner)
    s_mine = rounded_sum(*(a.astype(F32) + b.astype(F32) for a, b in (here, there)))
    for bit in range(1, seq_bits):
        s_other = flip_bits(s_mine, "seq", 1 << bit)
        if bit < seq_bits - 1:
            s_mine = rounded_sum(s_mine, s_other)

    grad_mix, grad_taps, grad_embed = call(
        functools.partial(finish_kernel, n_chan, width),
        [VMEM] * 5,
        [
            shape((BLOCKS, width, chans), F32),
            shape((TAPS, BLOCKS, width), F32),
            shape((BASES, width), F32),
        ],
        [HBM, VMEM, VMEM],
        [pltpu.VMEM((BLOCKS, width, chans), F32), pltpu.SemaphoreType.DMA((4,))],
        16,
        (1 << 24, 1 << 21),
    )(stack, s_mine, s_other, g_mine, g_other)
    return x2.T, jnp.swapaxes(grad_mix, 1, 2), jnp.swapaxes(grad_taps, 0, 1), grad_embed


def solution(mesh):
    in_specs = (
        P(("groups", "seq")),
        P(("groups", "seq"), "chan"),
        P(None, "chan"),
        P(None, None, "chan"),
        P(None, None, "chan"),
        P(),
    )
    out_specs = (
        P(("groups", "seq"), "chan"),
        P("groups", None, "chan"),
        P("groups", None, "chan"),
        P("groups", "chan"),
    )
    return jax.shard_map(body, mesh=mesh, in_specs=in_specs, out_specs=out_specs, check_vma=False)
```

```python
import functools
import math

import jax
import jax.numpy as jnp
from jax import lax
from jax.experimental import pallas as pl
from jax.experimental.pallas import tpu as pltpu
from jax.sharding import PartitionSpec as P

TAPS = 5
BASES = 4
BLOCKS = 2
DMAX = 8
HALF = TAPS // 2
REACH = HALF * DMAX
LANE = 128
JB = 32
GELU_SCALE = math.sqrt(2.0 / math.pi)
CUBIC = 0.044715
BF = jnp.bfloat16
F32 = jnp.float32
ROW_EMBED, ROW_TAPS0, ROW_TAPS1, TABLE = 0, BASES, BASES + TAPS, 16
ROW_GE, ROW_R, ROW_GT0, ROW_GT1, SUMS = 20, 24, 48, 56, 64


def dot(a, b, **kw):
    return jnp.dot(a, b, preferred_element_type=F32, **kw)


def dot_t(a, b):
    return lax.dot_general(a, b, (((1,), (1,)), ((), ())), preferred_element_type=F32)


def t_dot(a, b):
    return lax.dot_general(a, b, (((0,), (0,)), ((), ())), preferred_element_type=F32)


def iotas(shape):
    return lax.broadcasted_iota(jnp.int32, shape, 0), lax.broadcasted_iota(jnp.int32, shape, 1)


def as_bf(mask):
    return mask.astype(F32).astype(BF)


def reversal(size):
    row, col = iotas((size, size))
    return as_bf(row + col == size - 1)


def split_bf(x):
    high = x.astype(BF)
    return high, (x - high.astype(F32)).astype(BF)


def reverse_lanes(parts, rev):
    n = parts[0].shape[1] // LANE
    rows = [p.shape[0] for p in parts]
    pile = [p[:, t * LANE : (t + 1) * LANE] for p in parts for t in range(n)]
    turned = dot(jnp.concatenate(pile, axis=0), rev)
    out, first = [], 0
    for count in rows:
        tiles = [turned[first + t * count : first + (t + 1) * count] for t in range(n)]
        out.append(jnp.concatenate(tiles[::-1], axis=1))
        first += n * count
    return out


def reverse_wide(parts, rev):
    split = [split_bf(p) for p in parts]
    turned = reverse_lanes([q for pair in split for q in pair], rev)
    return [turned[2 * i] + turned[2 * i + 1] for i in range(len(parts))]


def xor_blocks(blocks, me):
    for bit in range(len(blocks).bit_length() - 1):
        swap = lax.bitwise_and(lax.shift_right_logical(me, bit), 1) == 1
        blocks = [jnp.where(swap, blocks[k ^ (1 << bit)], blocks[k]) for k in range(len(blocks))]
    return blocks


def gelu_parts(v):
    square = v * v
    tangent = jnp.tanh(v * (GELU_SCALE + (GELU_SCALE * CUBIC) * square))
    half = 0.5 + 0.5 * tangent
    value = v * half
    slope = half + (v * (1.0 - tangent * tangent)) * (
        0.5 * GELU_SCALE + (1.5 * GELU_SCALE * CUBIC) * square
    )
    return value, slope


def gelu_doubled(half):
    square = half * half
    cubic = (8.0 * GELU_SCALE * CUBIC) * square
    above = 1.0 + jnp.tanh(half * (2.0 * GELU_SCALE + cubic))
    value = half * above
    slope = above + value * ((2.0 - above) * (2.0 * GELU_SCALE + 3.0 * cubic))
    return value, slope


def select_rows(kind, rows):
    row, col = iotas((rows, TABLE))
    local = row % JB
    used = local < TAPS * BASES
    tap, letter = local // BASES, local % BASES
    want = {"tap0": ROW_TAPS0 + tap, "tap1": ROW_TAPS1 + tap, "letter": ROW_EMBED + letter}[kind]
    return as_bf(used & (col == want))


def one_hot_t(tokens):
    n = tokens[0].shape[1]
    inside = tokens[HALF] != 0
    row = lax.broadcasted_iota(jnp.int32, (2 * JB, n), 0)
    local = row % JB
    group = jnp.where(local < TAPS * BASES, local // BASES + TAPS * (row // JB), -1)
    seen = jnp.zeros((2 * JB, n), jnp.int32)
    for g, line in enumerate(tokens):
        line = jnp.where(inside, line, 0)
        seen = jnp.where(group == g, jnp.broadcast_to(line, (2 * JB, n)), seen)
    return (seen == local % BASES + 1).astype(F32)


def pack_kernel(width, mix_ref, embed_ref, taps_ref, tok_ref, out_ref, letters_ref, e_ref, t_ref, sems):
    big = pltpu.make_async_copy(mix_ref.at[0], out_ref.at[pl.ds(0, width)], sems.at[0])
    small = [
        pltpu.make_async_copy(embed_ref, e_ref, sems.at[1]),
        pltpu.make_async_copy(taps_ref, t_ref, sems.at[2]),
        pltpu.make_async_copy(tok_ref, letters_ref.at[0], sems.at[3]),
    ]
    for copy in small + [big]:
        copy.start()
    out_ref[width:, :] = jnp.zeros((TABLE, out_ref.shape[1]), BF)
    for copy in small:
        copy.wait()
    taps = t_ref[...].astype(F32)
    lines = [e_ref[...].astype(F32)]
    lines += [taps[j, block : block + 1, :] for block in range(BLOCKS) for j in range(TAPS)]
    lines.append(jnp.zeros((TABLE - BASES - 2 * TAPS, width), F32))
    out_ref[width:, :width] = jnp.concatenate(lines, axis=0).astype(BF)
    big.wait()


def local_kernel(n_chan, width, mix_ref, cot_ref, mixl_ref, cotl_ref, m_ref, c_ref, sems):
    first = pltpu.make_async_copy(mix_ref.at[1], m_ref, sems.at[0])
    second = pltpu.make_async_copy(cot_ref, c_ref, sems.at[1])
    first.start()
    second.start()
    first.wait()
    blocks = [m_ref[:, k * width : (k + 1) * width] for k in range(n_chan)]
    for k, block in enumerate(xor_blocks(blocks, lax.axis_index("chan"))):
        mixl_ref[:, k * width : (k + 1) * width] = block
    second.wait()
    cotl_ref[...] = c_ref[...].astype(F32).T.astype(BF)


def prep_kernel(n_seq, rows, dils, tok_ref, a_ref, hot_ref, hot1_ref):
    place = lax.axis_index("seq")

    def line(block):
        inside = jnp.logical_and(block >= 0, block < n_seq)
        safe = jnp.clip(block, 0, n_seq - 1)
        letters = tok_ref[pl.ds(lax.bitwise_xor(safe, place), 1), :] + 1
        return jnp.where(inside, letters, 0)

    def around(block):
        lines = [line(block - 1)[:, rows - LANE :], line(block), line(block + 1)[:, :LANE]]
        return jnp.concatenate(lines, axis=1)

    total = rows + 2 * LANE
    this = jnp.broadcast_to(around(place), (8, total))
    mirror = jnp.broadcast_to(around(n_seq - 1 - place), (8, total)).astype(F32).astype(BF)
    rev, n_tiles = reversal(LANE), total // LANE
    other = jnp.concatenate(
        [dot(mirror[:, t * LANE : (t + 1) * LANE], rev) for t in reversed(range(n_tiles))], axis=1
    ).astype(jnp.int32)

    def windows(dilation, margin, count):
        out = []
        for strand, source in ((1, this), (-1, other)):
            for j in range(TAPS):
                first = LANE - margin + strand * (j - HALF) * dilation
                out.append(pltpu.roll(source, total - first, 1)[:1, :count])
        return out

    hot = one_hot_t(windows(dils[0], REACH, a_ref.shape[0]))
    a_ref[...] = jnp.concatenate([hot, hot], axis=0).T.astype(BF)
    hot_ref[...] = hot.astype(BF)
    hot1_ref[...] = one_hot_t(windows(dils[1], 0, rows)).astype(BF)


def forward_kernel(n_chan, rows, width, scale, dils, *refs):
    tiles = n_chan * width // LANE
    pks, refs = refs[:n_chan], refs[n_chan:]
    (a_ref, mixl_ref, cot_ref), refs = refs[:3], refs[3:]
    (x2_ref, near_ref, far_ref, s_ref, st_ref, e_ref, et_ref), refs = refs[:7], refs[7:]
    x1_refs, refs = (refs[:tiles], refs[tiles : 2 * tiles]), refs[2 * tiles :]
    gp_refs, refs = (refs[:tiles], refs[tiles : 2 * tiles]), refs[2 * tiles :]
    w_ref, b_ref, m_ref, held, sem = refs
    chans = n_chan * width
    ext = rows + 2 * REACH
    me, dil = lax.axis_index("chan"), dils[1]
    rev = reversal(LANE)
    blocks = [slice(k * width, (k + 1) * width) for k in range(n_chan)]

    for k in range(n_chan):
        e_ref[:, blocks[k]] = pks[k][width:, :width]
    table = e_ref[...]
    plain = dot(select_rows("tap0", JB), table) * dot(select_rows("letter", JB), table)
    high, low = split_bf(plain)
    turned, turned_low, table_r = reverse_lanes([high, low, table], rev)
    et_ref[...] = table_r.astype(BF)
    b_ref[...] = jnp.concatenate([high, turned.astype(BF), low, turned_low.astype(BF)], axis=0)
    for k, block in enumerate(xor_blocks([b_ref[:, lanes] for lanes in blocks], me)):
        st_ref[:, blocks[k]] = block
    for k in range(n_chan):
        total = 0.5 * dot_t(st_ref[...], pks[k][:width, :])
        high, low = split_bf(total[: 2 * JB] + total[2 * JB :])
        w_ref[:, blocks[k]] = jnp.concatenate([high, low], axis=0)
    weights = w_ref[...]
    (swapped,) = reverse_lanes([weights], rev)
    order = [swapped[JB : 2 * JB], swapped[:JB], swapped[3 * JB :], swapped[2 * JB : 3 * JB]]
    weights_r = jnp.concatenate(order, axis=0).astype(BF)

    table, table_r = table.astype(F32), et_ref[...].astype(F32)
    centre = HALF * BASES
    keep = lax.broadcasted_iota(jnp.int32, (8, chans), 0) < BASES

    def lookup(source, first):
        lines = jnp.where(keep, source[:8], 0.0)
        above, below = jnp.zeros((first, chans), F32), jnp.zeros((4 * JB - first - 8, chans), F32)
        return jnp.concatenate([above, lines, below], axis=0).astype(BF)

    look, look_r = lookup(table, centre), lookup(table_r, JB + centre)
    chunk, mchunk = ext // 5, rows // 6
    for t in range(tiles):
        dst = slice(t * LANE, (t + 1) * LANE)
        for strand, (wr, er) in enumerate(((weights, look), (weights_r, look_r))):
            rhs = jnp.concatenate([wr[:, dst], er[:, dst]], axis=1)
            for i in range(5):
                where = pl.ds(i * chunk, chunk)
                both = dot(a_ref[where, :], rhs)
                value, slope = gelu_doubled(both[:, :LANE])
                x1_refs[strand][t][where, :] = both[:, LANE:] + value
                gp_refs[strand][t][where, :] = slope

        for i in range(6):
            first = i * mchunk
            terms = []
            for j in range(TAPS):
                shift = (j - HALF) * dil
                line = slice(ROW_TAPS1 + j, ROW_TAPS1 + j + 1)
                terms.append(table[line, dst] * x1_refs[0][t][pl.ds(first + REACH + shift, mchunk), :])
                terms.append(table_r[line, dst] * x1_refs[1][t][pl.ds(first + REACH - shift, mchunk), :])
            m_ref[first : first + mchunk, dst] = functools.reduce(jnp.add, terms).astype(BF)

    half = rows // 2
    n_own = pl.cdiv(width, LANE)
    for i in range(2):
        where = pl.ds(i * half, half)
        value, slope = gelu_parts(dot_t(m_ref[where, :], mixl_ref[...]))
        inner = pl.ds(REACH + i * half, half)
        own = jnp.concatenate([x1_refs[0][t][inner, :] for t in range(n_own)], axis=1)[:, :width]
        held[:, where] = (own + value).T.astype(BF)
        s_ref[where, :] = ((cot_ref[where, :].astype(F32) * scale) * slope).astype(BF)
    copy = pltpu.make_async_copy(held, x2_ref, sem)
    copy.start()

    part = t_dot(s_ref[...], m_ref[...]).astype(BF)
    odd = lax.axis_index("seq") % 2 == 1
    near_ref[...] = jnp.where(odd, part[width // 2 :], part[: width // 2])
    far_ref[...] = jnp.where(odd, part[: width // 2], part[width // 2 :])
    copy.wait()


def backward_kernel(n_chan, rows, width, scale, dils, *refs):
    tiles = n_chan * width // LANE
    (hot_ref, mixl_ref, cot_ref, s_ref, e_ref, et_ref), refs = refs[:6], refs[6:]
    x1_refs, refs = (refs[:tiles], refs[tiles : 2 * tiles]), refs[2 * tiles :]
    gp_refs, refs = (refs[:tiles], refs[tiles : 2 * tiles]), refs[2 * tiles :]
    (pb_ref, gt_ref, plain_ref, other_ref), refs = refs[:4], refs[4:]
    p_refs, s0_refs, (g2_ref,) = refs[:tiles], refs[tiles : 2 * tiles], refs[2 * tiles :]
    ext = rows + 2 * REACH
    padded = hot_ref.shape[1]
    dil = dils[1]
    taps_f, taps_r = 0.5 * e_ref[...].astype(F32), 0.5 * et_ref[...].astype(F32)

    edge = 2 * REACH
    n_own = pl.cdiv(width, LANE)
    g2 = cot_ref[...].astype(F32) * scale
    g2_ref[:, :REACH, :] = jnp.zeros((n_own, REACH, LANE), F32)
    g2_ref[:, rows + REACH :, :] = jnp.zeros((n_own, REACH, LANE), F32)
    g2 = jnp.concatenate([g2, jnp.zeros((rows, n_own * LANE - width), F32)], axis=1)
    for t in range(n_own):
        g2_ref[t, REACH : rows + REACH, :] = 0.5 * g2[:, t * LANE : (t + 1) * LANE]

    mchunk, chunk = rows // 6, ext // 5
    for t in range(tiles):
        dst = slice(t * LANE, (t + 1) * LANE)
        p_ref, s0_ref = p_refs[t], s0_refs[t]
        if t % 2 == 0:
            pair = dot(s_ref[...], mixl_ref[:, t * LANE : (t + 2) * LANE])
            pb_ref[:, t * LANE : (t + 2) * LANE] = pair.astype(BF)
        p_ref[:edge, :] = jnp.zeros((edge, LANE), F32)
        p_ref[rows + edge :, :] = jnp.zeros((edge, LANE), F32)
        p_ref[edge : rows + edge, :] = pair[:, (t % 2) * LANE : (t % 2 + 1) * LANE]
        s0_ref[ext:, :] = jnp.zeros((padded - ext, 2 * LANE), BF)
        for i in range(5):
            first = i * chunk
            where = pl.ds(first, chunk)
            fs, rs = [], []
            for j in range(TAPS):
                window = p_ref[pl.ds(first + REACH + (j - HALF) * dil, chunk), :]
                ahead, back = ROW_TAPS1 + j, ROW_TAPS1 + TAPS - 1 - j
                fs.append(taps_f[back : back + 1, dst] * window)
                rs.append(taps_r[ahead : ahead + 1, dst] * window)
            if t < n_own:
                fs.append(g2_ref[t, where, :])
            f, r = functools.reduce(jnp.add, fs), functools.reduce(jnp.add, rs)
            s0_ref[where, :LANE] = (f * gp_refs[0][t][where, :]).astype(BF)
            s0_ref[where, LANE:] = (r * gp_refs[1][t][where, :]).astype(BF)
        both = dot(hot_ref[...], s0_ref[...])
        plain_ref[:, dst], other_ref[:, dst] = both[:, :LANE], both[:, LANE:]

        sums = [None] * (2 * TAPS)
        for i in range(6):
            first = i * mchunk
            here = p_ref[pl.ds(edge + first, mchunk), :]
            for strand in range(2):
                for j in range(TAPS):
                    shift = (j - HALF) * dil * (1 - 2 * strand)
                    prod = here * x1_refs[strand][t][pl.ds(first + REACH + shift, mchunk), :]
                    part = prod.reshape(mchunk // 8, 8, LANE).sum(0)
                    slot = strand * TAPS + j
                    sums[slot] = part if i == 0 else sums[slot] + part
        for strand in range(2):
            lines = [jnp.sum(sums[strand * TAPS + j], axis=0, keepdims=True) for j in range(TAPS)]
            gt_ref[strand, :, dst] = jnp.concatenate(lines + [jnp.zeros((8 - TAPS, LANE), F32)], axis=0)


def collect_kernel(n_chan, width, scale, *refs):
    pks, refs = refs[:n_chan], refs[n_chan:]
    hot1_ref, cot_ref, e_ref, et_ref, pb_ref, gt_ref, plain_ref, other_ref = refs[:8]
    keep_ref, send_ref, dw_ref, st_ref, back_ref, tail_ref = refs[8:]
    chans = n_chan * width
    me, rev = lax.axis_index("chan"), reversal(LANE)
    blocks = [slice(k * width, (k + 1) * width) for k in range(n_chan)]
    table, table_r = e_ref[...], et_ref[...]

    by_tap = dot(hot1_ref[...], pb_ref[...])
    own_letters = dot(hot1_ref[:16, :], cot_ref[...]) * scale
    srow, scol = iotas((8, JB))
    sum_letter = as_bf((scol % BASES == srow) & (scol < TAPS * BASES))
    sum_tap = as_bf((scol // BASES == srow) & (scol < TAPS * BASES))

    def sums_of(sel, x):
        high, rest = split_bf(x)
        return dot(sel, high) + dot(sel, rest)

    sel1 = select_rows("tap1", JB)
    ahead = by_tap[:JB] * dot(sel1, table)
    other = by_tap[JB:] * dot(sel1, table_r)
    turned, other, taps_turned = reverse_wide([other_ref[...], other, gt_ref[1]], rev)
    sums = plain_ref[...] + jnp.concatenate([turned[JB:], turned[:JB]], axis=0)
    dw_ref[...] = sums
    letters = sums_of(sum_letter, ahead + other)
    tail_ref[8:16, :] = gt_ref[0] + taps_turned

    total = jnp.zeros((2 * JB, chans), F32)
    for k in range(n_chan):
        total = total + dot(dw_ref[:, blocks[k]].astype(BF), pks[k][:width, :])
    st_ref[...] = total
    for k, block in enumerate(xor_blocks([st_ref[:, lanes] for lanes in blocks], me)):
        back_ref[:, blocks[k]] = block
    (turned,) = reverse_wide([back_ref[JB:, :]], rev)
    both = back_ref[:JB, :] + turned
    tail_ref[0:8, :] = sums_of(sum_tap, both * dot(select_rows("letter", JB), table))
    letters = letters + sums_of(sum_letter, both * dot(select_rows("tap0", JB), table))
    tail_ref[16:24, :] = letters
    zeros = jnp.zeros((BASES, width), F32)
    own = jnp.concatenate([own_letters[HALF * BASES : (HALF + 1) * BASES, :], zeros], axis=0)
    for kk, lanes in enumerate(blocks):
        place, at = (keep_ref, send_ref)[kk % 2], kk // 2
        letters = tail_ref[16:24, lanes]
        if kk == 0:
            letters = letters + own
        place[at, :ROW_R, :] = jnp.concatenate([dw_ref[:ROW_GE, lanes], letters[:BASES]], axis=0)
        place[at, ROW_R : 2 * ROW_R, :] = dw_ref[JB : JB + ROW_R, lanes]
        place[at, ROW_GT0:, :] = tail_ref[0:16, lanes]


def add_kernel(a_ref, b_ref, first_ref, second_ref):
    first_ref[...] = (a_ref[0] + b_ref[0]).astype(BF)
    second_ref[...] = (a_ref[1] + b_ref[1]).astype(BF)


def finish_kernel(
    n_chan, width, st_ref, sa_ref, sb_ref, near_ref, far_ref, gm_ref, gt_ref, ge_ref, held, sems
):
    me, odd = lax.axis_index("chan"), lax.axis_index("seq") % 2
    half = width // 2
    copies = []

    def send(block, part):
        copies.append(pltpu.make_async_copy(held.at[block, part], gm_ref.at[block, part], sems.at[len(copies)]))
        copies[-1].start()

    for source, turn in ((near_ref, odd), (far_ref, 1 - odd)):
        lines = pl.ds(pl.multiple_of(turn * half, half), half)
        blocks = [source[:, k * width : (k + 1) * width].astype(F32) for k in range(n_chan)]
        for k, part in enumerate(xor_blocks(blocks, me)):
            held[1, lines, k * width : (k + 1) * width] = part
        send(1, lines)

    sums = sa_ref[...].astype(F32) + sb_ref[...].astype(F32)
    fill = jnp.zeros((JB - ROW_GE, width), F32)
    dw = jnp.concatenate([sums[:ROW_GE], fill, sums[ROW_R : ROW_R + ROW_GE], fill], axis=0).astype(BF)
    for i in range(2):
        lines = slice(i * half, (i + 1) * half)
        held[0, lines, :] = t_dot(dw[:, lines], st_ref[: 2 * JB, :])
        send(0, pl.ds(i * half, half))
    for j in range(TAPS):
        gt_ref[j, 0:1, :] = sums[ROW_GT0 + j : ROW_GT0 + j + 1]
        gt_ref[j, 1:2, :] = sums[ROW_GT1 + j : ROW_GT1 + j + 1]
    ge_ref[...] = sums[ROW_GE : ROW_GE + BASES]
    for copy in copies:
        copy.wait()


VMEM = pl.BlockSpec(memory_space=pltpu.VMEM)
SMEM = pl.BlockSpec(memory_space=pltpu.SMEM)
HBM = pl.BlockSpec(memory_space=pltpu.HBM)


def in_hbm(x):
    return pltpu.with_memory_space_constraint(x, pltpu.HBM)


def call(kernel, in_specs, out_shape, out_specs, scratch, limit, cost):
    flops, moved = cost
    return pl.pallas_call(
        kernel,
        out_shape=out_shape,
        in_specs=in_specs,
        out_specs=out_specs,
        scratch_shapes=scratch,
        compiler_params=pltpu.CompilerParams(vmem_limit_bytes=limit << 20),
        cost_estimate=pl.CostEstimate(flops=flops, bytes_accessed=moved, transcendentals=0),
    )


def flip_bits(x, axis, mask):
    return lax.ppermute(x, axis, [(i, i ^ mask) for i in range(lax.axis_size(axis))])


def body(tokens, cotangent, embed, taps, mix, dilations):
    rows, width = cotangent.shape
    n_seq, n_chan = lax.axis_size("seq"), lax.axis_size("chan")
    chans = n_chan * width
    tiles = chans // LANE
    ext = rows + 2 * REACH
    padded = pl.cdiv(ext, LANE) * LANE
    edge = 2 * REACH
    own_tiles = pl.cdiv(width, LANE)
    scale = 1.0 / math.sqrt(rows * n_seq)
    shape = jax.ShapeDtypeStruct
    mix_t = jnp.swapaxes(mix, 1, 2)

    pk, letters = call(
        functools.partial(pack_kernel, width),
        [HBM] * 4,
        [shape((width + TABLE, chans), BF), shape((1, rows), jnp.int32)],
        [VMEM] * 2,
        [
            pltpu.VMEM((BASES, width), BF),
            pltpu.VMEM((TAPS, BLOCKS, width), BF),
            pltpu.SemaphoreType.DMA((4,)),
        ],
        8,
        (0, width * chans * 4),
    )(in_hbm(mix_t), in_hbm(embed), in_hbm(jnp.swapaxes(taps, 0, 1)), in_hbm(tokens))

    seq_bits = n_seq.bit_length() - 1
    for bit in range(0, seq_bits, 2):
        masks = [k << bit for k in range(1, 1 << min(2, seq_bits - bit))]
        letters = jnp.concatenate([letters] + [flip_bits(letters, "seq", m) for m in masks], axis=0)

    mixl, cot = call(
        functools.partial(local_kernel, n_chan, width),
        [HBM, HBM],
        [shape((width, chans), BF), shape((rows, width), BF)],
        [VMEM] * 2,
        [
            pltpu.VMEM((width, chans), BF),
            pltpu.VMEM((width, rows), BF),
            pltpu.SemaphoreType.DMA((2,)),
        ],
        16,
        (1 << 20, 1 << 20),
    )(in_hbm(mix_t), in_hbm(cotangent.T))

    pks = [pk]
    for bit in reversed(range(n_chan.bit_length() - 1)):
        ready = [pks[0]] + [lax.optimization_barrier((p, letters, mixl, cot))[0] for p in pks[1:]]
        moved = [flip_bits(p, "chan", 1 << bit) for p in ready]
        pks = [q for pair in zip(pks, moved) for q in pair]

    hot_t, hot, hot1 = call(
        functools.partial(prep_kernel, n_seq, rows),
        [SMEM, VMEM],
        [shape((padded, 4 * JB), BF), shape((2 * JB, padded), BF), shape((2 * JB, rows), BF)],
        [VMEM] * 3,
        [],
        16,
        (1 << 20, 1 << 20),
    )(dilations, letters)

    rows_ext = shape((ext, LANE), F32)
    x2, near, far, s1, stack, table, table_r, *strands = call(
        functools.partial(forward_kernel, n_chan, rows, width, scale),
        [SMEM] + [VMEM] * (n_chan + 3),
        [
            shape((width, rows), BF),
            shape((width // 2, chans), BF),
            shape((width // 2, chans), BF),
            shape((rows, width), BF),
            shape((4 * JB, chans), BF),
            shape((TABLE, chans), BF),
            shape((TABLE, chans), BF),
        ]
        + [rows_ext] * (4 * tiles),
        [HBM] + [VMEM] * (6 + 4 * tiles),
        [
            pltpu.VMEM((4 * JB, chans), BF),
            pltpu.VMEM((4 * JB, chans), BF),
            pltpu.VMEM((rows, chans), BF),
            pltpu.VMEM((width, rows), BF),
            pltpu.SemaphoreType.DMA,
        ],
        32,
        (3 << 30, 8 << 20),
    )(dilations, *pks, hot_t, mixl, cot)

    arrived = flip_bits(far, "seq", 1)
    pb, gt, plain, other = call(
        functools.partial(backward_kernel, n_chan, rows, width, scale),
        [SMEM] + [VMEM] * (6 + 4 * tiles),
        [
            shape((rows, chans), BF),
            shape((2, 8, chans), F32),
            shape((2 * JB, chans), F32),
            shape((2 * JB, chans), F32),
        ],
        [VMEM] * 4,
        [pltpu.VMEM((rows + 2 * edge, LANE), F32)] * tiles
        + [pltpu.VMEM((padded, 2 * LANE), BF)] * tiles
        + [pltpu.VMEM((own_tiles, ext, LANE), F32)],
        40,
        (3 << 30, 8 << 20),
    )(dilations, hot, mixl, cot, s1, table, table_r, *strands)

    def rounded_sum(a, b):
        return lax.optimization_barrier((a.astype(F32) + b.astype(F32)).astype(BF))

    g_mine = rounded_sum(near, lax.optimization_barrier((arrived, plain))[0])
    gt = lax.optimization_barrier((gt, g_mine))[0]
    keep, send = call(
        functools.partial(collect_kernel, n_chan, width, scale),
        [VMEM] * (n_chan + 8),
        [shape((n_chan // 2, SUMS, width), F32)] * 2,
        [VMEM] * 2,
        [
            pltpu.VMEM((2 * JB, chans), F32),
            pltpu.VMEM((2 * JB, chans), F32),
            pltpu.VMEM((2 * JB, chans), F32),
            pltpu.VMEM((24, chans), F32),
        ],
        24,
        (1 << 20, 1 << 16),
    )(*pks, hot1, cot, table, table_r, pb, gt, plain, other)

    for bit in range(1, seq_bits):
        g_mine = rounded_sum(g_mine, flip_bits(g_mine, "seq", 1 << bit))
    g_other = flip_bits(g_mine, "seq", 1)
    last = n_chan.bit_length() - 2
    mine, theirs = keep, flip_bits(send, "chan", 1)
    for bit in range(1, last):
        mine = mine + theirs
        mine, theirs = mine[0::2], flip_bits(mine[1::2], "chan", 1 << bit)
    s_mine = call(
        add_kernel,
        [VMEM] * 2,
        [shape((SUMS, width), BF)] * 2,
        [VMEM] * 2,
        [],
        8,
        (0, 0),
    )(mine, theirs)
    order = sorted(range(seq_bits), key=lambda bit: (bit != 1, bit))
    jump = 1 << order[0]
    across = flip_bits(s_mine[1], "chan", 1 << last)
    along = flip_bits(s_mine[0], "seq", jump)
    places = [(i, j) for i in range(n_seq) for j in range(n_chan)]
    pairs = [(i * n_chan + j, (i ^ jump) * n_chan + (j ^ (1 << last))) for i, j in places]
    corner = lax.ppermute(s_mine[1], ("seq", "chan"), pairs)
    here, there = (s_mine[0], across), (along, corner)
    s_mine = rounded_sum(*(a.astype(F32) + b.astype(F32) for a, b in (here, there)))
    for bit in order[1:]:
        s_other = flip_bits(s_mine, "seq", 1 << bit)
        if bit != order[-1]:
            s_mine = rounded_sum(s_mine, s_other)

    grad_mix, grad_taps, grad_embed = call(
        functools.partial(finish_kernel, n_chan, width),
        [VMEM] * 5,
        [
            shape((BLOCKS, width, chans), F32),
            shape((TAPS, BLOCKS, width), F32),
            shape((BASES, width), F32),
        ],
        [HBM, VMEM, VMEM],
        [pltpu.VMEM((BLOCKS, width, chans), F32), pltpu.SemaphoreType.DMA((4,))],
        16,
        (1 << 24, 1 << 21),
    )(stack, s_mine, s_other, g_mine, g_other)
    return x2.T, jnp.swapaxes(grad_mix, 1, 2), jnp.swapaxes(grad_taps, 0, 1), grad_embed


def solution(mesh):
    in_specs = (
        P(("groups", "seq")),
        P(("groups", "seq"), "chan"),
        P(None, "chan"),
        P(None, None, "chan"),
        P(None, None, "chan"),
        P(),
    )
    out_specs = (
        P(("groups", "seq"), "chan"),
        P("groups", None, "chan"),
        P("groups", None, "chan"),
        P("groups", "chan"),
    )
    return jax.shard_map(body, mesh=mesh, in_specs=in_specs, out_specs=out_specs, check_vma=False)
```

```python
import functools
import math

import jax
import jax.numpy as jnp
from jax import lax
from jax.experimental import pallas as pl
from jax.experimental.pallas import tpu as pltpu
from jax.sharding import PartitionSpec as P

TAPS = 5
BASES = 4
BLOCKS = 2
DMAX = 8
HALF = TAPS // 2
REACH = HALF * DMAX
LANE = 128
JB = 32
GELU_SCALE = math.sqrt(2.0 / math.pi)
CUBIC = 0.044715
BF = jnp.bfloat16
F32 = jnp.float32
ROW_EMBED, ROW_TAPS0, ROW_TAPS1, TABLE = 0, BASES, BASES + TAPS, 16
ROW_GE, ROW_R, ROW_GT0, ROW_GT1, SUMS = 20, 24, 48, 56, 64


def dot(a, b, **kw):
    return jnp.dot(a, b, preferred_element_type=F32, **kw)


def dot_t(a, b):
    return lax.dot_general(a, b, (((1,), (1,)), ((), ())), preferred_element_type=F32)


def t_dot(a, b):
    return lax.dot_general(a, b, (((0,), (0,)), ((), ())), preferred_element_type=F32)


def iotas(shape):
    return lax.broadcasted_iota(jnp.int32, shape, 0), lax.broadcasted_iota(jnp.int32, shape, 1)


def as_bf(mask):
    return mask.astype(F32).astype(BF)


def reversal(size):
    row, col = iotas((size, size))
    return as_bf(row + col == size - 1)


def split_bf(x):
    high = x.astype(BF)
    return high, (x - high.astype(F32)).astype(BF)


def reverse_lanes(parts, rev):
    n = parts[0].shape[1] // LANE
    rows = [p.shape[0] for p in parts]
    pile = [p[:, t * LANE : (t + 1) * LANE] for p in parts for t in range(n)]
    turned = dot(jnp.concatenate(pile, axis=0), rev)
    out, first = [], 0
    for count in rows:
        tiles = [turned[first + t * count : first + (t + 1) * count] for t in range(n)]
        out.append(jnp.concatenate(tiles[::-1], axis=1))
        first += n * count
    return out


def reverse_wide(parts, rev):
    split = [split_bf(p) for p in parts]
    turned = reverse_lanes([q for pair in split for q in pair], rev)
    return [turned[2 * i] + turned[2 * i + 1] for i in range(len(parts))]


def xor_blocks(blocks, me):
    for bit in range(len(blocks).bit_length() - 1):
        swap = lax.bitwise_and(lax.shift_right_logical(me, bit), 1) == 1
        blocks = [jnp.where(swap, blocks[k ^ (1 << bit)], blocks[k]) for k in range(len(blocks))]
    return blocks


def gelu_parts(v):
    square = v * v
    tangent = jnp.tanh(v * (GELU_SCALE + (GELU_SCALE * CUBIC) * square))
    half = 0.5 + 0.5 * tangent
    value = v * half
    slope = half + (v * (1.0 - tangent * tangent)) * (
        0.5 * GELU_SCALE + (1.5 * GELU_SCALE * CUBIC) * square
    )
    return value, slope


def gelu_doubled(half):
    square = half * half
    cubic = (8.0 * GELU_SCALE * CUBIC) * square
    above = 1.0 + jnp.tanh(half * (2.0 * GELU_SCALE + cubic))
    value = half * above
    slope = above + value * ((2.0 - above) * (2.0 * GELU_SCALE + 3.0 * cubic))
    return value, slope


def select_rows(kind, rows):
    row, col = iotas((rows, TABLE))
    local = row % JB
    used = local < TAPS * BASES
    tap, letter = local // BASES, local % BASES
    want = {"tap0": ROW_TAPS0 + tap, "tap1": ROW_TAPS1 + tap, "letter": ROW_EMBED + letter}[kind]
    return as_bf(used & (col == want))


def one_hot_t(tokens):
    n = tokens[0].shape[1]
    inside = tokens[HALF] != 0
    row = lax.broadcasted_iota(jnp.int32, (2 * JB, n), 0)
    local = row % JB
    group = jnp.where(local < TAPS * BASES, local // BASES + TAPS * (row // JB), -1)
    seen = jnp.zeros((2 * JB, n), jnp.int32)
    for g, line in enumerate(tokens):
        line = jnp.where(inside, line, 0)
        seen = jnp.where(group == g, jnp.broadcast_to(line, (2 * JB, n)), seen)
    return (seen == local % BASES + 1).astype(F32)


def pack_kernel(width, mix_ref, embed_ref, taps_ref, tok_ref, out_ref, letters_ref, e_ref, t_ref, sems):
    big = pltpu.make_async_copy(mix_ref.at[0], out_ref.at[pl.ds(0, width)], sems.at[0])
    small = [
        pltpu.make_async_copy(embed_ref, e_ref, sems.at[1]),
        pltpu.make_async_copy(taps_ref, t_ref, sems.at[2]),
        pltpu.make_async_copy(tok_ref, letters_ref.at[0], sems.at[3]),
    ]
    for copy in small + [big]:
        copy.start()
    out_ref[width:, :] = jnp.zeros((TABLE, out_ref.shape[1]), BF)
    for copy in small:
        copy.wait()
    taps = t_ref[...].astype(F32)
    lines = [e_ref[...].astype(F32)]
    lines += [taps[j, block : block + 1, :] for block in range(BLOCKS) for j in range(TAPS)]
    lines.append(jnp.zeros((TABLE - BASES - 2 * TAPS, width), F32))
    out_ref[width:, :width] = jnp.concatenate(lines, axis=0).astype(BF)
    big.wait()


def local_kernel(n_chan, width, mix_ref, cot_ref, mixl_ref, cotl_ref, m_ref, c_ref, sems):
    first = pltpu.make_async_copy(mix_ref.at[1], m_ref, sems.at[0])
    second = pltpu.make_async_copy(cot_ref, c_ref, sems.at[1])
    first.start()
    second.start()
    first.wait()
    blocks = [m_ref[:, k * width : (k + 1) * width] for k in range(n_chan)]
    for k, block in enumerate(xor_blocks(blocks, lax.axis_index("chan"))):
        mixl_ref[:, k * width : (k + 1) * width] = block
    second.wait()
    cotl_ref[...] = c_ref[...].astype(F32).T.astype(BF)


def prep_kernel(n_seq, rows, dils, tok_ref, a_ref, hot_ref, hot1_ref):
    place = lax.axis_index("seq")

    def line(block):
        inside = jnp.logical_and(block >= 0, block < n_seq)
        safe = jnp.clip(block, 0, n_seq - 1)
        letters = tok_ref[pl.ds(lax.bitwise_xor(safe, place), 1), :] + 1
        return jnp.where(inside, letters, 0)

    def around(block):
        lines = [line(block - 1)[:, rows - LANE :], line(block), line(block + 1)[:, :LANE]]
        return jnp.concatenate(lines, axis=1)

    total = rows + 2 * LANE
    this = jnp.broadcast_to(around(place), (8, total))
    mirror = jnp.broadcast_to(around(n_seq - 1 - place), (8, total)).astype(F32).astype(BF)
    rev, n_tiles = reversal(LANE), total // LANE
    other = jnp.concatenate(
        [dot(mirror[:, t * LANE : (t + 1) * LANE], rev) for t in reversed(range(n_tiles))], axis=1
    ).astype(jnp.int32)

    def windows(dilation, margin, count):
        out = []
        for strand, source in ((1, this), (-1, other)):
            for j in range(TAPS):
                first = LANE - margin + strand * (j - HALF) * dilation
                out.append(pltpu.roll(source, total - first, 1)[:1, :count])
        return out

    hot = one_hot_t(windows(dils[0], REACH, a_ref.shape[0]))
    a_ref[...] = jnp.concatenate([hot, hot], axis=0).T.astype(BF)
    hot_ref[...] = hot.astype(BF)
    hot1_ref[...] = one_hot_t(windows(dils[1], 0, rows)).astype(BF)


def forward_kernel(n_chan, rows, width, scale, dils, *refs):
    tiles = n_chan * width // LANE
    pks, refs = refs[:n_chan], refs[n_chan:]
    (a_ref, mixl_ref, cot_ref), refs = refs[:3], refs[3:]
    (x2_ref, near_ref, far_ref, s_ref, st_ref, e_ref, et_ref), refs = refs[:7], refs[7:]
    x1_refs, refs = (refs[:tiles], refs[tiles : 2 * tiles]), refs[2 * tiles :]
    gp_refs, refs = (refs[:tiles], refs[tiles : 2 * tiles]), refs[2 * tiles :]
    w_ref, b_ref, m_ref, held, sem = refs
    chans = n_chan * width
    ext = rows + 2 * REACH
    me, dil = lax.axis_index("chan"), dils[1]
    rev = reversal(LANE)
    blocks = [slice(k * width, (k + 1) * width) for k in range(n_chan)]

    for k in range(n_chan):
        e_ref[:, blocks[k]] = pks[k][width:, :width]
    table = e_ref[...]
    plain = dot(select_rows("tap0", JB), table) * dot(select_rows("letter", JB), table)
    high, low = split_bf(plain)
    turned, turned_low, table_r = reverse_lanes([high, low, table], rev)
    et_ref[...] = table_r.astype(BF)
    b_ref[...] = jnp.concatenate([high, turned.astype(BF), low, turned_low.astype(BF)], axis=0)
    for k, block in enumerate(xor_blocks([b_ref[:, lanes] for lanes in blocks], me)):
        st_ref[:, blocks[k]] = block
    for k in range(n_chan):
        total = 0.5 * dot_t(st_ref[...], pks[k][:width, :])
        high, low = split_bf(total[: 2 * JB] + total[2 * JB :])
        w_ref[:, blocks[k]] = jnp.concatenate([high, low], axis=0)
    weights = w_ref[...]
    (swapped,) = reverse_lanes([weights], rev)
    order = [swapped[JB : 2 * JB], swapped[:JB], swapped[3 * JB :], swapped[2 * JB : 3 * JB]]
    weights_r = jnp.concatenate(order, axis=0).astype(BF)

    table, table_r = table.astype(F32), et_ref[...].astype(F32)
    centre = HALF * BASES
    keep = lax.broadcasted_iota(jnp.int32, (8, chans), 0) < BASES

    def lookup(source, first):
        lines = jnp.where(keep, source[:8], 0.0)
        above, below = jnp.zeros((first, chans), F32), jnp.zeros((4 * JB - first - 8, chans), F32)
        return jnp.concatenate([above, lines, below], axis=0).astype(BF)

    look, look_r = lookup(table, centre), lookup(table_r, JB + centre)
    chunk, mchunk = ext // 10, rows // 24
    for t in range(tiles):
        dst = slice(t * LANE, (t + 1) * LANE)
        for strand, (wr, er) in enumerate(((weights, look), (weights_r, look_r))):
            rhs = jnp.concatenate([wr[:, dst], er[:, dst]], axis=1)
            for i in range(10):
                where = pl.ds(i * chunk, chunk)
                both = dot(a_ref[where, :], rhs)
                value, slope = gelu_doubled(both[:, :LANE])
                x1_refs[strand][t][where, :] = both[:, LANE:] + value
                gp_refs[strand][t][where, :] = slope

        for i in range(24):
            first = i * mchunk
            terms = []
            for j in range(TAPS):
                shift = (j - HALF) * dil
                line = slice(ROW_TAPS1 + j, ROW_TAPS1 + j + 1)
                terms.append(table[line, dst] * x1_refs[0][t][pl.ds(first + REACH + shift, mchunk), :])
                terms.append(table_r[line, dst] * x1_refs[1][t][pl.ds(first + REACH - shift, mchunk), :])
            m_ref[first : first + mchunk, dst] = functools.reduce(jnp.add, terms).astype(BF)

    half = rows // 2
    n_own = pl.cdiv(width, LANE)
    for i in range(2):
        where = pl.ds(i * half, half)
        value, slope = gelu_parts(dot_t(m_ref[where, :], mixl_ref[...]))
        inner = pl.ds(REACH + i * half, half)
        own = jnp.concatenate([x1_refs[0][t][inner, :] for t in range(n_own)], axis=1)[:, :width]
        held[:, where] = (own + value).T.astype(BF)
        s_ref[where, :] = ((cot_ref[where, :].astype(F32) * scale) * slope).astype(BF)
    copy = pltpu.make_async_copy(held, x2_ref, sem)
    copy.start()

    part = t_dot(s_ref[...], m_ref[...]).astype(BF)
    odd = lax.axis_index("seq") % 2 == 1
    near_ref[...] = jnp.where(odd, part[width // 2 :], part[: width // 2])
    far_ref[...] = jnp.where(odd, part[: width // 2], part[width // 2 :])
    copy.wait()


def backward_kernel(n_chan, rows, width, scale, dils, *refs):
    tiles = n_chan * width // LANE
    (hot_ref, mixl_ref, cot_ref, s_ref, e_ref, et_ref), refs = refs[:6], refs[6:]
    x1_refs, refs = (refs[:tiles], refs[tiles : 2 * tiles]), refs[2 * tiles :]
    gp_refs, refs = (refs[:tiles], refs[tiles : 2 * tiles]), refs[2 * tiles :]
    (pb_ref, gt_ref, plain_ref, other_ref), refs = refs[:4], refs[4:]
    p_refs, s0_refs, (g2_ref,) = refs[:tiles], refs[tiles : 2 * tiles], refs[2 * tiles :]
    ext = rows + 2 * REACH
    padded = hot_ref.shape[1]
    dil = dils[1]
    taps_f, taps_r = 0.5 * e_ref[...].astype(F32), 0.5 * et_ref[...].astype(F32)

    edge = 2 * REACH
    n_own = pl.cdiv(width, LANE)
    g2 = cot_ref[...].astype(F32) * scale
    g2_ref[:, :REACH, :] = jnp.zeros((n_own, REACH, LANE), F32)
    g2_ref[:, rows + REACH :, :] = jnp.zeros((n_own, REACH, LANE), F32)
    g2 = jnp.concatenate([g2, jnp.zeros((rows, n_own * LANE - width), F32)], axis=1)
    for t in range(n_own):
        g2_ref[t, REACH : rows + REACH, :] = 0.5 * g2[:, t * LANE : (t + 1) * LANE]

    mchunk, chunk = rows // 12, ext // 10
    for t in range(tiles):
        dst = slice(t * LANE, (t + 1) * LANE)
        p_ref, s0_ref = p_refs[t], s0_refs[t]
        if t % 2 == 0:
            pair = dot(s_ref[...], mixl_ref[:, t * LANE : (t + 2) * LANE])
            pb_ref[:, t * LANE : (t + 2) * LANE] = pair.astype(BF)
        p_ref[:edge, :] = jnp.zeros((edge, LANE), F32)
        p_ref[rows + edge :, :] = jnp.zeros((edge, LANE), F32)
        p_ref[edge : rows + edge, :] = pair[:, (t % 2) * LANE : (t % 2 + 1) * LANE]
        s0_ref[ext:, :] = jnp.zeros((padded - ext, 2 * LANE), BF)
        for i in range(10):
            first = i * chunk
            where = pl.ds(first, chunk)
            fs, rs = [], []
            for j in range(TAPS):
                window = p_ref[pl.ds(first + REACH + (j - HALF) * dil, chunk), :]
                ahead, back = ROW_TAPS1 + j, ROW_TAPS1 + TAPS - 1 - j
                fs.append(taps_f[back : back + 1, dst] * window)
                rs.append(taps_r[ahead : ahead + 1, dst] * window)
            if t < n_own:
                fs.append(g2_ref[t, where, :])
            f, r = functools.reduce(jnp.add, fs), functools.reduce(jnp.add, rs)
            s0_ref[where, :LANE] = (f * gp_refs[0][t][where, :]).astype(BF)
            s0_ref[where, LANE:] = (r * gp_refs[1][t][where, :]).astype(BF)
        both = dot(hot_ref[...], s0_ref[...])
        plain_ref[:, dst], other_ref[:, dst] = both[:, :LANE], both[:, LANE:]

        sums = [None] * (2 * TAPS)
        for i in range(12):
            first = i * mchunk
            here = p_ref[pl.ds(edge + first, mchunk), :]
            for strand in range(2):
                for j in range(TAPS):
                    shift = (j - HALF) * dil * (1 - 2 * strand)
                    prod = here * x1_refs[strand][t][pl.ds(first + REACH + shift, mchunk), :]
                    part = prod.reshape(mchunk // 8, 8, LANE).sum(0)
                    slot = strand * TAPS + j
                    sums[slot] = part if i == 0 else sums[slot] + part
        for strand in range(2):
            lines = [jnp.sum(sums[strand * TAPS + j], axis=0, keepdims=True) for j in range(TAPS)]
            gt_ref[strand, :, dst] = jnp.concatenate(lines + [jnp.zeros((8 - TAPS, LANE), F32)], axis=0)


def collect_kernel(n_chan, width, scale, *refs):
    pks, refs = refs[:n_chan], refs[n_chan:]
    hot1_ref, cot_ref, e_ref, et_ref, pb_ref, gt_ref, plain_ref, other_ref = refs[:8]
    keep_ref, send_ref, dw_ref, st_ref, back_ref, tail_ref = refs[8:]
    chans = n_chan * width
    me, rev = lax.axis_index("chan"), reversal(LANE)
    blocks = [slice(k * width, (k + 1) * width) for k in range(n_chan)]
    table, table_r = e_ref[...], et_ref[...]

    by_tap = dot(hot1_ref[...], pb_ref[...])
    own_letters = dot(hot1_ref[:16, :], cot_ref[...]) * scale
    srow, scol = iotas((8, JB))
    sum_letter = as_bf((scol % BASES == srow) & (scol < TAPS * BASES))
    sum_tap = as_bf((scol // BASES == srow) & (scol < TAPS * BASES))

    def sums_of(sel, x):
        high, rest = split_bf(x)
        return dot(sel, high) + dot(sel, rest)

    sel1 = select_rows("tap1", JB)
    ahead = by_tap[:JB] * dot(sel1, table)
    other = by_tap[JB:] * dot(sel1, table_r)
    turned, other, taps_turned = reverse_wide([other_ref[...], other, gt_ref[1]], rev)
    sums = plain_ref[...] + jnp.concatenate([turned[JB:], turned[:JB]], axis=0)
    dw_ref[...] = sums
    letters = sums_of(sum_letter, ahead + other)
    tail_ref[8:16, :] = gt_ref[0] + taps_turned

    total = jnp.zeros((2 * JB, chans), F32)
    for k in range(n_chan):
        total = total + dot(dw_ref[:, blocks[k]].astype(BF), pks[k][:width, :])
    st_ref[...] = total
    for k, block in enumerate(xor_blocks([st_ref[:, lanes] for lanes in blocks], me)):
        back_ref[:, blocks[k]] = block
    (turned,) = reverse_wide([back_ref[JB:, :]], rev)
    both = back_ref[:JB, :] + turned
    tail_ref[0:8, :] = sums_of(sum_tap, both * dot(select_rows("letter", JB), table))
    letters = letters + sums_of(sum_letter, both * dot(select_rows("tap0", JB), table))
    tail_ref[16:24, :] = letters
    zeros = jnp.zeros((BASES, width), F32)
    own = jnp.concatenate([own_letters[HALF * BASES : (HALF + 1) * BASES, :], zeros], axis=0)
    for kk, lanes in enumerate(blocks):
        place, at = (keep_ref, send_ref)[kk % 2], kk // 2
        letters = tail_ref[16:24, lanes]
        if kk == 0:
            letters = letters + own
        place[at, :ROW_R, :] = jnp.concatenate([dw_ref[:ROW_GE, lanes], letters[:BASES]], axis=0)
        place[at, ROW_R : 2 * ROW_R, :] = dw_ref[JB : JB + ROW_R, lanes]
        place[at, ROW_GT0:, :] = tail_ref[0:16, lanes]


def add_kernel(a_ref, b_ref, first_ref, second_ref):
    first_ref[...] = (a_ref[0] + b_ref[0]).astype(BF)
    second_ref[...] = (a_ref[1] + b_ref[1]).astype(BF)


def finish_kernel(
    n_chan, width, st_ref, sa_ref, sb_ref, near_ref, far_ref, gm_ref, gt_ref, ge_ref, held, sems
):
    me, odd = lax.axis_index("chan"), lax.axis_index("seq") % 2
    half = width // 2
    copies = []

    def send(block, part):
        copies.append(pltpu.make_async_copy(held.at[block, part], gm_ref.at[block, part], sems.at[len(copies)]))
        copies[-1].start()

    for source, turn in ((near_ref, odd), (far_ref, 1 - odd)):
        lines = pl.ds(pl.multiple_of(turn * half, half), half)
        blocks = [source[:, k * width : (k + 1) * width].astype(F32) for k in range(n_chan)]
        for k, part in enumerate(xor_blocks(blocks, me)):
            held[1, lines, k * width : (k + 1) * width] = part
        send(1, lines)

    sums = sa_ref[...].astype(F32) + sb_ref[...].astype(F32)
    fill = jnp.zeros((JB - ROW_GE, width), F32)
    dw = jnp.concatenate([sums[:ROW_GE], fill, sums[ROW_R : ROW_R + ROW_GE], fill], axis=0).astype(BF)
    for i in range(2):
        lines = slice(i * half, (i + 1) * half)
        held[0, lines, :] = t_dot(dw[:, lines], st_ref[: 2 * JB, :])
        send(0, pl.ds(i * half, half))
    for j in range(TAPS):
        gt_ref[j, 0:1, :] = sums[ROW_GT0 + j : ROW_GT0 + j + 1]
        gt_ref[j, 1:2, :] = sums[ROW_GT1 + j : ROW_GT1 + j + 1]
    ge_ref[...] = sums[ROW_GE : ROW_GE + BASES]
    for copy in copies:
        copy.wait()


VMEM = pl.BlockSpec(memory_space=pltpu.VMEM)
SMEM = pl.BlockSpec(memory_space=pltpu.SMEM)
HBM = pl.BlockSpec(memory_space=pltpu.HBM)


def in_hbm(x):
    return pltpu.with_memory_space_constraint(x, pltpu.HBM)


def call(kernel, in_specs, out_shape, out_specs, scratch, limit, cost):
    flops, moved = cost
    return pl.pallas_call(
        kernel,
        out_shape=out_shape,
        in_specs=in_specs,
        out_specs=out_specs,
        scratch_shapes=scratch,
        compiler_params=pltpu.CompilerParams(vmem_limit_bytes=limit << 20),
        cost_estimate=pl.CostEstimate(flops=flops, bytes_accessed=moved, transcendentals=0),
    )


def flip_bits(x, axis, mask):
    return lax.ppermute(x, axis, [(i, i ^ mask) for i in range(lax.axis_size(axis))])


def body(tokens, cotangent, embed, taps, mix, dilations):
    rows, width = cotangent.shape
    n_seq, n_chan = lax.axis_size("seq"), lax.axis_size("chan")
    chans = n_chan * width
    tiles = chans // LANE
    ext = rows + 2 * REACH
    padded = pl.cdiv(ext, LANE) * LANE
    edge = 2 * REACH
    own_tiles = pl.cdiv(width, LANE)
    scale = 1.0 / math.sqrt(rows * n_seq)
    shape = jax.ShapeDtypeStruct
    mix_t = jnp.swapaxes(mix, 1, 2)

    pk, letters = call(
        functools.partial(pack_kernel, width),
        [HBM] * 4,
        [shape((width + TABLE, chans), BF), shape((1, rows), jnp.int32)],
        [VMEM] * 2,
        [
            pltpu.VMEM((BASES, width), BF),
            pltpu.VMEM((TAPS, BLOCKS, width), BF),
            pltpu.SemaphoreType.DMA((4,)),
        ],
        8,
        (0, width * chans * 4),
    )(in_hbm(mix_t), in_hbm(embed), in_hbm(jnp.swapaxes(taps, 0, 1)), in_hbm(tokens))

    seq_bits = n_seq.bit_length() - 1
    for bit in range(0, seq_bits, 2):
        masks = [k << bit for k in range(1, 1 << min(2, seq_bits - bit))]
        letters = jnp.concatenate([letters] + [flip_bits(letters, "seq", m) for m in masks], axis=0)

    mixl, cot = call(
        functools.partial(local_kernel, n_chan, width),
        [HBM, HBM],
        [shape((width, chans), BF), shape((rows, width), BF)],
        [VMEM] * 2,
        [
            pltpu.VMEM((width, chans), BF),
            pltpu.VMEM((width, rows), BF),
            pltpu.SemaphoreType.DMA((2,)),
        ],
        16,
        (1 << 20, 1 << 20),
    )(in_hbm(mix_t), in_hbm(cotangent.T))

    pks = [pk]
    for bit in reversed(range(n_chan.bit_length() - 1)):
        ready = [pks[0]] + [lax.optimization_barrier((p, letters, mixl, cot))[0] for p in pks[1:]]
        moved = [flip_bits(p, "chan", 1 << bit) for p in ready]
        pks = [q for pair in zip(pks, moved) for q in pair]

    hot_t, hot, hot1 = call(
        functools.partial(prep_kernel, n_seq, rows),
        [SMEM, VMEM],
        [shape((padded, 4 * JB), BF), shape((2 * JB, padded), BF), shape((2 * JB, rows), BF)],
        [VMEM] * 3,
        [],
        16,
        (1 << 20, 1 << 20),
    )(dilations, letters)

    rows_ext = shape((ext, LANE), F32)
    x2, near, far, s1, stack, table, table_r, *strands = call(
        functools.partial(forward_kernel, n_chan, rows, width, scale),
        [SMEM] + [VMEM] * (n_chan + 3),
        [
            shape((width, rows), BF),
            shape((width // 2, chans), BF),
            shape((width // 2, chans), BF),
            shape((rows, width), BF),
            shape((4 * JB, chans), BF),
            shape((TABLE, chans), BF),
            shape((TABLE, chans), BF),
        ]
        + [rows_ext] * (4 * tiles),
        [HBM] + [VMEM] * (6 + 4 * tiles),
        [
            pltpu.VMEM((4 * JB, chans), BF),
            pltpu.VMEM((4 * JB, chans), BF),
            pltpu.VMEM((rows, chans), BF),
            pltpu.VMEM((width, rows), BF),
            pltpu.SemaphoreType.DMA,
        ],
        32,
        (3 << 30, 8 << 20),
    )(dilations, *pks, hot_t, mixl, cot)

    arrived = flip_bits(far, "seq", 1)
    pb, gt, plain, other = call(
        functools.partial(backward_kernel, n_chan, rows, width, scale),
        [SMEM] + [VMEM] * (6 + 4 * tiles),
        [
            shape((rows, chans), BF),
            shape((2, 8, chans), F32),
            shape((2 * JB, chans), F32),
            shape((2 * JB, chans), F32),
        ],
        [VMEM] * 4,
        [pltpu.VMEM((rows + 2 * edge, LANE), F32)] * tiles
        + [pltpu.VMEM((padded, 2 * LANE), BF)] * tiles
        + [pltpu.VMEM((own_tiles, ext, LANE), F32)],
        40,
        (3 << 30, 8 << 20),
    )(dilations, hot, mixl, cot, s1, table, table_r, *strands)

    def rounded_sum(a, b):
        return lax.optimization_barrier((a.astype(F32) + b.astype(F32)).astype(BF))

    g_mine = rounded_sum(near, lax.optimization_barrier((arrived, plain))[0])
    gt = lax.optimization_barrier((gt, g_mine))[0]
    keep, send = call(
        functools.partial(collect_kernel, n_chan, width, scale),
        [VMEM] * (n_chan + 8),
        [shape((n_chan // 2, SUMS, width), F32)] * 2,
        [VMEM] * 2,
        [
            pltpu.VMEM((2 * JB, chans), F32),
            pltpu.VMEM((2 * JB, chans), F32),
            pltpu.VMEM((2 * JB, chans), F32),
            pltpu.VMEM((24, chans), F32),
        ],
        24,
        (1 << 20, 1 << 16),
    )(*pks, hot1, cot, table, table_r, pb, gt, plain, other)

    for bit in range(1, seq_bits):
        g_mine = rounded_sum(g_mine, flip_bits(g_mine, "seq", 1 << bit))
    g_other = flip_bits(g_mine, "seq", 1)
    last = n_chan.bit_length() - 2
    mine, theirs = keep, flip_bits(send, "chan", 1)
    for bit in range(1, last):
        mine = mine + theirs
        mine, theirs = mine[0::2], flip_bits(mine[1::2], "chan", 1 << bit)
    s_mine = call(
        add_kernel,
        [VMEM] * 2,
        [shape((SUMS, width), BF)] * 2,
        [VMEM] * 2,
        [],
        8,
        (0, 0),
    )(mine, theirs)
    across = flip_bits(s_mine[1], "chan", 1 << last)
    along = flip_bits(s_mine[0], "seq", 1)
    places = [(i, j) for i in range(n_seq) for j in range(n_chan)]
    pairs = [(i * n_chan + j, (i ^ 1) * n_chan + (j ^ (1 << last))) for i, j in places]
    corner = lax.ppermute(s_mine[1], ("seq", "chan"), pairs)
    here, there = (s_mine[0], across), (along, corner)
    s_mine = rounded_sum(*(a.astype(F32) + b.astype(F32) for a, b in (here, there)))
    for bit in range(1, seq_bits):
        s_other = flip_bits(s_mine, "seq", 1 << bit)
        if bit < seq_bits - 1:
            s_mine = rounded_sum(s_mine, s_other)

    grad_mix, grad_taps, grad_embed = call(
        functools.partial(finish_kernel, n_chan, width),
        [VMEM] * 5,
        [
            shape((BLOCKS, width, chans), F32),
            shape((TAPS, BLOCKS, width), F32),
            shape((BASES, width), F32),
        ],
        [HBM, VMEM, VMEM],
        [pltpu.VMEM((BLOCKS, width, chans), F32), pltpu.SemaphoreType.DMA((4,))],
        16,
        (1 << 24, 1 << 21),
    )(stack, s_mine, s_other, g_mine, g_other)
    return x2.T, jnp.swapaxes(grad_mix, 1, 2), jnp.swapaxes(grad_taps, 0, 1), grad_embed


def solution(mesh):
    in_specs = (
        P(("groups", "seq")),
        P(("groups", "seq"), "chan"),
        P(None, "chan"),
        P(None, None, "chan"),
        P(None, None, "chan"),
        P(),
    )
    out_specs = (
        P(("groups", "seq"), "chan"),
        P("groups", None, "chan"),
        P("groups", None, "chan"),
        P("groups", "chan"),
    )
    return jax.shard_map(body, mesh=mesh, in_specs=in_specs, out_specs=out_specs, check_vma=False)
```
